256 devices in a mesh: row: 16 (over z, core), col: 8 (over x_hi, y), feat: 2 (over x_lo).
Axes of the slice: x: 4 (x_hi: 2, x_lo: 2; x = x_hi * 2 + x_lo), y: 4, z: 8, core: 2. Of those that a mesh axis runs over, the one named last changes fastest.
Arguments:
- features: bfloat16 [65536, 256], P(('col', 'row'), 'feat'), may hold values from -6 to 6
- tile_rows: int32 [16, 8, 256], P('row', 'col'), may hold values from 0 to 31, as said below
- tile_cols: int32 [16, 8, 256], P('row', 'col'), may hold values from 0 to 63
- tile_count: int32 [16, 8], P('row', 'col'), may hold values from 64 to 256, as said below
- tile_values: bfloat16 [16, 8, 256, 128, 128], P('row', 'col'), may hold values from -0.21875 to 0.21875
- weights: bfloat16 [256, 256], replicated, may hold values from -0.375 to 0.375
- cotangent: bfloat16 [65536, 256], P(('row', 'col'), 'feat'), may hold values from -6 to 6
Outputs:
- activated: bfloat16 [65536, 256], P(('row', 'col'), 'feat')
- feature_grad: bfloat16 [65536, 256], P(('col', 'row'), 'feat')
- weight_grad: float32 [256, 256], P('feat')
The draws below stay inside these ranges and needn't reach their ends.
Inputs may be any that keep to these rules, and one draw needn't show every extreme that they name: `tile_rows`: block rows of a cell, unevenly loaded. `tile_count`: some cell has all 256 slots live.
All inputs are finite; a program needn't handle non-finite values.
Results may differ from the reference program's by a relative error of at most 0.027.
Values may be sent and summed in bfloat16 or wider, within the bound.
A program may use at most 128 MiB of HBM per device.

```python
import jax
import jax.numpy as jnp
from jax import lax

F = 256
TILE = 128
BLK = 4
TILES = 256
NODES = 65536
RB = 32
CB = 64
N_ROW = 16
N_COL = 8


def draw_tile_rows(key, part):
    first_key, second_key, order_key = jax.random.split(jax.random.fold_in(key, 11), 3)
    first = jax.random.randint(first_key, (N_ROW, N_COL, TILES), 0, BLK * N_COL)
    second = jax.random.randint(second_key, (N_ROW, N_COL, TILES), 0, BLK * N_COL)
    lower = jnp.minimum(first, second)
    ordering = jax.random.permutation(order_key, BLK * N_COL)
    return ordering[lower].astype(jnp.int32)


def draw_tile_cols(key, part):
    return jax.random.randint(jax.random.fold_in(key, 12), (N_ROW, N_COL, TILES), 0, BLK * N_ROW).astype(jnp.int32)


def draw_tile_count(key, part):
    count_key, pick_key = jax.random.split(jax.random.fold_in(key, 13), 2)
    counts = jax.random.randint(count_key, (N_ROW * N_COL,), TILES // 4, TILES + 1)
    chosen = jax.random.randint(pick_key, (), 0, N_ROW * N_COL)
    filled = jnp.where(jnp.arange(N_ROW * N_COL) == chosen, TILES, counts)
    return filled.reshape(N_ROW, N_COL).astype(jnp.int32)


def shard_levels(stream_key, shape, cuts, low, high):
    gain = 1.0
    for axis_at, shards_of in cuts:
        draws = jax.random.uniform(jax.random.fold_in(jax.random.fold_in(stream_key, 6), axis_at), (shards_of,), jnp.float32, low / len(cuts), high / len(cuts))
        gain = gain * jnp.repeat(jnp.exp(draws), shape[axis_at] // shards_of).reshape((-1,) + (1,) * (len(shape) - 1 - axis_at))
    return gain


def noise(own_key, extent, scale, bound, shards=(), dtype=jnp.bfloat16):
    array = scale * jax.random.normal(own_key, extent, jnp.float32)
    if shards:
        array = array * shard_levels(own_key, extent, shards, -0.22, 0.18)
    return jnp.clip(array, -bound, bound).astype(dtype)


def setup_inputs(seed: int = 0) -> dict:
    keys = jax.random.split(jax.random.key(seed), 8)
    return {
        "features": noise(keys[0], (NODES, F), 1.0, 6.0, ((0, 128), (1, 2))),
        "tile_rows": draw_tile_rows(jax.random.fold_in(keys[7], 71), 0),
        "tile_cols": draw_tile_cols(jax.random.fold_in(keys[7], 71), 0),
        "tile_count": draw_tile_count(jax.random.fold_in(keys[7], 71), 0),
        "tile_values": noise(keys[4], (N_ROW, N_COL, TILES, TILE, TILE), ((BLK / (0.6 * TILES * TILE)) ** 0.5), 0.21875, ((0, 16), (1, 8))),
        "weights": noise(keys[5], (F, F), F ** -0.5, 0.375),
        "cotangent": noise(keys[6], (NODES, F), 1.0, 6.0, ((0, 128), (1, 2))),
    }


def round_once(values):
    rounded = lax.optimization_barrier(values.astype(jnp.bfloat16))
    return rounded.astype(jnp.float32)


def forward_cell(cell_tiles, cell_rows, cell_cols, cell_count, group_feats):
    live_mask = (jnp.arange(TILES) < cell_count).astype(jnp.float32)
    gathered = group_feats[cell_cols].astype(jnp.float32)
    products = jnp.einsum("tij,tjf->tif", cell_tiles.astype(jnp.float32), gathered) * live_mask[:, None, None]
    partial_value = jnp.zeros((RB, TILE, F), jnp.float32).at[cell_rows].add(products)
    return round_once(partial_value)


def backward_cell(cell_tiles, cell_rows, cell_cols, cell_count, group_spread):
    live_mask = (jnp.arange(TILES) < cell_count).astype(jnp.float32)
    gathered = group_spread[cell_rows].astype(jnp.float32)
    products = jnp.einsum("tji,tjf->tif", cell_tiles.astype(jnp.float32), gathered) * live_mask[:, None, None]
    partial_value = jnp.zeros((CB, TILE, F), jnp.float32).at[cell_cols].add(products)
    return round_once(partial_value)


def reference(features, tile_rows, tile_cols, tile_count, tile_values, weights, cotangent):
    feat_groups = features.reshape(N_COL, CB, TILE, F)

    def over_rows(unused, inputs):
        row_tiles, row_rows, row_cols, row_count = inputs

        def over_cols(running, cell_in):
            cell_tiles, cell_rows, cell_cols, cell_count, group_feats = cell_in
            return running + forward_cell(cell_tiles, cell_rows, cell_cols, cell_count, group_feats), None

        running, _ = lax.scan(over_cols, jnp.zeros((RB, TILE, F), jnp.float32),
                              (row_tiles, row_rows, row_cols, row_count, feat_groups))
        return unused, running

    _, stacked = lax.scan(over_rows, jnp.float32(0.0), (tile_values, tile_rows, tile_cols, tile_count))
    aggregated = stacked.reshape(NODES, F).astype(jnp.bfloat16)
    hidden = jnp.dot(aggregated, weights, preferred_element_type=jnp.float32)
    negative = jnp.minimum(hidden, 0.0)
    activated = jnp.where(hidden > 0, hidden, jnp.expm1(negative)).astype(jnp.bfloat16)
    slope_factor = jnp.where(hidden > 0, 1.0, jnp.exp(negative))
    grad_out = (cotangent.astype(jnp.float32) * slope_factor).astype(jnp.bfloat16)
    weight_grad = jnp.dot(aggregated.T, grad_out, preferred_element_type=jnp.float32) * (NODES ** -0.5)
    spread = jnp.dot(grad_out, weights.T, preferred_element_type=jnp.float32).astype(jnp.bfloat16)
    spread_groups = spread.reshape(N_ROW, RB, TILE, F)

    def back_rows(running, inputs):
        row_tiles, row_rows, row_cols, row_count, group_spread = inputs

        def back_cols(inner, cell_in):
            cell_tiles, cell_rows, cell_cols, cell_count, col_index = cell_in
            term = backward_cell(cell_tiles, cell_rows, cell_cols, cell_count, group_spread)
            return inner.at[col_index].add(term), None

        running, _ = lax.scan(back_cols, running,
                              (row_tiles, row_rows, row_cols, row_count, jnp.arange(N_COL).astype(jnp.int32)))
        return running, None

    back_total, _ = lax.scan(back_rows, jnp.zeros((N_COL, CB, TILE, F), jnp.float32),
                             (tile_values, tile_rows, tile_cols, tile_count, spread_groups))
    feature_grad = back_total.reshape(NODES, F).astype(jnp.bfloat16)
    return activated, feature_grad, weight_grad
```

```python
import jax
import jax.numpy as jnp
from jax import lax
from jax.sharding import PartitionSpec as P


def shards(features, tile_rows, tile_cols, tile_count, tile_values, weights, cotangent):
    width = tile_values.shape[-1]
    slots = tile_values.shape[2]
    local_tiles = tile_values[0, 0]
    block_rows = tile_rows[0, 0]
    block_cols = tile_cols[0, 0]
    live_mask = (jnp.arange(slots) < tile_count[0, 0]).astype(jnp.float32)
    n_rowdev = lax.axis_size("row")
    n_coldev = lax.axis_size("col")
    local_blocks = features.shape[0] // width
    feat_half = features.shape[1]
    feat_index = lax.axis_index("feat")
    row_blocks = local_blocks * n_coldev
    col_blocks = local_blocks * n_rowdev
    node_total = features.shape[0] * n_rowdev * n_coldev
    panel = lax.all_gather(features, "row", axis=0, tiled=True)
    gathered = panel.reshape(col_blocks, width, feat_half)[block_cols]
    products = jnp.einsum("tij,tjf->tif", local_tiles, gathered, preferred_element_type=jnp.float32)
    products = products * live_mask[:, None, None]
    partial_value = (
        jnp.zeros((row_blocks, width, feat_half), jnp.float32).at[block_rows].add(products)
    )
    summed = lax.psum_scatter(
        partial_value.reshape(row_blocks * width, feat_half).astype(jnp.bfloat16),
        "col",
        scatter_dimension=0,
        tiled=True,
    )
    weight_rows = lax.dynamic_slice_in_dim(weights, feat_index * feat_half, feat_half, 0)
    mix_term = jnp.dot(summed, weight_rows, preferred_element_type=jnp.float32)
    hidden = lax.psum_scatter(
        mix_term.astype(jnp.bfloat16), "feat", scatter_dimension=1, tiled=True
    ).astype(jnp.float32)
    negative = jnp.minimum(hidden, 0.0)
    activated = jnp.where(hidden > 0, hidden, jnp.expm1(negative)).astype(jnp.bfloat16)
    slope_factor = jnp.where(hidden > 0, 1.0, jnp.exp(negative))
    grad_out = (cotangent.astype(jnp.float32) * slope_factor).astype(jnp.bfloat16)
    grad_whole = lax.all_gather(grad_out, "feat", axis=1, tiled=True)
    weight_term = lax.dot_general(
        summed, grad_whole, (((0,), (0,)), ((), ())), preferred_element_type=jnp.float32
    )
    n_feat = lax.axis_size("feat")
    slots = jnp.zeros((n_feat,) + weight_term.shape, jnp.float32)
    slots = lax.dynamic_update_slice_in_dim(slots, weight_term[None], feat_index, 0)
    slots = lax.psum(slots, ("row", "col", "feat"))
    weight_grad = lax.dynamic_index_in_dim(slots, feat_index, 0, keepdims=False) * node_total ** (-0.5)
    spread = lax.dot_general(
        grad_whole, weight_rows, (((1,), (1,)), ((), ())), preferred_element_type=jnp.float32
    ).astype(jnp.bfloat16)
    spread_panel = lax.all_gather(spread, "col", axis=0, tiled=True)
    spread_blocks = spread_panel.reshape(row_blocks, width, feat_half)[block_rows]
    back_products = jnp.einsum(
        "tji,tjf->tif", local_tiles, spread_blocks, preferred_element_type=jnp.float32
    )
    back_products = back_products * live_mask[:, None, None]
    back_partial = (
        jnp.zeros((col_blocks, width, feat_half), jnp.float32).at[block_cols].add(back_products)
    )
    back_summed = lax.psum_scatter(
        back_partial.reshape(col_blocks * width, feat_half).astype(jnp.bfloat16),
        "row",
        scatter_dimension=0,
        tiled=True,
    )
    return (activated, back_summed, weight_grad)


def solution(mesh):
    return jax.shard_map(
        shards,
        mesh=mesh,
        in_specs=(
            P(("col", "row"), "feat"),
            P("row", "col", None),
            P("row", "col", None),
            P("row", "col"),
            P("row", "col", None, None, None),
            P(),
            P(("row", "col"), "feat"),
        ),
        out_specs=(P(("row", "col"), "feat"), P(("col", "row"), "feat"), P("feat", None)),
        check_vma=False,
    )
```

```python
import functools

import jax
import jax.numpy as jnp
from jax import lax
from jax.experimental import pallas as pl
from jax.experimental.pallas import tpu as pltpu
from jax.sharding import PartitionSpec as P

GROUP = 8


def tile_kernel(transpose, rows_ref, cols_ref, count_ref, tiles_ref, panel_ref, out_ref, acc_ref):
    step = pl.program_id(0)
    width = tiles_ref.shape[-1]
    count = count_ref[0]

    @pl.when(step == 0)
    def _():
        acc_ref[...] = jnp.zeros_like(acc_ref)

    for j in range(GROUP):
        slot = step * GROUP + j

        @pl.when(slot < count)
        def _():
            src = rows_ref[slot] if transpose else cols_ref[slot]
            dst = cols_ref[slot] if transpose else rows_ref[slot]
            block = panel_ref[pl.ds(pl.multiple_of(src * width, width), width), :]
            tile = tiles_ref[j]
            if transpose:
                term = lax.dot_general(tile, block, (((0,), (0,)), ((), ())),
                                       preferred_element_type=jnp.float32)
            else:
                term = jnp.dot(tile, block, preferred_element_type=jnp.float32)
            rows = pl.ds(pl.multiple_of(dst * width, width), width)
            acc_ref[rows, :] += term

    @pl.when(step == pl.num_programs(0) - 1)
    def _():
        out_ref[...] = acc_ref[...].astype(out_ref.dtype)


def tile_products(tiles, rows, cols, count, panel, out_blocks, transpose):
    slots, width, _ = tiles.shape
    feat = panel.shape[1]
    steps = slots // GROUP

    def tiles_map(i, rows_ref, cols_ref, count_ref):
        last = jnp.maximum(count_ref[0] - 1, 0) // GROUP
        return (jnp.minimum(i, last), 0, 0)

    return pl.pallas_call(
        functools.partial(tile_kernel, transpose),
        out_shape=jax.ShapeDtypeStruct((out_blocks * width, feat), jnp.bfloat16),
        grid_spec=pltpu.PrefetchScalarGridSpec(
            num_scalar_prefetch=3,
            grid=(steps,),
            in_specs=[
                pl.BlockSpec((GROUP, width, width), tiles_map),
                pl.BlockSpec(panel.shape, lambda i, *_: (0, 0)),
            ],
            out_specs=pl.BlockSpec((out_blocks * width, feat), lambda i, *_: (0, 0)),
            scratch_shapes=[pltpu.VMEM((out_blocks * width, feat), jnp.float32)],
        ),
        compiler_params=pltpu.CompilerParams(dimension_semantics=("arbitrary",)),
        cost_estimate=pl.CostEstimate(
            flops=2 * slots * width * width * feat,
            bytes_accessed=tiles.size * 2 + panel.size * 2 + out_blocks * width * feat * 2,
            transcendentals=0,
        ),
    )(rows, cols, count, tiles, panel)


def shards(features, tile_rows, tile_cols, tile_count, tile_values, weights, cotangent):
    width = tile_values.shape[-1]
    local_tiles = tile_values[0, 0]
    block_rows = tile_rows[0, 0]
    block_cols = tile_cols[0, 0]
    count = tile_count[0, 0].reshape(1)
    n_rowdev = lax.axis_size("row")
    n_coldev = lax.axis_size("col")
    local_blocks = features.shape[0] // width
    feat_half = features.shape[1]
    feat_index = lax.axis_index("feat")
    row_blocks = local_blocks * n_coldev
    col_blocks = local_blocks * n_rowdev
    node_total = features.shape[0] * n_rowdev * n_coldev
    panel = lax.all_gather(features, "row", axis=0, tiled=True)
    partial_value = tile_products(local_tiles, block_rows, block_cols, count, panel,
                                  row_blocks, transpose=False)
    summed = lax.psum_scatter(partial_value, "col", scatter_dimension=0, tiled=True)
    weight_rows = lax.dynamic_slice_in_dim(weights, feat_index * feat_half, feat_half, 0)
    mix_term = jnp.dot(summed, weight_rows, preferred_element_type=jnp.float32)
    hidden = lax.psum_scatter(
        mix_term.astype(jnp.bfloat16), "feat", scatter_dimension=1, tiled=True
    ).astype(jnp.float32)
    negative = jnp.minimum(hidden, 0.0)
    activated = jnp.where(hidden > 0, hidden, jnp.expm1(negative)).astype(jnp.bfloat16)
    slope_factor = jnp.where(hidden > 0, 1.0, jnp.exp(negative))
    grad_out = (cotangent.astype(jnp.float32) * slope_factor).astype(jnp.bfloat16)
    grad_whole = lax.all_gather(grad_out, "feat", axis=1, tiled=True)
    weight_term = lax.dot_general(
        summed, grad_whole, (((0,), (0,)), ((), ())), preferred_element_type=jnp.float32
    )
    n_feat = lax.axis_size("feat")
    slots = jnp.zeros((n_feat,) + weight_term.shape, jnp.float32)
    slots = lax.dynamic_update_slice_in_dim(slots, weight_term[None], feat_index, 0)
    slots = lax.psum(slots, ("row", "col", "feat"))
    weight_grad = lax.dynamic_index_in_dim(slots, feat_index, 0, keepdims=False) * node_total ** (-0.5)
    spread = lax.dot_general(
        grad_whole, weight_rows, (((1,), (1,)), ((), ())), preferred_element_type=jnp.float32
    ).astype(jnp.bfloat16)
    spread_panel = lax.all_gather(spread, "col", axis=0, tiled=True)
    back_partial = tile_products(local_tiles, block_rows, block_cols, count, spread_panel,
                                 col_blocks, transpose=True)
    back_summed = lax.psum_scatter(back_partial, "row", scatter_dimension=0, tiled=True)
    return (activated, back_summed, weight_grad)


def solution(mesh):
    return jax.shard_map(
        shards,
        mesh=mesh,
        in_specs=(
            P(("col", "row"), "feat"),
            P("row", "col", None),
            P("row", "col", None),
            P("row", "col"),
            P("row", "col", None, None, None),
            P(),
            P(("row", "col"), "feat"),
        ),
        out_specs=(P(("row", "col"), "feat"), P(("col", "row"), "feat"), P("feat", None)),
        check_vma=False,
    )
```

```python
import functools

import jax
import jax.numpy as jnp
from jax import lax
from jax.experimental import pallas as pl
from jax.experimental.pallas import tpu as pltpu
from jax.sharding import PartitionSpec as P

GROUP = 8


def tile_kernel(transpose, rows_ref, cols_ref, count_ref, tiles_ref, panel_ref, out_ref, acc_ref):
    step = pl.program_id(0)
    width = tiles_ref.shape[-1]
    count = count_ref[0]

    @pl.when(step == 0)
    def _():
        acc_ref[...] = jnp.zeros_like(acc_ref)

    for j in range(GROUP):
        slot = step * GROUP + j

        @pl.when(slot < count)
        def _():
            src = rows_ref[slot] if transpose else cols_ref[slot]
            dst = cols_ref[slot] if transpose else rows_ref[slot]
            block = panel_ref[pl.ds(pl.multiple_of(src * width, width), width), :]
            tile = tiles_ref[j]
            if transpose:
                term = lax.dot_general(tile, block, (((0,), (0,)), ((), ())),
                                       preferred_element_type=jnp.float32)
            else:
                term = jnp.dot(tile, block, preferred_element_type=jnp.float32)
            rows = pl.ds(pl.multiple_of(dst * width, width), width)
            acc_ref[rows, :] += term

    @pl.when(step == pl.num_programs(0) - 1)
    def _():
        out_ref[...] = acc_ref[...].astype(out_ref.dtype)


def tile_products(tiles, rows, cols, count, panel, out_blocks, transpose):
    slots, width, _ = tiles.shape
    feat = panel.shape[1]
    steps = slots // GROUP

    def tiles_map(i, rows_ref, cols_ref, count_ref):
        last = jnp.maximum(count_ref[0] - 1, 0) // GROUP
        return (jnp.minimum(i, last), 0, 0)

    return pl.pallas_call(
        functools.partial(tile_kernel, transpose),
        out_shape=jax.ShapeDtypeStruct((out_blocks * width, feat), jnp.bfloat16),
        grid_spec=pltpu.PrefetchScalarGridSpec(
            num_scalar_prefetch=3,
            grid=(steps,),
            in_specs=[
                pl.BlockSpec((GROUP, width, width), tiles_map),
                pl.BlockSpec(panel.shape, lambda i, *_: (0, 0)),
            ],
            out_specs=pl.BlockSpec((out_blocks * width, feat), lambda i, *_: (0, 0)),
            scratch_shapes=[pltpu.VMEM((out_blocks * width, feat), jnp.float32)],
        ),
        compiler_params=pltpu.CompilerParams(dimension_semantics=("arbitrary",)),
        cost_estimate=pl.CostEstimate(
            flops=2 * slots * width * width * feat,
            bytes_accessed=tiles.size * 2 + panel.size * 2 + out_blocks * width * feat * 2,
            transcendentals=0,
        ),
    )(rows, cols, count, tiles, panel)


def mesh_coords(axis, peer):
    return tuple(peer if name == axis else lax.axis_index(name) for name in ("row", "col", "feat"))


def exchange_kernel(axis, mode, x_ref, o_ref, *scratch):
    n = lax.axis_size(axis)
    me = lax.axis_index(axis)
    if mode == "gather":
        recv_ref, (send_sems, recv_sems) = o_ref, scratch
    else:
        recv_ref, send_sems, recv_sems = scratch
    barrier = pltpu.get_barrier_semaphore()
    for d in range(1, n):
        peer = lax.rem(me + d, n)
        pl.semaphore_signal(barrier, inc=1, device_id=mesh_coords(axis, peer),
                            device_id_type=pl.DeviceIdType.MESH)
    pl.semaphore_wait(barrier, n - 1)
    copies = []
    for d in range(1, n):
        peer = lax.rem(me + d, n)
        src = x_ref if mode == "gather" else x_ref.at[peer]
        copy = pltpu.make_async_remote_copy(
            src_ref=src, dst_ref=recv_ref.at[me], send_sem=send_sems.at[d],
            recv_sem=recv_sems.at[me], device_id=mesh_coords(axis, peer),
            device_id_type=pl.DeviceIdType.MESH)
        copy.start()
        copies.append(copy)
    if mode == "gather":
        o_ref[me] = x_ref[...]
    else:
        total = x_ref[me].astype(jnp.float32)
    for d in range(1, n):
        src_dev = lax.rem(me + n - d, n)
        incoming = pltpu.make_async_remote_copy(
            src_ref=recv_ref.at[src_dev], dst_ref=recv_ref.at[src_dev], send_sem=send_sems.at[d],
            recv_sem=recv_sems.at[src_dev], device_id=mesh_coords(axis, src_dev),
            device_id_type=pl.DeviceIdType.MESH)
        incoming.wait_recv()
        if mode != "gather":
            total = total + recv_ref[src_dev].astype(jnp.float32)
    for copy in copies:
        copy.wait_send()
    if mode != "gather":
        o_ref[...] = total.astype(o_ref.dtype)


def exchange(x, axis, mode, collective_id):
    n = lax.axis_size(axis)
    if mode == "gather":
        out_shape = (n,) + x.shape
        scratch = []
    else:
        out_shape = x.shape[1:]
        scratch = [pltpu.VMEM(x.shape, x.dtype)]
    scratch += [pltpu.SemaphoreType.DMA((n,)), pltpu.SemaphoreType.DMA((n,))]
    return pl.pallas_call(
        functools.partial(exchange_kernel, axis, mode),
        out_shape=jax.ShapeDtypeStruct(out_shape, x.dtype),
        in_specs=[pl.BlockSpec(memory_space=pltpu.VMEM)],
        out_specs=pl.BlockSpec(memory_space=pltpu.VMEM),
        scratch_shapes=scratch,
        compiler_params=pltpu.CompilerParams(collective_id=collective_id, has_side_effects=True),
    )(x)


def shards(features, tile_rows, tile_cols, tile_count, tile_values, weights, cotangent):
    width = tile_values.shape[-1]
    local_tiles = tile_values[0, 0]
    block_rows = tile_rows[0, 0]
    block_cols = tile_cols[0, 0]
    count = tile_count[0, 0].reshape(1)
    n_rowdev = lax.axis_size("row")
    n_coldev = lax.axis_size("col")
    local_blocks = features.shape[0] // width
    feat_half = features.shape[1]
    feat_index = lax.axis_index("feat")
    row_blocks = local_blocks * n_coldev
    col_blocks = local_blocks * n_rowdev
    node_total = features.shape[0] * n_rowdev * n_coldev
    panel = exchange(features, "row", "gather", 0).reshape(-1, feat_half)
    partial_value = tile_products(local_tiles, block_rows, block_cols, count, panel,
                                  row_blocks, transpose=False)
    summed = exchange(partial_value.reshape(n_coldev, -1, feat_half), "col", "scatter", 1)
    weight_rows = lax.dynamic_slice_in_dim(weights, feat_index * feat_half, feat_half, 0)
    mix_term = jnp.dot(summed, weight_rows, preferred_element_type=jnp.float32)
    hidden = lax.psum_scatter(
        mix_term.astype(jnp.bfloat16), "feat", scatter_dimension=1, tiled=True
    ).astype(jnp.float32)
    negative = jnp.minimum(hidden, 0.0)
    activated = jnp.where(hidden > 0, hidden, jnp.expm1(negative)).astype(jnp.bfloat16)
    slope_factor = jnp.where(hidden > 0, 1.0, jnp.exp(negative))
    grad_out = (cotangent.astype(jnp.float32) * slope_factor).astype(jnp.bfloat16)
    grad_whole = lax.all_gather(grad_out, "feat", axis=1, tiled=True)
    weight_term = lax.dot_general(
        summed, grad_whole, (((0,), (0,)), ((), ())), preferred_element_type=jnp.float32
    )
    n_feat = lax.axis_size("feat")
    slots = jnp.zeros((n_feat,) + weight_term.shape, jnp.float32)
    slots = lax.dynamic_update_slice_in_dim(slots, weight_term[None], feat_index, 0)
    slots = lax.psum(slots, ("row", "col", "feat"))
    weight_grad = lax.dynamic_index_in_dim(slots, feat_index, 0, keepdims=False) * node_total ** (-0.5)
    spread = lax.dot_general(
        grad_whole, weight_rows, (((1,), (1,)), ((), ())), preferred_element_type=jnp.float32
    ).astype(jnp.bfloat16)
    spread_panel = exchange(spread, "col", "gather", 2).reshape(-1, feat_half)
    back_partial = tile_products(local_tiles, block_rows, block_cols, count, spread_panel,
                                 col_blocks, transpose=True)
    back_summed = exchange(back_partial.reshape(n_rowdev, -1, feat_half), "row", "scatter", 3)
    return (activated, back_summed, weight_grad)


def solution(mesh):
    return jax.shard_map(
        shards,
        mesh=mesh,
        in_specs=(
            P(("col", "row"), "feat"),
            P("row", "col", None),
            P("row", "col", None),
            P("row", "col"),
            P("row", "col", None, None, None),
            P(),
            P(("row", "col"), "feat"),
        ),
        out_specs=(P(("row", "col"), "feat"), P(("col", "row"), "feat"), P("feat", None)),
        check_vma=False,
    )
```

```python
import functools

import jax
import jax.numpy as jnp
from jax import lax
from jax.experimental import pallas as pl
from jax.experimental.pallas import tpu as pltpu
from jax.sharding import PartitionSpec as P

GROUP = 8


def tile_kernel(transpose, rows_ref, cols_ref, count_ref, tiles_ref, panel_ref, out_ref, acc_ref):
    step = pl.program_id(0)
    width = tiles_ref.shape[-1]
    count = count_ref[0]

    @pl.when(step == 0)
    def _():
        acc_ref[...] = jnp.zeros_like(acc_ref)

    for j in range(GROUP):
        slot = step * GROUP + j

        @pl.when(slot < count)
        def _():
            src = rows_ref[slot] if transpose else cols_ref[slot]
            dst = cols_ref[slot] if transpose else rows_ref[slot]
            block = panel_ref[pl.ds(pl.multiple_of(src * width, width), width), :]
            tile = tiles_ref[j]
            if transpose:
                term = lax.dot_general(tile, block, (((0,), (0,)), ((), ())),
                                       preferred_element_type=jnp.float32)
            else:
                term = jnp.dot(tile, block, preferred_element_type=jnp.float32)
            rows = pl.ds(pl.multiple_of(dst * width, width), width)
            acc_ref[rows, :] += term

    @pl.when(step == pl.num_programs(0) - 1)
    def _():
        out_ref[...] = acc_ref[...].astype(out_ref.dtype)


def tile_products(tiles, rows, cols, count, panel, out_blocks, transpose):
    slots, width, _ = tiles.shape
    feat = panel.shape[1]
    steps = slots // GROUP

    def tiles_map(i, rows_ref, cols_ref, count_ref):
        last = jnp.maximum(count_ref[0] - 1, 0) // GROUP
        return (jnp.minimum(i, last), 0, 0)

    return pl.pallas_call(
        functools.partial(tile_kernel, transpose),
        out_shape=jax.ShapeDtypeStruct((out_blocks * width, feat), jnp.bfloat16),
        grid_spec=pltpu.PrefetchScalarGridSpec(
            num_scalar_prefetch=3,
            grid=(steps,),
            in_specs=[
                pl.BlockSpec((GROUP, width, width), tiles_map),
                pl.BlockSpec(panel.shape, lambda i, *_: (0, 0)),
            ],
            out_specs=pl.BlockSpec((out_blocks * width, feat), lambda i, *_: (0, 0)),
            scratch_shapes=[pltpu.VMEM((out_blocks * width, feat), jnp.float32)],
        ),
        compiler_params=pltpu.CompilerParams(dimension_semantics=("arbitrary",)),
        cost_estimate=pl.CostEstimate(
            flops=2 * slots * width * width * feat,
            bytes_accessed=tiles.size * 2 + panel.size * 2 + out_blocks * width * feat * 2,
            transcendentals=0,
        ),
    )(rows, cols, count, tiles, panel)


def mesh_coords(axis, peer):
    return tuple(peer if name == axis else lax.axis_index(name) for name in ("row", "col", "feat"))


def exchange_kernel(axis, mode, x_ref, o_ref, *scratch):
    n = lax.axis_size(axis)
    me = lax.axis_index(axis)
    if mode == "gather":
        recv_ref, (send_sems, recv_sems) = o_ref, scratch
    else:
        recv_ref, send_sems, recv_sems = scratch
    barrier = pltpu.get_barrier_semaphore()
    for d in range(1, n):
        peer = lax.rem(me + d, n)
        pl.semaphore_signal(barrier, inc=1, device_id=mesh_coords(axis, peer),
                            device_id_type=pl.DeviceIdType.MESH)
    pl.semaphore_wait(barrier, n - 1)
    copies = []
    for d in range(1, n):
        peer = lax.rem(me + d, n)
        src = x_ref if mode == "gather" else x_ref.at[peer]
        copy = pltpu.make_async_remote_copy(
            src_ref=src, dst_ref=recv_ref.at[me], send_sem=send_sems.at[d],
            recv_sem=recv_sems.at[me], device_id=mesh_coords(axis, peer),
            device_id_type=pl.DeviceIdType.MESH)
        copy.start()
        copies.append(copy)
    if mode == "gather":
        o_ref[me] = x_ref[...]
    else:
        total = x_ref[me].astype(jnp.float32)
    for d in range(1, n):
        src_dev = lax.rem(me + n - d, n)
        incoming = pltpu.make_async_remote_copy(
            src_ref=recv_ref.at[src_dev], dst_ref=recv_ref.at[src_dev], send_sem=send_sems.at[d],
            recv_sem=recv_sems.at[src_dev], device_id=mesh_coords(axis, src_dev),
            device_id_type=pl.DeviceIdType.MESH)
        incoming.wait_recv()
        if mode != "gather":
            total = total + recv_ref[src_dev].astype(jnp.float32)
    for copy in copies:
        copy.wait_send()
    if mode != "gather":
        o_ref[...] = total.astype(o_ref.dtype)


def exchange(x, axis, mode, collective_id):
    n = lax.axis_size(axis)
    if mode == "gather":
        out_shape = (n,) + x.shape
        scratch = []
    else:
        out_shape = x.shape[1:]
        scratch = [pltpu.VMEM(x.shape, x.dtype)]
    scratch += [pltpu.SemaphoreType.DMA((n,)), pltpu.SemaphoreType.DMA((n,))]
    return pl.pallas_call(
        functools.partial(exchange_kernel, axis, mode),
        out_shape=jax.ShapeDtypeStruct(out_shape, x.dtype),
        in_specs=[pl.BlockSpec(memory_space=pltpu.VMEM)],
        out_specs=pl.BlockSpec(memory_space=pltpu.VMEM),
        scratch_shapes=scratch,
        compiler_params=pltpu.CompilerParams(collective_id=collective_id, has_side_effects=True),
    )(x)


def butterfly_partners():
    rounds = []
    for axis in ("row", "col"):
        bit = 1
        while bit < lax.axis_size(axis):
            rounds.append((axis, bit))
            bit *= 2
    return rounds


def allreduce_kernel(x_ref, o_ref, bufs, recv, send_sems, recv_sems):
    rounds = butterfly_partners()

    def partner(axis, bit):
        me = lax.axis_index(axis)
        return me + bit * (1 - 2 * ((me // bit) % 2))

    barrier = pltpu.get_barrier_semaphore()
    for axis, bit in rounds:
        pl.semaphore_signal(barrier, inc=1, device_id=mesh_coords(axis, partner(axis, bit)),
                            device_id_type=pl.DeviceIdType.MESH)
    pl.semaphore_wait(barrier, len(rounds))
    for k, (axis, bit) in enumerate(rounds):
        src = x_ref if k == 0 else bufs.at[k - 1]
        copy = pltpu.make_async_remote_copy(
            src_ref=src, dst_ref=recv.at[k], send_sem=send_sems.at[k], recv_sem=recv_sems.at[k],
            device_id=mesh_coords(axis, partner(axis, bit)), device_id_type=pl.DeviceIdType.MESH)
        copy.start()
        copy.wait()
        total = src[...] + recv[k]
        if k == len(rounds) - 1:
            o_ref[...] = total
        else:
            bufs[k] = total


def allreduce(x, collective_id):
    steps = len(butterfly_partners())
    return pl.pallas_call(
        allreduce_kernel,
        out_shape=jax.ShapeDtypeStruct(x.shape, x.dtype),
        in_specs=[pl.BlockSpec(memory_space=pltpu.VMEM)],
        out_specs=pl.BlockSpec(memory_space=pltpu.VMEM),
        scratch_shapes=[
            pltpu.VMEM((max(steps - 1, 1),) + x.shape, x.dtype),
            pltpu.VMEM((steps,) + x.shape, x.dtype),
            pltpu.SemaphoreType.DMA((steps,)),
            pltpu.SemaphoreType.DMA((steps,)),
        ],
        compiler_params=pltpu.CompilerParams(collective_id=collective_id, has_side_effects=True),
    )(x)


def shards(features, tile_rows, tile_cols, tile_count, tile_values, weights, cotangent):
    width = tile_values.shape[-1]
    local_tiles = tile_values[0, 0]
    block_rows = tile_rows[0, 0]
    block_cols = tile_cols[0, 0]
    count = tile_count[0, 0].reshape(1)
    n_rowdev = lax.axis_size("row")
    n_coldev = lax.axis_size("col")
    local_blocks = features.shape[0] // width
    feat_half = features.shape[1]
    feat_index = lax.axis_index("feat")
    row_blocks = local_blocks * n_coldev
    col_blocks = local_blocks * n_rowdev
    node_total = features.shape[0] * n_rowdev * n_coldev
    panel = exchange(features, "row", "gather", 0).reshape(-1, feat_half)
    partial_value = tile_products(local_tiles, block_rows, block_cols, count, panel,
                                  row_blocks, transpose=False)
    summed = exchange(partial_value.reshape(n_coldev, -1, feat_half), "col", "scatter", 1)
    weight_rows = lax.dynamic_slice_in_dim(weights, feat_index * feat_half, feat_half, 0)
    mix_term = jnp.dot(summed, weight_rows, preferred_element_type=jnp.float32)
    hidden = lax.psum_scatter(
        mix_term.astype(jnp.bfloat16), "feat", scatter_dimension=1, tiled=True
    ).astype(jnp.float32)
    negative = jnp.minimum(hidden, 0.0)
    activated = jnp.where(hidden > 0, hidden, jnp.expm1(negative)).astype(jnp.bfloat16)
    slope_factor = jnp.where(hidden > 0, 1.0, jnp.exp(negative))
    grad_out = (cotangent.astype(jnp.float32) * slope_factor).astype(jnp.bfloat16)
    grad_whole = lax.all_gather(grad_out, "feat", axis=1, tiled=True)
    weight_term = lax.dot_general(
        summed, grad_whole, (((0,), (0,)), ((), ())), preferred_element_type=jnp.float32
    )
    weight_grad = allreduce(weight_term, 4) * node_total ** (-0.5)
    spread = lax.dot_general(
        grad_whole, weight_rows, (((1,), (1,)), ((), ())), preferred_element_type=jnp.float32
    ).astype(jnp.bfloat16)
    spread_panel = exchange(spread, "col", "gather", 2).reshape(-1, feat_half)
    back_partial = tile_products(local_tiles, block_rows, block_cols, count, spread_panel,
                                 col_blocks, transpose=True)
    back_summed = exchange(back_partial.reshape(n_rowdev, -1, feat_half), "row", "scatter", 3)
    return (activated, back_summed, weight_grad)


def solution(mesh):
    return jax.shard_map(
        shards,
        mesh=mesh,
        in_specs=(
            P(("col", "row"), "feat"),
            P("row", "col", None),
            P("row", "col", None),
            P("row", "col"),
            P("row", "col", None, None, None),
            P(),
            P(("row", "col"), "feat"),
        ),
        out_specs=(P(("row", "col"), "feat"), P(("col", "row"), "feat"), P("feat", None)),
        check_vma=False,
    )
```

```python
import functools

import jax
import jax.numpy as jnp
from jax import lax
from jax.experimental import pallas as pl
from jax.experimental.pallas import tpu as pltpu
from jax.sharding import PartitionSpec as P

GROUP = 64


def tile_kernel(transpose, rows_ref, cols_ref, count_ref, tiles_ref, panel_ref, out_ref, acc_ref):
    step = pl.program_id(0)
    width = tiles_ref.shape[-1]
    count = count_ref[0]
    src_blocks = panel_ref.shape[0] // width
    dst_blocks = acc_ref.shape[0] // width

    @pl.when(step == 0)
    def _():
        acc_ref[...] = jnp.zeros_like(acc_ref)

    @pl.when(step * GROUP < count)
    def _():
        terms = []
        for j in range(GROUP):
            slot = step * GROUP + j
            src = rows_ref[slot] if transpose else cols_ref[slot]
            src = jnp.minimum(jnp.maximum(src, 0), src_blocks - 1)
            block = panel_ref[pl.ds(pl.multiple_of(src * width, width), width), :]
            tile = tiles_ref[j]
            if transpose:
                term = lax.dot_general(tile, block, (((0,), (0,)), ((), ())),
                                       preferred_element_type=jnp.float32)
            else:
                term = jnp.dot(tile, block, preferred_element_type=jnp.float32)
            terms.append(jnp.where(slot < count, term, 0.0))
        for j in range(GROUP):
            slot = step * GROUP + j
            dst = cols_ref[slot] if transpose else rows_ref[slot]
            dst = jnp.minimum(jnp.maximum(dst, 0), dst_blocks - 1)
            rows = pl.ds(pl.multiple_of(dst * width, width), width)
            acc_ref[rows, :] += terms[j]

    @pl.when(step == pl.num_programs(0) - 1)
    def _():
        out_ref[...] = acc_ref[...].astype(out_ref.dtype)


def tile_products(tiles, rows, cols, count, panel, out_blocks, transpose):
    slots, width, _ = tiles.shape
    feat = panel.shape[1]
    steps = slots // GROUP

    def tiles_map(i, rows_ref, cols_ref, count_ref):
        last = jnp.maximum(count_ref[0] - 1, 0) // GROUP
        return (jnp.minimum(i, last), 0, 0)

    return pl.pallas_call(
        functools.partial(tile_kernel, transpose),
        out_shape=jax.ShapeDtypeStruct((out_blocks * width, feat), jnp.bfloat16),
        grid_spec=pltpu.PrefetchScalarGridSpec(
            num_scalar_prefetch=3,
            grid=(steps,),
            in_specs=[
                pl.BlockSpec((GROUP, width, width), tiles_map),
                pl.BlockSpec(panel.shape, lambda i, *_: (0, 0)),
            ],
            out_specs=pl.BlockSpec((out_blocks * width, feat), lambda i, *_: (0, 0)),
            scratch_shapes=[pltpu.VMEM((out_blocks * width, feat), jnp.float32)],
        ),
        compiler_params=pltpu.CompilerParams(dimension_semantics=("arbitrary",)),
        cost_estimate=pl.CostEstimate(
            flops=2 * slots * width * width * feat,
            bytes_accessed=tiles.size * 2 + panel.size * 2 + out_blocks * width * feat * 2,
            transcendentals=0,
        ),
    )(rows, cols, count, tiles, panel)


def mesh_coords(axis, peer):
    return tuple(peer if name == axis else lax.axis_index(name) for name in ("row", "col", "feat"))


def exchange_kernel(axis, mode, x_ref, o_ref, *scratch):
    n = lax.axis_size(axis)
    me = lax.axis_index(axis)
    if mode == "gather":
        recv_ref, (send_sems, recv_sems) = o_ref, scratch
    else:
        recv_ref, send_sems, recv_sems = scratch
    barrier = pltpu.get_barrier_semaphore()
    for d in range(1, n):
        peer = lax.rem(me + d, n)
        pl.semaphore_signal(barrier, inc=1, device_id=mesh_coords(axis, peer),
                            device_id_type=pl.DeviceIdType.MESH)
    pl.semaphore_wait(barrier, n - 1)
    copies = []
    for d in range(1, n):
        peer = lax.rem(me + d, n)
        src = x_ref if mode == "gather" else x_ref.at[peer]
        copy = pltpu.make_async_remote_copy(
            src_ref=src, dst_ref=recv_ref.at[me], send_sem=send_sems.at[d],
            recv_sem=recv_sems.at[me], device_id=mesh_coords(axis, peer),
            device_id_type=pl.DeviceIdType.MESH)
        copy.start()
        copies.append(copy)
    if mode == "gather":
        o_ref[me] = x_ref[...]
    else:
        total = x_ref[me].astype(jnp.float32)
    for d in range(1, n):
        src_dev = lax.rem(me + n - d, n)
        incoming = pltpu.make_async_remote_copy(
            src_ref=recv_ref.at[src_dev], dst_ref=recv_ref.at[src_dev], send_sem=send_sems.at[d],
            recv_sem=recv_sems.at[src_dev], device_id=mesh_coords(axis, src_dev),
            device_id_type=pl.DeviceIdType.MESH)
        incoming.wait_recv()
        if mode != "gather":
            total = total + recv_ref[src_dev].astype(jnp.float32)
    for copy in copies:
        copy.wait_send()
    if mode != "gather":
        o_ref[...] = total.astype(o_ref.dtype)


def exchange(x, axis, mode, collective_id):
    n = lax.axis_size(axis)
    if mode == "gather":
        out_shape = (n,) + x.shape
        scratch = []
    else:
        out_shape = x.shape[1:]
        scratch = [pltpu.VMEM(x.shape, x.dtype)]
    scratch += [pltpu.SemaphoreType.DMA((n,)), pltpu.SemaphoreType.DMA((n,))]
    return pl.pallas_call(
        functools.partial(exchange_kernel, axis, mode),
        out_shape=jax.ShapeDtypeStruct(out_shape, x.dtype),
        in_specs=[pl.BlockSpec(memory_space=pltpu.VMEM)],
        out_specs=pl.BlockSpec(memory_space=pltpu.VMEM),
        scratch_shapes=scratch,
        compiler_params=pltpu.CompilerParams(collective_id=collective_id, has_side_effects=True),
    )(x)


def butterfly_partners():
    rounds = []
    for axis in ("row", "col"):
        bit = 1
        while bit < lax.axis_size(axis):
            rounds.append((axis, bit))
            bit *= 2
    return rounds


def allreduce_kernel(x_ref, o_ref, bufs, recv, send_sems, recv_sems):
    rounds = butterfly_partners()

    def partner(axis, bit):
        me = lax.axis_index(axis)
        return me + bit * (1 - 2 * ((me // bit) % 2))

    barrier = pltpu.get_barrier_semaphore()
    for axis, bit in rounds:
        pl.semaphore_signal(barrier, inc=1, device_id=mesh_coords(axis, partner(axis, bit)),
                            device_id_type=pl.DeviceIdType.MESH)
    pl.semaphore_wait(barrier, len(rounds))
    for k, (axis, bit) in enumerate(rounds):
        src = x_ref if k == 0 else bufs.at[k - 1]
        copy = pltpu.make_async_remote_copy(
            src_ref=src, dst_ref=recv.at[k], send_sem=send_sems.at[k], recv_sem=recv_sems.at[k],
            device_id=mesh_coords(axis, partner(axis, bit)), device_id_type=pl.DeviceIdType.MESH)
        copy.start()
        copy.wait()
        total = src[...] + recv[k]
        if k == len(rounds) - 1:
            o_ref[...] = total
        else:
            bufs[k] = total


def allreduce(x, collective_id):
    steps = len(butterfly_partners())
    return pl.pallas_call(
        allreduce_kernel,
        out_shape=jax.ShapeDtypeStruct(x.shape, x.dtype),
        in_specs=[pl.BlockSpec(memory_space=pltpu.VMEM)],
        out_specs=pl.BlockSpec(memory_space=pltpu.VMEM),
        scratch_shapes=[
            pltpu.VMEM((max(steps - 1, 1),) + x.shape, x.dtype),
            pltpu.VMEM((steps,) + x.shape, x.dtype),
            pltpu.SemaphoreType.DMA((steps,)),
            pltpu.SemaphoreType.DMA((steps,)),
        ],
        compiler_params=pltpu.CompilerParams(collective_id=collective_id, has_side_effects=True),
    )(x)


def shards(features, tile_rows, tile_cols, tile_count, tile_values, weights, cotangent):
    width = tile_values.shape[-1]
    local_tiles = tile_values[0, 0]
    block_rows = tile_rows[0, 0]
    block_cols = tile_cols[0, 0]
    count = tile_count[0, 0].reshape(1)
    n_rowdev = lax.axis_size("row")
    n_coldev = lax.axis_size("col")
    local_blocks = features.shape[0] // width
    feat_half = features.shape[1]
    feat_index = lax.axis_index("feat")
    row_blocks = local_blocks * n_coldev
    col_blocks = local_blocks * n_rowdev
    node_total = features.shape[0] * n_rowdev * n_coldev
    panel = exchange(features, "row", "gather", 0).reshape(-1, feat_half)
    partial_value = tile_products(local_tiles, block_rows, block_cols, count, panel,
                                  row_blocks, transpose=False)
    summed = exchange(partial_value.reshape(n_coldev, -1, feat_half), "col", "scatter", 1)
    weight_rows = lax.dynamic_slice_in_dim(weights, feat_index * feat_half, feat_half, 0)
    mix_term = jnp.dot(summed, weight_rows, preferred_element_type=jnp.float32)
    hidden = lax.psum_scatter(
        mix_term.astype(jnp.bfloat16), "feat", scatter_dimension=1, tiled=True
    ).astype(jnp.float32)
    negative = jnp.minimum(hidden, 0.0)
    activated = jnp.where(hidden > 0, hidden, jnp.expm1(negative)).astype(jnp.bfloat16)
    slope_factor = jnp.where(hidden > 0, 1.0, jnp.exp(negative))
    grad_out = (cotangent.astype(jnp.float32) * slope_factor).astype(jnp.bfloat16)
    grad_whole = lax.all_gather(grad_out, "feat", axis=1, tiled=True)
    weight_term = lax.dot_general(
        summed, grad_whole, (((0,), (0,)), ((), ())), preferred_element_type=jnp.float32
    )
    weight_grad = allreduce(weight_term, 4) * node_total ** (-0.5)
    spread = lax.dot_general(
        grad_whole, weight_rows, (((1,), (1,)), ((), ())), preferred_element_type=jnp.float32
    ).astype(jnp.bfloat16)
    spread_panel = exchange(spread, "col", "gather", 2).reshape(-1, feat_half)
    back_partial = tile_products(local_tiles, block_rows, block_cols, count, spread_panel,
                                 col_blocks, transpose=True)
    back_summed = exchange(back_partial.reshape(n_rowdev, -1, feat_half), "row", "scatter", 3)
    return (activated, back_summed, weight_grad)


def solution(mesh):
    return jax.shard_map(
        shards,
        mesh=mesh,
        in_specs=(
            P(("col", "row"), "feat"),
            P("row", "col", None),
            P("row", "col", None),
            P("row", "col"),
            P("row", "col", None, None, None),
            P(),
            P(("row", "col"), "feat"),
        ),
        out_specs=(P(("row", "col"), "feat"), P(("col", "row"), "feat"), P("feat", None)),
        check_vma=False,
    )
```

```python
import functools

import jax
import jax.numpy as jnp
from jax import lax
from jax.experimental import pallas as pl
from jax.experimental.pallas import tpu as pltpu
from jax.sharding import PartitionSpec as P

GROUP = 64


def tile_kernel(transpose, rows_ref, cols_ref, count_ref, tiles_ref, panel_ref, out_ref, acc_ref):
    step = pl.program_id(0)
    width = tiles_ref.shape[-1]
    count = count_ref[0]
    src_blocks = panel_ref.shape[0] // width
    dst_blocks = acc_ref.shape[0] // width

    @pl.when(step == 0)
    def _():
        acc_ref[...] = jnp.zeros_like(acc_ref)

    @pl.when(step * GROUP < count)
    def _():
        terms = []
        for j in range(GROUP):
            slot = step * GROUP + j
            src = rows_ref[slot] if transpose else cols_ref[slot]
            src = jnp.minimum(jnp.maximum(src, 0), src_blocks - 1)
            block = panel_ref[pl.ds(pl.multiple_of(src * width, width), width), :]
            tile = tiles_ref[j]
            if transpose:
                term = lax.dot_general(tile, block, (((0,), (0,)), ((), ())),
                                       preferred_element_type=jnp.float32)
            else:
                term = jnp.dot(tile, block, preferred_element_type=jnp.float32)
            terms.append(jnp.where(slot < count, term, 0.0))
        for j in range(GROUP):
            slot = step * GROUP + j
            dst = cols_ref[slot] if transpose else rows_ref[slot]
            dst = jnp.minimum(jnp.maximum(dst, 0), dst_blocks - 1)
            rows = pl.ds(pl.multiple_of(dst * width, width), width)
            acc_ref[rows, :] += terms[j]

    @pl.when(step == pl.num_programs(0) - 1)
    def _():
        out_ref[...] = acc_ref[...].astype(out_ref.dtype)


def tile_products(tiles, rows, cols, count, panel, out_blocks, transpose):
    slots, width, _ = tiles.shape
    feat = panel.shape[1]
    steps = slots // GROUP

    def tiles_map(i, rows_ref, cols_ref, count_ref):
        last = jnp.maximum(count_ref[0] - 1, 0) // GROUP
        return (jnp.minimum(i, last), 0, 0)

    return pl.pallas_call(
        functools.partial(tile_kernel, transpose),
        out_shape=jax.ShapeDtypeStruct((out_blocks * width, feat), jnp.bfloat16),
        grid_spec=pltpu.PrefetchScalarGridSpec(
            num_scalar_prefetch=3,
            grid=(steps,),
            in_specs=[
                pl.BlockSpec((GROUP, width, width), tiles_map),
                pl.BlockSpec(panel.shape, lambda i, *_: (0, 0)),
            ],
            out_specs=pl.BlockSpec((out_blocks * width, feat), lambda i, *_: (0, 0)),
            scratch_shapes=[pltpu.VMEM((out_blocks * width, feat), jnp.float32)],
        ),
        compiler_params=pltpu.CompilerParams(dimension_semantics=("arbitrary",)),
        cost_estimate=pl.CostEstimate(
            flops=2 * slots * width * width * feat,
            bytes_accessed=tiles.size * 2 + panel.size * 2 + out_blocks * width * feat * 2,
            transcendentals=0,
        ),
    )(rows, cols, count, tiles, panel)


def mesh_coords(axis, peer):
    return tuple(peer if name == axis else lax.axis_index(name) for name in ("row", "col", "feat"))


def exchange_kernel(axis, stride, size, mode, x_ref, o_ref, *scratch):
    index = lax.axis_index(axis)
    me = (index // stride) % size
    base = index - me * stride

    def member(k):
        return mesh_coords(axis, base + k * stride)

    if mode == "gather":
        recv_ref, (send_sems, recv_sems) = o_ref, scratch
    else:
        recv_ref, send_sems, recv_sems = scratch
    barrier = pltpu.get_barrier_semaphore()
    for d in range(1, size):
        pl.semaphore_signal(barrier, inc=1, device_id=member(lax.rem(me + d, size)),
                            device_id_type=pl.DeviceIdType.MESH)
    pl.semaphore_wait(barrier, size - 1)
    copies = []
    for d in range(1, size):
        peer = lax.rem(me + d, size)
        src = x_ref if mode == "gather" else x_ref.at[peer]
        copy = pltpu.make_async_remote_copy(
            src_ref=src, dst_ref=recv_ref.at[me], send_sem=send_sems.at[d],
            recv_sem=recv_sems.at[me], device_id=member(peer),
            device_id_type=pl.DeviceIdType.MESH)
        copy.start()
        copies.append(copy)
    if mode == "gather":
        o_ref[me] = x_ref[...]
    else:
        total = x_ref[me].astype(jnp.float32)
    for d in range(1, size):
        src_dev = lax.rem(me + size - d, size)
        incoming = pltpu.make_async_remote_copy(
            src_ref=recv_ref.at[src_dev], dst_ref=recv_ref.at[src_dev], send_sem=send_sems.at[d],
            recv_sem=recv_sems.at[src_dev], device_id=member(src_dev),
            device_id_type=pl.DeviceIdType.MESH)
        incoming.wait_recv()
        if mode != "gather":
            total = total + recv_ref[src_dev].astype(jnp.float32)
    for copy in copies:
        copy.wait_send()
    if mode != "gather":
        o_ref[...] = total.astype(o_ref.dtype)


def exchange(x, axis, mode, collective_id, stride=1, size=None):
    size = lax.axis_size(axis) if size is None else size
    if mode == "gather":
        out_shape = (size,) + x.shape
        scratch = []
    else:
        out_shape = x.shape[1:]
        scratch = [pltpu.VMEM(x.shape, x.dtype)]
    scratch += [pltpu.SemaphoreType.DMA((size,)), pltpu.SemaphoreType.DMA((size,))]
    return pl.pallas_call(
        functools.partial(exchange_kernel, axis, stride, size, mode),
        out_shape=jax.ShapeDtypeStruct(out_shape, x.dtype),
        in_specs=[pl.BlockSpec(memory_space=pltpu.VMEM)],
        out_specs=pl.BlockSpec(memory_space=pltpu.VMEM),
        scratch_shapes=scratch,
        compiler_params=pltpu.CompilerParams(collective_id=collective_id, has_side_effects=True),
    )(x)


def butterfly_partners():
    rounds = []
    for axis in ("row", "col"):
        bit = 1
        while bit < lax.axis_size(axis):
            rounds.append((axis, bit))
            bit *= 2
    return rounds


def allreduce_kernel(x_ref, o_ref, bufs, recv, send_sems, recv_sems):
    rounds = butterfly_partners()

    def partner(axis, bit):
        me = lax.axis_index(axis)
        return me + bit * (1 - 2 * ((me // bit) % 2))

    barrier = pltpu.get_barrier_semaphore()
    for axis, bit in rounds:
        pl.semaphore_signal(barrier, inc=1, device_id=mesh_coords(axis, partner(axis, bit)),
                            device_id_type=pl.DeviceIdType.MESH)
    pl.semaphore_wait(barrier, len(rounds))
    for k, (axis, bit) in enumerate(rounds):
        src = x_ref if k == 0 else bufs.at[k - 1]
        copy = pltpu.make_async_remote_copy(
            src_ref=src, dst_ref=recv.at[k], send_sem=send_sems.at[k], recv_sem=recv_sems.at[k],
            device_id=mesh_coords(axis, partner(axis, bit)), device_id_type=pl.DeviceIdType.MESH)
        copy.start()
        copy.wait()
        total = src[...] + recv[k]
        if k == len(rounds) - 1:
            o_ref[...] = total
        else:
            bufs[k] = total


def allreduce(x, collective_id):
    steps = len(butterfly_partners())
    return pl.pallas_call(
        allreduce_kernel,
        out_shape=jax.ShapeDtypeStruct(x.shape, x.dtype),
        in_specs=[pl.BlockSpec(memory_space=pltpu.VMEM)],
        out_specs=pl.BlockSpec(memory_space=pltpu.VMEM),
        scratch_shapes=[
            pltpu.VMEM((max(steps - 1, 1),) + x.shape, x.dtype),
            pltpu.VMEM((steps,) + x.shape, x.dtype),
            pltpu.SemaphoreType.DMA((steps,)),
            pltpu.SemaphoreType.DMA((steps,)),
        ],
        compiler_params=pltpu.CompilerParams(collective_id=collective_id, has_side_effects=True),
    )(x)


def shards(features, tile_rows, tile_cols, tile_count, tile_values, weights, cotangent):
    width = tile_values.shape[-1]
    local_tiles = tile_values[0, 0]
    block_rows = tile_rows[0, 0]
    block_cols = tile_cols[0, 0]
    count = tile_count[0, 0].reshape(1)
    n_rowdev = lax.axis_size("row")
    n_coldev = lax.axis_size("col")
    local_blocks = features.shape[0] // width
    feat_half = features.shape[1]
    feat_index = lax.axis_index("feat")
    row_blocks = local_blocks * n_coldev
    col_blocks = local_blocks * n_rowdev
    node_total = features.shape[0] * n_rowdev * n_coldev
    pair = 2 if n_rowdev % 2 == 0 else 1
    chips = n_rowdev // pair
    panel = exchange(features, "row", "gather", 0, stride=pair, size=chips)
    panel = exchange(panel, "row", "gather", 5, stride=1, size=pair).reshape(-1, feat_half)
    owner = block_cols // local_blocks
    block_cols = ((owner % pair) * chips + owner // pair) * local_blocks + block_cols % local_blocks
    partial_value = tile_products(local_tiles, block_rows, block_cols, count, panel,
                                  row_blocks, transpose=False)
    summed = exchange(partial_value.reshape(n_coldev, -1, feat_half), "col", "scatter", 1)
    weight_rows = lax.dynamic_slice_in_dim(weights, feat_index * feat_half, feat_half, 0)
    mix_term = jnp.dot(summed, weight_rows, preferred_element_type=jnp.float32)
    hidden = lax.psum_scatter(
        mix_term.astype(jnp.bfloat16), "feat", scatter_dimension=1, tiled=True
    ).astype(jnp.float32)
    negative = jnp.minimum(hidden, 0.0)
    activated = jnp.where(hidden > 0, hidden, jnp.expm1(negative)).astype(jnp.bfloat16)
    slope_factor = jnp.where(hidden > 0, 1.0, jnp.exp(negative))
    grad_out = (cotangent.astype(jnp.float32) * slope_factor).astype(jnp.bfloat16)
    grad_whole = lax.all_gather(grad_out, "feat", axis=1, tiled=True)
    weight_term = lax.dot_general(
        summed, grad_whole, (((0,), (0,)), ((), ())), preferred_element_type=jnp.float32
    )
    weight_grad = allreduce(weight_term, 4) * node_total ** (-0.5)
    spread = lax.dot_general(
        grad_whole, weight_rows, (((1,), (1,)), ((), ())), preferred_element_type=jnp.float32
    ).astype(jnp.bfloat16)
    spread_panel = exchange(spread, "col", "gather", 2).reshape(-1, feat_half)
    back_partial = tile_products(local_tiles, block_rows, block_cols, count, spread_panel,
                                 col_blocks, transpose=True)
    back_pairs = exchange(back_partial.reshape(pair, -1, feat_half), "row", "scatter", 3,
                          stride=1, size=pair)
    back_summed = exchange(back_pairs.reshape(chips, -1, feat_half), "row", "scatter", 6,
                           stride=pair, size=chips)
    return (activated, back_summed, weight_grad)


def solution(mesh):
    return jax.shard_map(
        shards,
        mesh=mesh,
        in_specs=(
            P(("col", "row"), "feat"),
            P("row", "col", None),
            P("row", "col", None),
            P("row", "col"),
            P("row", "col", None, None, None),
            P(),
            P(("row", "col"), "feat"),
        ),
        out_specs=(P(("row", "col"), "feat"), P(("col", "row"), "feat"), P("feat", None)),
        check_vma=False,
    )
```

```python
import functools

import jax
import jax.numpy as jnp
from jax import lax
from jax.experimental import pallas as pl
from jax.experimental.pallas import tpu as pltpu
from jax.sharding import PartitionSpec as P

GROUP = 64


def tile_kernel(transpose, rows_ref, cols_ref, count_ref, tiles_ref, panel_ref, out_ref, acc_ref):
    step = pl.program_id(0)
    width = tiles_ref.shape[-1]
    count = count_ref[0]
    src_blocks = panel_ref.shape[0] // width
    dst_blocks = acc_ref.shape[0] // width

    @pl.when(step == 0)
    def _():
        acc_ref[...] = jnp.zeros_like(acc_ref)

    @pl.when(step * GROUP < count)
    def _():
        terms = []
        for j in range(GROUP):
            slot = step * GROUP + j
            src = rows_ref[slot] if transpose else cols_ref[slot]
            src = jnp.minimum(jnp.maximum(src, 0), src_blocks - 1)
            block = panel_ref[pl.ds(pl.multiple_of(src * width, width), width), :]
            tile = tiles_ref[j]
            if transpose:
                term = lax.dot_general(tile, block, (((0,), (0,)), ((), ())),
                                       preferred_element_type=jnp.float32)
            else:
                term = jnp.dot(tile, block, preferred_element_type=jnp.float32)
            terms.append(jnp.where(slot < count, term, 0.0))
        for j in range(GROUP):
            slot = step * GROUP + j
            dst = cols_ref[slot] if transpose else rows_ref[slot]
            dst = jnp.minimum(jnp.maximum(dst, 0), dst_blocks - 1)
            rows = pl.ds(pl.multiple_of(dst * width, width), width)
            acc_ref[rows, :] += terms[j]

    @pl.when(step == pl.num_programs(0) - 1)
    def _():
        out_ref[...] = acc_ref[...].astype(out_ref.dtype)


def tile_products(tiles, rows, cols, count, panel, out_blocks, transpose):
    slots, width, _ = tiles.shape
    feat = panel.shape[1]
    steps = slots // GROUP

    def tiles_map(i, rows_ref, cols_ref, count_ref):
        last = jnp.maximum(count_ref[0] - 1, 0) // GROUP
        return (jnp.minimum(i, last), 0, 0)

    return pl.pallas_call(
        functools.partial(tile_kernel, transpose),
        out_shape=jax.ShapeDtypeStruct((out_blocks * width, feat), jnp.bfloat16),
        grid_spec=pltpu.PrefetchScalarGridSpec(
            num_scalar_prefetch=3,
            grid=(steps,),
            in_specs=[
                pl.BlockSpec((GROUP, width, width), tiles_map),
                pl.BlockSpec(panel.shape, lambda i, *_: (0, 0)),
            ],
            out_specs=pl.BlockSpec((out_blocks * width, feat), lambda i, *_: (0, 0)),
            scratch_shapes=[pltpu.VMEM((out_blocks * width, feat), jnp.float32)],
        ),
        compiler_params=pltpu.CompilerParams(dimension_semantics=("arbitrary",)),
        cost_estimate=pl.CostEstimate(
            flops=2 * slots * width * width * feat,
            bytes_accessed=tiles.size * 2 + panel.size * 2 + out_blocks * width * feat * 2,
            transcendentals=0,
        ),
    )(rows, cols, count, tiles, panel)


def mesh_coords(axis, peer):
    return tuple(peer if name == axis else lax.axis_index(name) for name in ("row", "col", "feat"))


def exchange_kernel(axis, stride, size, mode, x_ref, o_ref, *scratch):
    index = lax.axis_index(axis)
    me = (index // stride) % size
    base = index - me * stride

    def member(k):
        return mesh_coords(axis, base + k * stride)

    if mode == "gather":
        recv_ref, (send_sems, recv_sems) = o_ref, scratch
    else:
        recv_ref, send_sems, recv_sems = scratch
    barrier = pltpu.get_barrier_semaphore()
    for d in range(1, size):
        pl.semaphore_signal(barrier, inc=1, device_id=member(lax.rem(me + d, size)),
                            device_id_type=pl.DeviceIdType.MESH)
    pl.semaphore_wait(barrier, size - 1)
    copies = []
    for d in range(1, size):
        peer = lax.rem(me + d, size)
        src = x_ref if mode == "gather" else x_ref.at[peer]
        copy = pltpu.make_async_remote_copy(
            src_ref=src, dst_ref=recv_ref.at[me], send_sem=send_sems.at[d],
            recv_sem=recv_sems.at[me], device_id=member(peer),
            device_id_type=pl.DeviceIdType.MESH)
        copy.start()
        copies.append(copy)
    if mode == "gather":
        o_ref[me] = x_ref[...]
    else:
        total = x_ref[me].astype(jnp.float32)
    for d in range(1, size):
        src_dev = lax.rem(me + size - d, size)
        incoming = pltpu.make_async_remote_copy(
            src_ref=recv_ref.at[src_dev], dst_ref=recv_ref.at[src_dev], send_sem=send_sems.at[d],
            recv_sem=recv_sems.at[src_dev], device_id=member(src_dev),
            device_id_type=pl.DeviceIdType.MESH)
        incoming.wait_recv()
        if mode != "gather":
            total = total + recv_ref[src_dev].astype(jnp.float32)
    for copy in copies:
        copy.wait_send()
    if mode != "gather":
        o_ref[...] = total.astype(o_ref.dtype)


def exchange(x, axis, mode, collective_id, stride=1, size=None):
    size = lax.axis_size(axis) if size is None else size
    if mode == "gather":
        out_shape = (size,) + x.shape
        scratch = []
    else:
        out_shape = x.shape[1:]
        scratch = [pltpu.VMEM(x.shape, x.dtype)]
    scratch += [pltpu.SemaphoreType.DMA((size,)), pltpu.SemaphoreType.DMA((size,))]
    return pl.pallas_call(
        functools.partial(exchange_kernel, axis, stride, size, mode),
        out_shape=jax.ShapeDtypeStruct(out_shape, x.dtype),
        in_specs=[pl.BlockSpec(memory_space=pltpu.VMEM)],
        out_specs=pl.BlockSpec(memory_space=pltpu.VMEM),
        scratch_shapes=scratch,
        compiler_params=pltpu.CompilerParams(collective_id=collective_id, has_side_effects=True),
    )(x)


def reduction_plan(rows):
    pairs = []
    for bit in (1, 2, 4, 8, 16, 32, 64):
        for axis in ("row", "col"):
            if bit < lax.axis_size(axis):
                pairs.append((axis, bit))
    halving = []
    while pairs and rows // 2 >= 8 and rows % 16 == 0:
        halving.append(pairs.pop(0))
        rows //= 2
    return halving, pairs


def allreduce_kernel(x_ref, o_ref, recv, send_sems, recv_sems):
    halving, whole = reduction_plan(x_ref.shape[0])

    def bitval(axis, bit):
        return (lax.axis_index(axis) // bit) % 2

    def partner(axis, bit):
        return mesh_coords(axis, lax.axis_index(axis) + bit * (1 - 2 * bitval(axis, bit)))

    barrier = pltpu.get_barrier_semaphore()
    for axis, bit in halving + whole:
        pl.semaphore_signal(barrier, inc=1, device_id=partner(axis, bit),
                            device_id_type=pl.DeviceIdType.MESH)
    pl.semaphore_wait(barrier, len(halving) + len(whole))

    o_ref[...] = x_ref[...]
    k = 0

    def swap(k, axis, bit, send_rows, length):
        copy = pltpu.make_async_remote_copy(
            src_ref=o_ref.at[pl.ds(send_rows, length)], dst_ref=recv.at[k, pl.ds(0, length)],
            send_sem=send_sems.at[k], recv_sem=recv_sems.at[k],
            device_id=partner(axis, bit), device_id_type=pl.DeviceIdType.MESH)
        copy.start()
        copy.wait()

    lo = jnp.int32(0)
    length = x_ref.shape[0]
    starts = []
    for axis, bit in halving:
        length //= 2
        mine = bitval(axis, bit)
        starts.append(lo)
        keep = pl.multiple_of(lo + mine * length, 8)
        give = pl.multiple_of(lo + (1 - mine) * length, 8)
        swap(k, axis, bit, give, length)
        o_ref[pl.ds(keep, length)] = o_ref[pl.ds(keep, length)] + recv[k, pl.ds(0, length)]
        lo = keep
        k += 1
    for axis, bit in whole:
        swap(k, axis, bit, lo, length)
        o_ref[pl.ds(lo, length)] = o_ref[pl.ds(lo, length)] + recv[k, pl.ds(0, length)]
        k += 1
    for (axis, bit), base in zip(reversed(halving), reversed(starts)):
        mine = bitval(axis, bit)
        other = pl.multiple_of(base + (1 - mine) * length, 8)
        swap(k, axis, bit, lo, length)
        o_ref[pl.ds(other, length)] = recv[k, pl.ds(0, length)]
        lo = base
        length *= 2
        k += 1


def allreduce(x, collective_id):
    halving, whole = reduction_plan(x.shape[0])
    steps = 2 * len(halving) + len(whole)
    return pl.pallas_call(
        allreduce_kernel,
        out_shape=jax.ShapeDtypeStruct(x.shape, x.dtype),
        in_specs=[pl.BlockSpec(memory_space=pltpu.VMEM)],
        out_specs=pl.BlockSpec(memory_space=pltpu.VMEM),
        scratch_shapes=[
            pltpu.VMEM((steps, x.shape[0] // 2) + x.shape[1:], x.dtype),
            pltpu.SemaphoreType.DMA((steps,)),
            pltpu.SemaphoreType.DMA((steps,)),
        ],
        compiler_params=pltpu.CompilerParams(collective_id=collective_id, has_side_effects=True),
    )(x)


def shards(features, tile_rows, tile_cols, tile_count, tile_values, weights, cotangent):
    width = tile_values.shape[-1]
    local_tiles = tile_values[0, 0]
    block_rows = tile_rows[0, 0]
    block_cols = tile_cols[0, 0]
    count = tile_count[0, 0].reshape(1)
    n_rowdev = lax.axis_size("row")
    n_coldev = lax.axis_size("col")
    local_blocks = features.shape[0] // width
    feat_half = features.shape[1]
    feat_index = lax.axis_index("feat")
    row_blocks = local_blocks * n_coldev
    col_blocks = local_blocks * n_rowdev
    node_total = features.shape[0] * n_rowdev * n_coldev
    pair = 2 if n_rowdev % 2 == 0 else 1
    chips = n_rowdev // pair
    panel = exchange(features, "row", "gather", 0, stride=pair, size=chips)
    panel = exchange(panel, "row", "gather", 5, stride=1, size=pair).reshape(-1, feat_half)
    owner = block_cols // local_blocks
    block_cols = ((owner % pair) * chips + owner // pair) * local_blocks + block_cols % local_blocks
    partial_value = tile_products(local_tiles, block_rows, block_cols, count, panel,
                                  row_blocks, transpose=False)
    summed = exchange(partial_value.reshape(n_coldev, -1, feat_half), "col", "scatter", 1)
    weight_rows = lax.dynamic_slice_in_dim(weights, feat_index * feat_half, feat_half, 0)
    mix_term = jnp.dot(summed, weight_rows, preferred_element_type=jnp.float32)
    hidden = lax.psum_scatter(
        mix_term.astype(jnp.bfloat16), "feat", scatter_dimension=1, tiled=True
    ).astype(jnp.float32)
    negative = jnp.minimum(hidden, 0.0)
    activated = jnp.where(hidden > 0, hidden, jnp.expm1(negative)).astype(jnp.bfloat16)
    slope_factor = jnp.where(hidden > 0, 1.0, jnp.exp(negative))
    grad_out = (cotangent.astype(jnp.float32) * slope_factor).astype(jnp.bfloat16)
    grad_whole = lax.all_gather(grad_out, "feat", axis=1, tiled=True)
    weight_term = lax.dot_general(
        summed, grad_whole, (((0,), (0,)), ((), ())), preferred_element_type=jnp.float32
    )
    weight_grad = allreduce(weight_term, 4) * node_total ** (-0.5)
    spread = lax.dot_general(
        grad_whole, weight_rows, (((1,), (1,)), ((), ())), preferred_element_type=jnp.float32
    ).astype(jnp.bfloat16)
    spread_panel = exchange(spread, "col", "gather", 2).reshape(-1, feat_half)
    back_partial = tile_products(local_tiles, block_rows, block_cols, count, spread_panel,
                                 col_blocks, transpose=True)
    back_pairs = exchange(back_partial.reshape(pair, -1, feat_half), "row", "scatter", 3,
                          stride=1, size=pair)
    back_summed = exchange(back_pairs.reshape(chips, -1, feat_half), "row", "scatter", 6,
                           stride=pair, size=chips)
    return (activated, back_summed, weight_grad)


def solution(mesh):
    return jax.shard_map(
        shards,
        mesh=mesh,
        in_specs=(
            P(("col", "row"), "feat"),
            P("row", "col", None),
            P("row", "col", None),
            P("row", "col"),
            P("row", "col", None, None, None),
            P(),
            P(("row", "col"), "feat"),
        ),
        out_specs=(P(("row", "col"), "feat"), P(("col", "row"), "feat"), P("feat", None)),
        check_vma=False,
    )
```

```python
import functools

import jax
import jax.numpy as jnp
from jax import lax
from jax.experimental import pallas as pl
from jax.experimental.pallas import tpu as pltpu
from jax.sharding import PartitionSpec as P

GROUP = 64


def tile_kernel(transpose, rows_ref, cols_ref, count_ref, tiles_ref, panel_ref, out_ref, acc_ref):
    step = pl.program_id(0)
    width = tiles_ref.shape[-1]
    count = count_ref[0]
    src_blocks = panel_ref.shape[0] // width
    dst_blocks = acc_ref.shape[0] // width

    @pl.when(step == 0)
    def _():
        acc_ref[...] = jnp.zeros_like(acc_ref)

    @pl.when(step * GROUP < count)
    def _():
        terms = []
        for j in range(GROUP):
            slot = step * GROUP + j
            src = rows_ref[slot] if transpose else cols_ref[slot]
            src = jnp.minimum(jnp.maximum(src, 0), src_blocks - 1)
            block = panel_ref[pl.ds(pl.multiple_of(src * width, width), width), :]
            tile = tiles_ref[j]
            if transpose:
                term = lax.dot_general(tile, block, (((0,), (0,)), ((), ())),
                                       preferred_element_type=jnp.float32)
            else:
                term = jnp.dot(tile, block, preferred_element_type=jnp.float32)
            terms.append(jnp.where(slot < count, term, 0.0))
        for j in range(GROUP):
            slot = step * GROUP + j
            dst = cols_ref[slot] if transpose else rows_ref[slot]
            dst = jnp.minimum(jnp.maximum(dst, 0), dst_blocks - 1)
            rows = pl.ds(pl.multiple_of(dst * width, width), width)
            acc_ref[rows, :] += terms[j]

    @pl.when(step == pl.num_programs(0) - 1)
    def _():
        out_ref[...] = acc_ref[...].astype(out_ref.dtype)


def tile_products(tiles, rows, cols, count, panel, out_blocks, transpose):
    slots, width, _ = tiles.shape
    feat = panel.shape[1]
    steps = slots // GROUP

    def tiles_map(i, rows_ref, cols_ref, count_ref):
        last = jnp.maximum(count_ref[0] - 1, 0) // GROUP
        return (jnp.minimum(i, last), 0, 0)

    return pl.pallas_call(
        functools.partial(tile_kernel, transpose),
        out_shape=jax.ShapeDtypeStruct((out_blocks * width, feat), jnp.bfloat16),
        grid_spec=pltpu.PrefetchScalarGridSpec(
            num_scalar_prefetch=3,
            grid=(steps,),
            in_specs=[
                pl.BlockSpec((GROUP, width, width), tiles_map),
                pl.BlockSpec(panel.shape, lambda i, *_: (0, 0)),
            ],
            out_specs=pl.BlockSpec((out_blocks * width, feat), lambda i, *_: (0, 0)),
            scratch_shapes=[pltpu.VMEM((out_blocks * width, feat), jnp.float32)],
        ),
        compiler_params=pltpu.CompilerParams(dimension_semantics=("arbitrary",)),
        cost_estimate=pl.CostEstimate(
            flops=2 * slots * width * width * feat,
            bytes_accessed=tiles.size * 2 + panel.size * 2 + out_blocks * width * feat * 2,
            transcendentals=0,
        ),
    )(rows, cols, count, tiles, panel)


def mesh_coords(axis, peer):
    return tuple(peer if name == axis else lax.axis_index(name) for name in ("row", "col", "feat"))


def exchange_kernel(axis, stride, size, mode, x_ref, o_ref, *scratch):
    index = lax.axis_index(axis)
    me = (index // stride) % size
    base = index - me * stride

    def member(k):
        return mesh_coords(axis, base + k * stride)

    if mode == "gather":
        recv_ref, (send_sems, recv_sems) = o_ref, scratch
    else:
        recv_ref, send_sems, recv_sems = scratch
    barrier = pltpu.get_barrier_semaphore()
    for d in range(1, size):
        pl.semaphore_signal(barrier, inc=1, device_id=member(lax.rem(me + d, size)),
                            device_id_type=pl.DeviceIdType.MESH)
    pl.semaphore_wait(barrier, size - 1)
    copies = []
    for d in range(1, size):
        peer = lax.rem(me + d, size)
        src = x_ref if mode == "gather" else x_ref.at[peer]
        copy = pltpu.make_async_remote_copy(
            src_ref=src, dst_ref=recv_ref.at[me], send_sem=send_sems.at[d],
            recv_sem=recv_sems.at[me], device_id=member(peer),
            device_id_type=pl.DeviceIdType.MESH)
        copy.start()
        copies.append(copy)
    if mode == "gather":
        o_ref[me] = x_ref[...]
    else:
        total = x_ref[me].astype(jnp.float32)
    for d in range(1, size):
        src_dev = lax.rem(me + size - d, size)
        incoming = pltpu.make_async_remote_copy(
            src_ref=recv_ref.at[src_dev], dst_ref=recv_ref.at[src_dev], send_sem=send_sems.at[d],
            recv_sem=recv_sems.at[src_dev], device_id=member(src_dev),
            device_id_type=pl.DeviceIdType.MESH)
        incoming.wait_recv()
        if mode != "gather":
            total = total + recv_ref[src_dev].astype(jnp.float32)
    for copy in copies:
        copy.wait_send()
    if mode != "gather":
        o_ref[...] = total.astype(o_ref.dtype)


def exchange(x, axis, mode, collective_id, stride=1, size=None):
    size = lax.axis_size(axis) if size is None else size
    if mode == "gather":
        out_shape = (size,) + x.shape
        scratch = []
    else:
        out_shape = x.shape[1:]
        scratch = [pltpu.VMEM(x.shape, x.dtype)]
    scratch += [pltpu.SemaphoreType.DMA((size,)), pltpu.SemaphoreType.DMA((size,))]
    return pl.pallas_call(
        functools.partial(exchange_kernel, axis, stride, size, mode),
        out_shape=jax.ShapeDtypeStruct(out_shape, x.dtype),
        in_specs=[pl.BlockSpec(memory_space=pltpu.VMEM)],
        out_specs=pl.BlockSpec(memory_space=pltpu.VMEM),
        scratch_shapes=scratch,
        compiler_params=pltpu.CompilerParams(collective_id=collective_id, has_side_effects=True),
    )(x)


def reduction_plan(rows):
    pairs = []
    for bit in (1, 2, 4, 8, 16, 32, 64):
        for axis in ("row", "col"):
            if bit < lax.axis_size(axis):
                pairs.append((axis, bit))
    halving = []
    while pairs and rows // 2 >= 8 and rows % 16 == 0:
        halving.append(pairs.pop(0))
        rows //= 2
    return halving, pairs


def allreduce_kernel(x_ref, o_ref, recv, send_sems, recv_sems):
    halving, whole = reduction_plan(x_ref.shape[0])

    def bitval(axis, bit):
        return (lax.axis_index(axis) // bit) % 2

    def partner(axis, bit):
        return mesh_coords(axis, lax.axis_index(axis) + bit * (1 - 2 * bitval(axis, bit)))

    barrier = pltpu.get_barrier_semaphore()
    for axis, bit in halving + whole:
        pl.semaphore_signal(barrier, inc=1, device_id=partner(axis, bit),
                            device_id_type=pl.DeviceIdType.MESH)
    pl.semaphore_wait(barrier, len(halving) + len(whole))

    o_ref[...] = x_ref[...]
    k = 0

    def swap(k, axis, bit, send_rows, length):
        copy = pltpu.make_async_remote_copy(
            src_ref=o_ref.at[pl.ds(send_rows, length)], dst_ref=recv.at[k, pl.ds(0, length)],
            send_sem=send_sems.at[k], recv_sem=recv_sems.at[k],
            device_id=partner(axis, bit), device_id_type=pl.DeviceIdType.MESH)
        copy.start()
        copy.wait()

    lo = jnp.int32(0)
    length = x_ref.shape[0]
    starts = []
    for axis, bit in halving:
        length //= 2
        mine = bitval(axis, bit)
        starts.append(lo)
        keep = pl.multiple_of(lo + mine * length, 8)
        give = pl.multiple_of(lo + (1 - mine) * length, 8)
        swap(k, axis, bit, give, length)
        o_ref[pl.ds(keep, length)] = o_ref[pl.ds(keep, length)] + recv[k, pl.ds(0, length)]
        lo = keep
        k += 1
    for axis, bit in whole:
        swap(k, axis, bit, lo, length)
        o_ref[pl.ds(lo, length)] = o_ref[pl.ds(lo, length)] + recv[k, pl.ds(0, length)]
        k += 1
    for (axis, bit), base in zip(reversed(halving), reversed(starts)):
        mine = bitval(axis, bit)
        other = pl.multiple_of(base + (1 - mine) * length, 8)
        swap(k, axis, bit, lo, length)
        o_ref[pl.ds(other, length)] = recv[k, pl.ds(0, length)]
        lo = base
        length *= 2
        k += 1


def allreduce(x, collective_id):
    halving, whole = reduction_plan(x.shape[0])
    steps = 2 * len(halving) + len(whole)
    return pl.pallas_call(
        allreduce_kernel,
        out_shape=jax.ShapeDtypeStruct(x.shape, x.dtype),
        in_specs=[pl.BlockSpec(memory_space=pltpu.VMEM)],
        out_specs=pl.BlockSpec(memory_space=pltpu.VMEM),
        scratch_shapes=[
            pltpu.VMEM((steps, x.shape[0] // 2) + x.shape[1:], x.dtype),
            pltpu.SemaphoreType.DMA((steps,)),
            pltpu.SemaphoreType.DMA((steps,)),
        ],
        compiler_params=pltpu.CompilerParams(collective_id=collective_id, has_side_effects=True),
    )(x)


def shards(features, tile_rows, tile_cols, tile_count, tile_values, weights, cotangent):
    width = tile_values.shape[-1]
    local_tiles = tile_values[0, 0]
    block_rows = tile_rows[0, 0]
    block_cols = tile_cols[0, 0]
    count = tile_count[0, 0].reshape(1)
    n_rowdev = lax.axis_size("row")
    n_coldev = lax.axis_size("col")
    local_blocks = features.shape[0] // width
    feat_half = features.shape[1]
    feat_index = lax.axis_index("feat")
    row_blocks = local_blocks * n_coldev
    col_blocks = local_blocks * n_rowdev
    node_total = features.shape[0] * n_rowdev * n_coldev
    pair = 2 if n_rowdev % 2 == 0 else 1
    chips = n_rowdev // pair
    panel = exchange(features, "row", "gather", 0, stride=pair, size=chips)
    panel = exchange(panel, "row", "gather", 5, stride=1, size=pair).reshape(-1, feat_half)
    owner = block_cols // local_blocks
    block_cols = ((owner % pair) * chips + owner // pair) * local_blocks + block_cols % local_blocks
    partial_value = tile_products(local_tiles, block_rows, block_cols, count, panel,
                                  row_blocks, transpose=False)
    summed = exchange(partial_value.reshape(n_coldev, -1, feat_half), "col", "scatter", 1)
    n_feat = lax.axis_size("feat")
    agg_halves = exchange(summed, "feat", "gather", 7)
    weight_cols = lax.dynamic_slice_in_dim(weights, feat_index * feat_half, feat_half, 1)
    hidden = sum(
        jnp.dot(agg_halves[h], weight_cols[h * feat_half:(h + 1) * feat_half],
                preferred_element_type=jnp.float32)
        for h in range(n_feat)
    )
    negative = jnp.minimum(hidden, 0.0)
    activated = jnp.where(hidden > 0, hidden, jnp.expm1(negative)).astype(jnp.bfloat16)
    slope_factor = jnp.where(hidden > 0, 1.0, jnp.exp(negative))
    grad_out = (cotangent.astype(jnp.float32) * slope_factor).astype(jnp.bfloat16)
    grad_halves = exchange(grad_out, "feat", "gather", 8)
    weight_term = jnp.concatenate([
        lax.dot_general(summed, grad_halves[h], (((0,), (0,)), ((), ())),
                        preferred_element_type=jnp.float32)
        for h in range(n_feat)
    ], axis=1)
    weight_grad = allreduce(weight_term, 4) * node_total ** (-0.5)
    weight_rows = lax.dynamic_slice_in_dim(weights, feat_index * feat_half, feat_half, 0)
    spread = sum(
        lax.dot_general(grad_halves[h], weight_rows[:, h * feat_half:(h + 1) * feat_half],
                        (((1,), (1,)), ((), ())), preferred_element_type=jnp.float32)
        for h in range(n_feat)
    ).astype(jnp.bfloat16)
    spread_panel = exchange(spread, "col", "gather", 2).reshape(-1, feat_half)
    back_partial = tile_products(local_tiles, block_rows, block_cols, count, spread_panel,
                                 col_blocks, transpose=True)
    back_pairs = exchange(back_partial.reshape(pair, -1, feat_half), "row", "scatter", 3,
                          stride=1, size=pair)
    back_summed = exchange(back_pairs.reshape(chips, -1, feat_half), "row", "scatter", 6,
                           stride=pair, size=chips)
    return (activated, back_summed, weight_grad)


def solution(mesh):
    return jax.shard_map(
        shards,
        mesh=mesh,
        in_specs=(
            P(("col", "row"), "feat"),
            P("row", "col", None),
            P("row", "col", None),
            P("row", "col"),
            P("row", "col", None, None, None),
            P(),
            P(("row", "col"), "feat"),
        ),
        out_specs=(P(("row", "col"), "feat"), P(("col", "row"), "feat"), P("feat", None)),
        check_vma=False,
    )
```

```python
import functools

import jax
import jax.numpy as jnp
from jax import lax
from jax.experimental import pallas as pl
from jax.experimental.pallas import tpu as pltpu
from jax.sharding import PartitionSpec as P

GROUP = 64


def tile_kernel(transpose, rows_ref, cols_ref, count_ref, tiles_ref, panel_ref, out_ref, acc_ref):
    step = pl.program_id(0)
    width = tiles_ref.shape[-1]
    count = count_ref[0]
    src_blocks = panel_ref.shape[0] // width
    dst_blocks = acc_ref.shape[0] // width

    @pl.when(step == 0)
    def _():
        acc_ref[...] = jnp.zeros_like(acc_ref)

    @pl.when(step * GROUP < count)
    def _():
        terms = []
        for j in range(GROUP):
            slot = step * GROUP + j
            src = rows_ref[slot] if transpose else cols_ref[slot]
            src = jnp.minimum(jnp.maximum(src, 0), src_blocks - 1)
            block = panel_ref[pl.ds(pl.multiple_of(src * width, width), width), :]
            tile = tiles_ref[j]
            if transpose:
                term = lax.dot_general(tile, block, (((0,), (0,)), ((), ())),
                                       preferred_element_type=jnp.float32)
            else:
                term = jnp.dot(tile, block, preferred_element_type=jnp.float32)
            terms.append(jnp.where(slot < count, term, 0.0))
        for j in range(GROUP):
            slot = step * GROUP + j
            dst = cols_ref[slot] if transpose else rows_ref[slot]
            dst = jnp.minimum(jnp.maximum(dst, 0), dst_blocks - 1)
            rows = pl.ds(pl.multiple_of(dst * width, width), width)
            acc_ref[rows, :] += terms[j]

    @pl.when(step == pl.num_programs(0) - 1)
    def _():
        out_ref[...] = acc_ref[...].astype(out_ref.dtype)


def tile_products(tiles, rows, cols, count, panel, out_blocks, transpose):
    slots, width, _ = tiles.shape
    feat = panel.shape[1]
    steps = slots // GROUP

    def tiles_map(i, rows_ref, cols_ref, count_ref):
        last = jnp.maximum(count_ref[0] - 1, 0) // GROUP
        return (jnp.minimum(i, last), 0, 0)

    return pl.pallas_call(
        functools.partial(tile_kernel, transpose),
        out_shape=jax.ShapeDtypeStruct((out_blocks * width, feat), jnp.bfloat16),
        grid_spec=pltpu.PrefetchScalarGridSpec(
            num_scalar_prefetch=3,
            grid=(steps,),
            in_specs=[
                pl.BlockSpec((GROUP, width, width), tiles_map),
                pl.BlockSpec(panel.shape, lambda i, *_: (0, 0)),
            ],
            out_specs=pl.BlockSpec((out_blocks * width, feat), lambda i, *_: (0, 0)),
            scratch_shapes=[pltpu.VMEM((out_blocks * width, feat), jnp.float32)],
        ),
        compiler_params=pltpu.CompilerParams(dimension_semantics=("arbitrary",)),
        cost_estimate=pl.CostEstimate(
            flops=2 * slots * width * width * feat,
            bytes_accessed=tiles.size * 2 + panel.size * 2 + out_blocks * width * feat * 2,
            transcendentals=0,
        ),
    )(rows, cols, count, tiles, panel)


def mesh_coords(axis, peer):
    return tuple(peer if name == axis else lax.axis_index(name) for name in ("row", "col", "feat"))


def group_of(axis, stride, size):
    index = lax.axis_index(axis)
    me = (index // stride) % size
    base = index - me * stride
    return me, lambda k: mesh_coords(axis, base + k * stride)


def exchange_targets(axis, stride, size):
    me, member = group_of(axis, stride, size)
    return [member(lax.rem(me + d, size)) for d in range(1, size)]


def enter(targets):
    barrier = pltpu.get_barrier_semaphore()
    for target in targets:
        pl.semaphore_signal(barrier, inc=1, device_id=target, device_id_type=pl.DeviceIdType.MESH)
    pl.semaphore_wait(barrier, len(targets))


def exchange_start(axis, stride, size, mode, x_ref, recv_ref, send_sems, recv_sems):
    me, member = group_of(axis, stride, size)
    copies = []
    for d in range(1, size):
        peer = lax.rem(me + d, size)
        src = x_ref if mode == "gather" else x_ref.at[peer]
        copy = pltpu.make_async_remote_copy(
            src_ref=src, dst_ref=recv_ref.at[me], send_sem=send_sems.at[d],
            recv_sem=recv_sems.at[me], device_id=member(peer),
            device_id_type=pl.DeviceIdType.MESH)
        copy.start()
        copies.append(copy)
    return copies


def exchange_finish(axis, stride, size, mode, x_ref, o_ref, recv_ref, send_sems, recv_sems, copies):
    me, member = group_of(axis, stride, size)
    if mode == "gather":
        o_ref[me] = x_ref[...]
    else:
        total = x_ref[me].astype(jnp.float32)
    for d in range(1, size):
        src_dev = lax.rem(me + size - d, size)
        incoming = pltpu.make_async_remote_copy(
            src_ref=recv_ref.at[src_dev], dst_ref=recv_ref.at[src_dev], send_sem=send_sems.at[d],
            recv_sem=recv_sems.at[src_dev], device_id=member(src_dev),
            device_id_type=pl.DeviceIdType.MESH)
        incoming.wait_recv()
        if mode != "gather":
            total = total + recv_ref[src_dev].astype(jnp.float32)
    for copy in copies:
        copy.wait_send()
    if mode != "gather":
        o_ref[...] = total.astype(o_ref.dtype)


def exchange_kernel(axis, stride, size, mode, x_ref, o_ref, *scratch):
    if mode == "gather":
        recv_ref, (send_sems, recv_sems) = o_ref, scratch
    else:
        recv_ref, send_sems, recv_sems = scratch
    enter(exchange_targets(axis, stride, size))
    copies = exchange_start(axis, stride, size, mode, x_ref, recv_ref, send_sems, recv_sems)
    exchange_finish(axis, stride, size, mode, x_ref, o_ref, recv_ref, send_sems, recv_sems, copies)


def exchange_scratch(x, mode, size):
    scratch = [] if mode == "gather" else [pltpu.VMEM(x.shape, x.dtype)]
    return scratch + [pltpu.SemaphoreType.DMA((size,)), pltpu.SemaphoreType.DMA((size,))]


def exchange_shape(x, mode, size):
    shape = (size,) + x.shape if mode == "gather" else x.shape[1:]
    return jax.ShapeDtypeStruct(shape, x.dtype)


def exchange(x, axis, mode, collective_id, stride=1, size=None):
    size = lax.axis_size(axis) if size is None else size
    return pl.pallas_call(
        functools.partial(exchange_kernel, axis, stride, size, mode),
        out_shape=exchange_shape(x, mode, size),
        in_specs=[pl.BlockSpec(memory_space=pltpu.VMEM)],
        out_specs=pl.BlockSpec(memory_space=pltpu.VMEM),
        scratch_shapes=exchange_scratch(x, mode, size),
        compiler_params=pltpu.CompilerParams(collective_id=collective_id, has_side_effects=True),
    )(x)


def reduction_plan(rows):
    pairs = []
    for bit in (1, 2, 4, 8, 16, 32, 64):
        for axis in ("row", "col"):
            if bit < lax.axis_size(axis):
                pairs.append((axis, bit))
    halving = []
    while pairs and rows // 2 >= 8 and rows % 16 == 0:
        halving.append(pairs.pop(0))
        rows //= 2
    return halving, pairs


def bitval(axis, bit):
    return (lax.axis_index(axis) // bit) % 2


def partner(axis, bit):
    return mesh_coords(axis, lax.axis_index(axis) + bit * (1 - 2 * bitval(axis, bit)))


def reduce_targets(rows):
    halving, whole = reduction_plan(rows)
    return [partner(axis, bit) for axis, bit in halving + whole]


def reduce_rounds(x_ref, o_ref, recv, send_sems, recv_sems):
    halving, whole = reduction_plan(x_ref.shape[0])
    o_ref[...] = x_ref[...]
    k = 0

    def swap(k, axis, bit, send_rows, length):
        copy = pltpu.make_async_remote_copy(
            src_ref=o_ref.at[pl.ds(send_rows, length)], dst_ref=recv.at[k, pl.ds(0, length)],
            send_sem=send_sems.at[k], recv_sem=recv_sems.at[k],
            device_id=partner(axis, bit), device_id_type=pl.DeviceIdType.MESH)
        copy.start()
        copy.wait()

    lo = jnp.int32(0)
    length = x_ref.shape[0]
    starts = []
    for axis, bit in halving:
        length //= 2
        mine = bitval(axis, bit)
        starts.append(lo)
        keep = pl.multiple_of(lo + mine * length, 8)
        give = pl.multiple_of(lo + (1 - mine) * length, 8)
        swap(k, axis, bit, give, length)
        o_ref[pl.ds(keep, length)] = o_ref[pl.ds(keep, length)] + recv[k, pl.ds(0, length)]
        lo = keep
        k += 1
    for axis, bit in whole:
        swap(k, axis, bit, lo, length)
        o_ref[pl.ds(lo, length)] = o_ref[pl.ds(lo, length)] + recv[k, pl.ds(0, length)]
        k += 1
    for (axis, bit), base in zip(reversed(halving), reversed(starts)):
        mine = bitval(axis, bit)
        other = pl.multiple_of(base + (1 - mine) * length, 8)
        swap(k, axis, bit, lo, length)
        o_ref[pl.ds(other, length)] = recv[k, pl.ds(0, length)]
        lo = base
        length *= 2
        k += 1


def reduce_scratch(w):
    halving, whole = reduction_plan(w.shape[0])
    steps = 2 * len(halving) + len(whole)
    return [
        pltpu.VMEM((steps, w.shape[0] // 2) + w.shape[1:], w.dtype),
        pltpu.SemaphoreType.DMA((steps,)),
        pltpu.SemaphoreType.DMA((steps,)),
    ]


def gather_reduce_kernel(axis, x_ref, w_ref, o_ref, ow_ref, g_send, g_recv, recv, send_sems, recv_sems):
    size = lax.axis_size(axis)
    enter(exchange_targets(axis, 1, size) + reduce_targets(w_ref.shape[0]))
    copies = exchange_start(axis, 1, size, "gather", x_ref, o_ref, g_send, g_recv)
    reduce_rounds(w_ref, ow_ref, recv, send_sems, recv_sems)
    exchange_finish(axis, 1, size, "gather", x_ref, o_ref, o_ref, g_send, g_recv, copies)


def gather_and_reduce(x, w, axis, collective_id):
    size = lax.axis_size(axis)
    return pl.pallas_call(
        functools.partial(gather_reduce_kernel, axis),
        out_shape=(exchange_shape(x, "gather", size), jax.ShapeDtypeStruct(w.shape, w.dtype)),
        in_specs=[pl.BlockSpec(memory_space=pltpu.VMEM)] * 2,
        out_specs=(pl.BlockSpec(memory_space=pltpu.VMEM),) * 2,
        scratch_shapes=exchange_scratch(x, "gather", size) + reduce_scratch(w),
        compiler_params=pltpu.CompilerParams(collective_id=collective_id, has_side_effects=True),
    )(x, w)


def shards(features, tile_rows, tile_cols, tile_count, tile_values, weights, cotangent):
    width = tile_values.shape[-1]
    local_tiles = tile_values[0, 0]
    block_rows = tile_rows[0, 0]
    block_cols = tile_cols[0, 0]
    count = tile_count[0, 0].reshape(1)
    n_rowdev = lax.axis_size("row")
    n_coldev = lax.axis_size("col")
    local_blocks = features.shape[0] // width
    feat_half = features.shape[1]
    feat_index = lax.axis_index("feat")
    row_blocks = local_blocks * n_coldev
    col_blocks = local_blocks * n_rowdev
    node_total = features.shape[0] * n_rowdev * n_coldev
    pair = 2 if n_rowdev % 2 == 0 else 1
    chips = n_rowdev // pair
    panel = exchange(features, "row", "gather", 0, stride=pair, size=chips)
    panel = exchange(panel, "row", "gather", 5, stride=1, size=pair).reshape(-1, feat_half)
    owner = block_cols // local_blocks
    block_cols = ((owner % pair) * chips + owner // pair) * local_blocks + block_cols % local_blocks
    partial_value = tile_products(local_tiles, block_rows, block_cols, count, panel,
                                  row_blocks, transpose=False)
    summed = exchange(partial_value.reshape(n_coldev, -1, feat_half), "col", "scatter", 1)
    n_feat = lax.axis_size("feat")
    agg_halves = exchange(summed, "feat", "gather", 7)
    weight_cols = lax.dynamic_slice_in_dim(weights, feat_index * feat_half, feat_half, 1)
    hidden = sum(
        jnp.dot(agg_halves[h], weight_cols[h * feat_half:(h + 1) * feat_half],
                preferred_element_type=jnp.float32)
        for h in range(n_feat)
    )
    negative = jnp.minimum(hidden, 0.0)
    activated = jnp.where(hidden > 0, hidden, jnp.expm1(negative)).astype(jnp.bfloat16)
    slope_factor = jnp.where(hidden > 0, 1.0, jnp.exp(negative))
    grad_out = (cotangent.astype(jnp.float32) * slope_factor).astype(jnp.bfloat16)
    grad_halves = exchange(grad_out, "feat", "gather", 8)
    weight_term = jnp.concatenate([
        lax.dot_general(summed, grad_halves[h], (((0,), (0,)), ((), ())),
                        preferred_element_type=jnp.float32)
        for h in range(n_feat)
    ], axis=1)
    weight_rows = lax.dynamic_slice_in_dim(weights, feat_index * feat_half, feat_half, 0)
    spread = sum(
        lax.dot_general(grad_halves[h], weight_rows[:, h * feat_half:(h + 1) * feat_half],
                        (((1,), (1,)), ((), ())), preferred_element_type=jnp.float32)
        for h in range(n_feat)
    ).astype(jnp.bfloat16)
    spread_panel, weight_sum = gather_and_reduce(spread, weight_term, "col", 2)
    spread_panel = spread_panel.reshape(-1, feat_half)
    weight_grad = weight_sum * node_total ** (-0.5)
    back_partial = tile_products(local_tiles, block_rows, block_cols, count, spread_panel,
                                 col_blocks, transpose=True)
    back_pairs = exchange(back_partial.reshape(pair, -1, feat_half), "row", "scatter", 3,
                          stride=1, size=pair)
    back_summed = exchange(back_pairs.reshape(chips, -1, feat_half), "row", "scatter", 6,
                           stride=pair, size=chips)
    return (activated, back_summed, weight_grad)


def solution(mesh):
    return jax.shard_map(
        shards,
        mesh=mesh,
        in_specs=(
            P(("col", "row"), "feat"),
            P("row", "col", None),
            P("row", "col", None),
            P("row", "col"),
            P("row", "col", None, None, None),
            P(),
            P(("row", "col"), "feat"),
        ),
        out_specs=(P(("row", "col"), "feat"), P(("col", "row"), "feat"), P("feat", None)),
        check_vma=False,
    )
```

```python
import functools

import jax
import jax.numpy as jnp
from jax import lax
from jax.experimental import pallas as pl
from jax.experimental.pallas import tpu as pltpu
from jax.sharding import PartitionSpec as P

GROUP = 64


def tile_kernel(transpose, rows_ref, cols_ref, count_ref, tiles_ref, panel_ref, out_ref, acc_ref):
    step = pl.program_id(0)
    width = tiles_ref.shape[-1]
    count = count_ref[0]
    src_blocks = panel_ref.shape[0] // width
    dst_blocks = acc_ref.shape[0] // width

    @pl.when(step == 0)
    def _():
        acc_ref[...] = jnp.zeros_like(acc_ref)

    @pl.when(step * GROUP < count)
    def _():
        terms = []
        for j in range(GROUP):
            slot = step * GROUP + j
            src = rows_ref[slot] if transpose else cols_ref[slot]
            src = jnp.minimum(jnp.maximum(src, 0), src_blocks - 1)
            block = panel_ref[pl.ds(pl.multiple_of(src * width, width), width), :]
            tile = tiles_ref[j]
            if transpose:
                term = lax.dot_general(tile, block, (((0,), (0,)), ((), ())),
                                       preferred_element_type=jnp.float32)
            else:
                term = jnp.dot(tile, block, preferred_element_type=jnp.float32)
            terms.append(jnp.where(slot < count, term, 0.0))
        for j in range(GROUP):
            slot = step * GROUP + j
            dst = cols_ref[slot] if transpose else rows_ref[slot]
            dst = jnp.minimum(jnp.maximum(dst, 0), dst_blocks - 1)
            rows = pl.ds(pl.multiple_of(dst * width, width), width)
            acc_ref[rows, :] += terms[j]

    @pl.when(step == pl.num_programs(0) - 1)
    def _():
        out_ref[...] = acc_ref[...].astype(out_ref.dtype)


def tile_products(tiles, rows, cols, count, panel, out_blocks, transpose):
    slots, width, _ = tiles.shape
    feat = panel.shape[1]
    steps = slots // GROUP

    def tiles_map(i, rows_ref, cols_ref, count_ref):
        last = jnp.maximum(count_ref[0] - 1, 0) // GROUP
        return (jnp.minimum(i, last), 0, 0)

    return pl.pallas_call(
        functools.partial(tile_kernel, transpose),
        out_shape=jax.ShapeDtypeStruct((out_blocks * width, feat), jnp.bfloat16),
        grid_spec=pltpu.PrefetchScalarGridSpec(
            num_scalar_prefetch=3,
            grid=(steps,),
            in_specs=[
                pl.BlockSpec((GROUP, width, width), tiles_map),
                pl.BlockSpec(panel.shape, lambda i, *_: (0, 0)),
            ],
            out_specs=pl.BlockSpec((out_blocks * width, feat), lambda i, *_: (0, 0)),
            scratch_shapes=[pltpu.VMEM((out_blocks * width, feat), jnp.float32)],
        ),
        compiler_params=pltpu.CompilerParams(dimension_semantics=("arbitrary",)),
        cost_estimate=pl.CostEstimate(
            flops=2 * slots * width * width * feat,
            bytes_accessed=tiles.size * 2 + panel.size * 2 + out_blocks * width * feat * 2,
            transcendentals=0,
        ),
    )(rows, cols, count, tiles, panel)


def mesh_coords(axis, peer):
    return tuple(peer if name == axis else lax.axis_index(name) for name in ("row", "col", "feat"))


def group_of(axis, stride, size):
    index = lax.axis_index(axis)
    me = (index // stride) % size
    base = index - me * stride
    return me, lambda k: mesh_coords(axis, base + k * stride)


def exchange_targets(axis, stride, size):
    me, member = group_of(axis, stride, size)
    return [member(lax.rem(me + d, size)) for d in range(1, size)]


def enter(targets):
    barrier = pltpu.get_barrier_semaphore()
    for target in targets:
        pl.semaphore_signal(barrier, inc=1, device_id=target, device_id_type=pl.DeviceIdType.MESH)
    pl.semaphore_wait(barrier, len(targets))


def exchange_start(axis, stride, size, mode, x_ref, recv_ref, send_sems, recv_sems):
    me, member = group_of(axis, stride, size)
    copies = []
    for d in range(1, size):
        peer = lax.rem(me + d, size)
        src = x_ref if mode == "gather" else x_ref.at[peer]
        copy = pltpu.make_async_remote_copy(
            src_ref=src, dst_ref=recv_ref.at[me], send_sem=send_sems.at[d],
            recv_sem=recv_sems.at[me], device_id=member(peer),
            device_id_type=pl.DeviceIdType.MESH)
        copy.start()
        copies.append(copy)
    return copies


def exchange_finish(axis, stride, size, mode, x_ref, o_ref, recv_ref, send_sems, recv_sems, copies):
    me, member = group_of(axis, stride, size)
    if mode == "gather":
        o_ref[me] = x_ref[...]
    else:
        total = x_ref[me].astype(jnp.float32)
    for d in range(1, size):
        src_dev = lax.rem(me + size - d, size)
        incoming = pltpu.make_async_remote_copy(
            src_ref=recv_ref.at[src_dev], dst_ref=recv_ref.at[src_dev], send_sem=send_sems.at[d],
            recv_sem=recv_sems.at[src_dev], device_id=member(src_dev),
            device_id_type=pl.DeviceIdType.MESH)
        incoming.wait_recv()
        if mode != "gather":
            total = total + recv_ref[src_dev].astype(jnp.float32)
    for copy in copies:
        copy.wait_send()
    if mode != "gather":
        o_ref[...] = total.astype(o_ref.dtype)


def exchange_kernel(axis, stride, size, mode, x_ref, o_ref, *scratch):
    if mode == "gather":
        recv_ref, (send_sems, recv_sems) = o_ref, scratch
    else:
        recv_ref, send_sems, recv_sems = scratch
    enter(exchange_targets(axis, stride, size))
    copies = exchange_start(axis, stride, size, mode, x_ref, recv_ref, send_sems, recv_sems)
    exchange_finish(axis, stride, size, mode, x_ref, o_ref, recv_ref, send_sems, recv_sems, copies)


def exchange_scratch(x, mode, size):
    scratch = [] if mode == "gather" else [pltpu.VMEM(x.shape, x.dtype)]
    return scratch + [pltpu.SemaphoreType.DMA((size,)), pltpu.SemaphoreType.DMA((size,))]


def exchange_shape(x, mode, size):
    shape = (size,) + x.shape if mode == "gather" else x.shape[1:]
    return jax.ShapeDtypeStruct(shape, x.dtype)


def exchange(x, axis, mode, collective_id, stride=1, size=None):
    size = lax.axis_size(axis) if size is None else size
    return pl.pallas_call(
        functools.partial(exchange_kernel, axis, stride, size, mode),
        out_shape=exchange_shape(x, mode, size),
        in_specs=[pl.BlockSpec(memory_space=pltpu.VMEM)],
        out_specs=pl.BlockSpec(memory_space=pltpu.VMEM),
        scratch_shapes=exchange_scratch(x, mode, size),
        compiler_params=pltpu.CompilerParams(collective_id=collective_id, has_side_effects=True),
    )(x)


def pair_targets(chips):
    me, member = group_of("row", 2, chips)
    _, sibling = group_of("row", 1, 2)
    return [member(lax.rem(me + d, chips)) for d in range(1, chips)], sibling


def row_gather_kernel(chips, x_ref, o_ref, send_sems, recv_sems, fwd_send, fwd_recv):
    z_me, z_member = group_of("row", 2, chips)
    c_me, core_member = group_of("row", 1, 2)
    sibling = core_member(1 - c_me)
    peers, _ = pair_targets(chips)
    enter(peers + [sibling])
    copies = []
    for d in range(1, chips):
        peer = lax.rem(z_me + d, chips)
        copy = pltpu.make_async_remote_copy(
            src_ref=x_ref, dst_ref=o_ref.at[c_me, z_me], send_sem=send_sems.at[d],
            recv_sem=recv_sems.at[z_me], device_id=z_member(peer),
            device_id_type=pl.DeviceIdType.MESH)
        copy.start()
        copies.append(copy)
    own = pltpu.make_async_remote_copy(
        src_ref=x_ref, dst_ref=o_ref.at[c_me, z_me], send_sem=fwd_send.at[z_me],
        recv_sem=fwd_recv.at[z_me], device_id=sibling, device_id_type=pl.DeviceIdType.MESH)
    own.start()
    copies.append(own)
    o_ref[c_me, z_me] = x_ref[...]
    for d in range(1, chips):
        src_dev = lax.rem(z_me + chips - d, chips)
        incoming = pltpu.make_async_remote_copy(
            src_ref=o_ref.at[c_me, src_dev], dst_ref=o_ref.at[c_me, src_dev],
            send_sem=send_sems.at[d], recv_sem=recv_sems.at[src_dev],
            device_id=z_member(src_dev), device_id_type=pl.DeviceIdType.MESH)
        incoming.wait_recv()
        forward = pltpu.make_async_remote_copy(
            src_ref=o_ref.at[c_me, src_dev], dst_ref=o_ref.at[c_me, src_dev],
            send_sem=fwd_send.at[src_dev], recv_sem=fwd_recv.at[src_dev], device_id=sibling,
            device_id_type=pl.DeviceIdType.MESH)
        forward.start()
        copies.append(forward)
    for k in range(chips):
        incoming = pltpu.make_async_remote_copy(
            src_ref=o_ref.at[1 - c_me, k], dst_ref=o_ref.at[1 - c_me, k],
            send_sem=fwd_send.at[k], recv_sem=fwd_recv.at[k], device_id=sibling,
            device_id_type=pl.DeviceIdType.MESH)
        incoming.wait_recv()
    for copy in copies:
        copy.wait_send()


def row_gather(x, chips, collective_id):
    return pl.pallas_call(
        functools.partial(row_gather_kernel, chips),
        out_shape=jax.ShapeDtypeStruct((2, chips) + x.shape, x.dtype),
        in_specs=[pl.BlockSpec(memory_space=pltpu.VMEM)],
        out_specs=pl.BlockSpec(memory_space=pltpu.VMEM),
        scratch_shapes=[pltpu.SemaphoreType.DMA((chips,))] * 4,
        compiler_params=pltpu.CompilerParams(collective_id=collective_id, has_side_effects=True),
    )(x)


def row_scatter_kernel(chips, x_ref, o_ref, pair_recv, pair_sum, z_recv,
                       pair_send_sems, pair_recv_sems, z_send_sems, z_recv_sems):
    z_me, z_member = group_of("row", 2, chips)
    c_me, core_member = group_of("row", 1, 2)
    sibling = core_member(1 - c_me)
    peers, _ = pair_targets(chips)
    enter(peers + [sibling])
    copies = []
    for k in range(chips):
        copy = pltpu.make_async_remote_copy(
            src_ref=x_ref.at[1 - c_me, k], dst_ref=pair_recv.at[k], send_sem=pair_send_sems.at[k],
            recv_sem=pair_recv_sems.at[k], device_id=sibling, device_id_type=pl.DeviceIdType.MESH)
        copy.start()
        copies.append(copy)
    order = [lax.rem(z_me + d, chips) for d in range(1, chips)] + [z_me]
    for d, k in enumerate(order, start=1):
        incoming = pltpu.make_async_remote_copy(
            src_ref=pair_recv.at[k], dst_ref=pair_recv.at[k], send_sem=pair_send_sems.at[k],
            recv_sem=pair_recv_sems.at[k], device_id=sibling, device_id_type=pl.DeviceIdType.MESH)
        incoming.wait_recv()
        pair_sum[k] = (x_ref[c_me, k].astype(jnp.float32)
                       + pair_recv[k].astype(jnp.float32)).astype(pair_sum.dtype)
        if d < chips:
            copy = pltpu.make_async_remote_copy(
                src_ref=pair_sum.at[k], dst_ref=z_recv.at[z_me], send_sem=z_send_sems.at[d],
                recv_sem=z_recv_sems.at[z_me], device_id=z_member(k),
                device_id_type=pl.DeviceIdType.MESH)
            copy.start()
            copies.append(copy)
    total = pair_sum[z_me].astype(jnp.float32)
    for d in range(1, chips):
        src_dev = lax.rem(z_me + chips - d, chips)
        incoming = pltpu.make_async_remote_copy(
            src_ref=z_recv.at[src_dev], dst_ref=z_recv.at[src_dev], send_sem=z_send_sems.at[d],
            recv_sem=z_recv_sems.at[src_dev], device_id=z_member(src_dev),
            device_id_type=pl.DeviceIdType.MESH)
        incoming.wait_recv()
        total = total + z_recv[src_dev].astype(jnp.float32)
    for copy in copies:
        copy.wait_send()
    o_ref[...] = total.astype(o_ref.dtype)


def row_scatter(x, chips, collective_id):
    block = x.shape[2:]
    return pl.pallas_call(
        functools.partial(row_scatter_kernel, chips),
        out_shape=jax.ShapeDtypeStruct(block, x.dtype),
        in_specs=[pl.BlockSpec(memory_space=pltpu.VMEM)],
        out_specs=pl.BlockSpec(memory_space=pltpu.VMEM),
        scratch_shapes=[pltpu.VMEM((chips,) + block, x.dtype)] * 3
        + [pltpu.SemaphoreType.DMA((chips,))] * 4,
        compiler_params=pltpu.CompilerParams(collective_id=collective_id, has_side_effects=True),
    )(x)


def reduction_plan(rows):
    pairs = []
    for bit in (1, 2, 4, 8, 16, 32, 64):
        for axis in ("row", "col"):
            if bit < lax.axis_size(axis):
                pairs.append((axis, bit))
    halving = []
    while pairs and rows // 2 >= 8 and rows % 16 == 0:
        halving.append(pairs.pop(0))
        rows //= 2
    return halving, pairs


def bitval(axis, bit):
    return (lax.axis_index(axis) // bit) % 2


def partner(axis, bit):
    return mesh_coords(axis, lax.axis_index(axis) + bit * (1 - 2 * bitval(axis, bit)))


def reduce_targets(rows):
    halving, whole = reduction_plan(rows)
    return [partner(axis, bit) for axis, bit in halving + whole]


def reduce_rounds(x_ref, o_ref, recv, send_sems, recv_sems):
    halving, whole = reduction_plan(x_ref.shape[0])
    o_ref[...] = x_ref[...]
    k = 0

    def swap(k, axis, bit, send_rows, length):
        copy = pltpu.make_async_remote_copy(
            src_ref=o_ref.at[pl.ds(send_rows, length)], dst_ref=recv.at[k, pl.ds(0, length)],
            send_sem=send_sems.at[k], recv_sem=recv_sems.at[k],
            device_id=partner(axis, bit), device_id_type=pl.DeviceIdType.MESH)
        copy.start()
        copy.wait()

    lo = jnp.int32(0)
    length = x_ref.shape[0]
    starts = []
    for axis, bit in halving:
        length //= 2
        mine = bitval(axis, bit)
        starts.append(lo)
        keep = pl.multiple_of(lo + mine * length, 8)
        give = pl.multiple_of(lo + (1 - mine) * length, 8)
        swap(k, axis, bit, give, length)
        o_ref[pl.ds(keep, length)] = o_ref[pl.ds(keep, length)] + recv[k, pl.ds(0, length)]
        lo = keep
        k += 1
    for axis, bit in whole:
        swap(k, axis, bit, lo, length)
        o_ref[pl.ds(lo, length)] = o_ref[pl.ds(lo, length)] + recv[k, pl.ds(0, length)]
        k += 1
    for (axis, bit), base in zip(reversed(halving), reversed(starts)):
        mine = bitval(axis, bit)
        other = pl.multiple_of(base + (1 - mine) * length, 8)
        swap(k, axis, bit, lo, length)
        o_ref[pl.ds(other, length)] = recv[k, pl.ds(0, length)]
        lo = base
        length *= 2
        k += 1


def reduce_scratch(w):
    halving, whole = reduction_plan(w.shape[0])
    steps = 2 * len(halving) + len(whole)
    return [
        pltpu.VMEM((steps, w.shape[0] // 2) + w.shape[1:], w.dtype),
        pltpu.SemaphoreType.DMA((steps,)),
        pltpu.SemaphoreType.DMA((steps,)),
    ]


def gather_reduce_kernel(axis, x_ref, w_ref, o_ref, ow_ref, g_send, g_recv, recv, send_sems, recv_sems):
    size = lax.axis_size(axis)
    enter(exchange_targets(axis, 1, size) + reduce_targets(w_ref.shape[0]))
    copies = exchange_start(axis, 1, size, "gather", x_ref, o_ref, g_send, g_recv)
    reduce_rounds(w_ref, ow_ref, recv, send_sems, recv_sems)
    exchange_finish(axis, 1, size, "gather", x_ref, o_ref, o_ref, g_send, g_recv, copies)


def gather_and_reduce(x, w, axis, collective_id):
    size = lax.axis_size(axis)
    return pl.pallas_call(
        functools.partial(gather_reduce_kernel, axis),
        out_shape=(exchange_shape(x, "gather", size), jax.ShapeDtypeStruct(w.shape, w.dtype)),
        in_specs=[pl.BlockSpec(memory_space=pltpu.VMEM)] * 2,
        out_specs=(pl.BlockSpec(memory_space=pltpu.VMEM),) * 2,
        scratch_shapes=exchange_scratch(x, "gather", size) + reduce_scratch(w),
        compiler_params=pltpu.CompilerParams(collective_id=collective_id, has_side_effects=True),
    )(x, w)


def shards(features, tile_rows, tile_cols, tile_count, tile_values, weights, cotangent):
    width = tile_values.shape[-1]
    local_tiles = tile_values[0, 0]
    block_rows = tile_rows[0, 0]
    block_cols = tile_cols[0, 0]
    count = tile_count[0, 0].reshape(1)
    n_rowdev = lax.axis_size("row")
    n_coldev = lax.axis_size("col")
    local_blocks = features.shape[0] // width
    feat_half = features.shape[1]
    feat_index = lax.axis_index("feat")
    row_blocks = local_blocks * n_coldev
    col_blocks = local_blocks * n_rowdev
    node_total = features.shape[0] * n_rowdev * n_coldev
    pair = 2 if n_rowdev % 2 == 0 else 1
    chips = n_rowdev // pair
    if pair == 2:
        panel = row_gather(features, chips, 0).reshape(-1, feat_half)
    else:
        panel = exchange(features, "row", "gather", 0).reshape(-1, feat_half)
    owner = block_cols // local_blocks
    block_cols = ((owner % pair) * chips + owner // pair) * local_blocks + block_cols % local_blocks
    partial_value = tile_products(local_tiles, block_rows, block_cols, count, panel,
                                  row_blocks, transpose=False)
    summed = exchange(partial_value.reshape(n_coldev, -1, feat_half), "col", "scatter", 1)
    n_feat = lax.axis_size("feat")
    agg_halves = exchange(summed, "feat", "gather", 7)
    weight_cols = lax.dynamic_slice_in_dim(weights, feat_index * feat_half, feat_half, 1)
    hidden = sum(
        jnp.dot(agg_halves[h], weight_cols[h * feat_half:(h + 1) * feat_half],
                preferred_element_type=jnp.float32)
        for h in range(n_feat)
    )
    negative = jnp.minimum(hidden, 0.0)
    activated = jnp.where(hidden > 0, hidden, jnp.expm1(negative)).astype(jnp.bfloat16)
    slope_factor = jnp.where(hidden > 0, 1.0, jnp.exp(negative))
    grad_out = (cotangent.astype(jnp.float32) * slope_factor).astype(jnp.bfloat16)
    grad_halves = exchange(grad_out, "feat", "gather", 8)
    weight_term = jnp.concatenate([
        lax.dot_general(summed, grad_halves[h], (((0,), (0,)), ((), ())),
                        preferred_element_type=jnp.float32)
        for h in range(n_feat)
    ], axis=1)
    weight_rows = lax.dynamic_slice_in_dim(weights, feat_index * feat_half, feat_half, 0)
    spread = sum(
        lax.dot_general(grad_halves[h], weight_rows[:, h * feat_half:(h + 1) * feat_half],
                        (((1,), (1,)), ((), ())), preferred_element_type=jnp.float32)
        for h in range(n_feat)
    ).astype(jnp.bfloat16)
    spread_panel, weight_sum = gather_and_reduce(spread, weight_term, "col", 2)
    spread_panel = spread_panel.reshape(-1, feat_half)
    weight_grad = weight_sum * node_total ** (-0.5)
    back_partial = tile_products(local_tiles, block_rows, block_cols, count, spread_panel,
                                 col_blocks, transpose=True)
    if pair == 2:
        back_summed = row_scatter(back_partial.reshape(pair, chips, -1, feat_half), chips, 3)
    else:
        back_summed = exchange(back_partial.reshape(n_rowdev, -1, feat_half), "row", "scatter", 3)
    return (activated, back_summed, weight_grad)


def solution(mesh):
    return jax.shard_map(
        shards,
        mesh=mesh,
        in_specs=(
            P(("col", "row"), "feat"),
            P("row", "col", None),
            P("row", "col", None),
            P("row", "col"),
            P("row", "col", None, None, None),
            P(),
            P(("row", "col"), "feat"),
        ),
        out_specs=(P(("row", "col"), "feat"), P(("col", "row"), "feat"), P("feat", None)),
        check_vma=False,
    )
```

```python
import functools

import jax
import jax.numpy as jnp
from jax import lax
from jax.experimental import pallas as pl
from jax.experimental.pallas import tpu as pltpu
from jax.sharding import PartitionSpec as P

GROUP = 64


def tile_kernel(transpose, rows_ref, cols_ref, count_ref, tiles_ref, panel_ref, out_ref, acc_ref):
    step = pl.program_id(0)
    width = tiles_ref.shape[-1]
    count = count_ref[0]
    src_blocks = panel_ref.shape[0] // width
    dst_blocks = acc_ref.shape[0] // width

    @pl.when(step == 0)
    def _():
        acc_ref[...] = jnp.zeros_like(acc_ref)

    @pl.when(step * GROUP < count)
    def _():
        terms = []
        for j in range(GROUP):
            slot = step * GROUP + j
            src = rows_ref[slot] if transpose else cols_ref[slot]
            src = jnp.minimum(jnp.maximum(src, 0), src_blocks - 1)
            block = panel_ref[pl.ds(pl.multiple_of(src * width, width), width), :]
            tile = tiles_ref[j]
            if transpose:
                term = lax.dot_general(tile, block, (((0,), (0,)), ((), ())),
                                       preferred_element_type=jnp.float32)
            else:
                term = jnp.dot(tile, block, preferred_element_type=jnp.float32)
            terms.append(jnp.where(slot < count, term, 0.0))
        for j in range(GROUP):
            slot = step * GROUP + j
            dst = cols_ref[slot] if transpose else rows_ref[slot]
            dst = jnp.minimum(jnp.maximum(dst, 0), dst_blocks - 1)
            rows = pl.ds(pl.multiple_of(dst * width, width), width)
            acc_ref[rows, :] += terms[j]

    @pl.when(step == pl.num_programs(0) - 1)
    def _():
        out_ref[...] = acc_ref[...].astype(out_ref.dtype)


def tile_products(tiles, rows, cols, count, panel, out_blocks, transpose):
    slots, width, _ = tiles.shape
    feat = panel.shape[1]
    steps = slots // GROUP

    def tiles_map(i, rows_ref, cols_ref, count_ref):
        last = jnp.maximum(count_ref[0] - 1, 0) // GROUP
        return (jnp.minimum(i, last), 0, 0)

    return pl.pallas_call(
        functools.partial(tile_kernel, transpose),
        out_shape=jax.ShapeDtypeStruct((out_blocks * width, feat), jnp.bfloat16),
        grid_spec=pltpu.PrefetchScalarGridSpec(
            num_scalar_prefetch=3,
            grid=(steps,),
            in_specs=[
                pl.BlockSpec((GROUP, width, width), tiles_map),
                pl.BlockSpec(panel.shape, lambda i, *_: (0, 0)),
            ],
            out_specs=pl.BlockSpec((out_blocks * width, feat), lambda i, *_: (0, 0)),
            scratch_shapes=[pltpu.VMEM((out_blocks * width, feat), jnp.float32)],
        ),
        compiler_params=pltpu.CompilerParams(dimension_semantics=("arbitrary",)),
        cost_estimate=pl.CostEstimate(
            flops=2 * slots * width * width * feat,
            bytes_accessed=tiles.size * 2 + panel.size * 2 + out_blocks * width * feat * 2,
            transcendentals=0,
        ),
    )(rows, cols, count, tiles, panel)


def mesh_coords(axis, peer):
    return tuple(peer if name == axis else lax.axis_index(name) for name in ("row", "col", "feat"))


def group_of(axis, stride, size):
    index = lax.axis_index(axis)
    me = (index // stride) % size
    base = index - me * stride
    return me, lambda k: mesh_coords(axis, base + k * stride)


def exchange_targets(axis, stride, size):
    me, member = group_of(axis, stride, size)
    return [member(lax.rem(me + d, size)) for d in range(1, size)]


def enter(targets):
    barrier = pltpu.get_barrier_semaphore()
    for target in targets:
        pl.semaphore_signal(barrier, inc=1, device_id=target, device_id_type=pl.DeviceIdType.MESH)
    pl.semaphore_wait(barrier, len(targets))


def exchange_start(axis, stride, size, mode, x_ref, recv_ref, send_sems, recv_sems):
    me, member = group_of(axis, stride, size)
    copies = []
    for d in range(1, size):
        peer = lax.rem(me + d, size)
        src = x_ref if mode == "gather" else x_ref.at[peer]
        copy = pltpu.make_async_remote_copy(
            src_ref=src, dst_ref=recv_ref.at[me], send_sem=send_sems.at[d],
            recv_sem=recv_sems.at[me], device_id=member(peer),
            device_id_type=pl.DeviceIdType.MESH)
        copy.start()
        copies.append(copy)
    return copies


def exchange_finish(axis, stride, size, mode, x_ref, o_ref, recv_ref, send_sems, recv_sems, copies):
    me, member = group_of(axis, stride, size)
    if mode == "gather":
        o_ref[me] = x_ref[...]
    else:
        total = x_ref[me].astype(jnp.float32)
    for d in range(1, size):
        src_dev = lax.rem(me + size - d, size)
        incoming = pltpu.make_async_remote_copy(
            src_ref=recv_ref.at[src_dev], dst_ref=recv_ref.at[src_dev], send_sem=send_sems.at[d],
            recv_sem=recv_sems.at[src_dev], device_id=member(src_dev),
            device_id_type=pl.DeviceIdType.MESH)
        incoming.wait_recv()
        if mode != "gather":
            total = total + recv_ref[src_dev].astype(jnp.float32)
    for copy in copies:
        copy.wait_send()
    if mode != "gather":
        o_ref[...] = total.astype(o_ref.dtype)


def exchange_kernel(axis, stride, size, mode, x_ref, o_ref, *scratch):
    if mode == "gather":
        recv_ref, (send_sems, recv_sems) = o_ref, scratch
    else:
        recv_ref, send_sems, recv_sems = scratch
    enter(exchange_targets(axis, stride, size))
    copies = exchange_start(axis, stride, size, mode, x_ref, recv_ref, send_sems, recv_sems)
    exchange_finish(axis, stride, size, mode, x_ref, o_ref, recv_ref, send_sems, recv_sems, copies)


def exchange_scratch(x, mode, size):
    scratch = [] if mode == "gather" else [pltpu.VMEM(x.shape, x.dtype)]
    return scratch + [pltpu.SemaphoreType.DMA((size,)), pltpu.SemaphoreType.DMA((size,))]


def exchange_shape(x, mode, size):
    shape = (size,) + x.shape if mode == "gather" else x.shape[1:]
    return jax.ShapeDtypeStruct(shape, x.dtype)


def exchange(x, axis, mode, collective_id, stride=1, size=None):
    size = lax.axis_size(axis) if size is None else size
    return pl.pallas_call(
        functools.partial(exchange_kernel, axis, stride, size, mode),
        out_shape=exchange_shape(x, mode, size),
        in_specs=[pl.BlockSpec(memory_space=pltpu.VMEM)],
        out_specs=pl.BlockSpec(memory_space=pltpu.VMEM),
        scratch_shapes=exchange_scratch(x, mode, size),
        compiler_params=pltpu.CompilerParams(collective_id=collective_id, has_side_effects=True),
    )(x)


def pair_targets(chips):
    me, member = group_of("row", 2, chips)
    _, sibling = group_of("row", 1, 2)
    return [member(lax.rem(me + d, chips)) for d in range(1, chips)], sibling


def row_gather_kernel(chips, x_ref, o_ref, send_sems, recv_sems, fwd_send, fwd_recv):
    z_me, z_member = group_of("row", 2, chips)
    c_me, core_member = group_of("row", 1, 2)
    sibling = core_member(1 - c_me)
    peers, _ = pair_targets(chips)
    enter(peers + [sibling])
    copies = []
    for d in range(1, chips):
        peer = lax.rem(z_me + d, chips)
        copy = pltpu.make_async_remote_copy(
            src_ref=x_ref, dst_ref=o_ref.at[c_me, z_me], send_sem=send_sems.at[d],
            recv_sem=recv_sems.at[z_me], device_id=z_member(peer),
            device_id_type=pl.DeviceIdType.MESH)
        copy.start()
        copies.append(copy)
    own = pltpu.make_async_remote_copy(
        src_ref=x_ref, dst_ref=o_ref.at[c_me, z_me], send_sem=fwd_send.at[z_me],
        recv_sem=fwd_recv.at[z_me], device_id=sibling, device_id_type=pl.DeviceIdType.MESH)
    own.start()
    copies.append(own)
    o_ref[c_me, z_me] = x_ref[...]
    for d in range(1, chips):
        src_dev = lax.rem(z_me + chips - d, chips)
        incoming = pltpu.make_async_remote_copy(
            src_ref=o_ref.at[c_me, src_dev], dst_ref=o_ref.at[c_me, src_dev],
            send_sem=send_sems.at[d], recv_sem=recv_sems.at[src_dev],
            device_id=z_member(src_dev), device_id_type=pl.DeviceIdType.MESH)
        incoming.wait_recv()
        forward = pltpu.make_async_remote_copy(
            src_ref=o_ref.at[c_me, src_dev], dst_ref=o_ref.at[c_me, src_dev],
            send_sem=fwd_send.at[src_dev], recv_sem=fwd_recv.at[src_dev], device_id=sibling,
            device_id_type=pl.DeviceIdType.MESH)
        forward.start()
        copies.append(forward)
    for k in range(chips):
        incoming = pltpu.make_async_remote_copy(
            src_ref=o_ref.at[1 - c_me, k], dst_ref=o_ref.at[1 - c_me, k],
            send_sem=fwd_send.at[k], recv_sem=fwd_recv.at[k], device_id=sibling,
            device_id_type=pl.DeviceIdType.MESH)
        incoming.wait_recv()
    for copy in copies:
        copy.wait_send()


def row_gather(x, chips, collective_id):
    return pl.pallas_call(
        functools.partial(row_gather_kernel, chips),
        out_shape=jax.ShapeDtypeStruct((2, chips) + x.shape, x.dtype),
        in_specs=[pl.BlockSpec(memory_space=pltpu.VMEM)],
        out_specs=pl.BlockSpec(memory_space=pltpu.VMEM),
        scratch_shapes=[pltpu.SemaphoreType.DMA((chips,))] * 4,
        compiler_params=pltpu.CompilerParams(collective_id=collective_id, has_side_effects=True),
    )(x)


def row_scatter_kernel(chips, x_ref, o_ref, pair_recv, pair_sum, z_recv,
                       pair_send_sems, pair_recv_sems, z_send_sems, z_recv_sems):
    z_me, z_member = group_of("row", 2, chips)
    c_me, core_member = group_of("row", 1, 2)
    sibling = core_member(1 - c_me)
    peers, _ = pair_targets(chips)
    enter(peers + [sibling])
    copies = []
    for k in range(chips):
        copy = pltpu.make_async_remote_copy(
            src_ref=x_ref.at[1 - c_me, k], dst_ref=pair_recv.at[k], send_sem=pair_send_sems.at[k],
            recv_sem=pair_recv_sems.at[k], device_id=sibling, device_id_type=pl.DeviceIdType.MESH)
        copy.start()
        copies.append(copy)
    order = [lax.rem(z_me + d, chips) for d in range(1, chips)] + [z_me]
    for d, k in enumerate(order, start=1):
        incoming = pltpu.make_async_remote_copy(
            src_ref=pair_recv.at[k], dst_ref=pair_recv.at[k], send_sem=pair_send_sems.at[k],
            recv_sem=pair_recv_sems.at[k], device_id=sibling, device_id_type=pl.DeviceIdType.MESH)
        incoming.wait_recv()
        pair_sum[k] = (x_ref[c_me, k].astype(jnp.float32)
                       + pair_recv[k].astype(jnp.float32)).astype(pair_sum.dtype)
        if d < chips:
            copy = pltpu.make_async_remote_copy(
                src_ref=pair_sum.at[k], dst_ref=z_recv.at[z_me], send_sem=z_send_sems.at[d],
                recv_sem=z_recv_sems.at[z_me], device_id=z_member(k),
                device_id_type=pl.DeviceIdType.MESH)
            copy.start()
            copies.append(copy)
    total = pair_sum[z_me].astype(jnp.float32)
    for d in range(1, chips):
        src_dev = lax.rem(z_me + chips - d, chips)
        incoming = pltpu.make_async_remote_copy(
            src_ref=z_recv.at[src_dev], dst_ref=z_recv.at[src_dev], send_sem=z_send_sems.at[d],
            recv_sem=z_recv_sems.at[src_dev], device_id=z_member(src_dev),
            device_id_type=pl.DeviceIdType.MESH)
        incoming.wait_recv()
        total = total + z_recv[src_dev].astype(jnp.float32)
    for copy in copies:
        copy.wait_send()
    o_ref[...] = total.astype(o_ref.dtype)


def row_scatter(x, chips, collective_id):
    block = x.shape[2:]
    return pl.pallas_call(
        functools.partial(row_scatter_kernel, chips),
        out_shape=jax.ShapeDtypeStruct(block, x.dtype),
        in_specs=[pl.BlockSpec(memory_space=pltpu.VMEM)],
        out_specs=pl.BlockSpec(memory_space=pltpu.VMEM),
        scratch_shapes=[pltpu.VMEM((chips,) + block, x.dtype)] * 3
        + [pltpu.SemaphoreType.DMA((chips,))] * 4,
        compiler_params=pltpu.CompilerParams(collective_id=collective_id, has_side_effects=True),
    )(x)


def reduction_plan(rows):
    pairs = []
    for bit in (1, 2, 4, 8, 16, 32, 64):
        for axis in ("row", "col"):
            if bit < lax.axis_size(axis):
                pairs.append((axis, bit))
    halving = []
    while pairs and rows // 2 >= 8 and rows % 16 == 0:
        halving.append(pairs.pop(0))
        rows //= 2
    return halving, pairs


def bitval(axis, bit):
    return (lax.axis_index(axis) // bit) % 2


def partner(axis, bit):
    return mesh_coords(axis, lax.axis_index(axis) + bit * (1 - 2 * bitval(axis, bit)))


def reduce_targets(rows):
    halving, whole = reduction_plan(rows)
    return [partner(axis, bit) for axis, bit in halving + whole]


def reduce_rounds(x_ref, o_ref, recv, send_sems, recv_sems):
    halving, whole = reduction_plan(x_ref.shape[0])
    o_ref[...] = x_ref[...]
    k = 0

    def swap(k, axis, bit, send_rows, length):
        copy = pltpu.make_async_remote_copy(
            src_ref=o_ref.at[pl.ds(send_rows, length)], dst_ref=recv.at[k, pl.ds(0, length)],
            send_sem=send_sems.at[k], recv_sem=recv_sems.at[k],
            device_id=partner(axis, bit), device_id_type=pl.DeviceIdType.MESH)
        copy.start()
        copy.wait()

    lo = jnp.int32(0)
    length = x_ref.shape[0]
    starts = []
    for axis, bit in halving:
        length //= 2
        mine = bitval(axis, bit)
        starts.append(lo)
        keep = pl.multiple_of(lo + mine * length, 8)
        give = pl.multiple_of(lo + (1 - mine) * length, 8)
        swap(k, axis, bit, give, length)
        o_ref[pl.ds(keep, length)] = o_ref[pl.ds(keep, length)] + recv[k, pl.ds(0, length)]
        lo = keep
        k += 1
    for axis, bit in whole:
        swap(k, axis, bit, lo, length)
        o_ref[pl.ds(lo, length)] = o_ref[pl.ds(lo, length)] + recv[k, pl.ds(0, length)]
        k += 1
    for (axis, bit), base in zip(reversed(halving), reversed(starts)):
        mine = bitval(axis, bit)
        other = pl.multiple_of(base + (1 - mine) * length, 8)
        swap(k, axis, bit, lo, length)
        o_ref[pl.ds(other, length)] = recv[k, pl.ds(0, length)]
        lo = base
        length *= 2
        k += 1


def reduce_scratch(w):
    halving, whole = reduction_plan(w.shape[0])
    steps = 2 * len(halving) + len(whole)
    return [
        pltpu.VMEM((steps, w.shape[0] // 2) + w.shape[1:], w.dtype),
        pltpu.SemaphoreType.DMA((steps,)),
        pltpu.SemaphoreType.DMA((steps,)),
    ]


def radix_groups():
    n_row, n_col = lax.axis_size("row"), lax.axis_size("col")
    if n_row % 2 or n_col % 4:
        return None
    return ((("row", 1, 2), ("col", 1, 4)), ("row", 2, n_row // 2), ("col", 4, n_col // 4))


def first_group():
    (core, ring), _, _ = radix_groups()
    me_a, _ = group_of(*core)
    me_b, _ = group_of(*ring)
    size = core[2] * ring[2]
    me = me_a + core[2] * me_b
    row = lax.axis_index("row") - me_a * core[1]
    col = lax.axis_index("col") - me_b * ring[1]

    def member(m):
        return (row + (m % core[2]) * core[1], col + (m // core[2]) * ring[1], lax.axis_index("feat"))

    return me, size, member


def reduce_radix_targets():
    me, size, member = first_group()
    targets = [member(lax.rem(me + d, size)) for d in range(1, size)]
    _, z_group, x_group = radix_groups()
    return targets + exchange_targets(*z_group) + exchange_targets(*x_group)


def ordered_allreduce(group, value, recv, send_sems, recv_sems):
    axis, stride, size = group
    me, member = group_of(axis, stride, size)
    recv[me] = value
    copies = []
    for d in range(1, size):
        peer = lax.rem(me + d, size)
        copy = pltpu.make_async_remote_copy(
            src_ref=recv.at[me], dst_ref=recv.at[me], send_sem=send_sems.at[d],
            recv_sem=recv_sems.at[me], device_id=member(peer), device_id_type=pl.DeviceIdType.MESH)
        copy.start()
        copies.append(copy)
    for d in range(1, size):
        src_dev = lax.rem(me + size - d, size)
        pltpu.make_async_remote_copy(
            src_ref=recv.at[src_dev], dst_ref=recv.at[src_dev], send_sem=send_sems.at[d],
            recv_sem=recv_sems.at[src_dev], device_id=member(src_dev),
            device_id_type=pl.DeviceIdType.MESH).wait_recv()
    for copy in copies:
        copy.wait_send()
    total = recv[0]
    for k in range(1, size):
        total = total + recv[k]
    return total


def reduce_radix(w_ref, o_ref, seg_recv, z_recv, x_recv, sems):
    _, z_group, x_group = radix_groups()
    me, size, member = first_group()
    seg = w_ref.shape[0] // size
    mine = pl.ds(pl.multiple_of(me * seg, 8), seg)
    copies = []
    for d in range(1, size):
        peer = lax.rem(me + d, size)
        copy = pltpu.make_async_remote_copy(
            src_ref=w_ref.at[pl.ds(pl.multiple_of(peer * seg, 8), seg)], dst_ref=seg_recv.at[me],
            send_sem=sems.at[0, d], recv_sem=sems.at[1, me], device_id=member(peer),
            device_id_type=pl.DeviceIdType.MESH)
        copy.start()
        copies.append(copy)
    total = w_ref[mine]
    for d in range(1, size):
        src_dev = lax.rem(me + size - d, size)
        pltpu.make_async_remote_copy(
            src_ref=seg_recv.at[src_dev], dst_ref=seg_recv.at[src_dev], send_sem=sems.at[0, d],
            recv_sem=sems.at[1, src_dev], device_id=member(src_dev),
            device_id_type=pl.DeviceIdType.MESH).wait_recv()
        total = total + seg_recv[src_dev]
    for copy in copies:
        copy.wait_send()
    total = ordered_allreduce(z_group, total, z_recv, sems.at[2], sems.at[3])
    total = ordered_allreduce(x_group, total, x_recv, sems.at[4], sems.at[5])
    o_ref[mine] = total
    copies = []
    for d in range(1, size):
        peer = lax.rem(me + d, size)
        copy = pltpu.make_async_remote_copy(
            src_ref=o_ref.at[mine], dst_ref=o_ref.at[mine], send_sem=sems.at[6, d],
            recv_sem=sems.at[7, me], device_id=member(peer), device_id_type=pl.DeviceIdType.MESH)
        copy.start()
        copies.append(copy)
    for d in range(1, size):
        src_dev = lax.rem(me + size - d, size)
        rows = pl.ds(pl.multiple_of(src_dev * seg, 8), seg)
        pltpu.make_async_remote_copy(
            src_ref=o_ref.at[rows], dst_ref=o_ref.at[rows], send_sem=sems.at[6, d],
            recv_sem=sems.at[7, src_dev], device_id=member(src_dev),
            device_id_type=pl.DeviceIdType.MESH).wait_recv()
    for copy in copies:
        copy.wait_send()


def radix_scratch(w):
    (core, ring), z_group, x_group = radix_groups()
    size = core[2] * ring[2]
    seg = (w.shape[0] // size,) + w.shape[1:]
    width = max(size, z_group[2], x_group[2])
    return [
        pltpu.VMEM((size,) + seg, w.dtype),
        pltpu.VMEM((z_group[2],) + seg, w.dtype),
        pltpu.VMEM((x_group[2],) + seg, w.dtype),
        pltpu.SemaphoreType.DMA((8, width)),
    ]


def radix_fits(w):
    groups = radix_groups()
    if groups is None:
        return False
    size = groups[0][0][2] * groups[0][1][2]
    return w.shape[0] % (8 * size) == 0


def gather_radix_kernel(axis, x_ref, w_ref, o_ref, ow_ref, g_send, g_recv, *scratch):
    size = lax.axis_size(axis)
    enter(exchange_targets(axis, 1, size) + reduce_radix_targets())
    copies = exchange_start(axis, 1, size, "gather", x_ref, o_ref, g_send, g_recv)
    reduce_radix(w_ref, ow_ref, *scratch)
    exchange_finish(axis, 1, size, "gather", x_ref, o_ref, o_ref, g_send, g_recv, copies)


def gather_reduce_kernel(axis, x_ref, w_ref, o_ref, ow_ref, g_send, g_recv, recv, send_sems, recv_sems):
    size = lax.axis_size(axis)
    enter(exchange_targets(axis, 1, size) + reduce_targets(w_ref.shape[0]))
    copies = exchange_start(axis, 1, size, "gather", x_ref, o_ref, g_send, g_recv)
    reduce_rounds(w_ref, ow_ref, recv, send_sems, recv_sems)
    exchange_finish(axis, 1, size, "gather", x_ref, o_ref, o_ref, g_send, g_recv, copies)


def gather_and_reduce(x, w, axis, collective_id):
    size = lax.axis_size(axis)
    if radix_fits(w):
        kernel, scratch = gather_radix_kernel, radix_scratch(w)
    else:
        kernel, scratch = gather_reduce_kernel, reduce_scratch(w)
    return pl.pallas_call(
        functools.partial(kernel, axis),
        out_shape=(exchange_shape(x, "gather", size), jax.ShapeDtypeStruct(w.shape, w.dtype)),
        in_specs=[pl.BlockSpec(memory_space=pltpu.VMEM)] * 2,
        out_specs=(pl.BlockSpec(memory_space=pltpu.VMEM),) * 2,
        scratch_shapes=exchange_scratch(x, "gather", size) + scratch,
        compiler_params=pltpu.CompilerParams(collective_id=collective_id, has_side_effects=True),
    )(x, w)


def shards(features, tile_rows, tile_cols, tile_count, tile_values, weights, cotangent):
    width = tile_values.shape[-1]
    local_tiles = tile_values[0, 0]
    block_rows = tile_rows[0, 0]
    block_cols = tile_cols[0, 0]
    count = tile_count[0, 0].reshape(1)
    n_rowdev = lax.axis_size("row")
    n_coldev = lax.axis_size("col")
    local_blocks = features.shape[0] // width
    feat_half = features.shape[1]
    feat_index = lax.axis_index("feat")
    row_blocks = local_blocks * n_coldev
    col_blocks = local_blocks * n_rowdev
    node_total = features.shape[0] * n_rowdev * n_coldev
    pair = 2 if n_rowdev % 2 == 0 else 1
    chips = n_rowdev // pair
    if pair == 2:
        panel = row_gather(features, chips, 0).reshape(-1, feat_half)
    else:
        panel = exchange(features, "row", "gather", 0).reshape(-1, feat_half)
    owner = block_cols // local_blocks
    block_cols = ((owner % pair) * chips + owner // pair) * local_blocks + block_cols % local_blocks
    partial_value = tile_products(local_tiles, block_rows, block_cols, count, panel,
                                  row_blocks, transpose=False)
    summed = exchange(partial_value.reshape(n_coldev, -1, feat_half), "col", "scatter", 1)
    n_feat = lax.axis_size("feat")
    agg_halves = exchange(summed, "feat", "gather", 7)
    weight_cols = lax.dynamic_slice_in_dim(weights, feat_index * feat_half, feat_half, 1)
    hidden = sum(
        jnp.dot(agg_halves[h], weight_cols[h * feat_half:(h + 1) * feat_half],
                preferred_element_type=jnp.float32)
        for h in range(n_feat)
    )
    negative = jnp.minimum(hidden, 0.0)
    activated = jnp.where(hidden > 0, hidden, jnp.expm1(negative)).astype(jnp.bfloat16)
    slope_factor = jnp.where(hidden > 0, 1.0, jnp.exp(negative))
    grad_out = (cotangent.astype(jnp.float32) * slope_factor).astype(jnp.bfloat16)
    grad_halves = exchange(grad_out, "feat", "gather", 8)
    weight_term = jnp.concatenate([
        lax.dot_general(summed, grad_halves[h], (((0,), (0,)), ((), ())),
                        preferred_element_type=jnp.float32)
        for h in range(n_feat)
    ], axis=1)
    weight_rows = lax.dynamic_slice_in_dim(weights, feat_index * feat_half, feat_half, 0)
    spread = sum(
        lax.dot_general(grad_halves[h], weight_rows[:, h * feat_half:(h + 1) * feat_half],
                        (((1,), (1,)), ((), ())), preferred_element_type=jnp.float32)
        for h in range(n_feat)
    ).astype(jnp.bfloat16)
    spread_panel, weight_sum = gather_and_reduce(spread, weight_term, "col", 2)
    spread_panel = spread_panel.reshape(-1, feat_half)
    weight_grad = weight_sum * node_total ** (-0.5)
    back_partial = tile_products(local_tiles, block_rows, block_cols, count, spread_panel,
                                 col_blocks, transpose=True)
    if pair == 2:
        back_summed = row_scatter(back_partial.reshape(pair, chips, -1, feat_half), chips, 3)
    else:
        back_summed = exchange(back_partial.reshape(n_rowdev, -1, feat_half), "row", "scatter", 3)
    return (activated, back_summed, weight_grad)


def solution(mesh):
    return jax.shard_map(
        shards,
        mesh=mesh,
        in_specs=(
            P(("col", "row"), "feat"),
            P("row", "col", None),
            P("row", "col", None),
            P("row", "col"),
            P("row", "col", None, None, None),
            P(),
            P(("row", "col"), "feat"),
        ),
        out_specs=(P(("row", "col"), "feat"), P(("col", "row"), "feat"), P("feat", None)),
        check_vma=False,
    )
```

```python
import functools

import jax
import jax.numpy as jnp
from jax import lax
from jax.experimental import pallas as pl
from jax.experimental.pallas import tpu as pltpu
from jax.sharding import PartitionSpec as P

GROUP = 64


def tile_kernel(transpose, rows_ref, cols_ref, count_ref, tiles_ref, panel_ref, out_ref, acc_ref):
    step = pl.program_id(0)
    width = tiles_ref.shape[-1]
    count = count_ref[0]
    src_blocks = panel_ref.shape[0] // width
    dst_blocks = acc_ref.shape[0] // width

    @pl.when(step == 0)
    def _():
        acc_ref[...] = jnp.zeros_like(acc_ref)

    @pl.when(step * GROUP < count)
    def _():
        terms = []
        for j in range(GROUP):
            slot = step * GROUP + j
            src = rows_ref[slot] if transpose else cols_ref[slot]
            src = jnp.minimum(jnp.maximum(src, 0), src_blocks - 1)
            block = panel_ref[pl.ds(pl.multiple_of(src * width, width), width), :]
            tile = tiles_ref[j]
            if transpose:
                term = lax.dot_general(tile, block, (((0,), (0,)), ((), ())),
                                       preferred_element_type=jnp.float32)
            else:
                term = jnp.dot(tile, block, preferred_element_type=jnp.float32)
            terms.append(jnp.where(slot < count, term, 0.0))
        for j in range(GROUP):
            slot = step * GROUP + j
            dst = cols_ref[slot] if transpose else rows_ref[slot]
            dst = jnp.minimum(jnp.maximum(dst, 0), dst_blocks - 1)
            rows = pl.ds(pl.multiple_of(dst * width, width), width)
            acc_ref[rows, :] += terms[j]

    @pl.when(step == pl.num_programs(0) - 1)
    def _():
        out_ref[...] = acc_ref[...].astype(out_ref.dtype)


def tile_products(tiles, rows, cols, count, panel, out_blocks, transpose):
    slots, width, _ = tiles.shape
    feat = panel.shape[1]
    steps = slots // GROUP

    def tiles_map(i, rows_ref, cols_ref, count_ref):
        last = jnp.maximum(count_ref[0] - 1, 0) // GROUP
        return (jnp.minimum(i, last), 0, 0)

    return pl.pallas_call(
        functools.partial(tile_kernel, transpose),
        out_shape=jax.ShapeDtypeStruct((out_blocks * width, feat), jnp.bfloat16),
        grid_spec=pltpu.PrefetchScalarGridSpec(
            num_scalar_prefetch=3,
            grid=(steps,),
            in_specs=[
                pl.BlockSpec((GROUP, width, width), tiles_map),
                pl.BlockSpec(panel.shape, lambda i, *_: (0, 0)),
            ],
            out_specs=pl.BlockSpec((out_blocks * width, feat), lambda i, *_: (0, 0)),
            scratch_shapes=[pltpu.VMEM((out_blocks * width, feat), jnp.float32)],
        ),
        compiler_params=pltpu.CompilerParams(dimension_semantics=("arbitrary",)),
        cost_estimate=pl.CostEstimate(
            flops=2 * slots * width * width * feat,
            bytes_accessed=tiles.size * 2 + panel.size * 2 + out_blocks * width * feat * 2,
            transcendentals=0,
        ),
    )(rows, cols, count, tiles, panel)


def mesh_coords(axis, peer):
    return tuple(peer if name == axis else lax.axis_index(name) for name in ("row", "col", "feat"))


def group_of(axis, stride, size):
    index = lax.axis_index(axis)
    me = (index // stride) % size
    base = index - me * stride
    return me, lambda k: mesh_coords(axis, base + k * stride)


def exchange_targets(axis, stride, size):
    me, member = group_of(axis, stride, size)
    return [member(lax.rem(me + d, size)) for d in range(1, size)]


def enter(targets):
    barrier = pltpu.get_barrier_semaphore()
    for target in targets:
        pl.semaphore_signal(barrier, inc=1, device_id=target, device_id_type=pl.DeviceIdType.MESH)
    pl.semaphore_wait(barrier, len(targets))


def exchange_start(axis, stride, size, mode, x_ref, recv_ref, send_sems, recv_sems):
    me, member = group_of(axis, stride, size)
    copies = []
    for d in range(1, size):
        peer = lax.rem(me + d, size)
        src = x_ref if mode == "gather" else x_ref.at[peer]
        copy = pltpu.make_async_remote_copy(
            src_ref=src, dst_ref=recv_ref.at[me], send_sem=send_sems.at[d],
            recv_sem=recv_sems.at[me], device_id=member(peer),
            device_id_type=pl.DeviceIdType.MESH)
        copy.start()
        copies.append(copy)
    return copies


def exchange_finish(axis, stride, size, mode, x_ref, o_ref, recv_ref, send_sems, recv_sems, copies):
    me, member = group_of(axis, stride, size)
    if mode == "gather":
        o_ref[me] = x_ref[...]
    else:
        total = x_ref[me].astype(jnp.float32)
    for d in range(1, size):
        src_dev = lax.rem(me + size - d, size)
        incoming = pltpu.make_async_remote_copy(
            src_ref=recv_ref.at[src_dev], dst_ref=recv_ref.at[src_dev], send_sem=send_sems.at[d],
            recv_sem=recv_sems.at[src_dev], device_id=member(src_dev),
            device_id_type=pl.DeviceIdType.MESH)
        incoming.wait_recv()
        if mode != "gather":
            total = total + recv_ref[src_dev].astype(jnp.float32)
    for copy in copies:
        copy.wait_send()
    if mode != "gather":
        o_ref[...] = total.astype(o_ref.dtype)


def exchange_kernel(axis, stride, size, mode, x_ref, o_ref, *scratch):
    if mode == "gather":
        recv_ref, (send_sems, recv_sems) = o_ref, scratch
    else:
        recv_ref, send_sems, recv_sems = scratch
    enter(exchange_targets(axis, stride, size))
    copies = exchange_start(axis, stride, size, mode, x_ref, recv_ref, send_sems, recv_sems)
    exchange_finish(axis, stride, size, mode, x_ref, o_ref, recv_ref, send_sems, recv_sems, copies)


def exchange_scratch(x, mode, size):
    scratch = [] if mode == "gather" else [pltpu.VMEM(x.shape, x.dtype)]
    return scratch + [pltpu.SemaphoreType.DMA((size,)), pltpu.SemaphoreType.DMA((size,))]


def exchange_shape(x, mode, size):
    shape = (size,) + x.shape if mode == "gather" else x.shape[1:]
    return jax.ShapeDtypeStruct(shape, x.dtype)


def exchange(x, axis, mode, collective_id, stride=1, size=None):
    size = lax.axis_size(axis) if size is None else size
    return pl.pallas_call(
        functools.partial(exchange_kernel, axis, stride, size, mode),
        out_shape=exchange_shape(x, mode, size),
        in_specs=[pl.BlockSpec(memory_space=pltpu.VMEM)],
        out_specs=pl.BlockSpec(memory_space=pltpu.VMEM),
        scratch_shapes=exchange_scratch(x, mode, size),
        compiler_params=pltpu.CompilerParams(collective_id=collective_id, has_side_effects=True),
    )(x)


def pair_targets(chips):
    me, member = group_of("row", 2, chips)
    _, sibling = group_of("row", 1, 2)
    return [member(lax.rem(me + d, chips)) for d in range(1, chips)], sibling


def row_gather_kernel(chips, x_ref, o_ref, send_sems, recv_sems, fwd_send, fwd_recv):
    z_me, z_member = group_of("row", 2, chips)
    c_me, core_member = group_of("row", 1, 2)
    sibling = core_member(1 - c_me)
    peers, _ = pair_targets(chips)
    enter(peers + [sibling])
    copies = []
    for d in range(1, chips):
        peer = lax.rem(z_me + d, chips)
        copy = pltpu.make_async_remote_copy(
            src_ref=x_ref, dst_ref=o_ref.at[c_me, z_me], send_sem=send_sems.at[d],
            recv_sem=recv_sems.at[z_me], device_id=z_member(peer),
            device_id_type=pl.DeviceIdType.MESH)
        copy.start()
        copies.append(copy)
    own = pltpu.make_async_remote_copy(
        src_ref=x_ref, dst_ref=o_ref.at[c_me, z_me], send_sem=fwd_send.at[z_me],
        recv_sem=fwd_recv.at[z_me], device_id=sibling, device_id_type=pl.DeviceIdType.MESH)
    own.start()
    copies.append(own)
    o_ref[c_me, z_me] = x_ref[...]
    for d in range(1, chips):
        src_dev = lax.rem(z_me + chips - d, chips)
        incoming = pltpu.make_async_remote_copy(
            src_ref=o_ref.at[c_me, src_dev], dst_ref=o_ref.at[c_me, src_dev],
            send_sem=send_sems.at[d], recv_sem=recv_sems.at[src_dev],
            device_id=z_member(src_dev), device_id_type=pl.DeviceIdType.MESH)
        incoming.wait_recv()
        forward = pltpu.make_async_remote_copy(
            src_ref=o_ref.at[c_me, src_dev], dst_ref=o_ref.at[c_me, src_dev],
            send_sem=fwd_send.at[src_dev], recv_sem=fwd_recv.at[src_dev], device_id=sibling,
            device_id_type=pl.DeviceIdType.MESH)
        forward.start()
        copies.append(forward)
    for k in range(chips):
        incoming = pltpu.make_async_remote_copy(
            src_ref=o_ref.at[1 - c_me, k], dst_ref=o_ref.at[1 - c_me, k],
            send_sem=fwd_send.at[k], recv_sem=fwd_recv.at[k], device_id=sibling,
            device_id_type=pl.DeviceIdType.MESH)
        incoming.wait_recv()
    for copy in copies:
        copy.wait_send()


def row_gather(x, chips, collective_id):
    return pl.pallas_call(
        functools.partial(row_gather_kernel, chips),
        out_shape=jax.ShapeDtypeStruct((2, chips) + x.shape, x.dtype),
        in_specs=[pl.BlockSpec(memory_space=pltpu.VMEM)],
        out_specs=pl.BlockSpec(memory_space=pltpu.VMEM),
        scratch_shapes=[pltpu.SemaphoreType.DMA((chips,))] * 4,
        compiler_params=pltpu.CompilerParams(collective_id=collective_id, has_side_effects=True),
    )(x)


def row_scatter_kernel(chips, x_ref, o_ref, pair_recv, pair_sum, z_recv,
                       pair_send_sems, pair_recv_sems, z_send_sems, z_recv_sems):
    z_me, z_member = group_of("row", 2, chips)
    c_me, core_member = group_of("row", 1, 2)
    sibling = core_member(1 - c_me)
    peers, _ = pair_targets(chips)
    enter(peers + [sibling])
    copies = []
    for k in range(chips):
        copy = pltpu.make_async_remote_copy(
            src_ref=x_ref.at[1 - c_me, k], dst_ref=pair_recv.at[k], send_sem=pair_send_sems.at[k],
            recv_sem=pair_recv_sems.at[k], device_id=sibling, device_id_type=pl.DeviceIdType.MESH)
        copy.start()
        copies.append(copy)
    order = [lax.rem(z_me + d, chips) for d in range(1, chips)] + [z_me]
    for d, k in enumerate(order, start=1):
        incoming = pltpu.make_async_remote_copy(
            src_ref=pair_recv.at[k], dst_ref=pair_recv.at[k], send_sem=pair_send_sems.at[k],
            recv_sem=pair_recv_sems.at[k], device_id=sibling, device_id_type=pl.DeviceIdType.MESH)
        incoming.wait_recv()
        pair_sum[k] = (x_ref[c_me, k].astype(jnp.float32)
                       + pair_recv[k].astype(jnp.float32)).astype(pair_sum.dtype)
        if d < chips:
            copy = pltpu.make_async_remote_copy(
                src_ref=pair_sum.at[k], dst_ref=z_recv.at[z_me], send_sem=z_send_sems.at[d],
                recv_sem=z_recv_sems.at[z_me], device_id=z_member(k),
                device_id_type=pl.DeviceIdType.MESH)
            copy.start()
            copies.append(copy)
    total = pair_sum[z_me].astype(jnp.float32)
    for d in range(1, chips):
        src_dev = lax.rem(z_me + chips - d, chips)
        incoming = pltpu.make_async_remote_copy(
            src_ref=z_recv.at[src_dev], dst_ref=z_recv.at[src_dev], send_sem=z_send_sems.at[d],
            recv_sem=z_recv_sems.at[src_dev], device_id=z_member(src_dev),
            device_id_type=pl.DeviceIdType.MESH)
        incoming.wait_recv()
        total = total + z_recv[src_dev].astype(jnp.float32)
    for copy in copies:
        copy.wait_send()
    o_ref[...] = total.astype(o_ref.dtype)


def row_scatter(x, chips, collective_id):
    block = x.shape[2:]
    return pl.pallas_call(
        functools.partial(row_scatter_kernel, chips),
        out_shape=jax.ShapeDtypeStruct(block, x.dtype),
        in_specs=[pl.BlockSpec(memory_space=pltpu.VMEM)],
        out_specs=pl.BlockSpec(memory_space=pltpu.VMEM),
        scratch_shapes=[pltpu.VMEM((chips,) + block, x.dtype)] * 3
        + [pltpu.SemaphoreType.DMA((chips,))] * 4,
        compiler_params=pltpu.CompilerParams(collective_id=collective_id, has_side_effects=True),
    )(x)


def feat_push(value_ref, halves_ref, send_sems, recv_sems, slot):
    n = lax.axis_size("feat")
    me = lax.axis_index("feat")
    halves_ref[me] = value_ref[...]
    copies = []
    for d in range(1, n):
        peer = lax.rem(me + d, n)
        copy = pltpu.make_async_remote_copy(
            src_ref=halves_ref.at[me], dst_ref=halves_ref.at[me], send_sem=send_sems.at[slot, d],
            recv_sem=recv_sems.at[slot, me], device_id=mesh_coords("feat", peer),
            device_id_type=pl.DeviceIdType.MESH)
        copy.start()
        copies.append(copy)
    for d in range(1, n):
        src_dev = lax.rem(me + n - d, n)
        pltpu.make_async_remote_copy(
            src_ref=halves_ref.at[src_dev], dst_ref=halves_ref.at[src_dev],
            send_sem=send_sems.at[slot, d], recv_sem=recv_sems.at[slot, src_dev],
            device_id=mesh_coords("feat", src_dev), device_id_type=pl.DeviceIdType.MESH).wait_recv()
    for copy in copies:
        copy.wait_send()


def layer_kernel(x_ref, w_ref, cot_ref, summed_ref, hidden_ref, grad_ref,
                 recv_ref, send_sems, recv_sems, agg_ref, grad_out_ref, f_send, f_recv):
    n_col = lax.axis_size("col")
    n_feat = lax.axis_size("feat")
    me = lax.axis_index("feat")
    peers = [mesh_coords("feat", lax.rem(me + d, n_feat)) for d in range(1, n_feat)]
    enter(exchange_targets("col", 1, n_col) + peers)
    copies = exchange_start("col", 1, n_col, "scatter", x_ref, recv_ref, send_sems, recv_sems)
    exchange_finish("col", 1, n_col, "scatter", x_ref, summed_ref, recv_ref, send_sems, recv_sems,
                    copies)
    feat_push(summed_ref, agg_ref, f_send, f_recv, 0)
    half = agg_ref.shape[-1]
    hidden = jnp.dot(agg_ref[0], w_ref[pl.ds(0, half), :], preferred_element_type=jnp.float32)
    for h in range(1, n_feat):
        hidden = hidden + jnp.dot(agg_ref[h], w_ref[pl.ds(h * half, half), :],
                                  preferred_element_type=jnp.float32)
    hidden_ref[...] = hidden
    slope = jnp.where(hidden > 0, 1.0, jnp.exp(jnp.minimum(hidden, 0.0)))
    grad_out_ref[...] = (cot_ref[...].astype(jnp.float32) * slope).astype(grad_out_ref.dtype)
    feat_push(grad_out_ref, grad_ref, f_send, f_recv, 1)


def layer_step(partials, weight_cols, cotangent, collective_id):
    n_col = lax.axis_size("col")
    n_feat = lax.axis_size("feat")
    block = partials.shape[1:]
    vmem = pl.BlockSpec(memory_space=pltpu.VMEM)
    return pl.pallas_call(
        layer_kernel,
        out_shape=(
            jax.ShapeDtypeStruct(block, partials.dtype),
            jax.ShapeDtypeStruct(block, jnp.float32),
            jax.ShapeDtypeStruct((n_feat,) + block, jnp.bfloat16),
        ),
        in_specs=[vmem] * 3,
        out_specs=(vmem,) * 3,
        scratch_shapes=exchange_scratch(partials, "scatter", n_col) + [
            pltpu.VMEM((n_feat,) + block, partials.dtype),
            pltpu.VMEM(block, jnp.bfloat16),
            pltpu.SemaphoreType.DMA((2, n_feat)),
            pltpu.SemaphoreType.DMA((2, n_feat)),
        ],
        compiler_params=pltpu.CompilerParams(collective_id=collective_id, has_side_effects=True),
    )(partials, weight_cols, cotangent)


def reduction_plan(rows):
    pairs = []
    for bit in (1, 2, 4, 8, 16, 32, 64):
        for axis in ("row", "col"):
            if bit < lax.axis_size(axis):
                pairs.append((axis, bit))
    halving = []
    while pairs and rows // 2 >= 8 and rows % 16 == 0:
        halving.append(pairs.pop(0))
        rows //= 2
    return halving, pairs


def bitval(axis, bit):
    return (lax.axis_index(axis) // bit) % 2


def partner(axis, bit):
    return mesh_coords(axis, lax.axis_index(axis) + bit * (1 - 2 * bitval(axis, bit)))


def reduce_targets(rows):
    halving, whole = reduction_plan(rows)
    return [partner(axis, bit) for axis, bit in halving + whole]


def reduce_rounds(x_ref, o_ref, recv, send_sems, recv_sems):
    halving, whole = reduction_plan(x_ref.shape[0])
    o_ref[...] = x_ref[...]
    k = 0

    def swap(k, axis, bit, send_rows, length):
        copy = pltpu.make_async_remote_copy(
            src_ref=o_ref.at[pl.ds(send_rows, length)], dst_ref=recv.at[k, pl.ds(0, length)],
            send_sem=send_sems.at[k], recv_sem=recv_sems.at[k],
            device_id=partner(axis, bit), device_id_type=pl.DeviceIdType.MESH)
        copy.start()
        copy.wait()

    lo = jnp.int32(0)
    length = x_ref.shape[0]
    starts = []
    for axis, bit in halving:
        length //= 2
        mine = bitval(axis, bit)
        starts.append(lo)
        keep = pl.multiple_of(lo + mine * length, 8)
        give = pl.multiple_of(lo + (1 - mine) * length, 8)
        swap(k, axis, bit, give, length)
        o_ref[pl.ds(keep, length)] = o_ref[pl.ds(keep, length)] + recv[k, pl.ds(0, length)]
        lo = keep
        k += 1
    for axis, bit in whole:
        swap(k, axis, bit, lo, length)
        o_ref[pl.ds(lo, length)] = o_ref[pl.ds(lo, length)] + recv[k, pl.ds(0, length)]
        k += 1
    for (axis, bit), base in zip(reversed(halving), reversed(starts)):
        mine = bitval(axis, bit)
        other = pl.multiple_of(base + (1 - mine) * length, 8)
        swap(k, axis, bit, lo, length)
        o_ref[pl.ds(other, length)] = recv[k, pl.ds(0, length)]
        lo = base
        length *= 2
        k += 1


def reduce_scratch(w):
    halving, whole = reduction_plan(w.shape[0])
    steps = 2 * len(halving) + len(whole)
    return [
        pltpu.VMEM((steps, w.shape[0] // 2) + w.shape[1:], w.dtype),
        pltpu.SemaphoreType.DMA((steps,)),
        pltpu.SemaphoreType.DMA((steps,)),
    ]


def radix_groups():
    n_row, n_col = lax.axis_size("row"), lax.axis_size("col")
    if n_row % 2 or n_col % 4:
        return None
    return ((("row", 1, 2), ("col", 1, 4)), ("row", 2, n_row // 2), ("col", 4, n_col // 4))


def first_group():
    (core, ring), _, _ = radix_groups()
    me_a, _ = group_of(*core)
    me_b, _ = group_of(*ring)
    size = core[2] * ring[2]
    me = me_a + core[2] * me_b
    row = lax.axis_index("row") - me_a * core[1]
    col = lax.axis_index("col") - me_b * ring[1]

    def member(m):
        return (row + (m % core[2]) * core[1], col + (m // core[2]) * ring[1], lax.axis_index("feat"))

    return me, size, member


def reduce_radix_targets():
    me, size, member = first_group()
    targets = [member(lax.rem(me + d, size)) for d in range(1, size)]
    _, z_group, x_group = radix_groups()
    return targets + exchange_targets(*z_group) + exchange_targets(*x_group)


def ordered_allreduce(group, value, recv, send_sems, recv_sems):
    axis, stride, size = group
    me, member = group_of(axis, stride, size)
    recv[me] = value
    copies = []
    for d in range(1, size):
        peer = lax.rem(me + d, size)
        copy = pltpu.make_async_remote_copy(
            src_ref=recv.at[me], dst_ref=recv.at[me], send_sem=send_sems.at[d],
            recv_sem=recv_sems.at[me], device_id=member(peer), device_id_type=pl.DeviceIdType.MESH)
        copy.start()
        copies.append(copy)
    for d in range(1, size):
        src_dev = lax.rem(me + size - d, size)
        pltpu.make_async_remote_copy(
            src_ref=recv.at[src_dev], dst_ref=recv.at[src_dev], send_sem=send_sems.at[d],
            recv_sem=recv_sems.at[src_dev], device_id=member(src_dev),
            device_id_type=pl.DeviceIdType.MESH).wait_recv()
    for copy in copies:
        copy.wait_send()
    total = recv[0]
    for k in range(1, size):
        total = total + recv[k]
    return total


def reduce_radix(w_ref, o_ref, seg_recv, z_recv, x_recv, sems):
    _, z_group, x_group = radix_groups()
    me, size, member = first_group()
    seg = w_ref.shape[0] // size
    mine = pl.ds(pl.multiple_of(me * seg, 8), seg)
    copies = []
    for d in range(1, size):
        peer = lax.rem(me + d, size)
        copy = pltpu.make_async_remote_copy(
            src_ref=w_ref.at[pl.ds(pl.multiple_of(peer * seg, 8), seg)], dst_ref=seg_recv.at[me],
            send_sem=sems.at[0, d], recv_sem=sems.at[1, me], device_id=member(peer),
            device_id_type=pl.DeviceIdType.MESH)
        copy.start()
        copies.append(copy)
    total = w_ref[mine]
    for d in range(1, size):
        src_dev = lax.rem(me + size - d, size)
        pltpu.make_async_remote_copy(
            src_ref=seg_recv.at[src_dev], dst_ref=seg_recv.at[src_dev], send_sem=sems.at[0, d],
            recv_sem=sems.at[1, src_dev], device_id=member(src_dev),
            device_id_type=pl.DeviceIdType.MESH).wait_recv()
        total = total + seg_recv[src_dev]
    for copy in copies:
        copy.wait_send()
    total = ordered_allreduce(z_group, total, z_recv, sems.at[2], sems.at[3])
    total = ordered_allreduce(x_group, total, x_recv, sems.at[4], sems.at[5])
    o_ref[mine] = total
    copies = []
    for d in range(1, size):
        peer = lax.rem(me + d, size)
        copy = pltpu.make_async_remote_copy(
            src_ref=o_ref.at[mine], dst_ref=o_ref.at[mine], send_sem=sems.at[6, d],
            recv_sem=sems.at[7, me], device_id=member(peer), device_id_type=pl.DeviceIdType.MESH)
        copy.start()
        copies.append(copy)
    for d in range(1, size):
        src_dev = lax.rem(me + size - d, size)
        rows = pl.ds(pl.multiple_of(src_dev * seg, 8), seg)
        pltpu.make_async_remote_copy(
            src_ref=o_ref.at[rows], dst_ref=o_ref.at[rows], send_sem=sems.at[6, d],
            recv_sem=sems.at[7, src_dev], device_id=member(src_dev),
            device_id_type=pl.DeviceIdType.MESH).wait_recv()
    for copy in copies:
        copy.wait_send()


def radix_scratch(w):
    (core, ring), z_group, x_group = radix_groups()
    size = core[2] * ring[2]
    seg = (w.shape[0] // size,) + w.shape[1:]
    width = max(size, z_group[2], x_group[2])
    return [
        pltpu.VMEM((size,) + seg, w.dtype),
        pltpu.VMEM((z_group[2],) + seg, w.dtype),
        pltpu.VMEM((x_group[2],) + seg, w.dtype),
        pltpu.SemaphoreType.DMA((8, width)),
    ]


def radix_fits(w):
    groups = radix_groups()
    if groups is None:
        return False
    size = groups[0][0][2] * groups[0][1][2]
    return w.shape[0] % (8 * size) == 0


def gather_radix_kernel(axis, x_ref, w_ref, o_ref, ow_ref, g_send, g_recv, *scratch):
    size = lax.axis_size(axis)
    enter(exchange_targets(axis, 1, size) + reduce_radix_targets())
    copies = exchange_start(axis, 1, size, "gather", x_ref, o_ref, g_send, g_recv)
    reduce_radix(w_ref, ow_ref, *scratch)
    exchange_finish(axis, 1, size, "gather", x_ref, o_ref, o_ref, g_send, g_recv, copies)


def gather_reduce_kernel(axis, x_ref, w_ref, o_ref, ow_ref, g_send, g_recv, recv, send_sems, recv_sems):
    size = lax.axis_size(axis)
    enter(exchange_targets(axis, 1, size) + reduce_targets(w_ref.shape[0]))
    copies = exchange_start(axis, 1, size, "gather", x_ref, o_ref, g_send, g_recv)
    reduce_rounds(w_ref, ow_ref, recv, send_sems, recv_sems)
    exchange_finish(axis, 1, size, "gather", x_ref, o_ref, o_ref, g_send, g_recv, copies)


def gather_and_reduce(x, w, axis, collective_id):
    size = lax.axis_size(axis)
    if radix_fits(w):
        kernel, scratch = gather_radix_kernel, radix_scratch(w)
    else:
        kernel, scratch = gather_reduce_kernel, reduce_scratch(w)
    return pl.pallas_call(
        functools.partial(kernel, axis),
        out_shape=(exchange_shape(x, "gather", size), jax.ShapeDtypeStruct(w.shape, w.dtype)),
        in_specs=[pl.BlockSpec(memory_space=pltpu.VMEM)] * 2,
        out_specs=(pl.BlockSpec(memory_space=pltpu.VMEM),) * 2,
        scratch_shapes=exchange_scratch(x, "gather", size) + scratch,
        compiler_params=pltpu.CompilerParams(collective_id=collective_id, has_side_effects=True),
    )(x, w)


def shards(features, tile_rows, tile_cols, tile_count, tile_values, weights, cotangent):
    width = tile_values.shape[-1]
    local_tiles = tile_values[0, 0]
    block_rows = tile_rows[0, 0]
    block_cols = tile_cols[0, 0]
    count = tile_count[0, 0].reshape(1)
    n_rowdev = lax.axis_size("row")
    n_coldev = lax.axis_size("col")
    local_blocks = features.shape[0] // width
    feat_half = features.shape[1]
    feat_index = lax.axis_index("feat")
    row_blocks = local_blocks * n_coldev
    col_blocks = local_blocks * n_rowdev
    node_total = features.shape[0] * n_rowdev * n_coldev
    pair = 2 if n_rowdev % 2 == 0 else 1
    chips = n_rowdev // pair
    if pair == 2:
        panel = row_gather(features, chips, 0).reshape(-1, feat_half)
    else:
        panel = exchange(features, "row", "gather", 0).reshape(-1, feat_half)
    owner = block_cols // local_blocks
    block_cols = ((owner % pair) * chips + owner // pair) * local_blocks + block_cols % local_blocks
    partial_value = tile_products(local_tiles, block_rows, block_cols, count, panel,
                                  row_blocks, transpose=False)
    n_feat = lax.axis_size("feat")
    weight_cols = lax.dynamic_slice_in_dim(weights, feat_index * feat_half, feat_half, 1)
    summed, hidden, grad_halves = layer_step(partial_value.reshape(n_coldev, -1, feat_half),
                                             weight_cols, cotangent, 1)
    negative = jnp.minimum(hidden, 0.0)
    activated = jnp.where(hidden > 0, hidden, jnp.expm1(negative)).astype(jnp.bfloat16)
    weight_term = jnp.concatenate([
        lax.dot_general(summed, grad_halves[h], (((0,), (0,)), ((), ())),
                        preferred_element_type=jnp.float32)
        for h in range(n_feat)
    ], axis=1)
    weight_rows = lax.dynamic_slice_in_dim(weights, feat_index * feat_half, feat_half, 0)
    spread = sum(
        lax.dot_general(grad_halves[h], weight_rows[:, h * feat_half:(h + 1) * feat_half],
                        (((1,), (1,)), ((), ())), preferred_element_type=jnp.float32)
        for h in range(n_feat)
    ).astype(jnp.bfloat16)
    spread_panel, weight_sum = gather_and_reduce(spread, weight_term, "col", 2)
    spread_panel = spread_panel.reshape(-1, feat_half)
    weight_grad = weight_sum * node_total ** (-0.5)
    back_partial = tile_products(local_tiles, block_rows, block_cols, count, spread_panel,
                                 col_blocks, transpose=True)
    if pair == 2:
        back_summed = row_scatter(back_partial.reshape(pair, chips, -1, feat_half), chips, 3)
    else:
        back_summed = exchange(back_partial.reshape(n_rowdev, -1, feat_half), "row", "scatter", 3)
    return (activated, back_summed, weight_grad)


def solution(mesh):
    return jax.shard_map(
        shards,
        mesh=mesh,
        in_specs=(
            P(("col", "row"), "feat"),
            P("row", "col", None),
            P("row", "col", None),
            P("row", "col"),
            P("row", "col", None, None, None),
            P(),
            P(("row", "col"), "feat"),
        ),
        out_specs=(P(("row", "col"), "feat"), P(("col", "row"), "feat"), P("feat", None)),
        check_vma=False,
    )
```

```python
import functools

import jax
import jax.numpy as jnp
from jax import lax
from jax.experimental import pallas as pl
from jax.experimental.pallas import tpu as pltpu
from jax.sharding import PartitionSpec as P

GROUP = 64


def tile_kernel(transpose, rows_ref, cols_ref, count_ref, tiles_ref, panel_ref, out_ref, acc_ref):
    step = pl.program_id(0)
    width = tiles_ref.shape[-1]
    count = count_ref[0]
    src_blocks = panel_ref.shape[0] // width
    dst_blocks = acc_ref.shape[0] // width

    @pl.when(step == 0)
    def _():
        acc_ref[...] = jnp.zeros_like(acc_ref)

    @pl.when(step * GROUP < count)
    def _():
        terms = []
        for j in range(GROUP):
            slot = step * GROUP + j
            src = rows_ref[slot] if transpose else cols_ref[slot]
            src = jnp.minimum(jnp.maximum(src, 0), src_blocks - 1)
            block = panel_ref[pl.ds(pl.multiple_of(src * width, width), width), :]
            tile = tiles_ref[j]
            if transpose:
                term = lax.dot_general(tile, block, (((0,), (0,)), ((), ())),
                                       preferred_element_type=jnp.float32)
            else:
                term = jnp.dot(tile, block, preferred_element_type=jnp.float32)
            terms.append(jnp.where(slot < count, term, 0.0))
        for j in range(GROUP):
            slot = step * GROUP + j
            dst = cols_ref[slot] if transpose else rows_ref[slot]
            dst = jnp.minimum(jnp.maximum(dst, 0), dst_blocks - 1)
            rows = pl.ds(pl.multiple_of(dst * width, width), width)
            acc_ref[rows, :] += terms[j]

    @pl.when(step == pl.num_programs(0) - 1)
    def _():
        out_ref[...] = acc_ref[...].astype(out_ref.dtype)


def tile_products(tiles, rows, cols, count, panel, out_blocks, transpose):
    slots, width, _ = tiles.shape
    feat = panel.shape[1]
    steps = slots // GROUP

    def tiles_map(i, rows_ref, cols_ref, count_ref):
        last = jnp.maximum(count_ref[0] - 1, 0) // GROUP
        return (jnp.minimum(i, last), 0, 0)

    return pl.pallas_call(
        functools.partial(tile_kernel, transpose),
        out_shape=jax.ShapeDtypeStruct((out_blocks * width, feat), jnp.bfloat16),
        grid_spec=pltpu.PrefetchScalarGridSpec(
            num_scalar_prefetch=3,
            grid=(steps,),
            in_specs=[
                pl.BlockSpec((GROUP, width, width), tiles_map),
                pl.BlockSpec(panel.shape, lambda i, *_: (0, 0)),
            ],
            out_specs=pl.BlockSpec((out_blocks * width, feat), lambda i, *_: (0, 0)),
            scratch_shapes=[pltpu.VMEM((out_blocks * width, feat), jnp.float32)],
        ),
        compiler_params=pltpu.CompilerParams(dimension_semantics=("arbitrary",)),
        cost_estimate=pl.CostEstimate(
            flops=2 * slots * width * width * feat,
            bytes_accessed=tiles.size * 2 + panel.size * 2 + out_blocks * width * feat * 2,
            transcendentals=0,
        ),
    )(rows, cols, count, tiles, panel)


def mesh_coords(axis, peer):
    return tuple(peer if name == axis else lax.axis_index(name) for name in ("row", "col", "feat"))


def group_of(axis, stride, size):
    index = lax.axis_index(axis)
    me = (index // stride) % size
    base = index - me * stride
    return me, lambda k: mesh_coords(axis, base + k * stride)


def exchange_targets(axis, stride, size):
    me, member = group_of(axis, stride, size)
    return [member(lax.rem(me + d, size)) for d in range(1, size)]


def enter(targets):
    barrier = pltpu.get_barrier_semaphore()
    for target in targets:
        pl.semaphore_signal(barrier, inc=1, device_id=target, device_id_type=pl.DeviceIdType.MESH)
    pl.semaphore_wait(barrier, len(targets))


def exchange_start(axis, stride, size, mode, x_ref, recv_ref, send_sems, recv_sems):
    me, member = group_of(axis, stride, size)
    copies = []
    for d in range(1, size):
        peer = lax.rem(me + d, size)
        src = x_ref if mode == "gather" else x_ref.at[peer]
        copy = pltpu.make_async_remote_copy(
            src_ref=src, dst_ref=recv_ref.at[me], send_sem=send_sems.at[d],
            recv_sem=recv_sems.at[me], device_id=member(peer),
            device_id_type=pl.DeviceIdType.MESH)
        copy.start()
        copies.append(copy)
    return copies


def exchange_finish(axis, stride, size, mode, x_ref, o_ref, recv_ref, send_sems, recv_sems, copies):
    me, member = group_of(axis, stride, size)
    if mode == "gather":
        o_ref[me] = x_ref[...]
    else:
        total = x_ref[me].astype(jnp.float32)
    for d in range(1, size):
        src_dev = lax.rem(me + size - d, size)
        incoming = pltpu.make_async_remote_copy(
            src_ref=recv_ref.at[src_dev], dst_ref=recv_ref.at[src_dev], send_sem=send_sems.at[d],
            recv_sem=recv_sems.at[src_dev], device_id=member(src_dev),
            device_id_type=pl.DeviceIdType.MESH)
        incoming.wait_recv()
        if mode != "gather":
            total = total + recv_ref[src_dev].astype(jnp.float32)
    for copy in copies:
        copy.wait_send()
    if mode != "gather":
        o_ref[...] = total.astype(o_ref.dtype)


def exchange_kernel(axis, stride, size, mode, x_ref, o_ref, *scratch):
    if mode == "gather":
        recv_ref, (send_sems, recv_sems) = o_ref, scratch
    else:
        recv_ref, send_sems, recv_sems = scratch
    enter(exchange_targets(axis, stride, size))
    copies = exchange_start(axis, stride, size, mode, x_ref, recv_ref, send_sems, recv_sems)
    exchange_finish(axis, stride, size, mode, x_ref, o_ref, recv_ref, send_sems, recv_sems, copies)


def exchange_scratch(x, mode, size):
    scratch = [] if mode == "gather" else [pltpu.VMEM(x.shape, x.dtype)]
    return scratch + [pltpu.SemaphoreType.DMA((size,)), pltpu.SemaphoreType.DMA((size,))]


def exchange_shape(x, mode, size):
    shape = (size,) + x.shape if mode == "gather" else x.shape[1:]
    return jax.ShapeDtypeStruct(shape, x.dtype)


def exchange(x, axis, mode, collective_id, stride=1, size=None):
    size = lax.axis_size(axis) if size is None else size
    return pl.pallas_call(
        functools.partial(exchange_kernel, axis, stride, size, mode),
        out_shape=exchange_shape(x, mode, size),
        in_specs=[pl.BlockSpec(memory_space=pltpu.VMEM)],
        out_specs=pl.BlockSpec(memory_space=pltpu.VMEM),
        scratch_shapes=exchange_scratch(x, mode, size),
        compiler_params=pltpu.CompilerParams(collective_id=collective_id, has_side_effects=True),
    )(x)


def pair_targets(chips):
    me, member = group_of("row", 2, chips)
    _, sibling = group_of("row", 1, 2)
    return [member(lax.rem(me + d, chips)) for d in range(1, chips)], sibling


def row_gather_kernel(chips, x_ref, o_ref, send_sems, recv_sems, fwd_send, fwd_recv):
    z_me, z_member = group_of("row", 2, chips)
    c_me, core_member = group_of("row", 1, 2)
    sibling = core_member(1 - c_me)
    peers, _ = pair_targets(chips)
    enter(peers + [sibling])
    copies = []
    for d in range(1, chips):
        peer = lax.rem(z_me + d, chips)
        copy = pltpu.make_async_remote_copy(
            src_ref=x_ref, dst_ref=o_ref.at[c_me, z_me], send_sem=send_sems.at[d],
            recv_sem=recv_sems.at[z_me], device_id=z_member(peer),
            device_id_type=pl.DeviceIdType.MESH)
        copy.start()
        copies.append(copy)
    own = pltpu.make_async_remote_copy(
        src_ref=x_ref, dst_ref=o_ref.at[c_me, z_me], send_sem=fwd_send.at[z_me],
        recv_sem=fwd_recv.at[z_me], device_id=sibling, device_id_type=pl.DeviceIdType.MESH)
    own.start()
    copies.append(own)
    o_ref[c_me, z_me] = x_ref[...]
    for d in range(1, chips):
        src_dev = lax.rem(z_me + chips - d, chips)
        incoming = pltpu.make_async_remote_copy(
            src_ref=o_ref.at[c_me, src_dev], dst_ref=o_ref.at[c_me, src_dev],
            send_sem=send_sems.at[d], recv_sem=recv_sems.at[src_dev],
            device_id=z_member(src_dev), device_id_type=pl.DeviceIdType.MESH)
        incoming.wait_recv()
        forward = pltpu.make_async_remote_copy(
            src_ref=o_ref.at[c_me, src_dev], dst_ref=o_ref.at[c_me, src_dev],
            send_sem=fwd_send.at[src_dev], recv_sem=fwd_recv.at[src_dev], device_id=sibling,
            device_id_type=pl.DeviceIdType.MESH)
        forward.start()
        copies.append(forward)
    for k in range(chips):
        incoming = pltpu.make_async_remote_copy(
            src_ref=o_ref.at[1 - c_me, k], dst_ref=o_ref.at[1 - c_me, k],
            send_sem=fwd_send.at[k], recv_sem=fwd_recv.at[k], device_id=sibling,
            device_id_type=pl.DeviceIdType.MESH)
        incoming.wait_recv()
    for copy in copies:
        copy.wait_send()


def row_gather(x, chips, collective_id):
    return pl.pallas_call(
        functools.partial(row_gather_kernel, chips),
        out_shape=jax.ShapeDtypeStruct((2, chips) + x.shape, x.dtype),
        in_specs=[pl.BlockSpec(memory_space=pltpu.VMEM)],
        out_specs=pl.BlockSpec(memory_space=pltpu.VMEM),
        scratch_shapes=[pltpu.SemaphoreType.DMA((chips,))] * 4,
        compiler_params=pltpu.CompilerParams(collective_id=collective_id, has_side_effects=True),
    )(x)


def row_scatter_kernel(chips, x_ref, o_ref, pair_recv, pair_sum, z_recv,
                       pair_send_sems, pair_recv_sems, z_send_sems, z_recv_sems):
    z_me, z_member = group_of("row", 2, chips)
    c_me, core_member = group_of("row", 1, 2)
    sibling = core_member(1 - c_me)
    peers, _ = pair_targets(chips)
    enter(peers + [sibling])
    copies = []
    for k in range(chips):
        copy = pltpu.make_async_remote_copy(
            src_ref=x_ref.at[1 - c_me, k], dst_ref=pair_recv.at[k], send_sem=pair_send_sems.at[k],
            recv_sem=pair_recv_sems.at[k], device_id=sibling, device_id_type=pl.DeviceIdType.MESH)
        copy.start()
        copies.append(copy)
    order = [lax.rem(z_me + d, chips) for d in range(1, chips)] + [z_me]
    for d, k in enumerate(order, start=1):
        incoming = pltpu.make_async_remote_copy(
            src_ref=pair_recv.at[k], dst_ref=pair_recv.at[k], send_sem=pair_send_sems.at[k],
            recv_sem=pair_recv_sems.at[k], device_id=sibling, device_id_type=pl.DeviceIdType.MESH)
        incoming.wait_recv()
        pair_sum[k] = (x_ref[c_me, k].astype(jnp.float32)
                       + pair_recv[k].astype(jnp.float32)).astype(pair_sum.dtype)
        if d < chips:
            copy = pltpu.make_async_remote_copy(
                src_ref=pair_sum.at[k], dst_ref=z_recv.at[z_me], send_sem=z_send_sems.at[d],
                recv_sem=z_recv_sems.at[z_me], device_id=z_member(k),
                device_id_type=pl.DeviceIdType.MESH)
            copy.start()
            copies.append(copy)
    total = pair_sum[z_me].astype(jnp.float32)
    for d in range(1, chips):
        src_dev = lax.rem(z_me + chips - d, chips)
        incoming = pltpu.make_async_remote_copy(
            src_ref=z_recv.at[src_dev], dst_ref=z_recv.at[src_dev], send_sem=z_send_sems.at[d],
            recv_sem=z_recv_sems.at[src_dev], device_id=z_member(src_dev),
            device_id_type=pl.DeviceIdType.MESH)
        incoming.wait_recv()
        total = total + z_recv[src_dev].astype(jnp.float32)
    for copy in copies:
        copy.wait_send()
    o_ref[...] = total.astype(o_ref.dtype)


def row_scatter(x, chips, collective_id):
    block = x.shape[2:]
    return pl.pallas_call(
        functools.partial(row_scatter_kernel, chips),
        out_shape=jax.ShapeDtypeStruct(block, x.dtype),
        in_specs=[pl.BlockSpec(memory_space=pltpu.VMEM)],
        out_specs=pl.BlockSpec(memory_space=pltpu.VMEM),
        scratch_shapes=[pltpu.VMEM((chips,) + block, x.dtype)] * 3
        + [pltpu.SemaphoreType.DMA((chips,))] * 4,
        compiler_params=pltpu.CompilerParams(collective_id=collective_id, has_side_effects=True),
    )(x)


def feat_push(value_ref, halves_ref, send_sems, recv_sems, slot):
    n = lax.axis_size("feat")
    me = lax.axis_index("feat")
    halves_ref[me] = value_ref[...]
    copies = []
    for d in range(1, n):
        peer = lax.rem(me + d, n)
        copy = pltpu.make_async_remote_copy(
            src_ref=halves_ref.at[me], dst_ref=halves_ref.at[me], send_sem=send_sems.at[slot, d],
            recv_sem=recv_sems.at[slot, me], device_id=mesh_coords("feat", peer),
            device_id_type=pl.DeviceIdType.MESH)
        copy.start()
        copies.append(copy)
    for d in range(1, n):
        src_dev = lax.rem(me + n - d, n)
        pltpu.make_async_remote_copy(
            src_ref=halves_ref.at[src_dev], dst_ref=halves_ref.at[src_dev],
            send_sem=send_sems.at[slot, d], recv_sem=recv_sems.at[slot, src_dev],
            device_id=mesh_coords("feat", src_dev), device_id_type=pl.DeviceIdType.MESH).wait_recv()
    for copy in copies:
        copy.wait_send()


def layer_kernel(x_ref, w_ref, wr_ref, cot_ref, hidden_ref, term_ref, spread_ref,
                 recv_ref, send_sems, recv_sems, summed_ref, agg_ref, grad_out_ref, grad_ref,
                 f_send, f_recv):
    n_col = lax.axis_size("col")
    n_feat = lax.axis_size("feat")
    me = lax.axis_index("feat")
    peers = [mesh_coords("feat", lax.rem(me + d, n_feat)) for d in range(1, n_feat)]
    enter(exchange_targets("col", 1, n_col) + peers)
    copies = exchange_start("col", 1, n_col, "scatter", x_ref, recv_ref, send_sems, recv_sems)
    exchange_finish("col", 1, n_col, "scatter", x_ref, summed_ref, recv_ref, send_sems, recv_sems,
                    copies)
    feat_push(summed_ref, agg_ref, f_send, f_recv, 0)
    half = agg_ref.shape[-1]
    hidden = jnp.dot(agg_ref[0], w_ref[pl.ds(0, half), :], preferred_element_type=jnp.float32)
    for h in range(1, n_feat):
        hidden = hidden + jnp.dot(agg_ref[h], w_ref[pl.ds(h * half, half), :],
                                  preferred_element_type=jnp.float32)
    hidden_ref[...] = hidden
    slope = jnp.where(hidden > 0, 1.0, jnp.exp(jnp.minimum(hidden, 0.0)))
    grad_out_ref[...] = (cot_ref[...].astype(jnp.float32) * slope).astype(grad_out_ref.dtype)
    feat_push(grad_out_ref, grad_ref, f_send, f_recv, 1)
    spread = None
    for h in range(n_feat):
        columns = pl.ds(h * half, half)
        term_ref[:, columns] = lax.dot_general(
            summed_ref[...], grad_ref[h], (((0,), (0,)), ((), ())),
            preferred_element_type=jnp.float32)
        part = lax.dot_general(grad_ref[h], wr_ref[:, columns], (((1,), (1,)), ((), ())),
                               preferred_element_type=jnp.float32)
        spread = part if spread is None else spread + part
    spread_ref[...] = spread.astype(spread_ref.dtype)


def layer_step(partials, weight_cols, weight_rows, cotangent, collective_id):
    n_col = lax.axis_size("col")
    n_feat = lax.axis_size("feat")
    block = partials.shape[1:]
    half = block[-1]
    vmem = pl.BlockSpec(memory_space=pltpu.VMEM)
    return pl.pallas_call(
        layer_kernel,
        out_shape=(
            jax.ShapeDtypeStruct(block, jnp.float32),
            jax.ShapeDtypeStruct((half, n_feat * half), jnp.float32),
            jax.ShapeDtypeStruct(block, jnp.bfloat16),
        ),
        in_specs=[vmem] * 4,
        out_specs=(vmem,) * 3,
        scratch_shapes=exchange_scratch(partials, "scatter", n_col) + [
            pltpu.VMEM(block, partials.dtype),
            pltpu.VMEM((n_feat,) + block, partials.dtype),
            pltpu.VMEM(block, jnp.bfloat16),
            pltpu.VMEM((n_feat,) + block, jnp.bfloat16),
            pltpu.SemaphoreType.DMA((2, n_feat)),
            pltpu.SemaphoreType.DMA((2, n_feat)),
        ],
        compiler_params=pltpu.CompilerParams(collective_id=collective_id, has_side_effects=True),
    )(partials, weight_cols, weight_rows, cotangent)


def reduction_plan(rows):
    pairs = []
    for bit in (1, 2, 4, 8, 16, 32, 64):
        for axis in ("row", "col"):
            if bit < lax.axis_size(axis):
                pairs.append((axis, bit))
    halving = []
    while pairs and rows // 2 >= 8 and rows % 16 == 0:
        halving.append(pairs.pop(0))
        rows //= 2
    return halving, pairs


def bitval(axis, bit):
    return (lax.axis_index(axis) // bit) % 2


def partner(axis, bit):
    return mesh_coords(axis, lax.axis_index(axis) + bit * (1 - 2 * bitval(axis, bit)))


def reduce_targets(rows):
    halving, whole = reduction_plan(rows)
    return [partner(axis, bit) for axis, bit in halving + whole]


def reduce_rounds(x_ref, o_ref, recv, send_sems, recv_sems):
    halving, whole = reduction_plan(x_ref.shape[0])
    o_ref[...] = x_ref[...]
    k = 0

    def swap(k, axis, bit, send_rows, length):
        copy = pltpu.make_async_remote_copy(
            src_ref=o_ref.at[pl.ds(send_rows, length)], dst_ref=recv.at[k, pl.ds(0, length)],
            send_sem=send_sems.at[k], recv_sem=recv_sems.at[k],
            device_id=partner(axis, bit), device_id_type=pl.DeviceIdType.MESH)
        copy.start()
        copy.wait()

    lo = jnp.int32(0)
    length = x_ref.shape[0]
    starts = []
    for axis, bit in halving:
        length //= 2
        mine = bitval(axis, bit)
        starts.append(lo)
        keep = pl.multiple_of(lo + mine * length, 8)
        give = pl.multiple_of(lo + (1 - mine) * length, 8)
        swap(k, axis, bit, give, length)
        o_ref[pl.ds(keep, length)] = o_ref[pl.ds(keep, length)] + recv[k, pl.ds(0, length)]
        lo = keep
        k += 1
    for axis, bit in whole:
        swap(k, axis, bit, lo, length)
        o_ref[pl.ds(lo, length)] = o_ref[pl.ds(lo, length)] + recv[k, pl.ds(0, length)]
        k += 1
    for (axis, bit), base in zip(reversed(halving), reversed(starts)):
        mine = bitval(axis, bit)
        other = pl.multiple_of(base + (1 - mine) * length, 8)
        swap(k, axis, bit, lo, length)
        o_ref[pl.ds(other, length)] = recv[k, pl.ds(0, length)]
        lo = base
        length *= 2
        k += 1


def reduce_scratch(w):
    halving, whole = reduction_plan(w.shape[0])
    steps = 2 * len(halving) + len(whole)
    return [
        pltpu.VMEM((steps, w.shape[0] // 2) + w.shape[1:], w.dtype),
        pltpu.SemaphoreType.DMA((steps,)),
        pltpu.SemaphoreType.DMA((steps,)),
    ]


def radix_groups():
    n_row, n_col = lax.axis_size("row"), lax.axis_size("col")
    if n_row % 2 or n_col % 4:
        return None
    return ((("row", 1, 2), ("col", 1, 4)), ("row", 2, n_row // 2), ("col", 4, n_col // 4))


def first_group():
    (core, ring), _, _ = radix_groups()
    me_a, _ = group_of(*core)
    me_b, _ = group_of(*ring)
    size = core[2] * ring[2]
    me = me_a + core[2] * me_b
    row = lax.axis_index("row") - me_a * core[1]
    col = lax.axis_index("col") - me_b * ring[1]

    def member(m):
        return (row + (m % core[2]) * core[1], col + (m // core[2]) * ring[1], lax.axis_index("feat"))

    return me, size, member


def reduce_radix_targets():
    me, size, member = first_group()
    targets = [member(lax.rem(me + d, size)) for d in range(1, size)]
    _, z_group, x_group = radix_groups()
    return targets + exchange_targets(*z_group) + exchange_targets(*x_group)


def ordered_allreduce(group, value, recv, send_sems, recv_sems):
    axis, stride, size = group
    me, member = group_of(axis, stride, size)
    recv[me] = value
    copies = []
    for d in range(1, size):
        peer = lax.rem(me + d, size)
        copy = pltpu.make_async_remote_copy(
            src_ref=recv.at[me], dst_ref=recv.at[me], send_sem=send_sems.at[d],
            recv_sem=recv_sems.at[me], device_id=member(peer), device_id_type=pl.DeviceIdType.MESH)
        copy.start()
        copies.append(copy)
    for d in range(1, size):
        src_dev = lax.rem(me + size - d, size)
        pltpu.make_async_remote_copy(
            src_ref=recv.at[src_dev], dst_ref=recv.at[src_dev], send_sem=send_sems.at[d],
            recv_sem=recv_sems.at[src_dev], device_id=member(src_dev),
            device_id_type=pl.DeviceIdType.MESH).wait_recv()
    for copy in copies:
        copy.wait_send()
    total = recv[0]
    for k in range(1, size):
        total = total + recv[k]
    return total


def reduce_radix(w_ref, o_ref, seg_recv, z_recv, x_recv, sems):
    _, z_group, x_group = radix_groups()
    me, size, member = first_group()
    seg = w_ref.shape[0] // size
    mine = pl.ds(pl.multiple_of(me * seg, 8), seg)
    copies = []
    for d in range(1, size):
        peer = lax.rem(me + d, size)
        copy = pltpu.make_async_remote_copy(
            src_ref=w_ref.at[pl.ds(pl.multiple_of(peer * seg, 8), seg)], dst_ref=seg_recv.at[me],
            send_sem=sems.at[0, d], recv_sem=sems.at[1, me], device_id=member(peer),
            device_id_type=pl.DeviceIdType.MESH)
        copy.start()
        copies.append(copy)
    total = w_ref[mine]
    for d in range(1, size):
        src_dev = lax.rem(me + size - d, size)
        pltpu.make_async_remote_copy(
            src_ref=seg_recv.at[src_dev], dst_ref=seg_recv.at[src_dev], send_sem=sems.at[0, d],
            recv_sem=sems.at[1, src_dev], device_id=member(src_dev),
            device_id_type=pl.DeviceIdType.MESH).wait_recv()
        total = total + seg_recv[src_dev]
    for copy in copies:
        copy.wait_send()
    total = ordered_allreduce(z_group, total, z_recv, sems.at[2], sems.at[3])
    total = ordered_allreduce(x_group, total, x_recv, sems.at[4], sems.at[5])
    o_ref[mine] = total
    copies = []
    for d in range(1, size):
        peer = lax.rem(me + d, size)
        copy = pltpu.make_async_remote_copy(
            src_ref=o_ref.at[mine], dst_ref=o_ref.at[mine], send_sem=sems.at[6, d],
            recv_sem=sems.at[7, me], device_id=member(peer), device_id_type=pl.DeviceIdType.MESH)
        copy.start()
        copies.append(copy)
    for d in range(1, size):
        src_dev = lax.rem(me + size - d, size)
        rows = pl.ds(pl.multiple_of(src_dev * seg, 8), seg)
        pltpu.make_async_remote_copy(
            src_ref=o_ref.at[rows], dst_ref=o_ref.at[rows], send_sem=sems.at[6, d],
            recv_sem=sems.at[7, src_dev], device_id=member(src_dev),
            device_id_type=pl.DeviceIdType.MESH).wait_recv()
    for copy in copies:
        copy.wait_send()


def radix_scratch(w):
    (core, ring), z_group, x_group = radix_groups()
    size = core[2] * ring[2]
    seg = (w.shape[0] // size,) + w.shape[1:]
    width = max(size, z_group[2], x_group[2])
    return [
        pltpu.VMEM((size,) + seg, w.dtype),
        pltpu.VMEM((z_group[2],) + seg, w.dtype),
        pltpu.VMEM((x_group[2],) + seg, w.dtype),
        pltpu.SemaphoreType.DMA((8, width)),
    ]


def radix_fits(w):
    groups = radix_groups()
    if groups is None:
        return False
    size = groups[0][0][2] * groups[0][1][2]
    return w.shape[0] % (8 * size) == 0


def gather_radix_kernel(axis, x_ref, w_ref, o_ref, ow_ref, g_send, g_recv, *scratch):
    size = lax.axis_size(axis)
    enter(exchange_targets(axis, 1, size) + reduce_radix_targets())
    copies = exchange_start(axis, 1, size, "gather", x_ref, o_ref, g_send, g_recv)
    reduce_radix(w_ref, ow_ref, *scratch)
    exchange_finish(axis, 1, size, "gather", x_ref, o_ref, o_ref, g_send, g_recv, copies)


def gather_reduce_kernel(axis, x_ref, w_ref, o_ref, ow_ref, g_send, g_recv, recv, send_sems, recv_sems):
    size = lax.axis_size(axis)
    enter(exchange_targets(axis, 1, size) + reduce_targets(w_ref.shape[0]))
    copies = exchange_start(axis, 1, size, "gather", x_ref, o_ref, g_send, g_recv)
    reduce_rounds(w_ref, ow_ref, recv, send_sems, recv_sems)
    exchange_finish(axis, 1, size, "gather", x_ref, o_ref, o_ref, g_send, g_recv, copies)


def gather_and_reduce(x, w, axis, collective_id):
    size = lax.axis_size(axis)
    if radix_fits(w):
        kernel, scratch = gather_radix_kernel, radix_scratch(w)
    else:
        kernel, scratch = gather_reduce_kernel, reduce_scratch(w)
    return pl.pallas_call(
        functools.partial(kernel, axis),
        out_shape=(exchange_shape(x, "gather", size), jax.ShapeDtypeStruct(w.shape, w.dtype)),
        in_specs=[pl.BlockSpec(memory_space=pltpu.VMEM)] * 2,
        out_specs=(pl.BlockSpec(memory_space=pltpu.VMEM),) * 2,
        scratch_shapes=exchange_scratch(x, "gather", size) + scratch,
        compiler_params=pltpu.CompilerParams(collective_id=collective_id, has_side_effects=True),
    )(x, w)


def shards(features, tile_rows, tile_cols, tile_count, tile_values, weights, cotangent):
    width = tile_values.shape[-1]
    local_tiles = tile_values[0, 0]
    block_rows = tile_rows[0, 0]
    block_cols = tile_cols[0, 0]
    count = tile_count[0, 0].reshape(1)
    n_rowdev = lax.axis_size("row")
    n_coldev = lax.axis_size("col")
    local_blocks = features.shape[0] // width
    feat_half = features.shape[1]
    feat_index = lax.axis_index("feat")
    row_blocks = local_blocks * n_coldev
    col_blocks = local_blocks * n_rowdev
    node_total = features.shape[0] * n_rowdev * n_coldev
    pair = 2 if n_rowdev % 2 == 0 else 1
    chips = n_rowdev // pair
    if pair == 2:
        panel = row_gather(features, chips, 0).reshape(-1, feat_half)
    else:
        panel = exchange(features, "row", "gather", 0).reshape(-1, feat_half)
    owner = block_cols // local_blocks
    block_cols = ((owner % pair) * chips + owner // pair) * local_blocks + block_cols % local_blocks
    partial_value = tile_products(local_tiles, block_rows, block_cols, count, panel,
                                  row_blocks, transpose=False)
    weight_cols = lax.dynamic_slice_in_dim(weights, feat_index * feat_half, feat_half, 1)
    weight_rows = lax.dynamic_slice_in_dim(weights, feat_index * feat_half, feat_half, 0)
    hidden, weight_term, spread = layer_step(partial_value.reshape(n_coldev, -1, feat_half),
                                             weight_cols, weight_rows, cotangent, 1)
    negative = jnp.minimum(hidden, 0.0)
    activated = jnp.where(hidden > 0, hidden, jnp.expm1(negative)).astype(jnp.bfloat16)
    spread_panel, weight_sum = gather_and_reduce(spread, weight_term, "col", 2)
    spread_panel = spread_panel.reshape(-1, feat_half)
    weight_grad = weight_sum * node_total ** (-0.5)
    back_partial = tile_products(local_tiles, block_rows, block_cols, count, spread_panel,
                                 col_blocks, transpose=True)
    if pair == 2:
        back_summed = row_scatter(back_partial.reshape(pair, chips, -1, feat_half), chips, 3)
    else:
        back_summed = exchange(back_partial.reshape(n_rowdev, -1, feat_half), "row", "scatter", 3)
    return (activated, back_summed, weight_grad)


def solution(mesh):
    return jax.shard_map(
        shards,
        mesh=mesh,
        in_specs=(
            P(("col", "row"), "feat"),
            P("row", "col", None),
            P("row", "col", None),
            P("row", "col"),
            P("row", "col", None, None, None),
            P(),
            P(("row", "col"), "feat"),
        ),
        out_specs=(P(("row", "col"), "feat"), P(("col", "row"), "feat"), P("feat", None)),
        check_vma=False,
    )
```

```python
import functools

import jax
import jax.numpy as jnp
from jax import lax
from jax.experimental import pallas as pl
from jax.experimental.pallas import tpu as pltpu
from jax.sharding import PartitionSpec as P

GROUP = 64


def tile_kernel(transpose, rows_ref, cols_ref, count_ref, tiles_ref, panel_ref, out_ref, acc_ref):
    step = pl.program_id(0)
    width = tiles_ref.shape[-1]
    count = count_ref[0]
    src_blocks = panel_ref.shape[0] // width
    dst_blocks = acc_ref.shape[0] // width

    @pl.when(step == 0)
    def _():
        acc_ref[...] = jnp.zeros_like(acc_ref)

    @pl.when(step * GROUP < count)
    def _():
        terms = []
        for j in range(GROUP):
            slot = step * GROUP + j
            src = rows_ref[slot] if transpose else cols_ref[slot]
            src = jnp.minimum(jnp.maximum(src, 0), src_blocks - 1)
            block = panel_ref[pl.ds(pl.multiple_of(src * width, width), width), :]
            tile = tiles_ref[j]
            if transpose:
                term = lax.dot_general(tile, block, (((0,), (0,)), ((), ())),
                                       preferred_element_type=jnp.float32)
            else:
                term = jnp.dot(tile, block, preferred_element_type=jnp.float32)
            terms.append(jnp.where(slot < count, term, 0.0))
        for j in range(GROUP):
            slot = step * GROUP + j
            dst = cols_ref[slot] if transpose else rows_ref[slot]
            dst = jnp.minimum(jnp.maximum(dst, 0), dst_blocks - 1)
            rows = pl.ds(pl.multiple_of(dst * width, width), width)
            acc_ref[rows, :] += terms[j]

    @pl.when(step == pl.num_programs(0) - 1)
    def _():
        out_ref[...] = acc_ref[...].astype(out_ref.dtype)


def tile_products(tiles, rows, cols, count, panel, out_blocks, transpose):
    slots, width, _ = tiles.shape
    feat = panel.shape[1]
    steps = slots // GROUP

    def tiles_map(i, rows_ref, cols_ref, count_ref):
        last = jnp.maximum(count_ref[0] - 1, 0) // GROUP
        return (jnp.minimum(i, last), 0, 0)

    return pl.pallas_call(
        functools.partial(tile_kernel, transpose),
        out_shape=jax.ShapeDtypeStruct((out_blocks * width, feat), jnp.bfloat16),
        grid_spec=pltpu.PrefetchScalarGridSpec(
            num_scalar_prefetch=3,
            grid=(steps,),
            in_specs=[
                pl.BlockSpec((GROUP, width, width), tiles_map),
                pl.BlockSpec(panel.shape, lambda i, *_: (0, 0)),
            ],
            out_specs=pl.BlockSpec((out_blocks * width, feat), lambda i, *_: (0, 0)),
            scratch_shapes=[pltpu.VMEM((out_blocks * width, feat), jnp.float32)],
        ),
        compiler_params=pltpu.CompilerParams(dimension_semantics=("arbitrary",)),
        cost_estimate=pl.CostEstimate(
            flops=2 * slots * width * width * feat,
            bytes_accessed=tiles.size * 2 + panel.size * 2 + out_blocks * width * feat * 2,
            transcendentals=0,
        ),
    )(rows, cols, count, tiles, panel)


def mesh_coords(axis, peer):
    return tuple(peer if name == axis else lax.axis_index(name) for name in ("row", "col", "feat"))


def group_of(axis, stride, size):
    index = lax.axis_index(axis)
    me = (index // stride) % size
    base = index - me * stride
    return me, lambda k: mesh_coords(axis, base + k * stride)


def exchange_targets(axis, stride, size):
    me, member = group_of(axis, stride, size)
    return [member(lax.rem(me + d, size)) for d in range(1, size)]


def enter(targets):
    barrier = pltpu.get_barrier_semaphore()
    for target in targets:
        pl.semaphore_signal(barrier, inc=1, device_id=target, device_id_type=pl.DeviceIdType.MESH)
    pl.semaphore_wait(barrier, len(targets))


def exchange_start(axis, stride, size, mode, x_ref, recv_ref, send_sems, recv_sems):
    me, member = group_of(axis, stride, size)
    copies = []
    for d in range(1, size):
        peer = lax.rem(me + d, size)
        src = x_ref if mode == "gather" else x_ref.at[peer]
        copy = pltpu.make_async_remote_copy(
            src_ref=src, dst_ref=recv_ref.at[me], send_sem=send_sems.at[d],
            recv_sem=recv_sems.at[me], device_id=member(peer),
            device_id_type=pl.DeviceIdType.MESH)
        copy.start()
        copies.append(copy)
    return copies


def exchange_finish(axis, stride, size, mode, x_ref, o_ref, recv_ref, send_sems, recv_sems, copies):
    me, member = group_of(axis, stride, size)
    if mode == "gather":
        o_ref[me] = x_ref[...]
    else:
        total = x_ref[me].astype(jnp.float32)
    for d in range(1, size):
        src_dev = lax.rem(me + size - d, size)
        incoming = pltpu.make_async_remote_copy(
            src_ref=recv_ref.at[src_dev], dst_ref=recv_ref.at[src_dev], send_sem=send_sems.at[d],
            recv_sem=recv_sems.at[src_dev], device_id=member(src_dev),
            device_id_type=pl.DeviceIdType.MESH)
        incoming.wait_recv()
        if mode != "gather":
            total = total + recv_ref[src_dev].astype(jnp.float32)
    for copy in copies:
        copy.wait_send()
    if mode != "gather":
        o_ref[...] = total.astype(o_ref.dtype)


def exchange_kernel(axis, stride, size, mode, x_ref, o_ref, *scratch):
    if mode == "gather":
        recv_ref, (send_sems, recv_sems) = o_ref, scratch
    else:
        recv_ref, send_sems, recv_sems = scratch
    enter(exchange_targets(axis, stride, size))
    copies = exchange_start(axis, stride, size, mode, x_ref, recv_ref, send_sems, recv_sems)
    exchange_finish(axis, stride, size, mode, x_ref, o_ref, recv_ref, send_sems, recv_sems, copies)


def exchange_scratch(x, mode, size):
    scratch = [] if mode == "gather" else [pltpu.VMEM(x.shape, x.dtype)]
    return scratch + [pltpu.SemaphoreType.DMA((size,)), pltpu.SemaphoreType.DMA((size,))]


def exchange_shape(x, mode, size):
    shape = (size,) + x.shape if mode == "gather" else x.shape[1:]
    return jax.ShapeDtypeStruct(shape, x.dtype)


def exchange(x, axis, mode, collective_id, stride=1, size=None):
    size = lax.axis_size(axis) if size is None else size
    return pl.pallas_call(
        functools.partial(exchange_kernel, axis, stride, size, mode),
        out_shape=exchange_shape(x, mode, size),
        in_specs=[pl.BlockSpec(memory_space=pltpu.VMEM)],
        out_specs=pl.BlockSpec(memory_space=pltpu.VMEM),
        scratch_shapes=exchange_scratch(x, mode, size),
        compiler_params=pltpu.CompilerParams(collective_id=collective_id, has_side_effects=True),
    )(x)


def pair_targets(chips):
    me, member = group_of("row", 2, chips)
    _, sibling = group_of("row", 1, 2)
    return [member(lax.rem(me + d, chips)) for d in range(1, chips)], sibling


def row_gather_kernel(chips, x_ref, o_ref, send_sems, recv_sems, fwd_send, fwd_recv):
    z_me, z_member = group_of("row", 2, chips)
    c_me, core_member = group_of("row", 1, 2)
    sibling = core_member(1 - c_me)
    peers, _ = pair_targets(chips)
    enter(peers + [sibling])
    copies = []
    for d in range(1, chips):
        peer = lax.rem(z_me + d, chips)
        copy = pltpu.make_async_remote_copy(
            src_ref=x_ref, dst_ref=o_ref.at[c_me, z_me], send_sem=send_sems.at[d],
            recv_sem=recv_sems.at[z_me], device_id=z_member(peer),
            device_id_type=pl.DeviceIdType.MESH)
        copy.start()
        copies.append(copy)
    own = pltpu.make_async_remote_copy(
        src_ref=x_ref, dst_ref=o_ref.at[c_me, z_me], send_sem=fwd_send.at[z_me],
        recv_sem=fwd_recv.at[z_me], device_id=sibling, device_id_type=pl.DeviceIdType.MESH)
    own.start()
    copies.append(own)
    o_ref[c_me, z_me] = x_ref[...]
    for d in range(1, chips):
        src_dev = lax.rem(z_me + chips - d, chips)
        incoming = pltpu.make_async_remote_copy(
            src_ref=o_ref.at[c_me, src_dev], dst_ref=o_ref.at[c_me, src_dev],
            send_sem=send_sems.at[d], recv_sem=recv_sems.at[src_dev],
            device_id=z_member(src_dev), device_id_type=pl.DeviceIdType.MESH)
        incoming.wait_recv()
        forward = pltpu.make_async_remote_copy(
            src_ref=o_ref.at[c_me, src_dev], dst_ref=o_ref.at[c_me, src_dev],
            send_sem=fwd_send.at[src_dev], recv_sem=fwd_recv.at[src_dev], device_id=sibling,
            device_id_type=pl.DeviceIdType.MESH)
        forward.start()
        copies.append(forward)
    for k in range(chips):
        incoming = pltpu.make_async_remote_copy(
            src_ref=o_ref.at[1 - c_me, k], dst_ref=o_ref.at[1 - c_me, k],
            send_sem=fwd_send.at[k], recv_sem=fwd_recv.at[k], device_id=sibling,
            device_id_type=pl.DeviceIdType.MESH)
        incoming.wait_recv()
    for copy in copies:
        copy.wait_send()


def row_gather(x, chips, collective_id):
    return pl.pallas_call(
        functools.partial(row_gather_kernel, chips),
        out_shape=jax.ShapeDtypeStruct((2, chips) + x.shape, x.dtype),
        in_specs=[pl.BlockSpec(memory_space=pltpu.VMEM)],
        out_specs=pl.BlockSpec(memory_space=pltpu.VMEM),
        scratch_shapes=[pltpu.SemaphoreType.DMA((chips,))] * 4,
        compiler_params=pltpu.CompilerParams(collective_id=collective_id, has_side_effects=True),
    )(x)


def row_scatter_kernel(chips, x_ref, o_ref, pair_recv, pair_sum, z_recv,
                       pair_send_sems, pair_recv_sems, z_send_sems, z_recv_sems):
    z_me, z_member = group_of("row", 2, chips)
    c_me, core_member = group_of("row", 1, 2)
    sibling = core_member(1 - c_me)
    peers, _ = pair_targets(chips)
    enter(peers + [sibling])
    copies = []
    for k in range(chips):
        copy = pltpu.make_async_remote_copy(
            src_ref=x_ref.at[1 - c_me, k], dst_ref=pair_recv.at[k], send_sem=pair_send_sems.at[k],
            recv_sem=pair_recv_sems.at[k], device_id=sibling, device_id_type=pl.DeviceIdType.MESH)
        copy.start()
        copies.append(copy)
    order = [lax.rem(z_me + d, chips) for d in range(1, chips)] + [z_me]
    for d, k in enumerate(order, start=1):
        incoming = pltpu.make_async_remote_copy(
            src_ref=pair_recv.at[k], dst_ref=pair_recv.at[k], send_sem=pair_send_sems.at[k],
            recv_sem=pair_recv_sems.at[k], device_id=sibling, device_id_type=pl.DeviceIdType.MESH)
        incoming.wait_recv()
        pair_sum[k] = (x_ref[c_me, k].astype(jnp.float32)
                       + pair_recv[k].astype(jnp.float32)).astype(pair_sum.dtype)
        if d < chips:
            copy = pltpu.make_async_remote_copy(
                src_ref=pair_sum.at[k], dst_ref=z_recv.at[z_me], send_sem=z_send_sems.at[d],
                recv_sem=z_recv_sems.at[z_me], device_id=z_member(k),
                device_id_type=pl.DeviceIdType.MESH)
            copy.start()
            copies.append(copy)
    total = pair_sum[z_me].astype(jnp.float32)
    for d in range(1, chips):
        src_dev = lax.rem(z_me + chips - d, chips)
        incoming = pltpu.make_async_remote_copy(
            src_ref=z_recv.at[src_dev], dst_ref=z_recv.at[src_dev], send_sem=z_send_sems.at[d],
            recv_sem=z_recv_sems.at[src_dev], device_id=z_member(src_dev),
            device_id_type=pl.DeviceIdType.MESH)
        incoming.wait_recv()
        total = total + z_recv[src_dev].astype(jnp.float32)
    for copy in copies:
        copy.wait_send()
    o_ref[...] = total.astype(o_ref.dtype)


def row_scatter(x, chips, collective_id):
    block = x.shape[2:]
    return pl.pallas_call(
        functools.partial(row_scatter_kernel, chips),
        out_shape=jax.ShapeDtypeStruct(block, x.dtype),
        in_specs=[pl.BlockSpec(memory_space=pltpu.VMEM)],
        out_specs=pl.BlockSpec(memory_space=pltpu.VMEM),
        scratch_shapes=[pltpu.VMEM((chips,) + block, x.dtype)] * 3
        + [pltpu.SemaphoreType.DMA((chips,))] * 4,
        compiler_params=pltpu.CompilerParams(collective_id=collective_id, has_side_effects=True),
    )(x)


def feat_push(value_ref, halves_ref, send_sems, recv_sems, slot):
    n = lax.axis_size("feat")
    me = lax.axis_index("feat")
    halves_ref[me] = value_ref[...]
    copies = []
    for d in range(1, n):
        peer = lax.rem(me + d, n)
        copy = pltpu.make_async_remote_copy(
            src_ref=halves_ref.at[me], dst_ref=halves_ref.at[me], send_sem=send_sems.at[slot, d],
            recv_sem=recv_sems.at[slot, me], device_id=mesh_coords("feat", peer),
            device_id_type=pl.DeviceIdType.MESH)
        copy.start()
        copies.append(copy)
    for d in range(1, n):
        src_dev = lax.rem(me + n - d, n)
        pltpu.make_async_remote_copy(
            src_ref=halves_ref.at[src_dev], dst_ref=halves_ref.at[src_dev],
            send_sem=send_sems.at[slot, d], recv_sem=recv_sems.at[slot, src_dev],
            device_id=mesh_coords("feat", src_dev), device_id_type=pl.DeviceIdType.MESH).wait_recv()
    for copy in copies:
        copy.wait_send()


def layer_kernel(x_ref, w_ref, wr_ref, cot_ref, hidden_ref, panel_ref, sum_ref,
                 recv_ref, send_sems, recv_sems, summed_ref, agg_ref, grad_out_ref, grad_ref,
                 f_send, f_recv, term_ref, spread_ref, g_send, g_recv, *reduce_scratch):
    n_col = lax.axis_size("col")
    n_feat = lax.axis_size("feat")
    me = lax.axis_index("feat")
    peers = [mesh_coords("feat", lax.rem(me + d, n_feat)) for d in range(1, n_feat)]
    radix = len(reduce_scratch) == 4
    others = reduce_radix_targets() if radix else reduce_targets(term_ref.shape[0])
    enter(exchange_targets("col", 1, n_col) + peers + exchange_targets("col", 1, n_col) + others)
    copies = exchange_start("col", 1, n_col, "scatter", x_ref, recv_ref, send_sems, recv_sems)
    exchange_finish("col", 1, n_col, "scatter", x_ref, summed_ref, recv_ref, send_sems, recv_sems,
                    copies)
    feat_push(summed_ref, agg_ref, f_send, f_recv, 0)
    half = agg_ref.shape[-1]
    hidden = jnp.dot(agg_ref[0], w_ref[pl.ds(0, half), :], preferred_element_type=jnp.float32)
    for h in range(1, n_feat):
        hidden = hidden + jnp.dot(agg_ref[h], w_ref[pl.ds(h * half, half), :],
                                  preferred_element_type=jnp.float32)
    hidden_ref[...] = hidden
    slope = jnp.where(hidden > 0, 1.0, jnp.exp(jnp.minimum(hidden, 0.0)))
    grad_out_ref[...] = (cot_ref[...].astype(jnp.float32) * slope).astype(grad_out_ref.dtype)
    feat_push(grad_out_ref, grad_ref, f_send, f_recv, 1)
    spread = None
    for h in range(n_feat):
        columns = pl.ds(h * half, half)
        term_ref[:, columns] = lax.dot_general(
            summed_ref[...], grad_ref[h], (((0,), (0,)), ((), ())),
            preferred_element_type=jnp.float32)
        part = lax.dot_general(grad_ref[h], wr_ref[:, columns], (((1,), (1,)), ((), ())),
                               preferred_element_type=jnp.float32)
        spread = part if spread is None else spread + part
    spread_ref[...] = spread.astype(spread_ref.dtype)
    copies = exchange_start("col", 1, n_col, "gather", spread_ref, panel_ref, g_send, g_recv)
    if radix:
        reduce_radix(term_ref, sum_ref, *reduce_scratch)
    else:
        reduce_rounds(term_ref, sum_ref, *reduce_scratch)
    exchange_finish("col", 1, n_col, "gather", spread_ref, panel_ref, panel_ref, g_send, g_recv,
                    copies)


def layer_step(partials, weight_cols, weight_rows, cotangent, collective_id):
    n_col = lax.axis_size("col")
    n_feat = lax.axis_size("feat")
    block = partials.shape[1:]
    half = block[-1]
    term = jax.ShapeDtypeStruct((half, n_feat * half), jnp.float32)
    reduce_space = radix_scratch(term) if radix_fits(term) else reduce_scratch(term)
    vmem = pl.BlockSpec(memory_space=pltpu.VMEM)
    return pl.pallas_call(
        layer_kernel,
        out_shape=(
            jax.ShapeDtypeStruct(block, jnp.float32),
            jax.ShapeDtypeStruct((n_col,) + block, jnp.bfloat16),
            term,
        ),
        in_specs=[vmem] * 4,
        out_specs=(vmem,) * 3,
        scratch_shapes=exchange_scratch(partials, "scatter", n_col) + [
            pltpu.VMEM(block, partials.dtype),
            pltpu.VMEM((n_feat,) + block, partials.dtype),
            pltpu.VMEM(block, jnp.bfloat16),
            pltpu.VMEM((n_feat,) + block, jnp.bfloat16),
            pltpu.SemaphoreType.DMA((2, n_feat)),
            pltpu.SemaphoreType.DMA((2, n_feat)),
            pltpu.VMEM(term.shape, term.dtype),
            pltpu.VMEM(block, jnp.bfloat16),
            pltpu.SemaphoreType.DMA((n_col,)),
            pltpu.SemaphoreType.DMA((n_col,)),
        ] + reduce_space,
        compiler_params=pltpu.CompilerParams(collective_id=collective_id, has_side_effects=True),
    )(partials, weight_cols, weight_rows, cotangent)


def reduction_plan(rows):
    pairs = []
    for bit in (1, 2, 4, 8, 16, 32, 64):
        for axis in ("row", "col"):
            if bit < lax.axis_size(axis):
                pairs.append((axis, bit))
    halving = []
    while pairs and rows // 2 >= 8 and rows % 16 == 0:
        halving.append(pairs.pop(0))
        rows //= 2
    return halving, pairs


def bitval(axis, bit):
    return (lax.axis_index(axis) // bit) % 2


def partner(axis, bit):
    return mesh_coords(axis, lax.axis_index(axis) + bit * (1 - 2 * bitval(axis, bit)))


def reduce_targets(rows):
    halving, whole = reduction_plan(rows)
    return [partner(axis, bit) for axis, bit in halving + whole]


def reduce_rounds(x_ref, o_ref, recv, send_sems, recv_sems):
    halving, whole = reduction_plan(x_ref.shape[0])
    o_ref[...] = x_ref[...]
    k = 0

    def swap(k, axis, bit, send_rows, length):
        copy = pltpu.make_async_remote_copy(
            src_ref=o_ref.at[pl.ds(send_rows, length)], dst_ref=recv.at[k, pl.ds(0, length)],
            send_sem=send_sems.at[k], recv_sem=recv_sems.at[k],
            device_id=partner(axis, bit), device_id_type=pl.DeviceIdType.MESH)
        copy.start()
        copy.wait()

    lo = jnp.int32(0)
    length = x_ref.shape[0]
    starts = []
    for axis, bit in halving:
        length //= 2
        mine = bitval(axis, bit)
        starts.append(lo)
        keep = pl.multiple_of(lo + mine * length, 8)
        give = pl.multiple_of(lo + (1 - mine) * length, 8)
        swap(k, axis, bit, give, length)
        o_ref[pl.ds(keep, length)] = o_ref[pl.ds(keep, length)] + recv[k, pl.ds(0, length)]
        lo = keep
        k += 1
    for axis, bit in whole:
        swap(k, axis, bit, lo, length)
        o_ref[pl.ds(lo, length)] = o_ref[pl.ds(lo, length)] + recv[k, pl.ds(0, length)]
        k += 1
    for (axis, bit), base in zip(reversed(halving), reversed(starts)):
        mine = bitval(axis, bit)
        other = pl.multiple_of(base + (1 - mine) * length, 8)
        swap(k, axis, bit, lo, length)
        o_ref[pl.ds(other, length)] = recv[k, pl.ds(0, length)]
        lo = base
        length *= 2
        k += 1


def reduce_scratch(w):
    halving, whole = reduction_plan(w.shape[0])
    steps = 2 * len(halving) + len(whole)
    return [
        pltpu.VMEM((steps, w.shape[0] // 2) + w.shape[1:], w.dtype),
        pltpu.SemaphoreType.DMA((steps,)),
        pltpu.SemaphoreType.DMA((steps,)),
    ]


def radix_groups():
    n_row, n_col = lax.axis_size("row"), lax.axis_size("col")
    if n_row % 2 or n_col % 4:
        return None
    return ((("row", 1, 2), ("col", 1, 4)), ("row", 2, n_row // 2), ("col", 4, n_col // 4))


def first_group():
    (core, ring), _, _ = radix_groups()
    me_a, _ = group_of(*core)
    me_b, _ = group_of(*ring)
    size = core[2] * ring[2]
    me = me_a + core[2] * me_b
    row = lax.axis_index("row") - me_a * core[1]
    col = lax.axis_index("col") - me_b * ring[1]

    def member(m):
        return (row + (m % core[2]) * core[1], col + (m // core[2]) * ring[1], lax.axis_index("feat"))

    return me, size, member


def reduce_radix_targets():
    me, size, member = first_group()
    targets = [member(lax.rem(me + d, size)) for d in range(1, size)]
    _, z_group, x_group = radix_groups()
    return targets + exchange_targets(*z_group) + exchange_targets(*x_group)


def ordered_allreduce(group, value, recv, send_sems, recv_sems):
    axis, stride, size = group
    me, member = group_of(axis, stride, size)
    recv[me] = value
    copies = []
    for d in range(1, size):
        peer = lax.rem(me + d, size)
        copy = pltpu.make_async_remote_copy(
            src_ref=recv.at[me], dst_ref=recv.at[me], send_sem=send_sems.at[d],
            recv_sem=recv_sems.at[me], device_id=member(peer), device_id_type=pl.DeviceIdType.MESH)
        copy.start()
        copies.append(copy)
    for d in range(1, size):
        src_dev = lax.rem(me + size - d, size)
        pltpu.make_async_remote_copy(
            src_ref=recv.at[src_dev], dst_ref=recv.at[src_dev], send_sem=send_sems.at[d],
            recv_sem=recv_sems.at[src_dev], device_id=member(src_dev),
            device_id_type=pl.DeviceIdType.MESH).wait_recv()
    for copy in copies:
        copy.wait_send()
    total = recv[0]
    for k in range(1, size):
        total = total + recv[k]
    return total


def reduce_radix(w_ref, o_ref, seg_recv, z_recv, x_recv, sems):
    _, z_group, x_group = radix_groups()
    me, size, member = first_group()
    seg = w_ref.shape[0] // size
    mine = pl.ds(pl.multiple_of(me * seg, 8), seg)
    copies = []
    for d in range(1, size):
        peer = lax.rem(me + d, size)
        copy = pltpu.make_async_remote_copy(
            src_ref=w_ref.at[pl.ds(pl.multiple_of(peer * seg, 8), seg)], dst_ref=seg_recv.at[me],
            send_sem=sems.at[0, d], recv_sem=sems.at[1, me], device_id=member(peer),
            device_id_type=pl.DeviceIdType.MESH)
        copy.start()
        copies.append(copy)
    total = w_ref[mine]
    for d in range(1, size):
        src_dev = lax.rem(me + size - d, size)
        pltpu.make_async_remote_copy(
            src_ref=seg_recv.at[src_dev], dst_ref=seg_recv.at[src_dev], send_sem=sems.at[0, d],
            recv_sem=sems.at[1, src_dev], device_id=member(src_dev),
            device_id_type=pl.DeviceIdType.MESH).wait_recv()
        total = total + seg_recv[src_dev]
    for copy in copies:
        copy.wait_send()
    total = ordered_allreduce(z_group, total, z_recv, sems.at[2], sems.at[3])
    total = ordered_allreduce(x_group, total, x_recv, sems.at[4], sems.at[5])
    o_ref[mine] = total
    copies = []
    for d in range(1, size):
        peer = lax.rem(me + d, size)
        copy = pltpu.make_async_remote_copy(
            src_ref=o_ref.at[mine], dst_ref=o_ref.at[mine], send_sem=sems.at[6, d],
            recv_sem=sems.at[7, me], device_id=member(peer), device_id_type=pl.DeviceIdType.MESH)
        copy.start()
        copies.append(copy)
    for d in range(1, size):
        src_dev = lax.rem(me + size - d, size)
        rows = pl.ds(pl.multiple_of(src_dev * seg, 8), seg)
        pltpu.make_async_remote_copy(
            src_ref=o_ref.at[rows], dst_ref=o_ref.at[rows], send_sem=sems.at[6, d],
            recv_sem=sems.at[7, src_dev], device_id=member(src_dev),
            device_id_type=pl.DeviceIdType.MESH).wait_recv()
    for copy in copies:
        copy.wait_send()


def radix_scratch(w):
    (core, ring), z_group, x_group = radix_groups()
    size = core[2] * ring[2]
    seg = (w.shape[0] // size,) + w.shape[1:]
    width = max(size, z_group[2], x_group[2])
    return [
        pltpu.VMEM((size,) + seg, w.dtype),
        pltpu.VMEM((z_group[2],) + seg, w.dtype),
        pltpu.VMEM((x_group[2],) + seg, w.dtype),
        pltpu.SemaphoreType.DMA((8, width)),
    ]


def radix_fits(w):
    groups = radix_groups()
    if groups is None:
        return False
    size = groups[0][0][2] * groups[0][1][2]
    return w.shape[0] % (8 * size) == 0


def gather_radix_kernel(axis, x_ref, w_ref, o_ref, ow_ref, g_send, g_recv, *scratch):
    size = lax.axis_size(axis)
    enter(exchange_targets(axis, 1, size) + reduce_radix_targets())
    copies = exchange_start(axis, 1, size, "gather", x_ref, o_ref, g_send, g_recv)
    reduce_radix(w_ref, ow_ref, *scratch)
    exchange_finish(axis, 1, size, "gather", x_ref, o_ref, o_ref, g_send, g_recv, copies)


def gather_reduce_kernel(axis, x_ref, w_ref, o_ref, ow_ref, g_send, g_recv, recv, send_sems, recv_sems):
    size = lax.axis_size(axis)
    enter(exchange_targets(axis, 1, size) + reduce_targets(w_ref.shape[0]))
    copies = exchange_start(axis, 1, size, "gather", x_ref, o_ref, g_send, g_recv)
    reduce_rounds(w_ref, ow_ref, recv, send_sems, recv_sems)
    exchange_finish(axis, 1, size, "gather", x_ref, o_ref, o_ref, g_send, g_recv, copies)


def gather_and_reduce(x, w, axis, collective_id):
    size = lax.axis_size(axis)
    if radix_fits(w):
        kernel, scratch = gather_radix_kernel, radix_scratch(w)
    else:
        kernel, scratch = gather_reduce_kernel, reduce_scratch(w)
    return pl.pallas_call(
        functools.partial(kernel, axis),
        out_shape=(exchange_shape(x, "gather", size), jax.ShapeDtypeStruct(w.shape, w.dtype)),
        in_specs=[pl.BlockSpec(memory_space=pltpu.VMEM)] * 2,
        out_specs=(pl.BlockSpec(memory_space=pltpu.VMEM),) * 2,
        scratch_shapes=exchange_scratch(x, "gather", size) + scratch,
        compiler_params=pltpu.CompilerParams(collective_id=collective_id, has_side_effects=True),
    )(x, w)


def shards(features, tile_rows, tile_cols, tile_count, tile_values, weights, cotangent):
    width = tile_values.shape[-1]
    local_tiles = tile_values[0, 0]
    block_rows = tile_rows[0, 0]
    block_cols = tile_cols[0, 0]
    count = tile_count[0, 0].reshape(1)
    n_rowdev = lax.axis_size("row")
    n_coldev = lax.axis_size("col")
    local_blocks = features.shape[0] // width
    feat_half = features.shape[1]
    feat_index = lax.axis_index("feat")
    row_blocks = local_blocks * n_coldev
    col_blocks = local_blocks * n_rowdev
    node_total = features.shape[0] * n_rowdev * n_coldev
    pair = 2 if n_rowdev % 2 == 0 else 1
    chips = n_rowdev // pair
    if pair == 2:
        panel = row_gather(features, chips, 0).reshape(-1, feat_half)
    else:
        panel = exchange(features, "row", "gather", 0).reshape(-1, feat_half)
    owner = block_cols // local_blocks
    block_cols = ((owner % pair) * chips + owner // pair) * local_blocks + block_cols % local_blocks
    partial_value = tile_products(local_tiles, block_rows, block_cols, count, panel,
                                  row_blocks, transpose=False)
    weight_cols = lax.dynamic_slice_in_dim(weights, feat_index * feat_half, feat_half, 1)
    weight_rows = lax.dynamic_slice_in_dim(weights, feat_index * feat_half, feat_half, 0)
    hidden, spread_panel, weight_sum = layer_step(partial_value.reshape(n_coldev, -1, feat_half),
                                                  weight_cols, weight_rows, cotangent, 1)
    negative = jnp.minimum(hidden, 0.0)
    activated = jnp.where(hidden > 0, hidden, jnp.expm1(negative)).astype(jnp.bfloat16)
    spread_panel = spread_panel.reshape(-1, feat_half)
    weight_grad = weight_sum * node_total ** (-0.5)
    back_partial = tile_products(local_tiles, block_rows, block_cols, count, spread_panel,
                                 col_blocks, transpose=True)
    if pair == 2:
        back_summed = row_scatter(back_partial.reshape(pair, chips, -1, feat_half), chips, 3)
    else:
        back_summed = exchange(back_partial.reshape(n_rowdev, -1, feat_half), "row", "scatter", 3)
    return (activated, back_summed, weight_grad)


def solution(mesh):
    return jax.shard_map(
        shards,
        mesh=mesh,
        in_specs=(
            P(("col", "row"), "feat"),
            P("row", "col", None),
            P("row", "col", None),
            P("row", "col"),
            P("row", "col", None, None, None),
            P(),
            P(("row", "col"), "feat"),
        ),
        out_specs=(P(("row", "col"), "feat"), P(("col", "row"), "feat"), P("feat", None)),
        check_vma=False,
    )
```

```python
import functools

import jax
import jax.numpy as jnp
from jax import lax
from jax.experimental import pallas as pl
from jax.experimental.pallas import tpu as pltpu
from jax.sharding import PartitionSpec as P

GROUP = 128


def tile_kernel(transpose, rows_ref, cols_ref, count_ref, tiles_ref, panel_ref, out_ref, acc_ref):
    step = pl.program_id(0)
    width = tiles_ref.shape[-1]
    count = count_ref[0]
    src_blocks = panel_ref.shape[0] // width
    dst_blocks = acc_ref.shape[0] // width

    @pl.when(step == 0)
    def _():
        acc_ref[...] = jnp.zeros_like(acc_ref)

    @pl.when(step * GROUP < count)
    def _():
        terms = []
        for j in range(GROUP):
            slot = step * GROUP + j
            src = rows_ref[slot] if transpose else cols_ref[slot]
            src = jnp.minimum(jnp.maximum(src, 0), src_blocks - 1)
            block = panel_ref[pl.ds(pl.multiple_of(src * width, width), width), :]
            tile = tiles_ref[j]
            if transpose:
                term = lax.dot_general(tile, block, (((0,), (0,)), ((), ())),
                                       preferred_element_type=jnp.float32)
            else:
                term = jnp.dot(tile, block, preferred_element_type=jnp.float32)
            terms.append(jnp.where(slot < count, term, 0.0))
        for j in range(GROUP):
            slot = step * GROUP + j
            dst = cols_ref[slot] if transpose else rows_ref[slot]
            dst = jnp.minimum(jnp.maximum(dst, 0), dst_blocks - 1)
            rows = pl.ds(pl.multiple_of(dst * width, width), width)
            acc_ref[rows, :] += terms[j]

    @pl.when(step == pl.num_programs(0) - 1)
    def _():
        out_ref[...] = acc_ref[...].astype(out_ref.dtype)


def tile_products(tiles, rows, cols, count, panel, out_blocks, transpose):
    slots, width, _ = tiles.shape
    feat = panel.shape[1]
    steps = slots // GROUP

    def tiles_map(i, rows_ref, cols_ref, count_ref):
        last = jnp.maximum(count_ref[0] - 1, 0) // GROUP
        return (jnp.minimum(i, last), 0, 0)

    return pl.pallas_call(
        functools.partial(tile_kernel, transpose),
        out_shape=jax.ShapeDtypeStruct((out_blocks * width, feat), jnp.bfloat16),
        grid_spec=pltpu.PrefetchScalarGridSpec(
            num_scalar_prefetch=3,
            grid=(steps,),
            in_specs=[
                pl.BlockSpec((GROUP, width, width), tiles_map),
                pl.BlockSpec(panel.shape, lambda i, *_: (0, 0)),
            ],
            out_specs=pl.BlockSpec((out_blocks * width, feat), lambda i, *_: (0, 0)),
            scratch_shapes=[pltpu.VMEM((out_blocks * width, feat), jnp.float32)],
        ),
        compiler_params=pltpu.CompilerParams(dimension_semantics=("arbitrary",)),
        cost_estimate=pl.CostEstimate(
            flops=2 * slots * width * width * feat,
            bytes_accessed=tiles.size * 2 + panel.size * 2 + out_blocks * width * feat * 2,
            transcendentals=0,
        ),
    )(rows, cols, count, tiles, panel)


def mesh_coords(axis, peer):
    return tuple(peer if name == axis else lax.axis_index(name) for name in ("row", "col", "feat"))


def group_of(axis, stride, size):
    index = lax.axis_index(axis)
    me = (index // stride) % size
    base = index - me * stride
    return me, lambda k: mesh_coords(axis, base + k * stride)


def exchange_targets(axis, stride, size):
    me, member = group_of(axis, stride, size)
    return [member(lax.rem(me + d, size)) for d in range(1, size)]


def enter(targets):
    barrier = pltpu.get_barrier_semaphore()
    for target in targets:
        pl.semaphore_signal(barrier, inc=1, device_id=target, device_id_type=pl.DeviceIdType.MESH)
    pl.semaphore_wait(barrier, len(targets))


def exchange_start(axis, stride, size, mode, x_ref, recv_ref, send_sems, recv_sems):
    me, member = group_of(axis, stride, size)
    copies = []
    for d in range(1, size):
        peer = lax.rem(me + d, size)
        src = x_ref if mode == "gather" else x_ref.at[peer]
        copy = pltpu.make_async_remote_copy(
            src_ref=src, dst_ref=recv_ref.at[me], send_sem=send_sems.at[d],
            recv_sem=recv_sems.at[me], device_id=member(peer),
            device_id_type=pl.DeviceIdType.MESH)
        copy.start()
        copies.append(copy)
    return copies


def exchange_finish(axis, stride, size, mode, x_ref, o_ref, recv_ref, send_sems, recv_sems, copies):
    me, member = group_of(axis, stride, size)
    if mode == "gather":
        o_ref[me] = x_ref[...]
    else:
        total = x_ref[me].astype(jnp.float32)
    for d in range(1, size):
        src_dev = lax.rem(me + size - d, size)
        incoming = pltpu.make_async_remote_copy(
            src_ref=recv_ref.at[src_dev], dst_ref=recv_ref.at[src_dev], send_sem=send_sems.at[d],
            recv_sem=recv_sems.at[src_dev], device_id=member(src_dev),
            device_id_type=pl.DeviceIdType.MESH)
        incoming.wait_recv()
        if mode != "gather":
            total = total + recv_ref[src_dev].astype(jnp.float32)
    for copy in copies:
        copy.wait_send()
    if mode != "gather":
        o_ref[...] = total.astype(o_ref.dtype)


def exchange_kernel(axis, stride, size, mode, x_ref, o_ref, *scratch):
    if mode == "gather":
        recv_ref, (send_sems, recv_sems) = o_ref, scratch
    else:
        recv_ref, send_sems, recv_sems = scratch
    enter(exchange_targets(axis, stride, size))
    copies = exchange_start(axis, stride, size, mode, x_ref, recv_ref, send_sems, recv_sems)
    exchange_finish(axis, stride, size, mode, x_ref, o_ref, recv_ref, send_sems, recv_sems, copies)


def exchange_scratch(x, mode, size):
    scratch = [] if mode == "gather" else [pltpu.VMEM(x.shape, x.dtype)]
    return scratch + [pltpu.SemaphoreType.DMA((size,)), pltpu.SemaphoreType.DMA((size,))]


def exchange_shape(x, mode, size):
    shape = (size,) + x.shape if mode == "gather" else x.shape[1:]
    return jax.ShapeDtypeStruct(shape, x.dtype)


def exchange(x, axis, mode, collective_id, stride=1, size=None):
    size = lax.axis_size(axis) if size is None else size
    return pl.pallas_call(
        functools.partial(exchange_kernel, axis, stride, size, mode),
        out_shape=exchange_shape(x, mode, size),
        in_specs=[pl.BlockSpec(memory_space=pltpu.VMEM)],
        out_specs=pl.BlockSpec(memory_space=pltpu.VMEM),
        scratch_shapes=exchange_scratch(x, mode, size),
        compiler_params=pltpu.CompilerParams(collective_id=collective_id, has_side_effects=True),
    )(x)


def pair_targets(chips):
    me, member = group_of("row", 2, chips)
    _, sibling = group_of("row", 1, 2)
    return [member(lax.rem(me + d, chips)) for d in range(1, chips)], sibling


def row_gather_kernel(chips, x_ref, o_ref, send_sems, recv_sems, fwd_send, fwd_recv):
    z_me, z_member = group_of("row", 2, chips)
    c_me, core_member = group_of("row", 1, 2)
    sibling = core_member(1 - c_me)
    peers, _ = pair_targets(chips)
    enter(peers + [sibling])
    copies = []
    for d in range(1, chips):
        peer = lax.rem(z_me + d, chips)
        copy = pltpu.make_async_remote_copy(
            src_ref=x_ref, dst_ref=o_ref.at[c_me, z_me], send_sem=send_sems.at[d],
            recv_sem=recv_sems.at[z_me], device_id=z_member(peer),
            device_id_type=pl.DeviceIdType.MESH)
        copy.start()
        copies.append(copy)
    own = pltpu.make_async_remote_copy(
        src_ref=x_ref, dst_ref=o_ref.at[c_me, z_me], send_sem=fwd_send.at[z_me],
        recv_sem=fwd_recv.at[z_me], device_id=sibling, device_id_type=pl.DeviceIdType.MESH)
    own.start()
    copies.append(own)
    o_ref[c_me, z_me] = x_ref[...]
    for d in range(1, chips):
        src_dev = lax.rem(z_me + chips - d, chips)
        incoming = pltpu.make_async_remote_copy(
            src_ref=o_ref.at[c_me, src_dev], dst_ref=o_ref.at[c_me, src_dev],
            send_sem=send_sems.at[d], recv_sem=recv_sems.at[src_dev],
            device_id=z_member(src_dev), device_id_type=pl.DeviceIdType.MESH)
        incoming.wait_recv()
        forward = pltpu.make_async_remote_copy(
            src_ref=o_ref.at[c_me, src_dev], dst_ref=o_ref.at[c_me, src_dev],
            send_sem=fwd_send.at[src_dev], recv_sem=fwd_recv.at[src_dev], device_id=sibling,
            device_id_type=pl.DeviceIdType.MESH)
        forward.start()
        copies.append(forward)
    for k in range(chips):
        incoming = pltpu.make_async_remote_copy(
            src_ref=o_ref.at[1 - c_me, k], dst_ref=o_ref.at[1 - c_me, k],
            send_sem=fwd_send.at[k], recv_sem=fwd_recv.at[k], device_id=sibling,
            device_id_type=pl.DeviceIdType.MESH)
        incoming.wait_recv()
    for copy in copies:
        copy.wait_send()


def row_gather(x, chips, collective_id):
    return pl.pallas_call(
        functools.partial(row_gather_kernel, chips),
        out_shape=jax.ShapeDtypeStruct((2, chips) + x.shape, x.dtype),
        in_specs=[pl.BlockSpec(memory_space=pltpu.VMEM)],
        out_specs=pl.BlockSpec(memory_space=pltpu.VMEM),
        scratch_shapes=[pltpu.SemaphoreType.DMA((chips,))] * 4,
        compiler_params=pltpu.CompilerParams(collective_id=collective_id, has_side_effects=True),
    )(x)


def row_scatter_kernel(chips, x_ref, o_ref, pair_recv, pair_sum, z_recv,
                       pair_send_sems, pair_recv_sems, z_send_sems, z_recv_sems):
    z_me, z_member = group_of("row", 2, chips)
    c_me, core_member = group_of("row", 1, 2)
    sibling = core_member(1 - c_me)
    peers, _ = pair_targets(chips)
    enter(peers + [sibling])
    copies = []
    for k in range(chips):
        copy = pltpu.make_async_remote_copy(
            src_ref=x_ref.at[1 - c_me, k], dst_ref=pair_recv.at[k], send_sem=pair_send_sems.at[k],
            recv_sem=pair_recv_sems.at[k], device_id=sibling, device_id_type=pl.DeviceIdType.MESH)
        copy.start()
        copies.append(copy)
    order = [lax.rem(z_me + d, chips) for d in range(1, chips)] + [z_me]
    for d, k in enumerate(order, start=1):
        incoming = pltpu.make_async_remote_copy(
            src_ref=pair_recv.at[k], dst_ref=pair_recv.at[k], send_sem=pair_send_sems.at[k],
            recv_sem=pair_recv_sems.at[k], device_id=sibling, device_id_type=pl.DeviceIdType.MESH)
        incoming.wait_recv()
        pair_sum[k] = (x_ref[c_me, k].astype(jnp.float32)
                       + pair_recv[k].astype(jnp.float32)).astype(pair_sum.dtype)
        if d < chips:
            copy = pltpu.make_async_remote_copy(
                src_ref=pair_sum.at[k], dst_ref=z_recv.at[z_me], send_sem=z_send_sems.at[d],
                recv_sem=z_recv_sems.at[z_me], device_id=z_member(k),
                device_id_type=pl.DeviceIdType.MESH)
            copy.start()
            copies.append(copy)
    total = pair_sum[z_me].astype(jnp.float32)
    for d in range(1, chips):
        src_dev = lax.rem(z_me + chips - d, chips)
        incoming = pltpu.make_async_remote_copy(
            src_ref=z_recv.at[src_dev], dst_ref=z_recv.at[src_dev], send_sem=z_send_sems.at[d],
            recv_sem=z_recv_sems.at[src_dev], device_id=z_member(src_dev),
            device_id_type=pl.DeviceIdType.MESH)
        incoming.wait_recv()
        total = total + z_recv[src_dev].astype(jnp.float32)
    for copy in copies:
        copy.wait_send()
    o_ref[...] = total.astype(o_ref.dtype)


def row_scatter(x, chips, collective_id):
    block = x.shape[2:]
    return pl.pallas_call(
        functools.partial(row_scatter_kernel, chips),
        out_shape=jax.ShapeDtypeStruct(block, x.dtype),
        in_specs=[pl.BlockSpec(memory_space=pltpu.VMEM)],
        out_specs=pl.BlockSpec(memory_space=pltpu.VMEM),
        scratch_shapes=[pltpu.VMEM((chips,) + block, x.dtype)] * 3
        + [pltpu.SemaphoreType.DMA((chips,))] * 4,
        compiler_params=pltpu.CompilerParams(collective_id=collective_id, has_side_effects=True),
    )(x)


def feat_push(value_ref, halves_ref, send_sems, recv_sems, slot):
    n = lax.axis_size("feat")
    me = lax.axis_index("feat")
    halves_ref[me] = value_ref[...]
    copies = []
    for d in range(1, n):
        peer = lax.rem(me + d, n)
        copy = pltpu.make_async_remote_copy(
            src_ref=halves_ref.at[me], dst_ref=halves_ref.at[me], send_sem=send_sems.at[slot, d],
            recv_sem=recv_sems.at[slot, me], device_id=mesh_coords("feat", peer),
            device_id_type=pl.DeviceIdType.MESH)
        copy.start()
        copies.append(copy)
    for d in range(1, n):
        src_dev = lax.rem(me + n - d, n)
        pltpu.make_async_remote_copy(
            src_ref=halves_ref.at[src_dev], dst_ref=halves_ref.at[src_dev],
            send_sem=send_sems.at[slot, d], recv_sem=recv_sems.at[slot, src_dev],
            device_id=mesh_coords("feat", src_dev), device_id_type=pl.DeviceIdType.MESH).wait_recv()
    for copy in copies:
        copy.wait_send()


def layer_kernel(x_ref, w_ref, wr_ref, cot_ref, hidden_ref, panel_ref, sum_ref,
                 recv_ref, send_sems, recv_sems, summed_ref, agg_ref, grad_out_ref, grad_ref,
                 f_send, f_recv, term_ref, spread_ref, g_send, g_recv, *reduce_scratch):
    n_col = lax.axis_size("col")
    n_feat = lax.axis_size("feat")
    me = lax.axis_index("feat")
    peers = [mesh_coords("feat", lax.rem(me + d, n_feat)) for d in range(1, n_feat)]
    radix = len(reduce_scratch) == 4
    others = reduce_radix_targets() if radix else reduce_targets(term_ref.shape[0])
    enter(exchange_targets("col", 1, n_col) + peers + exchange_targets("col", 1, n_col) + others)
    copies = exchange_start("col", 1, n_col, "scatter", x_ref, recv_ref, send_sems, recv_sems)
    exchange_finish("col", 1, n_col, "scatter", x_ref, summed_ref, recv_ref, send_sems, recv_sems,
                    copies)
    feat_push(summed_ref, agg_ref, f_send, f_recv, 0)
    half = agg_ref.shape[-1]
    hidden = jnp.dot(agg_ref[0], w_ref[pl.ds(0, half), :], preferred_element_type=jnp.float32)
    for h in range(1, n_feat):
        hidden = hidden + jnp.dot(agg_ref[h], w_ref[pl.ds(h * half, half), :],
                                  preferred_element_type=jnp.float32)
    hidden_ref[...] = hidden
    slope = jnp.where(hidden > 0, 1.0, jnp.exp(jnp.minimum(hidden, 0.0)))
    grad_out_ref[...] = (cot_ref[...].astype(jnp.float32) * slope).astype(grad_out_ref.dtype)
    feat_push(grad_out_ref, grad_ref, f_send, f_recv, 1)
    spread = None
    for h in range(n_feat):
        columns = pl.ds(h * half, half)
        term_ref[:, columns] = lax.dot_general(
            summed_ref[...], grad_ref[h], (((0,), (0,)), ((), ())),
            preferred_element_type=jnp.float32)
        part = lax.dot_general(grad_ref[h], wr_ref[:, columns], (((1,), (1,)), ((), ())),
                               preferred_element_type=jnp.float32)
        spread = part if spread is None else spread + part
    spread_ref[...] = spread.astype(spread_ref.dtype)
    copies = exchange_start("col", 1, n_col, "gather", spread_ref, panel_ref, g_send, g_recv)
    if radix:
        reduce_radix(term_ref, sum_ref, *reduce_scratch)
    else:
        reduce_rounds(term_ref, sum_ref, *reduce_scratch)
    exchange_finish("col", 1, n_col, "gather", spread_ref, panel_ref, panel_ref, g_send, g_recv,
                    copies)


def layer_step(partials, weight_cols, weight_rows, cotangent, collective_id):
    n_col = lax.axis_size("col")
    n_feat = lax.axis_size("feat")
    block = partials.shape[1:]
    half = block[-1]
    term = jax.ShapeDtypeStruct((half, n_feat * half), jnp.float32)
    reduce_space = radix_scratch(term) if radix_fits(term) else reduce_scratch(term)
    vmem = pl.BlockSpec(memory_space=pltpu.VMEM)
    return pl.pallas_call(
        layer_kernel,
        out_shape=(
            jax.ShapeDtypeStruct(block, jnp.float32),
            jax.ShapeDtypeStruct((n_col,) + block, jnp.bfloat16),
            term,
        ),
        in_specs=[vmem] * 4,
        out_specs=(vmem,) * 3,
        scratch_shapes=exchange_scratch(partials, "scatter", n_col) + [
            pltpu.VMEM(block, partials.dtype),
            pltpu.VMEM((n_feat,) + block, partials.dtype),
            pltpu.VMEM(block, jnp.bfloat16),
            pltpu.VMEM((n_feat,) + block, jnp.bfloat16),
            pltpu.SemaphoreType.DMA((2, n_feat)),
            pltpu.SemaphoreType.DMA((2, n_feat)),
            pltpu.VMEM(term.shape, term.dtype),
            pltpu.VMEM(block, jnp.bfloat16),
            pltpu.SemaphoreType.DMA((n_col,)),
            pltpu.SemaphoreType.DMA((n_col,)),
        ] + reduce_space,
        compiler_params=pltpu.CompilerParams(collective_id=collective_id, has_side_effects=True),
    )(partials, weight_cols, weight_rows, cotangent)


def reduction_plan(rows):
    pairs = []
    for bit in (1, 2, 4, 8, 16, 32, 64):
        for axis in ("row", "col"):
            if bit < lax.axis_size(axis):
                pairs.append((axis, bit))
    halving = []
    while pairs and rows // 2 >= 8 and rows % 16 == 0:
        halving.append(pairs.pop(0))
        rows //= 2
    return halving, pairs


def bitval(axis, bit):
    return (lax.axis_index(axis) // bit) % 2


def partner(axis, bit):
    return mesh_coords(axis, lax.axis_index(axis) + bit * (1 - 2 * bitval(axis, bit)))


def reduce_targets(rows):
    halving, whole = reduction_plan(rows)
    return [partner(axis, bit) for axis, bit in halving + whole]


def reduce_rounds(x_ref, o_ref, recv, send_sems, recv_sems):
    halving, whole = reduction_plan(x_ref.shape[0])
    o_ref[...] = x_ref[...]
    k = 0

    def swap(k, axis, bit, send_rows, length):
        copy = pltpu.make_async_remote_copy(
            src_ref=o_ref.at[pl.ds(send_rows, length)], dst_ref=recv.at[k, pl.ds(0, length)],
            send_sem=send_sems.at[k], recv_sem=recv_sems.at[k],
            device_id=partner(axis, bit), device_id_type=pl.DeviceIdType.MESH)
        copy.start()
        copy.wait()

    lo = jnp.int32(0)
    length = x_ref.shape[0]
    starts = []
    for axis, bit in halving:
        length //= 2
        mine = bitval(axis, bit)
        starts.append(lo)
        keep = pl.multiple_of(lo + mine * length, 8)
        give = pl.multiple_of(lo + (1 - mine) * length, 8)
        swap(k, axis, bit, give, length)
        o_ref[pl.ds(keep, length)] = o_ref[pl.ds(keep, length)] + recv[k, pl.ds(0, length)]
        lo = keep
        k += 1
    for axis, bit in whole:
        swap(k, axis, bit, lo, length)
        o_ref[pl.ds(lo, length)] = o_ref[pl.ds(lo, length)] + recv[k, pl.ds(0, length)]
        k += 1
    for (axis, bit), base in zip(reversed(halving), reversed(starts)):
        mine = bitval(axis, bit)
        other = pl.multiple_of(base + (1 - mine) * length, 8)
        swap(k, axis, bit, lo, length)
        o_ref[pl.ds(other, length)] = recv[k, pl.ds(0, length)]
        lo = base
        length *= 2
        k += 1


def reduce_scratch(w):
    halving, whole = reduction_plan(w.shape[0])
    steps = 2 * len(halving) + len(whole)
    return [
        pltpu.VMEM((steps, w.shape[0] // 2) + w.shape[1:], w.dtype),
        pltpu.SemaphoreType.DMA((steps,)),
        pltpu.SemaphoreType.DMA((steps,)),
    ]


def radix_groups():
    n_row, n_col = lax.axis_size("row"), lax.axis_size("col")
    if n_row % 2 or n_col % 4:
        return None
    return ((("row", 1, 2), ("col", 1, 4)), ("row", 2, n_row // 2), ("col", 4, n_col // 4))


def first_group():
    (core, ring), _, _ = radix_groups()
    me_a, _ = group_of(*core)
    me_b, _ = group_of(*ring)
    size = core[2] * ring[2]
    me = me_a + core[2] * me_b
    row = lax.axis_index("row") - me_a * core[1]
    col = lax.axis_index("col") - me_b * ring[1]

    def member(m):
        return (row + (m % core[2]) * core[1], col + (m // core[2]) * ring[1], lax.axis_index("feat"))

    return me, size, member


def reduce_radix_targets():
    me, size, member = first_group()
    targets = [member(lax.rem(me + d, size)) for d in range(1, size)]
    _, z_group, x_group = radix_groups()
    return targets + exchange_targets(*z_group) + exchange_targets(*x_group)


def ordered_allreduce(group, value, recv, send_sems, recv_sems):
    axis, stride, size = group
    me, member = group_of(axis, stride, size)
    recv[me] = value
    copies = []
    for d in range(1, size):
        peer = lax.rem(me + d, size)
        copy = pltpu.make_async_remote_copy(
            src_ref=recv.at[me], dst_ref=recv.at[me], send_sem=send_sems.at[d],
            recv_sem=recv_sems.at[me], device_id=member(peer), device_id_type=pl.DeviceIdType.MESH)
        copy.start()
        copies.append(copy)
    for d in range(1, size):
        src_dev = lax.rem(me + size - d, size)
        pltpu.make_async_remote_copy(
            src_ref=recv.at[src_dev], dst_ref=recv.at[src_dev], send_sem=send_sems.at[d],
            recv_sem=recv_sems.at[src_dev], device_id=member(src_dev),
            device_id_type=pl.DeviceIdType.MESH).wait_recv()
    for copy in copies:
        copy.wait_send()
    total = recv[0]
    for k in range(1, size):
        total = total + recv[k]
    return total


def reduce_radix(w_ref, o_ref, seg_recv, z_recv, x_recv, sems):
    _, z_group, x_group = radix_groups()
    me, size, member = first_group()
    seg = w_ref.shape[0] // size
    mine = pl.ds(pl.multiple_of(me * seg, 8), seg)
    copies = []
    for d in range(1, size):
        peer = lax.rem(me + d, size)
        copy = pltpu.make_async_remote_copy(
            src_ref=w_ref.at[pl.ds(pl.multiple_of(peer * seg, 8), seg)], dst_ref=seg_recv.at[me],
            send_sem=sems.at[0, d], recv_sem=sems.at[1, me], device_id=member(peer),
            device_id_type=pl.DeviceIdType.MESH)
        copy.start()
        copies.append(copy)
    total = w_ref[mine]
    for d in range(1, size):
        src_dev = lax.rem(me + size - d, size)
        pltpu.make_async_remote_copy(
            src_ref=seg_recv.at[src_dev], dst_ref=seg_recv.at[src_dev], send_sem=sems.at[0, d],
            recv_sem=sems.at[1, src_dev], device_id=member(src_dev),
            device_id_type=pl.DeviceIdType.MESH).wait_recv()
        total = total + seg_recv[src_dev]
    for copy in copies:
        copy.wait_send()
    total = ordered_allreduce(z_group, total, z_recv, sems.at[2], sems.at[3])
    total = ordered_allreduce(x_group, total, x_recv, sems.at[4], sems.at[5])
    o_ref[mine] = total
    copies = []
    for d in range(1, size):
        peer = lax.rem(me + d, size)
        copy = pltpu.make_async_remote_copy(
            src_ref=o_ref.at[mine], dst_ref=o_ref.at[mine], send_sem=sems.at[6, d],
            recv_sem=sems.at[7, me], device_id=member(peer), device_id_type=pl.DeviceIdType.MESH)
        copy.start()
        copies.append(copy)
    for d in range(1, size):
        src_dev = lax.rem(me + size - d, size)
        rows = pl.ds(pl.multiple_of(src_dev * seg, 8), seg)
        pltpu.make_async_remote_copy(
            src_ref=o_ref.at[rows], dst_ref=o_ref.at[rows], send_sem=sems.at[6, d],
            recv_sem=sems.at[7, src_dev], device_id=member(src_dev),
            device_id_type=pl.DeviceIdType.MESH).wait_recv()
    for copy in copies:
        copy.wait_send()


def radix_scratch(w):
    (core, ring), z_group, x_group = radix_groups()
    size = core[2] * ring[2]
    seg = (w.shape[0] // size,) + w.shape[1:]
    width = max(size, z_group[2], x_group[2])
    return [
        pltpu.VMEM((size,) + seg, w.dtype),
        pltpu.VMEM((z_group[2],) + seg, w.dtype),
        pltpu.VMEM((x_group[2],) + seg, w.dtype),
        pltpu.SemaphoreType.DMA((8, width)),
    ]


def radix_fits(w):
    groups = radix_groups()
    if groups is None:
        return False
    size = groups[0][0][2] * groups[0][1][2]
    return w.shape[0] % (8 * size) == 0


def gather_radix_kernel(axis, x_ref, w_ref, o_ref, ow_ref, g_send, g_recv, *scratch):
    size = lax.axis_size(axis)
    enter(exchange_targets(axis, 1, size) + reduce_radix_targets())
    copies = exchange_start(axis, 1, size, "gather", x_ref, o_ref, g_send, g_recv)
    reduce_radix(w_ref, ow_ref, *scratch)
    exchange_finish(axis, 1, size, "gather", x_ref, o_ref, o_ref, g_send, g_recv, copies)


def gather_reduce_kernel(axis, x_ref, w_ref, o_ref, ow_ref, g_send, g_recv, recv, send_sems, recv_sems):
    size = lax.axis_size(axis)
    enter(exchange_targets(axis, 1, size) + reduce_targets(w_ref.shape[0]))
    copies = exchange_start(axis, 1, size, "gather", x_ref, o_ref, g_send, g_recv)
    reduce_rounds(w_ref, ow_ref, recv, send_sems, recv_sems)
    exchange_finish(axis, 1, size, "gather", x_ref, o_ref, o_ref, g_send, g_recv, copies)


def gather_and_reduce(x, w, axis, collective_id):
    size = lax.axis_size(axis)
    if radix_fits(w):
        kernel, scratch = gather_radix_kernel, radix_scratch(w)
    else:
        kernel, scratch = gather_reduce_kernel, reduce_scratch(w)
    return pl.pallas_call(
        functools.partial(kernel, axis),
        out_shape=(exchange_shape(x, "gather", size), jax.ShapeDtypeStruct(w.shape, w.dtype)),
        in_specs=[pl.BlockSpec(memory_space=pltpu.VMEM)] * 2,
        out_specs=(pl.BlockSpec(memory_space=pltpu.VMEM),) * 2,
        scratch_shapes=exchange_scratch(x, "gather", size) + scratch,
        compiler_params=pltpu.CompilerParams(collective_id=collective_id, has_side_effects=True),
    )(x, w)


def shards(features, tile_rows, tile_cols, tile_count, tile_values, weights, cotangent):
    width = tile_values.shape[-1]
    local_tiles = tile_values[0, 0]
    block_rows = tile_rows[0, 0]
    block_cols = tile_cols[0, 0]
    count = tile_count[0, 0].reshape(1)
    n_rowdev = lax.axis_size("row")
    n_coldev = lax.axis_size("col")
    local_blocks = features.shape[0] // width
    feat_half = features.shape[1]
    feat_index = lax.axis_index("feat")
    row_blocks = local_blocks * n_coldev
    col_blocks = local_blocks * n_rowdev
    node_total = features.shape[0] * n_rowdev * n_coldev
    pair = 2 if n_rowdev % 2 == 0 else 1
    chips = n_rowdev // pair
    if pair == 2:
        panel = row_gather(features, chips, 0).reshape(-1, feat_half)
    else:
        panel = exchange(features, "row", "gather", 0).reshape(-1, feat_half)
    owner = block_cols // local_blocks
    block_cols = ((owner % pair) * chips + owner // pair) * local_blocks + block_cols % local_blocks
    partial_value = tile_products(local_tiles, block_rows, block_cols, count, panel,
                                  row_blocks, transpose=False)
    weight_cols = lax.dynamic_slice_in_dim(weights, feat_index * feat_half, feat_half, 1)
    weight_rows = lax.dynamic_slice_in_dim(weights, feat_index * feat_half, feat_half, 0)
    hidden, spread_panel, weight_sum = layer_step(partial_value.reshape(n_coldev, -1, feat_half),
                                                  weight_cols, weight_rows, cotangent, 1)
    negative = jnp.minimum(hidden, 0.0)
    activated = jnp.where(hidden > 0, hidden, jnp.expm1(negative)).astype(jnp.bfloat16)
    spread_panel = spread_panel.reshape(-1, feat_half)
    weight_grad = weight_sum * node_total ** (-0.5)
    back_partial = tile_products(local_tiles, block_rows, block_cols, count, spread_panel,
                                 col_blocks, transpose=True)
    if pair == 2:
        back_summed = row_scatter(back_partial.reshape(pair, chips, -1, feat_half), chips, 3)
    else:
        back_summed = exchange(back_partial.reshape(n_rowdev, -1, feat_half), "row", "scatter", 3)
    return (activated, back_summed, weight_grad)


def solution(mesh):
    return jax.shard_map(
        shards,
        mesh=mesh,
        in_specs=(
            P(("col", "row"), "feat"),
            P("row", "col", None),
            P("row", "col", None),
            P("row", "col"),
            P("row", "col", None, None, None),
            P(),
            P(("row", "col"), "feat"),
        ),
        out_specs=(P(("row", "col"), "feat"), P(("col", "row"), "feat"), P("feat", None)),
        check_vma=False,
    )
```

```python
import functools

import jax
import jax.numpy as jnp
from jax import lax
from jax.experimental import pallas as pl
from jax.experimental.pallas import tpu as pltpu
from jax.sharding import PartitionSpec as P

GROUP = 64


def tile_kernel(transpose, remap, rows_ref, cols_ref, count_ref, tiles_ref, panel_ref, out_ref, acc_ref):
    step = pl.program_id(0)
    width = tiles_ref.shape[-1]
    count = count_ref[0]
    src_blocks = panel_ref.shape[0] // width
    dst_blocks = acc_ref.shape[0] // width

    @pl.when(step == 0)
    def _():
        acc_ref[...] = jnp.zeros_like(acc_ref)

    @pl.when(step * GROUP < count)
    def _():
        terms = []
        for j in range(GROUP):
            slot = step * GROUP + j
            src = rows_ref[slot] if transpose else remap(cols_ref[slot])
            src = jnp.minimum(jnp.maximum(src, 0), src_blocks - 1)
            block = panel_ref[pl.ds(pl.multiple_of(src * width, width), width), :]
            tile = tiles_ref[j]
            if transpose:
                term = lax.dot_general(tile, block, (((0,), (0,)), ((), ())),
                                       preferred_element_type=jnp.float32)
            else:
                term = jnp.dot(tile, block, preferred_element_type=jnp.float32)
            terms.append(jnp.where(slot < count, term, 0.0))
        for j in range(GROUP):
            slot = step * GROUP + j
            dst = remap(cols_ref[slot]) if transpose else rows_ref[slot]
            dst = jnp.minimum(jnp.maximum(dst, 0), dst_blocks - 1)
            rows = pl.ds(pl.multiple_of(dst * width, width), width)
            acc_ref[rows, :] += terms[j]

    @pl.when(step == pl.num_programs(0) - 1)
    def _():
        out_ref[...] = acc_ref[...].astype(out_ref.dtype)


def tile_products(tiles, rows, cols, count, panel, out_blocks, transpose, remap):
    slots, width, _ = tiles.shape
    feat = panel.shape[1]
    steps = slots // GROUP

    def tiles_map(i, rows_ref, cols_ref, count_ref):
        last = jnp.maximum(count_ref[0] - 1, 0) // GROUP
        return (jnp.minimum(i, last), 0, 0)

    return pl.pallas_call(
        functools.partial(tile_kernel, transpose, remap),
        out_shape=jax.ShapeDtypeStruct((out_blocks * width, feat), jnp.bfloat16),
        grid_spec=pltpu.PrefetchScalarGridSpec(
            num_scalar_prefetch=3,
            grid=(steps,),
            in_specs=[
                pl.BlockSpec((GROUP, width, width), tiles_map),
                pl.BlockSpec(panel.shape, lambda i, *_: (0, 0)),
            ],
            out_specs=pl.BlockSpec((out_blocks * width, feat), lambda i, *_: (0, 0)),
            scratch_shapes=[pltpu.VMEM((out_blocks * width, feat), jnp.float32)],
        ),
        compiler_params=pltpu.CompilerParams(dimension_semantics=("arbitrary",)),
        cost_estimate=pl.CostEstimate(
            flops=2 * slots * width * width * feat,
            bytes_accessed=tiles.size * 2 + panel.size * 2 + out_blocks * width * feat * 2,
            transcendentals=0,
        ),
    )(rows, cols, count, tiles, panel)


def mesh_coords(axis, peer):
    return tuple(peer if name == axis else lax.axis_index(name) for name in ("row", "col", "feat"))


def group_of(axis, stride, size):
    index = lax.axis_index(axis)
    me = (index // stride) % size
    base = index - me * stride
    return me, lambda k: mesh_coords(axis, base + k * stride)


def exchange_targets(axis, stride, size):
    me, member = group_of(axis, stride, size)
    return [member(lax.rem(me + d, size)) for d in range(1, size)]


def enter(targets):
    barrier = pltpu.get_barrier_semaphore()
    for target in targets:
        pl.semaphore_signal(barrier, inc=1, device_id=target, device_id_type=pl.DeviceIdType.MESH)
    pl.semaphore_wait(barrier, len(targets))


def exchange_start(axis, stride, size, mode, x_ref, recv_ref, send_sems, recv_sems):
    me, member = group_of(axis, stride, size)
    copies = []
    for d in range(1, size):
        peer = lax.rem(me + d, size)
        src = x_ref if mode == "gather" else x_ref.at[peer]
        copy = pltpu.make_async_remote_copy(
            src_ref=src, dst_ref=recv_ref.at[me], send_sem=send_sems.at[d],
            recv_sem=recv_sems.at[me], device_id=member(peer),
            device_id_type=pl.DeviceIdType.MESH)
        copy.start()
        copies.append(copy)
    return copies


def exchange_finish(axis, stride, size, mode, x_ref, o_ref, recv_ref, send_sems, recv_sems, copies):
    me, member = group_of(axis, stride, size)
    if mode == "gather":
        o_ref[me] = x_ref[...]
    else:
        total = x_ref[me].astype(jnp.float32)
    for d in range(1, size):
        src_dev = lax.rem(me + size - d, size)
        incoming = pltpu.make_async_remote_copy(
            src_ref=recv_ref.at[src_dev], dst_ref=recv_ref.at[src_dev], send_sem=send_sems.at[d],
            recv_sem=recv_sems.at[src_dev], device_id=member(src_dev),
            device_id_type=pl.DeviceIdType.MESH)
        incoming.wait_recv()
        if mode != "gather":
            total = total + recv_ref[src_dev].astype(jnp.float32)
    for copy in copies:
        copy.wait_send()
    if mode != "gather":
        o_ref[...] = total.astype(o_ref.dtype)


def exchange_kernel(axis, stride, size, mode, x_ref, o_ref, *scratch):
    if mode == "gather":
        recv_ref, (send_sems, recv_sems) = o_ref, scratch
    else:
        recv_ref, send_sems, recv_sems = scratch
    enter(exchange_targets(axis, stride, size))
    copies = exchange_start(axis, stride, size, mode, x_ref, recv_ref, send_sems, recv_sems)
    exchange_finish(axis, stride, size, mode, x_ref, o_ref, recv_ref, send_sems, recv_sems, copies)


def exchange_scratch(x, mode, size):
    scratch = [] if mode == "gather" else [pltpu.VMEM(x.shape, x.dtype)]
    return scratch + [pltpu.SemaphoreType.DMA((size,)), pltpu.SemaphoreType.DMA((size,))]


def exchange_shape(x, mode, size):
    shape = (size,) + x.shape if mode == "gather" else x.shape[1:]
    return jax.ShapeDtypeStruct(shape, x.dtype)


def exchange(x, axis, mode, collective_id, stride=1, size=None):
    size = lax.axis_size(axis) if size is None else size
    return pl.pallas_call(
        functools.partial(exchange_kernel, axis, stride, size, mode),
        out_shape=exchange_shape(x, mode, size),
        in_specs=[pl.BlockSpec(memory_space=pltpu.VMEM)],
        out_specs=pl.BlockSpec(memory_space=pltpu.VMEM),
        scratch_shapes=exchange_scratch(x, mode, size),
        compiler_params=pltpu.CompilerParams(collective_id=collective_id, has_side_effects=True),
    )(x)


def pair_targets(chips):
    me, member = group_of("row", 2, chips)
    _, sibling = group_of("row", 1, 2)
    return [member(lax.rem(me + d, chips)) for d in range(1, chips)], sibling


def row_gather_kernel(chips, x_ref, o_ref, send_sems, recv_sems, fwd_send, fwd_recv):
    z_me, z_member = group_of("row", 2, chips)
    c_me, core_member = group_of("row", 1, 2)
    sibling = core_member(1 - c_me)
    peers, _ = pair_targets(chips)
    enter(peers + [sibling])
    copies = []
    for d in range(1, chips):
        peer = lax.rem(z_me + d, chips)
        copy = pltpu.make_async_remote_copy(
            src_ref=x_ref, dst_ref=o_ref.at[c_me, z_me], send_sem=send_sems.at[d],
            recv_sem=recv_sems.at[z_me], device_id=z_member(peer),
            device_id_type=pl.DeviceIdType.MESH)
        copy.start()
        copies.append(copy)
    own = pltpu.make_async_remote_copy(
        src_ref=x_ref, dst_ref=o_ref.at[c_me, z_me], send_sem=fwd_send.at[z_me],
        recv_sem=fwd_recv.at[z_me], device_id=sibling, device_id_type=pl.DeviceIdType.MESH)
    own.start()
    copies.append(own)
    o_ref[c_me, z_me] = x_ref[...]
    for d in range(1, chips):
        src_dev = lax.rem(z_me + chips - d, chips)
        incoming = pltpu.make_async_remote_copy(
            src_ref=o_ref.at[c_me, src_dev], dst_ref=o_ref.at[c_me, src_dev],
            send_sem=send_sems.at[d], recv_sem=recv_sems.at[src_dev],
            device_id=z_member(src_dev), device_id_type=pl.DeviceIdType.MESH)
        incoming.wait_recv()
        forward = pltpu.make_async_remote_copy(
            src_ref=o_ref.at[c_me, src_dev], dst_ref=o_ref.at[c_me, src_dev],
            send_sem=fwd_send.at[src_dev], recv_sem=fwd_recv.at[src_dev], device_id=sibling,
            device_id_type=pl.DeviceIdType.MESH)
        forward.start()
        copies.append(forward)
    for k in range(chips):
        incoming = pltpu.make_async_remote_copy(
            src_ref=o_ref.at[1 - c_me, k], dst_ref=o_ref.at[1 - c_me, k],
            send_sem=fwd_send.at[k], recv_sem=fwd_recv.at[k], device_id=sibling,
            device_id_type=pl.DeviceIdType.MESH)
        incoming.wait_recv()
    for copy in copies:
        copy.wait_send()


def row_gather(x, chips, collective_id):
    return pl.pallas_call(
        functools.partial(row_gather_kernel, chips),
        out_shape=jax.ShapeDtypeStruct((2, chips) + x.shape, x.dtype),
        in_specs=[pl.BlockSpec(memory_space=pltpu.VMEM)],
        out_specs=pl.BlockSpec(memory_space=pltpu.VMEM),
        scratch_shapes=[pltpu.SemaphoreType.DMA((chips,))] * 4,
        compiler_params=pltpu.CompilerParams(collective_id=collective_id, has_side_effects=True),
    )(x)


def row_scatter_kernel(chips, x_ref, o_ref, pair_recv, pair_sum, z_recv,
                       pair_send_sems, pair_recv_sems, z_send_sems, z_recv_sems):
    z_me, z_member = group_of("row", 2, chips)
    c_me, core_member = group_of("row", 1, 2)
    sibling = core_member(1 - c_me)
    peers, _ = pair_targets(chips)
    enter(peers + [sibling])
    copies = []
    for k in range(chips):
        copy = pltpu.make_async_remote_copy(
            src_ref=x_ref.at[1 - c_me, k], dst_ref=pair_recv.at[k], send_sem=pair_send_sems.at[k],
            recv_sem=pair_recv_sems.at[k], device_id=sibling, device_id_type=pl.DeviceIdType.MESH)
        copy.start()
        copies.append(copy)
    order = [lax.rem(z_me + d, chips) for d in range(1, chips)] + [z_me]
    for d, k in enumerate(order, start=1):
        incoming = pltpu.make_async_remote_copy(
            src_ref=pair_recv.at[k], dst_ref=pair_recv.at[k], send_sem=pair_send_sems.at[k],
            recv_sem=pair_recv_sems.at[k], device_id=sibling, device_id_type=pl.DeviceIdType.MESH)
        incoming.wait_recv()
        pair_sum[k] = (x_ref[c_me, k].astype(jnp.float32)
                       + pair_recv[k].astype(jnp.float32)).astype(pair_sum.dtype)
        if d < chips:
            copy = pltpu.make_async_remote_copy(
                src_ref=pair_sum.at[k], dst_ref=z_recv.at[z_me], send_sem=z_send_sems.at[d],
                recv_sem=z_recv_sems.at[z_me], device_id=z_member(k),
                device_id_type=pl.DeviceIdType.MESH)
            copy.start()
            copies.append(copy)
    total = pair_sum[z_me].astype(jnp.float32)
    for d in range(1, chips):
        src_dev = lax.rem(z_me + chips - d, chips)
        incoming = pltpu.make_async_remote_copy(
            src_ref=z_recv.at[src_dev], dst_ref=z_recv.at[src_dev], send_sem=z_send_sems.at[d],
            recv_sem=z_recv_sems.at[src_dev], device_id=z_member(src_dev),
            device_id_type=pl.DeviceIdType.MESH)
        incoming.wait_recv()
        total = total + z_recv[src_dev].astype(jnp.float32)
    for copy in copies:
        copy.wait_send()
    o_ref[...] = total.astype(o_ref.dtype)


def row_scatter(x, chips, collective_id):
    block = x.shape[2:]
    return pl.pallas_call(
        functools.partial(row_scatter_kernel, chips),
        out_shape=jax.ShapeDtypeStruct(block, x.dtype),
        in_specs=[pl.BlockSpec(memory_space=pltpu.VMEM)],
        out_specs=pl.BlockSpec(memory_space=pltpu.VMEM),
        scratch_shapes=[pltpu.VMEM((chips,) + block, x.dtype)] * 3
        + [pltpu.SemaphoreType.DMA((chips,))] * 4,
        compiler_params=pltpu.CompilerParams(collective_id=collective_id, has_side_effects=True),
    )(x)


def feat_push(value_ref, halves_ref, send_sems, recv_sems, slot):
    n = lax.axis_size("feat")
    me = lax.axis_index("feat")
    halves_ref[me] = value_ref[...]
    copies = []
    for d in range(1, n):
        peer = lax.rem(me + d, n)
        copy = pltpu.make_async_remote_copy(
            src_ref=halves_ref.at[me], dst_ref=halves_ref.at[me], send_sem=send_sems.at[slot, d],
            recv_sem=recv_sems.at[slot, me], device_id=mesh_coords("feat", peer),
            device_id_type=pl.DeviceIdType.MESH)
        copy.start()
        copies.append(copy)
    for d in range(1, n):
        src_dev = lax.rem(me + n - d, n)
        pltpu.make_async_remote_copy(
            src_ref=halves_ref.at[src_dev], dst_ref=halves_ref.at[src_dev],
            send_sem=send_sems.at[slot, d], recv_sem=recv_sems.at[slot, src_dev],
            device_id=mesh_coords("feat", src_dev), device_id_type=pl.DeviceIdType.MESH).wait_recv()
    for copy in copies:
        copy.wait_send()


def layer_kernel(x_ref, w_ref, wr_ref, cot_ref, hidden_ref, panel_ref, sum_ref,
                 recv_ref, send_sems, recv_sems, summed_ref, agg_ref, grad_out_ref, grad_ref,
                 f_send, f_recv, term_ref, spread_ref, g_send, g_recv, *reduce_scratch):
    n_col = lax.axis_size("col")
    n_feat = lax.axis_size("feat")
    me = lax.axis_index("feat")
    peers = [mesh_coords("feat", lax.rem(me + d, n_feat)) for d in range(1, n_feat)]
    radix = len(reduce_scratch) == 4
    others = reduce_radix_targets() if radix else reduce_targets(term_ref.shape[0])
    enter(exchange_targets("col", 1, n_col) + peers + exchange_targets("col", 1, n_col) + others)
    copies = exchange_start("col", 1, n_col, "scatter", x_ref, recv_ref, send_sems, recv_sems)
    exchange_finish("col", 1, n_col, "scatter", x_ref, summed_ref, recv_ref, send_sems, recv_sems,
                    copies)
    feat_push(summed_ref, agg_ref, f_send, f_recv, 0)
    half = agg_ref.shape[-1]
    hidden = jnp.dot(agg_ref[0], w_ref[pl.ds(0, half), :], preferred_element_type=jnp.float32)
    for h in range(1, n_feat):
        hidden = hidden + jnp.dot(agg_ref[h], w_ref[pl.ds(h * half, half), :],
                                  preferred_element_type=jnp.float32)
    negative = jnp.minimum(hidden, 0.0)
    below = jnp.tanh(negative * 0.5) * (jnp.exp(negative) + 1.0)
    hidden_ref[...] = jnp.where(hidden > 0, hidden, below).astype(hidden_ref.dtype)
    slope = jnp.where(hidden > 0, 1.0, jnp.exp(jnp.minimum(hidden, 0.0)))
    grad_out_ref[...] = (cot_ref[...].astype(jnp.float32) * slope).astype(grad_out_ref.dtype)
    feat_push(grad_out_ref, grad_ref, f_send, f_recv, 1)
    spread = None
    for h in range(n_feat):
        columns = pl.ds(h * half, half)
        term_ref[:, columns] = lax.dot_general(
            summed_ref[...], grad_ref[h], (((0,), (0,)), ((), ())),
            preferred_element_type=jnp.float32)
        part = lax.dot_general(grad_ref[h], wr_ref[:, columns], (((1,), (1,)), ((), ())),
                               preferred_element_type=jnp.float32)
        spread = part if spread is None else spread + part
    spread_ref[...] = spread.astype(spread_ref.dtype)
    copies = exchange_start("col", 1, n_col, "gather", spread_ref, panel_ref, g_send, g_recv)
    if radix:
        reduce_radix(term_ref, sum_ref, *reduce_scratch)
    else:
        reduce_rounds(term_ref, sum_ref, *reduce_scratch)
    exchange_finish("col", 1, n_col, "gather", spread_ref, panel_ref, panel_ref, g_send, g_recv,
                    copies)


def layer_step(partials, weight_cols, weight_rows, cotangent, collective_id):
    n_col = lax.axis_size("col")
    n_feat = lax.axis_size("feat")
    block = partials.shape[1:]
    half = block[-1]
    term = jax.ShapeDtypeStruct((half, n_feat * half), jnp.float32)
    reduce_space = radix_scratch(term) if radix_fits(term) else reduce_scratch(term)
    vmem = pl.BlockSpec(memory_space=pltpu.VMEM)
    return pl.pallas_call(
        layer_kernel,
        out_shape=(
            jax.ShapeDtypeStruct(block, jnp.bfloat16),
            jax.ShapeDtypeStruct((n_col,) + block, jnp.bfloat16),
            term,
        ),
        in_specs=[vmem] * 4,
        out_specs=(vmem,) * 3,
        scratch_shapes=exchange_scratch(partials, "scatter", n_col) + [
            pltpu.VMEM(block, partials.dtype),
            pltpu.VMEM((n_feat,) + block, partials.dtype),
            pltpu.VMEM(block, jnp.bfloat16),
            pltpu.VMEM((n_feat,) + block, jnp.bfloat16),
            pltpu.SemaphoreType.DMA((2, n_feat)),
            pltpu.SemaphoreType.DMA((2, n_feat)),
            pltpu.VMEM(term.shape, term.dtype),
            pltpu.VMEM(block, jnp.bfloat16),
            pltpu.SemaphoreType.DMA((n_col,)),
            pltpu.SemaphoreType.DMA((n_col,)),
        ] + reduce_space,
        compiler_params=pltpu.CompilerParams(collective_id=collective_id, has_side_effects=True),
    )(partials, weight_cols, weight_rows, cotangent)


def reduction_plan(rows):
    pairs = []
    for bit in (1, 2, 4, 8, 16, 32, 64):
        for axis in ("row", "col"):
            if bit < lax.axis_size(axis):
                pairs.append((axis, bit))
    halving = []
    while pairs and rows // 2 >= 8 and rows % 16 == 0:
        halving.append(pairs.pop(0))
        rows //= 2
    return halving, pairs


def bitval(axis, bit):
    return (lax.axis_index(axis) // bit) % 2


def partner(axis, bit):
    return mesh_coords(axis, lax.axis_index(axis) + bit * (1 - 2 * bitval(axis, bit)))


def reduce_targets(rows):
    halving, whole = reduction_plan(rows)
    return [partner(axis, bit) for axis, bit in halving + whole]


def reduce_rounds(x_ref, o_ref, recv, send_sems, recv_sems):
    halving, whole = reduction_plan(x_ref.shape[0])
    o_ref[...] = x_ref[...]
    k = 0

    def swap(k, axis, bit, send_rows, length):
        copy = pltpu.make_async_remote_copy(
            src_ref=o_ref.at[pl.ds(send_rows, length)], dst_ref=recv.at[k, pl.ds(0, length)],
            send_sem=send_sems.at[k], recv_sem=recv_sems.at[k],
            device_id=partner(axis, bit), device_id_type=pl.DeviceIdType.MESH)
        copy.start()
        copy.wait()

    lo = jnp.int32(0)
    length = x_ref.shape[0]
    starts = []
    for axis, bit in halving:
        length //= 2
        mine = bitval(axis, bit)
        starts.append(lo)
        keep = pl.multiple_of(lo + mine * length, 8)
        give = pl.multiple_of(lo + (1 - mine) * length, 8)
        swap(k, axis, bit, give, length)
        o_ref[pl.ds(keep, length)] = o_ref[pl.ds(keep, length)] + recv[k, pl.ds(0, length)]
        lo = keep
        k += 1
    for axis, bit in whole:
        swap(k, axis, bit, lo, length)
        o_ref[pl.ds(lo, length)] = o_ref[pl.ds(lo, length)] + recv[k, pl.ds(0, length)]
        k += 1
    for (axis, bit), base in zip(reversed(halving), reversed(starts)):
        mine = bitval(axis, bit)
        other = pl.multiple_of(base + (1 - mine) * length, 8)
        swap(k, axis, bit, lo, length)
        o_ref[pl.ds(other, length)] = recv[k, pl.ds(0, length)]
        lo = base
        length *= 2
        k += 1


def reduce_scratch(w):
    halving, whole = reduction_plan(w.shape[0])
    steps = 2 * len(halving) + len(whole)
    return [
        pltpu.VMEM((steps, w.shape[0] // 2) + w.shape[1:], w.dtype),
        pltpu.SemaphoreType.DMA((steps,)),
        pltpu.SemaphoreType.DMA((steps,)),
    ]


def radix_groups():
    n_row, n_col = lax.axis_size("row"), lax.axis_size("col")
    if n_row % 2 or n_col % 4:
        return None
    return ((("row", 1, 2), ("col", 1, 4)), ("row", 2, n_row // 2), ("col", 4, n_col // 4))


def first_group():
    (core, ring), _, _ = radix_groups()
    me_a, _ = group_of(*core)
    me_b, _ = group_of(*ring)
    size = core[2] * ring[2]
    me = me_a + core[2] * me_b
    row = lax.axis_index("row") - me_a * core[1]
    col = lax.axis_index("col") - me_b * ring[1]

    def member(m):
        return (row + (m % core[2]) * core[1], col + (m // core[2]) * ring[1], lax.axis_index("feat"))

    return me, size, member


def reduce_radix_targets():
    me, size, member = first_group()
    targets = [member(lax.rem(me + d, size)) for d in range(1, size)]
    _, z_group, x_group = radix_groups()
    return targets + exchange_targets(*z_group) + exchange_targets(*x_group)


def ordered_allreduce(group, value, recv, send_sems, recv_sems):
    axis, stride, size = group
    me, member = group_of(axis, stride, size)
    recv[me] = value
    copies = []
    for d in range(1, size):
        peer = lax.rem(me + d, size)
        copy = pltpu.make_async_remote_copy(
            src_ref=recv.at[me], dst_ref=recv.at[me], send_sem=send_sems.at[d],
            recv_sem=recv_sems.at[me], device_id=member(peer), device_id_type=pl.DeviceIdType.MESH)
        copy.start()
        copies.append(copy)
    for d in range(1, size):
        src_dev = lax.rem(me + size - d, size)
        pltpu.make_async_remote_copy(
            src_ref=recv.at[src_dev], dst_ref=recv.at[src_dev], send_sem=send_sems.at[d],
            recv_sem=recv_sems.at[src_dev], device_id=member(src_dev),
            device_id_type=pl.DeviceIdType.MESH).wait_recv()
    for copy in copies:
        copy.wait_send()
    total = recv[0]
    for k in range(1, size):
        total = total + recv[k]
    return total


def reduce_radix(w_ref, o_ref, seg_recv, z_recv, x_recv, sems):
    _, z_group, x_group = radix_groups()
    me, size, member = first_group()
    seg = w_ref.shape[0] // size
    mine = pl.ds(pl.multiple_of(me * seg, 8), seg)
    copies = []
    for d in range(1, size):
        peer = lax.rem(me + d, size)
        copy = pltpu.make_async_remote_copy(
            src_ref=w_ref.at[pl.ds(pl.multiple_of(peer * seg, 8), seg)], dst_ref=seg_recv.at[me],
            send_sem=sems.at[0, d], recv_sem=sems.at[1, me], device_id=member(peer),
            device_id_type=pl.DeviceIdType.MESH)
        copy.start()
        copies.append(copy)
    total = w_ref[mine]
    for d in range(1, size):
        src_dev = lax.rem(me + size - d, size)
        pltpu.make_async_remote_copy(
            src_ref=seg_recv.at[src_dev], dst_ref=seg_recv.at[src_dev], send_sem=sems.at[0, d],
            recv_sem=sems.at[1, src_dev], device_id=member(src_dev),
            device_id_type=pl.DeviceIdType.MESH).wait_recv()
        total = total + seg_recv[src_dev]
    for copy in copies:
        copy.wait_send()
    total = ordered_allreduce(z_group, total, z_recv, sems.at[2], sems.at[3])
    total = ordered_allreduce(x_group, total, x_recv, sems.at[4], sems.at[5])
    o_ref[mine] = total
    copies = []
    for d in range(1, size):
        peer = lax.rem(me + d, size)
        copy = pltpu.make_async_remote_copy(
            src_ref=o_ref.at[mine], dst_ref=o_ref.at[mine], send_sem=sems.at[6, d],
            recv_sem=sems.at[7, me], device_id=member(peer), device_id_type=pl.DeviceIdType.MESH)
        copy.start()
        copies.append(copy)
    for d in range(1, size):
        src_dev = lax.rem(me + size - d, size)
        rows = pl.ds(pl.multiple_of(src_dev * seg, 8), seg)
        pltpu.make_async_remote_copy(
            src_ref=o_ref.at[rows], dst_ref=o_ref.at[rows], send_sem=sems.at[6, d],
            recv_sem=sems.at[7, src_dev], device_id=member(src_dev),
            device_id_type=pl.DeviceIdType.MESH).wait_recv()
    for copy in copies:
        copy.wait_send()


def radix_scratch(w):
    (core, ring), z_group, x_group = radix_groups()
    size = core[2] * ring[2]
    seg = (w.shape[0] // size,) + w.shape[1:]
    width = max(size, z_group[2], x_group[2])
    return [
        pltpu.VMEM((size,) + seg, w.dtype),
        pltpu.VMEM((z_group[2],) + seg, w.dtype),
        pltpu.VMEM((x_group[2],) + seg, w.dtype),
        pltpu.SemaphoreType.DMA((8, width)),
    ]


def radix_fits(w):
    groups = radix_groups()
    if groups is None:
        return False
    size = groups[0][0][2] * groups[0][1][2]
    return w.shape[0] % (8 * size) == 0


def gather_radix_kernel(axis, x_ref, w_ref, o_ref, ow_ref, g_send, g_recv, *scratch):
    size = lax.axis_size(axis)
    enter(exchange_targets(axis, 1, size) + reduce_radix_targets())
    copies = exchange_start(axis, 1, size, "gather", x_ref, o_ref, g_send, g_recv)
    reduce_radix(w_ref, ow_ref, *scratch)
    exchange_finish(axis, 1, size, "gather", x_ref, o_ref, o_ref, g_send, g_recv, copies)


def gather_reduce_kernel(axis, x_ref, w_ref, o_ref, ow_ref, g_send, g_recv, recv, send_sems, recv_sems):
    size = lax.axis_size(axis)
    enter(exchange_targets(axis, 1, size) + reduce_targets(w_ref.shape[0]))
    copies = exchange_start(axis, 1, size, "gather", x_ref, o_ref, g_send, g_recv)
    reduce_rounds(w_ref, ow_ref, recv, send_sems, recv_sems)
    exchange_finish(axis, 1, size, "gather", x_ref, o_ref, o_ref, g_send, g_recv, copies)


def gather_and_reduce(x, w, axis, collective_id):
    size = lax.axis_size(axis)
    if radix_fits(w):
        kernel, scratch = gather_radix_kernel, radix_scratch(w)
    else:
        kernel, scratch = gather_reduce_kernel, reduce_scratch(w)
    return pl.pallas_call(
        functools.partial(kernel, axis),
        out_shape=(exchange_shape(x, "gather", size), jax.ShapeDtypeStruct(w.shape, w.dtype)),
        in_specs=[pl.BlockSpec(memory_space=pltpu.VMEM)] * 2,
        out_specs=(pl.BlockSpec(memory_space=pltpu.VMEM),) * 2,
        scratch_shapes=exchange_scratch(x, "gather", size) + scratch,
        compiler_params=pltpu.CompilerParams(collective_id=collective_id, has_side_effects=True),
    )(x, w)


def shards(features, tile_rows, tile_cols, tile_count, tile_values, weights, cotangent):
    width = tile_values.shape[-1]
    local_tiles = tile_values[0, 0]
    block_rows = tile_rows[0, 0]
    block_cols = tile_cols[0, 0]
    count = tile_count[0, 0].reshape(1)
    n_rowdev = lax.axis_size("row")
    n_coldev = lax.axis_size("col")
    local_blocks = features.shape[0] // width
    feat_half = features.shape[1]
    feat_index = lax.axis_index("feat")
    row_blocks = local_blocks * n_coldev
    col_blocks = local_blocks * n_rowdev
    node_total = features.shape[0] * n_rowdev * n_coldev
    pair = 2 if n_rowdev % 2 == 0 else 1
    chips = n_rowdev // pair
    if pair == 2:
        panel = row_gather(features, chips, 0).reshape(-1, feat_half)
    else:
        panel = exchange(features, "row", "gather", 0).reshape(-1, feat_half)

    def remap(col):
        owner = col // local_blocks
        return ((owner % pair) * chips + owner // pair) * local_blocks + col % local_blocks

    partial_value = tile_products(local_tiles, block_rows, block_cols, count, panel,
                                  row_blocks, transpose=False, remap=remap)
    weight_cols = lax.dynamic_slice_in_dim(weights, feat_index * feat_half, feat_half, 1)
    weight_rows = lax.dynamic_slice_in_dim(weights, feat_index * feat_half, feat_half, 0)
    activated, spread_panel, weight_sum = layer_step(partial_value.reshape(n_coldev, -1, feat_half),
                                                  weight_cols, weight_rows, cotangent, 1)
    spread_panel = spread_panel.reshape(-1, feat_half)
    weight_grad = weight_sum * node_total ** (-0.5)
    back_partial = tile_products(local_tiles, block_rows, block_cols, count, spread_panel,
                                 col_blocks, transpose=True, remap=remap)
    if pair == 2:
        back_summed = row_scatter(back_partial.reshape(pair, chips, -1, feat_half), chips, 3)
    else:
        back_summed = exchange(back_partial.reshape(n_rowdev, -1, feat_half), "row", "scatter", 3)
    return (activated, back_summed, weight_grad)


def solution(mesh):
    return jax.shard_map(
        shards,
        mesh=mesh,
        in_specs=(
            P(("col", "row"), "feat"),
            P("row", "col", None),
            P("row", "col", None),
            P("row", "col"),
            P("row", "col", None, None, None),
            P(),
            P(("row", "col"), "feat"),
        ),
        out_specs=(P(("row", "col"), "feat"), P(("col", "row"), "feat"), P("feat", None)),
        check_vma=False,
    )
```

```python
import functools

import jax
import jax.numpy as jnp
from jax import lax
from jax.experimental import pallas as pl
from jax.experimental.pallas import tpu as pltpu
from jax.sharding import PartitionSpec as P

GROUP = 64


def tile_kernel(transpose, remap, rows_ref, cols_ref, count_ref, tiles_ref, panel_ref, out_ref, acc_ref):
    step = pl.program_id(0)
    width = tiles_ref.shape[-1]
    count = count_ref[0]
    src_blocks = panel_ref.shape[0] // width
    dst_blocks = acc_ref.shape[0] // width

    @pl.when(step == 0)
    def _():
        acc_ref[...] = jnp.zeros_like(acc_ref)

    @pl.when(step * GROUP < count)
    def _():
        terms = []
        for j in range(GROUP):
            slot = step * GROUP + j
            src = rows_ref[slot] if transpose else remap(cols_ref[slot])
            src = jnp.minimum(jnp.maximum(src, 0), src_blocks - 1)
            block = panel_ref[pl.ds(pl.multiple_of(src * width, width), width), :]
            tile = tiles_ref[j]
            if transpose:
                term = lax.dot_general(tile, block, (((0,), (0,)), ((), ())),
                                       preferred_element_type=jnp.float32)
            else:
                term = jnp.dot(tile, block, preferred_element_type=jnp.float32)
            terms.append(jnp.where(slot < count, term, 0.0))
        for j in range(GROUP):
            slot = step * GROUP + j
            dst = remap(cols_ref[slot]) if transpose else rows_ref[slot]
            dst = jnp.minimum(jnp.maximum(dst, 0), dst_blocks - 1)
            rows = pl.ds(pl.multiple_of(dst * width, width), width)
            acc_ref[rows, :] += terms[j]

    @pl.when(step == pl.num_programs(0) - 1)
    def _():
        out_ref[...] = acc_ref[...].astype(out_ref.dtype)


def tile_products(tiles, rows, cols, count, panel, out_blocks, transpose, remap):
    slots, width, _ = tiles.shape
    feat = panel.shape[1]
    steps = slots // GROUP

    def tiles_map(i, rows_ref, cols_ref, count_ref):
        last = jnp.maximum(count_ref[0] - 1, 0) // GROUP
        return (jnp.minimum(i, last), 0, 0)

    return pl.pallas_call(
        functools.partial(tile_kernel, transpose, remap),
        out_shape=jax.ShapeDtypeStruct((out_blocks * width, feat), jnp.bfloat16),
        grid_spec=pltpu.PrefetchScalarGridSpec(
            num_scalar_prefetch=3,
            grid=(steps,),
            in_specs=[
                pl.BlockSpec((GROUP, width, width), tiles_map),
                pl.BlockSpec(panel.shape, lambda i, *_: (0, 0)),
            ],
            out_specs=pl.BlockSpec((out_blocks * width, feat), lambda i, *_: (0, 0)),
            scratch_shapes=[pltpu.VMEM((out_blocks * width, feat), jnp.float32)],
        ),
        compiler_params=pltpu.CompilerParams(dimension_semantics=("arbitrary",)),
        cost_estimate=pl.CostEstimate(
            flops=2 * slots * width * width * feat,
            bytes_accessed=tiles.size * 2 + panel.size * 2 + out_blocks * width * feat * 2,
            transcendentals=0,
        ),
    )(rows, cols, count, tiles, panel)


def mesh_coords(axis, peer):
    return tuple(peer if name == axis else lax.axis_index(name) for name in ("row", "col", "feat"))


def group_of(axis, stride, size):
    index = lax.axis_index(axis)
    me = (index // stride) % size
    base = index - me * stride
    return me, lambda k: mesh_coords(axis, base + k * stride)


def exchange_targets(axis, stride, size):
    me, member = group_of(axis, stride, size)
    return [member(lax.rem(me + d, size)) for d in range(1, size)]


def enter(targets):
    barrier = pltpu.get_barrier_semaphore()
    for target in targets:
        pl.semaphore_signal(barrier, inc=1, device_id=target, device_id_type=pl.DeviceIdType.MESH)
    pl.semaphore_wait(barrier, len(targets))


def exchange_start(axis, stride, size, mode, x_ref, recv_ref, send_sems, recv_sems):
    me, member = group_of(axis, stride, size)
    copies = []
    for d in range(1, size):
        peer = lax.rem(me + d, size)
        src = x_ref if mode == "gather" else x_ref.at[peer]
        copy = pltpu.make_async_remote_copy(
            src_ref=src, dst_ref=recv_ref.at[me], send_sem=send_sems.at[d],
            recv_sem=recv_sems.at[me], device_id=member(peer),
            device_id_type=pl.DeviceIdType.MESH)
        copy.start()
        copies.append(copy)
    return copies


def exchange_finish(axis, stride, size, mode, x_ref, o_ref, recv_ref, send_sems, recv_sems, copies):
    me, member = group_of(axis, stride, size)
    if mode == "gather":
        o_ref[me] = x_ref[...]
    else:
        total = x_ref[me].astype(jnp.float32)
    for d in range(1, size):
        src_dev = lax.rem(me + size - d, size)
        incoming = pltpu.make_async_remote_copy(
            src_ref=recv_ref.at[src_dev], dst_ref=recv_ref.at[src_dev], send_sem=send_sems.at[d],
            recv_sem=recv_sems.at[src_dev], device_id=member(src_dev),
            device_id_type=pl.DeviceIdType.MESH)
        incoming.wait_recv()
        if mode != "gather":
            total = total + recv_ref[src_dev].astype(jnp.float32)
    for copy in copies:
        copy.wait_send()
    if mode != "gather":
        o_ref[...] = total.astype(o_ref.dtype)


def exchange_kernel(axis, stride, size, mode, x_ref, o_ref, *scratch):
    if mode == "gather":
        recv_ref, (send_sems, recv_sems) = o_ref, scratch
    else:
        recv_ref, send_sems, recv_sems = scratch
    enter(exchange_targets(axis, stride, size))
    copies = exchange_start(axis, stride, size, mode, x_ref, recv_ref, send_sems, recv_sems)
    exchange_finish(axis, stride, size, mode, x_ref, o_ref, recv_ref, send_sems, recv_sems, copies)


def exchange_scratch(x, mode, size):
    scratch = [] if mode == "gather" else [pltpu.VMEM(x.shape, x.dtype)]
    return scratch + [pltpu.SemaphoreType.DMA((size,)), pltpu.SemaphoreType.DMA((size,))]


def exchange_shape(x, mode, size):
    shape = (size,) + x.shape if mode == "gather" else x.shape[1:]
    return jax.ShapeDtypeStruct(shape, x.dtype)


def exchange(x, axis, mode, collective_id, stride=1, size=None):
    size = lax.axis_size(axis) if size is None else size
    return pl.pallas_call(
        functools.partial(exchange_kernel, axis, stride, size, mode),
        out_shape=exchange_shape(x, mode, size),
        in_specs=[pl.BlockSpec(memory_space=pltpu.VMEM)],
        out_specs=pl.BlockSpec(memory_space=pltpu.VMEM),
        scratch_shapes=exchange_scratch(x, mode, size),
        compiler_params=pltpu.CompilerParams(collective_id=collective_id, has_side_effects=True),
    )(x)


def pair_targets(chips):
    me, member = group_of("row", 2, chips)
    _, sibling = group_of("row", 1, 2)
    return [member(lax.rem(me + d, chips)) for d in range(1, chips)], sibling


def row_gather_kernel(chips, x_ref, o_ref, send_sems, recv_sems, fwd_send, fwd_recv):
    z_me, z_member = group_of("row", 2, chips)
    c_me, core_member = group_of("row", 1, 2)
    sibling = core_member(1 - c_me)
    peers, _ = pair_targets(chips)
    enter(peers + [sibling])
    copies = []
    for d in range(1, chips):
        peer = lax.rem(z_me + d, chips)
        copy = pltpu.make_async_remote_copy(
            src_ref=x_ref, dst_ref=o_ref.at[c_me, z_me], send_sem=send_sems.at[d],
            recv_sem=recv_sems.at[z_me], device_id=z_member(peer),
            device_id_type=pl.DeviceIdType.MESH)
        copy.start()
        copies.append(copy)
    own = pltpu.make_async_remote_copy(
        src_ref=x_ref, dst_ref=o_ref.at[c_me, z_me], send_sem=fwd_send.at[z_me],
        recv_sem=fwd_recv.at[z_me], device_id=sibling, device_id_type=pl.DeviceIdType.MESH)
    own.start()
    copies.append(own)
    o_ref[c_me, z_me] = x_ref[...]
    for d in range(1, chips):
        src_dev = lax.rem(z_me + chips - d, chips)
        incoming = pltpu.make_async_remote_copy(
            src_ref=o_ref.at[c_me, src_dev], dst_ref=o_ref.at[c_me, src_dev],
            send_sem=send_sems.at[d], recv_sem=recv_sems.at[src_dev],
            device_id=z_member(src_dev), device_id_type=pl.DeviceIdType.MESH)
        incoming.wait_recv()
        forward = pltpu.make_async_remote_copy(
            src_ref=o_ref.at[c_me, src_dev], dst_ref=o_ref.at[c_me, src_dev],
            send_sem=fwd_send.at[src_dev], recv_sem=fwd_recv.at[src_dev], device_id=sibling,
            device_id_type=pl.DeviceIdType.MESH)
        forward.start()
        copies.append(forward)
    for k in range(chips):
        incoming = pltpu.make_async_remote_copy(
            src_ref=o_ref.at[1 - c_me, k], dst_ref=o_ref.at[1 - c_me, k],
            send_sem=fwd_send.at[k], recv_sem=fwd_recv.at[k], device_id=sibling,
            device_id_type=pl.DeviceIdType.MESH)
        incoming.wait_recv()
    for copy in copies:
        copy.wait_send()


def row_gather(x, chips, collective_id):
    return pl.pallas_call(
        functools.partial(row_gather_kernel, chips),
        out_shape=jax.ShapeDtypeStruct((2, chips) + x.shape, x.dtype),
        in_specs=[pl.BlockSpec(memory_space=pltpu.VMEM)],
        out_specs=pl.BlockSpec(memory_space=pltpu.VMEM),
        scratch_shapes=[pltpu.SemaphoreType.DMA((chips,))] * 4,
        compiler_params=pltpu.CompilerParams(collective_id=collective_id, has_side_effects=True),
    )(x)


def row_scatter_kernel(chips, x_ref, o_ref, pair_recv, pair_sum, z_recv,
                       pair_send_sems, pair_recv_sems, z_send_sems, z_recv_sems):
    z_me, z_member = group_of("row", 2, chips)
    c_me, core_member = group_of("row", 1, 2)
    sibling = core_member(1 - c_me)
    peers, _ = pair_targets(chips)
    enter(peers + [sibling])
    copies = []
    for k in range(chips):
        copy = pltpu.make_async_remote_copy(
            src_ref=x_ref.at[1 - c_me, k], dst_ref=pair_recv.at[k], send_sem=pair_send_sems.at[k],
            recv_sem=pair_recv_sems.at[k], device_id=sibling, device_id_type=pl.DeviceIdType.MESH)
        copy.start()
        copies.append(copy)
    order = [lax.rem(z_me + d, chips) for d in range(1, chips)] + [z_me]
    for d, k in enumerate(order, start=1):
        incoming = pltpu.make_async_remote_copy(
            src_ref=pair_recv.at[k], dst_ref=pair_recv.at[k], send_sem=pair_send_sems.at[k],
            recv_sem=pair_recv_sems.at[k], device_id=sibling, device_id_type=pl.DeviceIdType.MESH)
        incoming.wait_recv()
        pair_sum[k] = (x_ref[c_me, k].astype(jnp.float32)
                       + pair_recv[k].astype(jnp.float32)).astype(pair_sum.dtype)
        if d < chips:
            copy = pltpu.make_async_remote_copy(
                src_ref=pair_sum.at[k], dst_ref=z_recv.at[z_me], send_sem=z_send_sems.at[d],
                recv_sem=z_recv_sems.at[z_me], device_id=z_member(k),
                device_id_type=pl.DeviceIdType.MESH)
            copy.start()
            copies.append(copy)
    total = pair_sum[z_me].astype(jnp.float32)
    for d in range(1, chips):
        src_dev = lax.rem(z_me + chips - d, chips)
        incoming = pltpu.make_async_remote_copy(
            src_ref=z_recv.at[src_dev], dst_ref=z_recv.at[src_dev], send_sem=z_send_sems.at[d],
            recv_sem=z_recv_sems.at[src_dev], device_id=z_member(src_dev),
            device_id_type=pl.DeviceIdType.MESH)
        incoming.wait_recv()
        total = total + z_recv[src_dev].astype(jnp.float32)
    for copy in copies:
        copy.wait_send()
    o_ref[...] = total.astype(o_ref.dtype)


def row_scatter(x, chips, collective_id):
    block = x.shape[2:]
    return pl.pallas_call(
        functools.partial(row_scatter_kernel, chips),
        out_shape=jax.ShapeDtypeStruct(block, x.dtype),
        in_specs=[pl.BlockSpec(memory_space=pltpu.VMEM)],
        out_specs=pl.BlockSpec(memory_space=pltpu.VMEM),
        scratch_shapes=[pltpu.VMEM((chips,) + block, x.dtype)] * 3
        + [pltpu.SemaphoreType.DMA((chips,))] * 4,
        compiler_params=pltpu.CompilerParams(collective_id=collective_id, has_side_effects=True),
    )(x)


def feat_push(value_ref, halves_ref, send_sems, recv_sems, slot):
    n = lax.axis_size("feat")
    me = lax.axis_index("feat")
    halves_ref[me] = value_ref[...]
    copies = []
    for d in range(1, n):
        peer = lax.rem(me + d, n)
        copy = pltpu.make_async_remote_copy(
            src_ref=halves_ref.at[me], dst_ref=halves_ref.at[me], send_sem=send_sems.at[slot, d],
            recv_sem=recv_sems.at[slot, me], device_id=mesh_coords("feat", peer),
            device_id_type=pl.DeviceIdType.MESH)
        copy.start()
        copies.append(copy)
    for d in range(1, n):
        src_dev = lax.rem(me + n - d, n)
        pltpu.make_async_remote_copy(
            src_ref=halves_ref.at[src_dev], dst_ref=halves_ref.at[src_dev],
            send_sem=send_sems.at[slot, d], recv_sem=recv_sems.at[slot, src_dev],
            device_id=mesh_coords("feat", src_dev), device_id_type=pl.DeviceIdType.MESH).wait_recv()
    for copy in copies:
        copy.wait_send()


def layer_kernel(x_ref, w_ref, wr_ref, cot_ref, hidden_ref, panel_ref, sum_ref,
                 recv_ref, send_sems, recv_sems, summed_ref, agg_ref, grad_out_ref, grad_ref,
                 f_send, f_recv, term_ref, spread_ref, g_send, g_recv, *reduce_scratch):
    n_col = lax.axis_size("col")
    n_feat = lax.axis_size("feat")
    me = lax.axis_index("feat")
    peers = [mesh_coords("feat", lax.rem(me + d, n_feat)) for d in range(1, n_feat)]
    radix = len(reduce_scratch) == 4
    others = reduce_radix_targets() if radix else reduce_targets(term_ref.shape[0])
    enter(exchange_targets("col", 1, n_col) + peers + exchange_targets("col", 1, n_col) + others)
    copies = exchange_start("col", 1, n_col, "scatter", x_ref, recv_ref, send_sems, recv_sems)
    exchange_finish("col", 1, n_col, "scatter", x_ref, summed_ref, recv_ref, send_sems, recv_sems,
                    copies)
    feat_push(summed_ref, agg_ref, f_send, f_recv, 0)
    half = agg_ref.shape[-1]
    hidden = jnp.dot(agg_ref[0], w_ref[pl.ds(0, half), :], preferred_element_type=jnp.float32)
    for h in range(1, n_feat):
        hidden = hidden + jnp.dot(agg_ref[h], w_ref[pl.ds(h * half, half), :],
                                  preferred_element_type=jnp.float32)
    hidden_ref[...] = hidden
    slope = jnp.where(hidden > 0, 1.0, jnp.exp(jnp.minimum(hidden, 0.0)))
    grad_out_ref[...] = (cot_ref[...].astype(jnp.float32) * slope).astype(grad_out_ref.dtype)
    feat_push(grad_out_ref, grad_ref, f_send, f_recv, 1)
    spread = None
    for h in range(n_feat):
        columns = pl.ds(h * half, half)
        term_ref[:, columns] = lax.dot_general(
            summed_ref[...], grad_ref[h], (((0,), (0,)), ((), ())),
            preferred_element_type=jnp.float32)
        part = lax.dot_general(grad_ref[h], wr_ref[:, columns], (((1,), (1,)), ((), ())),
                               preferred_element_type=jnp.float32)
        spread = part if spread is None else spread + part
    spread_ref[...] = spread.astype(spread_ref.dtype)
    copies = exchange_start("col", 1, n_col, "gather", spread_ref, panel_ref, g_send, g_recv)
    if radix:
        reduce_radix(term_ref, sum_ref, *reduce_scratch)
    else:
        reduce_rounds(term_ref, sum_ref, *reduce_scratch)
    exchange_finish("col", 1, n_col, "gather", spread_ref, panel_ref, panel_ref, g_send, g_recv,
                    copies)


def layer_step(partials, weight_cols, weight_rows, cotangent, collective_id):
    n_col = lax.axis_size("col")
    n_feat = lax.axis_size("feat")
    block = partials.shape[1:]
    half = block[-1]
    term = jax.ShapeDtypeStruct((half, n_feat * half), jnp.float32)
    reduce_space = radix_scratch(term) if radix_fits(term) else reduce_scratch(term)
    vmem = pl.BlockSpec(memory_space=pltpu.VMEM)
    return pl.pallas_call(
        layer_kernel,
        out_shape=(
            jax.ShapeDtypeStruct(block, jnp.float32),
            jax.ShapeDtypeStruct((n_col,) + block, jnp.bfloat16),
            term,
        ),
        in_specs=[vmem] * 4,
        out_specs=(vmem,) * 3,
        scratch_shapes=exchange_scratch(partials, "scatter", n_col) + [
            pltpu.VMEM(block, partials.dtype),
            pltpu.VMEM((n_feat,) + block, partials.dtype),
            pltpu.VMEM(block, jnp.bfloat16),
            pltpu.VMEM((n_feat,) + block, jnp.bfloat16),
            pltpu.SemaphoreType.DMA((2, n_feat)),
            pltpu.SemaphoreType.DMA((2, n_feat)),
            pltpu.VMEM(term.shape, term.dtype),
            pltpu.VMEM(block, jnp.bfloat16),
            pltpu.SemaphoreType.DMA((n_col,)),
            pltpu.SemaphoreType.DMA((n_col,)),
        ] + reduce_space,
        compiler_params=pltpu.CompilerParams(collective_id=collective_id, has_side_effects=True),
    )(partials, weight_cols, weight_rows, cotangent)


def reduction_plan(rows):
    pairs = []
    for bit in (1, 2, 4, 8, 16, 32, 64):
        for axis in ("row", "col"):
            if bit < lax.axis_size(axis):
                pairs.append((axis, bit))
    halving = []
    while pairs and rows // 2 >= 8 and rows % 16 == 0:
        halving.append(pairs.pop(0))
        rows //= 2
    return halving, pairs


def bitval(axis, bit):
    return (lax.axis_index(axis) // bit) % 2


def partner(axis, bit):
    return mesh_coords(axis, lax.axis_index(axis) + bit * (1 - 2 * bitval(axis, bit)))


def reduce_targets(rows):
    halving, whole = reduction_plan(rows)
    return [partner(axis, bit) for axis, bit in halving + whole]


def reduce_rounds(x_ref, o_ref, recv, send_sems, recv_sems):
    halving, whole = reduction_plan(x_ref.shape[0])
    o_ref[...] = x_ref[...]
    k = 0

    def swap(k, axis, bit, send_rows, length):
        copy = pltpu.make_async_remote_copy(
            src_ref=o_ref.at[pl.ds(send_rows, length)], dst_ref=recv.at[k, pl.ds(0, length)],
            send_sem=send_sems.at[k], recv_sem=recv_sems.at[k],
            device_id=partner(axis, bit), device_id_type=pl.DeviceIdType.MESH)
        copy.start()
        copy.wait()

    lo = jnp.int32(0)
    length = x_ref.shape[0]
    starts = []
    for axis, bit in halving:
        length //= 2
        mine = bitval(axis, bit)
        starts.append(lo)
        keep = pl.multiple_of(lo + mine * length, 8)
        give = pl.multiple_of(lo + (1 - mine) * length, 8)
        swap(k, axis, bit, give, length)
        o_ref[pl.ds(keep, length)] = o_ref[pl.ds(keep, length)] + recv[k, pl.ds(0, length)]
        lo = keep
        k += 1
    for axis, bit in whole:
        swap(k, axis, bit, lo, length)
        o_ref[pl.ds(lo, length)] = o_ref[pl.ds(lo, length)] + recv[k, pl.ds(0, length)]
        k += 1
    for (axis, bit), base in zip(reversed(halving), reversed(starts)):
        mine = bitval(axis, bit)
        other = pl.multiple_of(base + (1 - mine) * length, 8)
        swap(k, axis, bit, lo, length)
        o_ref[pl.ds(other, length)] = recv[k, pl.ds(0, length)]
        lo = base
        length *= 2
        k += 1


def reduce_scratch(w):
    halving, whole = reduction_plan(w.shape[0])
    steps = 2 * len(halving) + len(whole)
    return [
        pltpu.VMEM((steps, w.shape[0] // 2) + w.shape[1:], w.dtype),
        pltpu.SemaphoreType.DMA((steps,)),
        pltpu.SemaphoreType.DMA((steps,)),
    ]


def radix_groups():
    n_row, n_col = lax.axis_size("row"), lax.axis_size("col")
    if n_row % 2 or n_col % 4:
        return None
    return ((("row", 1, 2), ("col", 1, 4)), ("row", 2, n_row // 2), ("col", 4, n_col // 4))


def first_group():
    (core, ring), _, _ = radix_groups()
    me_a, _ = group_of(*core)
    me_b, _ = group_of(*ring)
    size = core[2] * ring[2]
    me = me_a + core[2] * me_b
    row = lax.axis_index("row") - me_a * core[1]
    col = lax.axis_index("col") - me_b * ring[1]

    def member(m):
        return (row + (m % core[2]) * core[1], col + (m // core[2]) * ring[1], lax.axis_index("feat"))

    return me, size, member


def reduce_radix_targets():
    me, size, member = first_group()
    targets = [member(lax.rem(me + d, size)) for d in range(1, size)]
    _, z_group, x_group = radix_groups()
    return targets + exchange_targets(*z_group) + exchange_targets(*x_group)


def ordered_allreduce(group, value, recv, send_sems, recv_sems):
    axis, stride, size = group
    me, member = group_of(axis, stride, size)
    recv[me] = value
    copies = []
    for d in range(1, size):
        peer = lax.rem(me + d, size)
        copy = pltpu.make_async_remote_copy(
            src_ref=recv.at[me], dst_ref=recv.at[me], send_sem=send_sems.at[d],
            recv_sem=recv_sems.at[me], device_id=member(peer), device_id_type=pl.DeviceIdType.MESH)
        copy.start()
        copies.append(copy)
    for d in range(1, size):
        src_dev = lax.rem(me + size - d, size)
        pltpu.make_async_remote_copy(
            src_ref=recv.at[src_dev], dst_ref=recv.at[src_dev], send_sem=send_sems.at[d],
            recv_sem=recv_sems.at[src_dev], device_id=member(src_dev),
            device_id_type=pl.DeviceIdType.MESH).wait_recv()
    for copy in copies:
        copy.wait_send()
    total = recv[0]
    for k in range(1, size):
        total = total + recv[k]
    return total


def reduce_radix(w_ref, o_ref, seg_recv, z_recv, x_recv, sems):
    _, z_group, x_group = radix_groups()
    me, size, member = first_group()
    seg = w_ref.shape[0] // size
    mine = pl.ds(pl.multiple_of(me * seg, 8), seg)
    copies = []
    for d in range(1, size):
        peer = lax.rem(me + d, size)
        copy = pltpu.make_async_remote_copy(
            src_ref=w_ref.at[pl.ds(pl.multiple_of(peer * seg, 8), seg)], dst_ref=seg_recv.at[me],
            send_sem=sems.at[0, d], recv_sem=sems.at[1, me], device_id=member(peer),
            device_id_type=pl.DeviceIdType.MESH)
        copy.start()
        copies.append(copy)
    total = w_ref[mine]
    for d in range(1, size):
        src_dev = lax.rem(me + size - d, size)
        pltpu.make_async_remote_copy(
            src_ref=seg_recv.at[src_dev], dst_ref=seg_recv.at[src_dev], send_sem=sems.at[0, d],
            recv_sem=sems.at[1, src_dev], device_id=member(src_dev),
            device_id_type=pl.DeviceIdType.MESH).wait_recv()
        total = total + seg_recv[src_dev]
    for copy in copies:
        copy.wait_send()
    total = ordered_allreduce(z_group, total, z_recv, sems.at[2], sems.at[3])
    total = ordered_allreduce(x_group, total, x_recv, sems.at[4], sems.at[5])
    o_ref[mine] = total
    copies = []
    for d in range(1, size):
        peer = lax.rem(me + d, size)
        copy = pltpu.make_async_remote_copy(
            src_ref=o_ref.at[mine], dst_ref=o_ref.at[mine], send_sem=sems.at[6, d],
            recv_sem=sems.at[7, me], device_id=member(peer), device_id_type=pl.DeviceIdType.MESH)
        copy.start()
        copies.append(copy)
    for d in range(1, size):
        src_dev = lax.rem(me + size - d, size)
        rows = pl.ds(pl.multiple_of(src_dev * seg, 8), seg)
        pltpu.make_async_remote_copy(
            src_ref=o_ref.at[rows], dst_ref=o_ref.at[rows], send_sem=sems.at[6, d],
            recv_sem=sems.at[7, src_dev], device_id=member(src_dev),
            device_id_type=pl.DeviceIdType.MESH).wait_recv()
    for copy in copies:
        copy.wait_send()


def radix_scratch(w):
    (core, ring), z_group, x_group = radix_groups()
    size = core[2] * ring[2]
    seg = (w.shape[0] // size,) + w.shape[1:]
    width = max(size, z_group[2], x_group[2])
    return [
        pltpu.VMEM((size,) + seg, w.dtype),
        pltpu.VMEM((z_group[2],) + seg, w.dtype),
        pltpu.VMEM((x_group[2],) + seg, w.dtype),
        pltpu.SemaphoreType.DMA((8, width)),
    ]


def radix_fits(w):
    groups = radix_groups()
    if groups is None:
        return False
    size = groups[0][0][2] * groups[0][1][2]
    return w.shape[0] % (8 * size) == 0


def gather_radix_kernel(axis, x_ref, w_ref, o_ref, ow_ref, g_send, g_recv, *scratch):
    size = lax.axis_size(axis)
    enter(exchange_targets(axis, 1, size) + reduce_radix_targets())
    copies = exchange_start(axis, 1, size, "gather", x_ref, o_ref, g_send, g_recv)
    reduce_radix(w_ref, ow_ref, *scratch)
    exchange_finish(axis, 1, size, "gather", x_ref, o_ref, o_ref, g_send, g_recv, copies)


def gather_reduce_kernel(axis, x_ref, w_ref, o_ref, ow_ref, g_send, g_recv, recv, send_sems, recv_sems):
    size = lax.axis_size(axis)
    enter(exchange_targets(axis, 1, size) + reduce_targets(w_ref.shape[0]))
    copies = exchange_start(axis, 1, size, "gather", x_ref, o_ref, g_send, g_recv)
    reduce_rounds(w_ref, ow_ref, recv, send_sems, recv_sems)
    exchange_finish(axis, 1, size, "gather", x_ref, o_ref, o_ref, g_send, g_recv, copies)


def gather_and_reduce(x, w, axis, collective_id):
    size = lax.axis_size(axis)
    if radix_fits(w):
        kernel, scratch = gather_radix_kernel, radix_scratch(w)
    else:
        kernel, scratch = gather_reduce_kernel, reduce_scratch(w)
    return pl.pallas_call(
        functools.partial(kernel, axis),
        out_shape=(exchange_shape(x, "gather", size), jax.ShapeDtypeStruct(w.shape, w.dtype)),
        in_specs=[pl.BlockSpec(memory_space=pltpu.VMEM)] * 2,
        out_specs=(pl.BlockSpec(memory_space=pltpu.VMEM),) * 2,
        scratch_shapes=exchange_scratch(x, "gather", size) + scratch,
        compiler_params=pltpu.CompilerParams(collective_id=collective_id, has_side_effects=True),
    )(x, w)


def shards(features, tile_rows, tile_cols, tile_count, tile_values, weights, cotangent):
    width = tile_values.shape[-1]
    local_tiles = tile_values[0, 0]
    block_rows = tile_rows[0, 0]
    block_cols = tile_cols[0, 0]
    count = tile_count[0, 0].reshape(1)
    n_rowdev = lax.axis_size("row")
    n_coldev = lax.axis_size("col")
    local_blocks = features.shape[0] // width
    feat_half = features.shape[1]
    feat_index = lax.axis_index("feat")
    row_blocks = local_blocks * n_coldev
    col_blocks = local_blocks * n_rowdev
    node_total = features.shape[0] * n_rowdev * n_coldev
    pair = 2 if n_rowdev % 2 == 0 else 1
    chips = n_rowdev // pair
    if pair == 2:
        panel = row_gather(features, chips, 0).reshape(-1, feat_half)
    else:
        panel = exchange(features, "row", "gather", 0).reshape(-1, feat_half)

    def remap(col):
        owner = col // local_blocks
        return ((owner % pair) * chips + owner // pair) * local_blocks + col % local_blocks

    partial_value = tile_products(local_tiles, block_rows, block_cols, count, panel,
                                  row_blocks, transpose=False, remap=remap)
    weight_cols = lax.dynamic_slice_in_dim(weights, feat_index * feat_half, feat_half, 1)
    weight_rows = lax.dynamic_slice_in_dim(weights, feat_index * feat_half, feat_half, 0)
    hidden, spread_panel, weight_sum = layer_step(partial_value.reshape(n_coldev, -1, feat_half),
                                                  weight_cols, weight_rows, cotangent, 1)
    negative = jnp.minimum(hidden, 0.0)
    activated = jnp.where(hidden > 0, hidden, jnp.expm1(negative)).astype(jnp.bfloat16)
    spread_panel = spread_panel.reshape(-1, feat_half)
    weight_grad = weight_sum * node_total ** (-0.5)
    back_partial = tile_products(local_tiles, block_rows, block_cols, count, spread_panel,
                                 col_blocks, transpose=True, remap=remap)
    if pair == 2:
        back_summed = row_scatter(back_partial.reshape(pair, chips, -1, feat_half), chips, 3)
    else:
        back_summed = exchange(back_partial.reshape(n_rowdev, -1, feat_half), "row", "scatter", 3)
    return (activated, back_summed, weight_grad)


def solution(mesh):
    return jax.shard_map(
        shards,
        mesh=mesh,
        in_specs=(
            P(("col", "row"), "feat"),
            P("row", "col", None),
            P("row", "col", None),
            P("row", "col"),
            P("row", "col", None, None, None),
            P(),
            P(("row", "col"), "feat"),
        ),
        out_specs=(P(("row", "col"), "feat"), P(("col", "row"), "feat"), P("feat", None)),
        check_vma=False,
    )
```

```python
import functools

import jax
import jax.numpy as jnp
from jax import lax
from jax.experimental import pallas as pl
from jax.experimental.pallas import tpu as pltpu
from jax.sharding import PartitionSpec as P

GROUP = 64


def tile_kernel(transpose, rows_ref, cols_ref, count_ref, tiles_ref, panel_ref, out_ref, acc_ref):
    step = pl.program_id(0)
    width = tiles_ref.shape[-1]
    count = count_ref[0]
    src_blocks = panel_ref.shape[0] // width
    dst_blocks = acc_ref.shape[0] // width

    @pl.when(step == 0)
    def _():
        acc_ref[...] = jnp.zeros_like(acc_ref)

    @pl.when(step * GROUP < count)
    def _():
        terms = []
        for j in range(GROUP):
            slot = step * GROUP + j
            src = rows_ref[slot] if transpose else cols_ref[slot]
            src = jnp.minimum(jnp.maximum(src, 0), src_blocks - 1)
            block = panel_ref[pl.ds(pl.multiple_of(src * width, width), width), :]
            tile = tiles_ref[j]
            if transpose:
                term = lax.dot_general(tile, block, (((0,), (0,)), ((), ())),
                                       preferred_element_type=jnp.float32)
            else:
                term = jnp.dot(tile, block, preferred_element_type=jnp.float32)
            terms.append(jnp.where(slot < count, term, 0.0))
        for j in range(GROUP):
            slot = step * GROUP + j
            dst = cols_ref[slot] if transpose else rows_ref[slot]
            dst = jnp.minimum(jnp.maximum(dst, 0), dst_blocks - 1)
            rows = pl.ds(pl.multiple_of(dst * width, width), width)
            acc_ref[rows, :] += terms[j]

    @pl.when(step == pl.num_programs(0) - 1)
    def _():
        out_ref[...] = acc_ref[...].astype(out_ref.dtype)


def tile_products(tiles, rows, cols, count, panel, out_blocks, transpose):
    slots, width, _ = tiles.shape
    feat = panel.shape[1]
    steps = slots // GROUP

    def tiles_map(i, rows_ref, cols_ref, count_ref):
        last = jnp.maximum(count_ref[0] - 1, 0) // GROUP
        return (jnp.minimum(i, last), 0, 0)

    return pl.pallas_call(
        functools.partial(tile_kernel, transpose),
        out_shape=jax.ShapeDtypeStruct((out_blocks * width, feat), jnp.bfloat16),
        grid_spec=pltpu.PrefetchScalarGridSpec(
            num_scalar_prefetch=3,
            grid=(steps,),
            in_specs=[
                pl.BlockSpec((GROUP, width, width), tiles_map),
                pl.BlockSpec(panel.shape, lambda i, *_: (0, 0)),
            ],
            out_specs=pl.BlockSpec((out_blocks * width, feat), lambda i, *_: (0, 0)),
            scratch_shapes=[pltpu.VMEM((out_blocks * width, feat), jnp.float32)],
        ),
        compiler_params=pltpu.CompilerParams(dimension_semantics=("arbitrary",)),
        cost_estimate=pl.CostEstimate(
            flops=2 * slots * width * width * feat,
            bytes_accessed=tiles.size * 2 + panel.size * 2 + out_blocks * width * feat * 2,
            transcendentals=0,
        ),
    )(rows, cols, count, tiles, panel)


def mesh_coords(axis, peer):
    return tuple(peer if name == axis else lax.axis_index(name) for name in ("row", "col", "feat"))


def group_of(axis, stride, size):
    index = lax.axis_index(axis)
    me = (index // stride) % size
    base = index - me * stride
    return me, lambda k: mesh_coords(axis, base + k * stride)


def exchange_targets(axis, stride, size):
    me, member = group_of(axis, stride, size)
    return [member(lax.rem(me + d, size)) for d in range(1, size)]


def enter(targets):
    barrier = pltpu.get_barrier_semaphore()
    for target in targets:
        pl.semaphore_signal(barrier, inc=1, device_id=target, device_id_type=pl.DeviceIdType.MESH)
    pl.semaphore_wait(barrier, len(targets))


def exchange_start(axis, stride, size, mode, x_ref, recv_ref, send_sems, recv_sems):
    me, member = group_of(axis, stride, size)
    copies = []
    for d in range(1, size):
        peer = lax.rem(me + d, size)
        src = x_ref if mode == "gather" else x_ref.at[peer]
        copy = pltpu.make_async_remote_copy(
            src_ref=src, dst_ref=recv_ref.at[me], send_sem=send_sems.at[d],
            recv_sem=recv_sems.at[me], device_id=member(peer),
            device_id_type=pl.DeviceIdType.MESH)
        copy.start()
        copies.append(copy)
    return copies


def exchange_finish(axis, stride, size, mode, x_ref, o_ref, recv_ref, send_sems, recv_sems, copies):
    me, member = group_of(axis, stride, size)
    if mode == "gather":
        o_ref[me] = x_ref[...]
    else:
        total = x_ref[me].astype(jnp.float32)
    for d in range(1, size):
        src_dev = lax.rem(me + size - d, size)
        incoming = pltpu.make_async_remote_copy(
            src_ref=recv_ref.at[src_dev], dst_ref=recv_ref.at[src_dev], send_sem=send_sems.at[d],
            recv_sem=recv_sems.at[src_dev], device_id=member(src_dev),
            device_id_type=pl.DeviceIdType.MESH)
        incoming.wait_recv()
        if mode != "gather":
            total = total + recv_ref[src_dev].astype(jnp.float32)
    for copy in copies:
        copy.wait_send()
    if mode != "gather":
        o_ref[...] = total.astype(o_ref.dtype)


def exchange_kernel(axis, stride, size, mode, x_ref, o_ref, *scratch):
    if mode == "gather":
        recv_ref, (send_sems, recv_sems) = o_ref, scratch
    else:
        recv_ref, send_sems, recv_sems = scratch
    enter(exchange_targets(axis, stride, size))
    copies = exchange_start(axis, stride, size, mode, x_ref, recv_ref, send_sems, recv_sems)
    exchange_finish(axis, stride, size, mode, x_ref, o_ref, recv_ref, send_sems, recv_sems, copies)


def exchange_scratch(x, mode, size):
    scratch = [] if mode == "gather" else [pltpu.VMEM(x.shape, x.dtype)]
    return scratch + [pltpu.SemaphoreType.DMA((size,)), pltpu.SemaphoreType.DMA((size,))]


def exchange_shape(x, mode, size):
    shape = (size,) + x.shape if mode == "gather" else x.shape[1:]
    return jax.ShapeDtypeStruct(shape, x.dtype)


def exchange(x, axis, mode, collective_id, stride=1, size=None):
    size = lax.axis_size(axis) if size is None else size
    return pl.pallas_call(
        functools.partial(exchange_kernel, axis, stride, size, mode),
        out_shape=exchange_shape(x, mode, size),
        in_specs=[pl.BlockSpec(memory_space=pltpu.VMEM)],
        out_specs=pl.BlockSpec(memory_space=pltpu.VMEM),
        scratch_shapes=exchange_scratch(x, mode, size),
        compiler_params=pltpu.CompilerParams(collective_id=collective_id, has_side_effects=True),
    )(x)


def pair_targets(chips):
    me, member = group_of("row", 2, chips)
    _, sibling = group_of("row", 1, 2)
    return [member(lax.rem(me + d, chips)) for d in range(1, chips)], sibling


def far_first(size):
    return sorted(range(1, size), key=lambda d: -min(d, size - d))


def row_gather_kernel(chips, x_ref, o_ref, send_sems, recv_sems, fwd_send, fwd_recv):
    z_me, z_member = group_of("row", 2, chips)
    c_me, core_member = group_of("row", 1, 2)
    sibling = core_member(1 - c_me)
    peers, _ = pair_targets(chips)
    enter(peers + [sibling])
    copies = []
    for d in far_first(chips):
        peer = lax.rem(z_me + d, chips)
        copy = pltpu.make_async_remote_copy(
            src_ref=x_ref, dst_ref=o_ref.at[c_me, z_me], send_sem=send_sems.at[d],
            recv_sem=recv_sems.at[z_me], device_id=z_member(peer),
            device_id_type=pl.DeviceIdType.MESH)
        copy.start()
        copies.append(copy)
    own = pltpu.make_async_remote_copy(
        src_ref=x_ref, dst_ref=o_ref.at[c_me, z_me], send_sem=fwd_send.at[z_me],
        recv_sem=fwd_recv.at[z_me], device_id=sibling, device_id_type=pl.DeviceIdType.MESH)
    own.start()
    copies.append(own)
    o_ref[c_me, z_me] = x_ref[...]
    for d in range(1, chips):
        src_dev = lax.rem(z_me + chips - d, chips)
        incoming = pltpu.make_async_remote_copy(
            src_ref=o_ref.at[c_me, src_dev], dst_ref=o_ref.at[c_me, src_dev],
            send_sem=send_sems.at[d], recv_sem=recv_sems.at[src_dev],
            device_id=z_member(src_dev), device_id_type=pl.DeviceIdType.MESH)
        incoming.wait_recv()
        forward = pltpu.make_async_remote_copy(
            src_ref=o_ref.at[c_me, src_dev], dst_ref=o_ref.at[c_me, src_dev],
            send_sem=fwd_send.at[src_dev], recv_sem=fwd_recv.at[src_dev], device_id=sibling,
            device_id_type=pl.DeviceIdType.MESH)
        forward.start()
        copies.append(forward)
    for k in range(chips):
        incoming = pltpu.make_async_remote_copy(
            src_ref=o_ref.at[1 - c_me, k], dst_ref=o_ref.at[1 - c_me, k],
            send_sem=fwd_send.at[k], recv_sem=fwd_recv.at[k], device_id=sibling,
            device_id_type=pl.DeviceIdType.MESH)
        incoming.wait_recv()
    for copy in copies:
        copy.wait_send()


def row_gather(x, chips, collective_id):
    return pl.pallas_call(
        functools.partial(row_gather_kernel, chips),
        out_shape=jax.ShapeDtypeStruct((2, chips) + x.shape, x.dtype),
        in_specs=[pl.BlockSpec(memory_space=pltpu.VMEM)],
        out_specs=pl.BlockSpec(memory_space=pltpu.VMEM),
        scratch_shapes=[pltpu.SemaphoreType.DMA((chips,))] * 4,
        compiler_params=pltpu.CompilerParams(collective_id=collective_id, has_side_effects=True),
    )(x)


def row_scatter_kernel(chips, x_ref, o_ref, pair_recv, pair_sum, z_recv,
                       pair_send_sems, pair_recv_sems, z_send_sems, z_recv_sems):
    z_me, z_member = group_of("row", 2, chips)
    c_me, core_member = group_of("row", 1, 2)
    sibling = core_member(1 - c_me)
    peers, _ = pair_targets(chips)
    enter(peers + [sibling])
    copies = []
    for k in range(chips):
        copy = pltpu.make_async_remote_copy(
            src_ref=x_ref.at[1 - c_me, k], dst_ref=pair_recv.at[k], send_sem=pair_send_sems.at[k],
            recv_sem=pair_recv_sems.at[k], device_id=sibling, device_id_type=pl.DeviceIdType.MESH)
        copy.start()
        copies.append(copy)
    offsets = far_first(chips)
    order = [lax.rem(z_me + d, chips) for d in offsets] + [z_me]
    for d, k in zip(offsets + [chips], order):
        incoming = pltpu.make_async_remote_copy(
            src_ref=pair_recv.at[k], dst_ref=pair_recv.at[k], send_sem=pair_send_sems.at[k],
            recv_sem=pair_recv_sems.at[k], device_id=sibling, device_id_type=pl.DeviceIdType.MESH)
        incoming.wait_recv()
        pair_sum[k] = (x_ref[c_me, k].astype(jnp.float32)
                       + pair_recv[k].astype(jnp.float32)).astype(pair_sum.dtype)
        if d < chips:
            copy = pltpu.make_async_remote_copy(
                src_ref=pair_sum.at[k], dst_ref=z_recv.at[z_me], send_sem=z_send_sems.at[d],
                recv_sem=z_recv_sems.at[z_me], device_id=z_member(k),
                device_id_type=pl.DeviceIdType.MESH)
            copy.start()
            copies.append(copy)
    total = pair_sum[z_me].astype(jnp.float32)
    for d in range(1, chips):
        src_dev = lax.rem(z_me + chips - d, chips)
        incoming = pltpu.make_async_remote_copy(
            src_ref=z_recv.at[src_dev], dst_ref=z_recv.at[src_dev], send_sem=z_send_sems.at[d],
            recv_sem=z_recv_sems.at[src_dev], device_id=z_member(src_dev),
            device_id_type=pl.DeviceIdType.MESH)
        incoming.wait_recv()
        total = total + z_recv[src_dev].astype(jnp.float32)
    for copy in copies:
        copy.wait_send()
    o_ref[...] = total.astype(o_ref.dtype)


def row_scatter(x, chips, collective_id):
    block = x.shape[2:]
    return pl.pallas_call(
        functools.partial(row_scatter_kernel, chips),
        out_shape=jax.ShapeDtypeStruct(block, x.dtype),
        in_specs=[pl.BlockSpec(memory_space=pltpu.VMEM)],
        out_specs=pl.BlockSpec(memory_space=pltpu.VMEM),
        scratch_shapes=[pltpu.VMEM((chips,) + block, x.dtype)] * 3
        + [pltpu.SemaphoreType.DMA((chips,))] * 4,
        compiler_params=pltpu.CompilerParams(collective_id=collective_id, has_side_effects=True),
    )(x)


def feat_push(value_ref, halves_ref, send_sems, recv_sems, slot):
    n = lax.axis_size("feat")
    me = lax.axis_index("feat")
    halves_ref[me] = value_ref[...]
    copies = []
    for d in range(1, n):
        peer = lax.rem(me + d, n)
        copy = pltpu.make_async_remote_copy(
            src_ref=halves_ref.at[me], dst_ref=halves_ref.at[me], send_sem=send_sems.at[slot, d],
            recv_sem=recv_sems.at[slot, me], device_id=mesh_coords("feat", peer),
            device_id_type=pl.DeviceIdType.MESH)
        copy.start()
        copies.append(copy)
    for d in range(1, n):
        src_dev = lax.rem(me + n - d, n)
        pltpu.make_async_remote_copy(
            src_ref=halves_ref.at[src_dev], dst_ref=halves_ref.at[src_dev],
            send_sem=send_sems.at[slot, d], recv_sem=recv_sems.at[slot, src_dev],
            device_id=mesh_coords("feat", src_dev), device_id_type=pl.DeviceIdType.MESH).wait_recv()
    for copy in copies:
        copy.wait_send()


def layer_kernel(x_ref, w_ref, wr_ref, cot_ref, hidden_ref, panel_ref, sum_ref,
                 recv_ref, send_sems, recv_sems, summed_ref, agg_ref, grad_out_ref, grad_ref,
                 f_send, f_recv, term_ref, spread_ref, g_send, g_recv, *reduce_scratch):
    n_col = lax.axis_size("col")
    n_feat = lax.axis_size("feat")
    me = lax.axis_index("feat")
    peers = [mesh_coords("feat", lax.rem(me + d, n_feat)) for d in range(1, n_feat)]
    radix = len(reduce_scratch) == 4
    others = reduce_radix_targets() if radix else reduce_targets(term_ref.shape[0])
    enter(exchange_targets("col", 1, n_col) + peers + exchange_targets("col", 1, n_col) + others)
    copies = exchange_start("col", 1, n_col, "scatter", x_ref, recv_ref, send_sems, recv_sems)
    exchange_finish("col", 1, n_col, "scatter", x_ref, summed_ref, recv_ref, send_sems, recv_sems,
                    copies)
    feat_push(summed_ref, agg_ref, f_send, f_recv, 0)
    half = agg_ref.shape[-1]
    hidden = jnp.dot(agg_ref[0], w_ref[pl.ds(0, half), :], preferred_element_type=jnp.float32)
    for h in range(1, n_feat):
        hidden = hidden + jnp.dot(agg_ref[h], w_ref[pl.ds(h * half, half), :],
                                  preferred_element_type=jnp.float32)
    hidden_ref[...] = hidden
    slope = jnp.where(hidden > 0, 1.0, jnp.exp(jnp.minimum(hidden, 0.0)))
    grad_out_ref[...] = (cot_ref[...].astype(jnp.float32) * slope).astype(grad_out_ref.dtype)
    feat_push(grad_out_ref, grad_ref, f_send, f_recv, 1)
    spread = None
    for h in range(n_feat):
        columns = pl.ds(h * half, half)
        term_ref[:, columns] = lax.dot_general(
            summed_ref[...], grad_ref[h], (((0,), (0,)), ((), ())),
            preferred_element_type=jnp.float32)
        part = lax.dot_general(grad_ref[h], wr_ref[:, columns], (((1,), (1,)), ((), ())),
                               preferred_element_type=jnp.float32)
        spread = part if spread is None else spread + part
    spread_ref[...] = spread.astype(spread_ref.dtype)
    copies = exchange_start("col", 1, n_col, "gather", spread_ref, panel_ref, g_send, g_recv)
    if radix:
        reduce_radix(term_ref, sum_ref, *reduce_scratch)
    else:
        reduce_rounds(term_ref, sum_ref, *reduce_scratch)
    exchange_finish("col", 1, n_col, "gather", spread_ref, panel_ref, panel_ref, g_send, g_recv,
                    copies)


def layer_step(partials, weight_cols, weight_rows, cotangent, collective_id):
    n_col = lax.axis_size("col")
    n_feat = lax.axis_size("feat")
    block = partials.shape[1:]
    half = block[-1]
    term = jax.ShapeDtypeStruct((half, n_feat * half), jnp.float32)
    reduce_space = radix_scratch(term) if radix_fits(term) else reduce_scratch(term)
    vmem = pl.BlockSpec(memory_space=pltpu.VMEM)
    return pl.pallas_call(
        layer_kernel,
        out_shape=(
            jax.ShapeDtypeStruct(block, jnp.float32),
            jax.ShapeDtypeStruct((n_col,) + block, jnp.bfloat16),
            term,
        ),
        in_specs=[vmem] * 4,
        out_specs=(vmem,) * 3,
        scratch_shapes=exchange_scratch(partials, "scatter", n_col) + [
            pltpu.VMEM(block, partials.dtype),
            pltpu.VMEM((n_feat,) + block, partials.dtype),
            pltpu.VMEM(block, jnp.bfloat16),
            pltpu.VMEM((n_feat,) + block, jnp.bfloat16),
            pltpu.SemaphoreType.DMA((2, n_feat)),
            pltpu.SemaphoreType.DMA((2, n_feat)),
            pltpu.VMEM(term.shape, term.dtype),
            pltpu.VMEM(block, jnp.bfloat16),
            pltpu.SemaphoreType.DMA((n_col,)),
            pltpu.SemaphoreType.DMA((n_col,)),
        ] + reduce_space,
        compiler_params=pltpu.CompilerParams(collective_id=collective_id, has_side_effects=True),
    )(partials, weight_cols, weight_rows, cotangent)


def reduction_plan(rows):
    pairs = []
    for bit in (1, 2, 4, 8, 16, 32, 64):
        for axis in ("row", "col"):
            if bit < lax.axis_size(axis):
                pairs.append((axis, bit))
    halving = []
    while pairs and rows // 2 >= 8 and rows % 16 == 0:
        halving.append(pairs.pop(0))
        rows //= 2
    return halving, pairs


def bitval(axis, bit):
    return (lax.axis_index(axis) // bit) % 2


def partner(axis, bit):
    return mesh_coords(axis, lax.axis_index(axis) + bit * (1 - 2 * bitval(axis, bit)))


def reduce_targets(rows):
    halving, whole = reduction_plan(rows)
    return [partner(axis, bit) for axis, bit in halving + whole]


def reduce_rounds(x_ref, o_ref, recv, send_sems, recv_sems):
    halving, whole = reduction_plan(x_ref.shape[0])
    o_ref[...] = x_ref[...]
    k = 0

    def swap(k, axis, bit, send_rows, length):
        copy = pltpu.make_async_remote_copy(
            src_ref=o_ref.at[pl.ds(send_rows, length)], dst_ref=recv.at[k, pl.ds(0, length)],
            send_sem=send_sems.at[k], recv_sem=recv_sems.at[k],
            device_id=partner(axis, bit), device_id_type=pl.DeviceIdType.MESH)
        copy.start()
        copy.wait()

    lo = jnp.int32(0)
    length = x_ref.shape[0]
    starts = []
    for axis, bit in halving:
        length //= 2
        mine = bitval(axis, bit)
        starts.append(lo)
        keep = pl.multiple_of(lo + mine * length, 8)
        give = pl.multiple_of(lo + (1 - mine) * length, 8)
        swap(k, axis, bit, give, length)
        o_ref[pl.ds(keep, length)] = o_ref[pl.ds(keep, length)] + recv[k, pl.ds(0, length)]
        lo = keep
        k += 1
    for axis, bit in whole:
        swap(k, axis, bit, lo, length)
        o_ref[pl.ds(lo, length)] = o_ref[pl.ds(lo, length)] + recv[k, pl.ds(0, length)]
        k += 1
    for (axis, bit), base in zip(reversed(halving), reversed(starts)):
        mine = bitval(axis, bit)
        other = pl.multiple_of(base + (1 - mine) * length, 8)
        swap(k, axis, bit, lo, length)
        o_ref[pl.ds(other, length)] = recv[k, pl.ds(0, length)]
        lo = base
        length *= 2
        k += 1


def reduce_scratch(w):
    halving, whole = reduction_plan(w.shape[0])
    steps = 2 * len(halving) + len(whole)
    return [
        pltpu.VMEM((steps, w.shape[0] // 2) + w.shape[1:], w.dtype),
        pltpu.SemaphoreType.DMA((steps,)),
        pltpu.SemaphoreType.DMA((steps,)),
    ]


def radix_groups():
    n_row, n_col = lax.axis_size("row"), lax.axis_size("col")
    if n_row % 2 or n_col % 4:
        return None
    return ((("row", 1, 2), ("col", 1, 4)), ("row", 2, n_row // 2), ("col", 4, n_col // 4))


def first_group():
    (core, ring), _, _ = radix_groups()
    me_a, _ = group_of(*core)
    me_b, _ = group_of(*ring)
    size = core[2] * ring[2]
    me = me_a + core[2] * me_b
    row = lax.axis_index("row") - me_a * core[1]
    col = lax.axis_index("col") - me_b * ring[1]

    def member(m):
        return (row + (m % core[2]) * core[1], col + (m // core[2]) * ring[1], lax.axis_index("feat"))

    return me, size, member


def reduce_radix_targets():
    me, size, member = first_group()
    targets = [member(lax.rem(me + d, size)) for d in range(1, size)]
    _, z_group, x_group = radix_groups()
    return targets + exchange_targets(*z_group) + exchange_targets(*x_group)


def ordered_allreduce(group, value, recv, send_sems, recv_sems):
    axis, stride, size = group
    me, member = group_of(axis, stride, size)
    recv[me] = value
    copies = []
    for d in range(1, size):
        peer = lax.rem(me + d, size)
        copy = pltpu.make_async_remote_copy(
            src_ref=recv.at[me], dst_ref=recv.at[me], send_sem=send_sems.at[d],
            recv_sem=recv_sems.at[me], device_id=member(peer), device_id_type=pl.DeviceIdType.MESH)
        copy.start()
        copies.append(copy)
    for d in range(1, size):
        src_dev = lax.rem(me + size - d, size)
        pltpu.make_async_remote_copy(
            src_ref=recv.at[src_dev], dst_ref=recv.at[src_dev], send_sem=send_sems.at[d],
            recv_sem=recv_sems.at[src_dev], device_id=member(src_dev),
            device_id_type=pl.DeviceIdType.MESH).wait_recv()
    for copy in copies:
        copy.wait_send()
    total = recv[0]
    for k in range(1, size):
        total = total + recv[k]
    return total


def reduce_radix(w_ref, o_ref, seg_recv, z_recv, x_recv, sems):
    _, z_group, x_group = radix_groups()
    me, size, member = first_group()
    seg = w_ref.shape[0] // size
    mine = pl.ds(pl.multiple_of(me * seg, 8), seg)
    copies = []
    for d in range(1, size):
        peer = lax.rem(me + d, size)
        copy = pltpu.make_async_remote_copy(
            src_ref=w_ref.at[pl.ds(pl.multiple_of(peer * seg, 8), seg)], dst_ref=seg_recv.at[me],
            send_sem=sems.at[0, d], recv_sem=sems.at[1, me], device_id=member(peer),
            device_id_type=pl.DeviceIdType.MESH)
        copy.start()
        copies.append(copy)
    total = w_ref[mine]
    for d in range(1, size):
        src_dev = lax.rem(me + size - d, size)
        pltpu.make_async_remote_copy(
            src_ref=seg_recv.at[src_dev], dst_ref=seg_recv.at[src_dev], send_sem=sems.at[0, d],
            recv_sem=sems.at[1, src_dev], device_id=member(src_dev),
            device_id_type=pl.DeviceIdType.MESH).wait_recv()
        total = total + seg_recv[src_dev]
    for copy in copies:
        copy.wait_send()
    total = ordered_allreduce(z_group, total, z_recv, sems.at[2], sems.at[3])
    total = ordered_allreduce(x_group, total, x_recv, sems.at[4], sems.at[5])
    o_ref[mine] = total
    copies = []
    for d in range(1, size):
        peer = lax.rem(me + d, size)
        copy = pltpu.make_async_remote_copy(
            src_ref=o_ref.at[mine], dst_ref=o_ref.at[mine], send_sem=sems.at[6, d],
            recv_sem=sems.at[7, me], device_id=member(peer), device_id_type=pl.DeviceIdType.MESH)
        copy.start()
        copies.append(copy)
    for d in range(1, size):
        src_dev = lax.rem(me + size - d, size)
        rows = pl.ds(pl.multiple_of(src_dev * seg, 8), seg)
        pltpu.make_async_remote_copy(
            src_ref=o_ref.at[rows], dst_ref=o_ref.at[rows], send_sem=sems.at[6, d],
            recv_sem=sems.at[7, src_dev], device_id=member(src_dev),
            device_id_type=pl.DeviceIdType.MESH).wait_recv()
    for copy in copies:
        copy.wait_send()


def radix_scratch(w):
    (core, ring), z_group, x_group = radix_groups()
    size = core[2] * ring[2]
    seg = (w.shape[0] // size,) + w.shape[1:]
    width = max(size, z_group[2], x_group[2])
    return [
        pltpu.VMEM((size,) + seg, w.dtype),
        pltpu.VMEM((z_group[2],) + seg, w.dtype),
        pltpu.VMEM((x_group[2],) + seg, w.dtype),
        pltpu.SemaphoreType.DMA((8, width)),
    ]


def radix_fits(w):
    groups = radix_groups()
    if groups is None:
        return False
    size = groups[0][0][2] * groups[0][1][2]
    return w.shape[0] % (8 * size) == 0


def gather_radix_kernel(axis, x_ref, w_ref, o_ref, ow_ref, g_send, g_recv, *scratch):
    size = lax.axis_size(axis)
    enter(exchange_targets(axis, 1, size) + reduce_radix_targets())
    copies = exchange_start(axis, 1, size, "gather", x_ref, o_ref, g_send, g_recv)
    reduce_radix(w_ref, ow_ref, *scratch)
    exchange_finish(axis, 1, size, "gather", x_ref, o_ref, o_ref, g_send, g_recv, copies)


def gather_reduce_kernel(axis, x_ref, w_ref, o_ref, ow_ref, g_send, g_recv, recv, send_sems, recv_sems):
    size = lax.axis_size(axis)
    enter(exchange_targets(axis, 1, size) + reduce_targets(w_ref.shape[0]))
    copies = exchange_start(axis, 1, size, "gather", x_ref, o_ref, g_send, g_recv)
    reduce_rounds(w_ref, ow_ref, recv, send_sems, recv_sems)
    exchange_finish(axis, 1, size, "gather", x_ref, o_ref, o_ref, g_send, g_recv, copies)


def gather_and_reduce(x, w, axis, collective_id):
    size = lax.axis_size(axis)
    if radix_fits(w):
        kernel, scratch = gather_radix_kernel, radix_scratch(w)
    else:
        kernel, scratch = gather_reduce_kernel, reduce_scratch(w)
    return pl.pallas_call(
        functools.partial(kernel, axis),
        out_shape=(exchange_shape(x, "gather", size), jax.ShapeDtypeStruct(w.shape, w.dtype)),
        in_specs=[pl.BlockSpec(memory_space=pltpu.VMEM)] * 2,
        out_specs=(pl.BlockSpec(memory_space=pltpu.VMEM),) * 2,
        scratch_shapes=exchange_scratch(x, "gather", size) + scratch,
        compiler_params=pltpu.CompilerParams(collective_id=collective_id, has_side_effects=True),
    )(x, w)


def shards(features, tile_rows, tile_cols, tile_count, tile_values, weights, cotangent):
    width = tile_values.shape[-1]
    local_tiles = tile_values[0, 0]
    block_rows = tile_rows[0, 0]
    block_cols = tile_cols[0, 0]
    count = tile_count[0, 0].reshape(1)
    n_rowdev = lax.axis_size("row")
    n_coldev = lax.axis_size("col")
    local_blocks = features.shape[0] // width
    feat_half = features.shape[1]
    feat_index = lax.axis_index("feat")
    row_blocks = local_blocks * n_coldev
    col_blocks = local_blocks * n_rowdev
    node_total = features.shape[0] * n_rowdev * n_coldev
    pair = 2 if n_rowdev % 2 == 0 else 1
    chips = n_rowdev // pair
    if pair == 2:
        panel = row_gather(features, chips, 0).reshape(-1, feat_half)
    else:
        panel = exchange(features, "row", "gather", 0).reshape(-1, feat_half)
    owner = block_cols // local_blocks
    block_cols = ((owner % pair) * chips + owner // pair) * local_blocks + block_cols % local_blocks
    partial_value = tile_products(local_tiles, block_rows, block_cols, count, panel,
                                  row_blocks, transpose=False)
    weight_cols = lax.dynamic_slice_in_dim(weights, feat_index * feat_half, feat_half, 1)
    weight_rows = lax.dynamic_slice_in_dim(weights, feat_index * feat_half, feat_half, 0)
    hidden, spread_panel, weight_sum = layer_step(partial_value.reshape(n_coldev, -1, feat_half),
                                                  weight_cols, weight_rows, cotangent, 1)
    negative = jnp.minimum(hidden, 0.0)
    activated = jnp.where(hidden > 0, hidden, jnp.expm1(negative)).astype(jnp.bfloat16)
    spread_panel = spread_panel.reshape(-1, feat_half)
    weight_grad = weight_sum * node_total ** (-0.5)
    back_partial = tile_products(local_tiles, block_rows, block_cols, count, spread_panel,
                                 col_blocks, transpose=True)
    if pair == 2:
        back_summed = row_scatter(back_partial.reshape(pair, chips, -1, feat_half), chips, 3)
    else:
        back_summed = exchange(back_partial.reshape(n_rowdev, -1, feat_half), "row", "scatter", 3)
    return (activated, back_summed, weight_grad)


def solution(mesh):
    return jax.shard_map(
        shards,
        mesh=mesh,
        in_specs=(
            P(("col", "row"), "feat"),
            P("row", "col", None),
            P("row", "col", None),
            P("row", "col"),
            P("row", "col", None, None, None),
            P(),
            P(("row", "col"), "feat"),
        ),
        out_specs=(P(("row", "col"), "feat"), P(("col", "row"), "feat"), P("feat", None)),
        check_vma=False,
    )
```

```python
import functools

import jax
import jax.numpy as jnp
from jax import lax
from jax.experimental import pallas as pl
from jax.experimental.pallas import tpu as pltpu
from jax.sharding import PartitionSpec as P

GROUP = 64


def tile_kernel(transpose, rows_ref, cols_ref, count_ref, tiles_ref, panel_ref, out_ref, acc_ref):
    step = pl.program_id(0)
    width = tiles_ref.shape[-1]
    count = count_ref[0]
    src_blocks = panel_ref.shape[0] // width
    dst_blocks = acc_ref.shape[0] // width

    @pl.when(step == 0)
    def _():
        acc_ref[...] = jnp.zeros_like(acc_ref)

    @pl.when(step * GROUP < count)
    def _():
        terms = []
        for j in range(GROUP):
            slot = step * GROUP + j
            src = rows_ref[slot] if transpose else cols_ref[slot]
            src = jnp.minimum(jnp.maximum(src, 0), src_blocks - 1)
            block = panel_ref[pl.ds(pl.multiple_of(src * width, width), width), :]
            tile = tiles_ref[j]
            if transpose:
                term = lax.dot_general(tile, block, (((0,), (0,)), ((), ())),
                                       preferred_element_type=jnp.float32)
            else:
                term = jnp.dot(tile, block, preferred_element_type=jnp.float32)
            terms.append(jnp.where(slot < count, term, 0.0))
        for j in range(GROUP):
            slot = step * GROUP + j
            dst = cols_ref[slot] if transpose else rows_ref[slot]
            dst = jnp.minimum(jnp.maximum(dst, 0), dst_blocks - 1)
            rows = pl.ds(pl.multiple_of(dst * width, width), width)
            acc_ref[rows, :] += terms[j]

    @pl.when(step == pl.num_programs(0) - 1)
    def _():
        out_ref[...] = acc_ref[...].astype(out_ref.dtype)


def tile_products(tiles, rows, cols, count, panel, out_blocks, transpose):
    slots, width, _ = tiles.shape
    feat = panel.shape[1]
    steps = slots // GROUP

    def tiles_map(i, rows_ref, cols_ref, count_ref):
        last = jnp.maximum(count_ref[0] - 1, 0) // GROUP
        return (jnp.minimum(i, last), 0, 0)

    return pl.pallas_call(
        functools.partial(tile_kernel, transpose),
        out_shape=jax.ShapeDtypeStruct((out_blocks * width, feat), jnp.bfloat16),
        grid_spec=pltpu.PrefetchScalarGridSpec(
            num_scalar_prefetch=3,
            grid=(steps,),
            in_specs=[
                pl.BlockSpec((GROUP, width, width), tiles_map),
                pl.BlockSpec(panel.shape, lambda i, *_: (0, 0)),
            ],
            out_specs=pl.BlockSpec((out_blocks * width, feat), lambda i, *_: (0, 0)),
            scratch_shapes=[pltpu.VMEM((out_blocks * width, feat), jnp.float32)],
        ),
        compiler_params=pltpu.CompilerParams(dimension_semantics=("arbitrary",)),
        cost_estimate=pl.CostEstimate(
            flops=2 * slots * width * width * feat,
            bytes_accessed=tiles.size * 2 + panel.size * 2 + out_blocks * width * feat * 2,
            transcendentals=0,
        ),
    )(rows, cols, count, tiles, panel)


def mesh_coords(axis, peer):
    return tuple(peer if name == axis else lax.axis_index(name) for name in ("row", "col", "feat"))


def group_of(axis, stride, size):
    index = lax.axis_index(axis)
    me = (index // stride) % size
    base = index - me * stride
    return me, lambda k: mesh_coords(axis, base + k * stride)


def exchange_targets(axis, stride, size):
    me, member = group_of(axis, stride, size)
    return [member(lax.rem(me + d, size)) for d in range(1, size)]


def enter(targets):
    barrier = pltpu.get_barrier_semaphore()
    for target in targets:
        pl.semaphore_signal(barrier, inc=1, device_id=target, device_id_type=pl.DeviceIdType.MESH)
    pl.semaphore_wait(barrier, len(targets))


def exchange_start(axis, stride, size, mode, x_ref, recv_ref, send_sems, recv_sems):
    me, member = group_of(axis, stride, size)
    copies = []
    for d in range(1, size):
        peer = lax.rem(me + d, size)
        src = x_ref if mode == "gather" else x_ref.at[peer]
        copy = pltpu.make_async_remote_copy(
            src_ref=src, dst_ref=recv_ref.at[me], send_sem=send_sems.at[d],
            recv_sem=recv_sems.at[me], device_id=member(peer),
            device_id_type=pl.DeviceIdType.MESH)
        copy.start()
        copies.append(copy)
    return copies


def exchange_finish(axis, stride, size, mode, x_ref, o_ref, recv_ref, send_sems, recv_sems, copies):
    me, member = group_of(axis, stride, size)
    if mode == "gather":
        o_ref[me] = x_ref[...]
    else:
        total = x_ref[me].astype(jnp.float32)
    for d in range(1, size):
        src_dev = lax.rem(me + size - d, size)
        incoming = pltpu.make_async_remote_copy(
            src_ref=recv_ref.at[src_dev], dst_ref=recv_ref.at[src_dev], send_sem=send_sems.at[d],
            recv_sem=recv_sems.at[src_dev], device_id=member(src_dev),
            device_id_type=pl.DeviceIdType.MESH)
        incoming.wait_recv()
        if mode != "gather":
            total = total + recv_ref[src_dev].astype(jnp.float32)
    for copy in copies:
        copy.wait_send()
    if mode != "gather":
        o_ref[...] = total.astype(o_ref.dtype)


def exchange_kernel(axis, stride, size, mode, x_ref, o_ref, *scratch):
    if mode == "gather":
        recv_ref, (send_sems, recv_sems) = o_ref, scratch
    else:
        recv_ref, send_sems, recv_sems = scratch
    enter(exchange_targets(axis, stride, size))
    copies = exchange_start(axis, stride, size, mode, x_ref, recv_ref, send_sems, recv_sems)
    exchange_finish(axis, stride, size, mode, x_ref, o_ref, recv_ref, send_sems, recv_sems, copies)


def exchange_scratch(x, mode, size):
    scratch = [] if mode == "gather" else [pltpu.VMEM(x.shape, x.dtype)]
    return scratch + [pltpu.SemaphoreType.DMA((size,)), pltpu.SemaphoreType.DMA((size,))]


def exchange_shape(x, mode, size):
    shape = (size,) + x.shape if mode == "gather" else x.shape[1:]
    return jax.ShapeDtypeStruct(shape, x.dtype)


def exchange(x, axis, mode, collective_id, stride=1, size=None):
    size = lax.axis_size(axis) if size is None else size
    return pl.pallas_call(
        functools.partial(exchange_kernel, axis, stride, size, mode),
        out_shape=exchange_shape(x, mode, size),
        in_specs=[pl.BlockSpec(memory_space=pltpu.VMEM)],
        out_specs=pl.BlockSpec(memory_space=pltpu.VMEM),
        scratch_shapes=exchange_scratch(x, mode, size),
        compiler_params=pltpu.CompilerParams(collective_id=collective_id, has_side_effects=True),
    )(x)


def pair_targets(chips):
    me, member = group_of("row", 2, chips)
    _, sibling = group_of("row", 1, 2)
    return [member(lax.rem(me + d, chips)) for d in range(1, chips)], sibling


def row_gather_kernel(chips, x_ref, o_ref, send_sems, recv_sems, fwd_send, fwd_recv):
    z_me, z_member = group_of("row", 2, chips)
    c_me, core_member = group_of("row", 1, 2)
    sibling = core_member(1 - c_me)
    peers, _ = pair_targets(chips)
    enter(peers + [sibling])
    copies = []
    for d in range(1, chips):
        peer = lax.rem(z_me + d, chips)
        copy = pltpu.make_async_remote_copy(
            src_ref=x_ref, dst_ref=o_ref.at[c_me, z_me], send_sem=send_sems.at[d],
            recv_sem=recv_sems.at[z_me], device_id=z_member(peer),
            device_id_type=pl.DeviceIdType.MESH)
        copy.start()
        copies.append(copy)
    own = pltpu.make_async_remote_copy(
        src_ref=x_ref, dst_ref=o_ref.at[c_me, z_me], send_sem=fwd_send.at[z_me],
        recv_sem=fwd_recv.at[z_me], device_id=sibling, device_id_type=pl.DeviceIdType.MESH)
    own.start()
    copies.append(own)
    o_ref[c_me, z_me] = x_ref[...]
    for d in range(1, chips):
        src_dev = lax.rem(z_me + chips - d, chips)
        incoming = pltpu.make_async_remote_copy(
            src_ref=o_ref.at[c_me, src_dev], dst_ref=o_ref.at[c_me, src_dev],
            send_sem=send_sems.at[d], recv_sem=recv_sems.at[src_dev],
            device_id=z_member(src_dev), device_id_type=pl.DeviceIdType.MESH)
        incoming.wait_recv()
        forward = pltpu.make_async_remote_copy(
            src_ref=o_ref.at[c_me, src_dev], dst_ref=o_ref.at[c_me, src_dev],
            send_sem=fwd_send.at[src_dev], recv_sem=fwd_recv.at[src_dev], device_id=sibling,
            device_id_type=pl.DeviceIdType.MESH)
        forward.start()
        copies.append(forward)
    for k in range(chips):
        incoming = pltpu.make_async_remote_copy(
            src_ref=o_ref.at[1 - c_me, k], dst_ref=o_ref.at[1 - c_me, k],
            send_sem=fwd_send.at[k], recv_sem=fwd_recv.at[k], device_id=sibling,
            device_id_type=pl.DeviceIdType.MESH)
        incoming.wait_recv()
    for copy in copies:
        copy.wait_send()


def row_gather(x, chips, collective_id):
    return pl.pallas_call(
        functools.partial(row_gather_kernel, chips),
        out_shape=jax.ShapeDtypeStruct((2, chips) + x.shape, x.dtype),
        in_specs=[pl.BlockSpec(memory_space=pltpu.VMEM)],
        out_specs=pl.BlockSpec(memory_space=pltpu.VMEM),
        scratch_shapes=[pltpu.SemaphoreType.DMA((chips,))] * 4,
        compiler_params=pltpu.CompilerParams(collective_id=collective_id, has_side_effects=True),
    )(x)


def row_scatter_kernel(chips, x_ref, o_ref, pair_recv, pair_sum, z_recv,
                       pair_send_sems, pair_recv_sems, z_send_sems, z_recv_sems):
    z_me, z_member = group_of("row", 2, chips)
    c_me, core_member = group_of("row", 1, 2)
    sibling = core_member(1 - c_me)
    peers, _ = pair_targets(chips)
    enter(peers + [sibling])
    copies = []
    for k in range(chips):
        copy = pltpu.make_async_remote_copy(
            src_ref=x_ref.at[1 - c_me, k], dst_ref=pair_recv.at[k], send_sem=pair_send_sems.at[k],
            recv_sem=pair_recv_sems.at[k], device_id=sibling, device_id_type=pl.DeviceIdType.MESH)
        copy.start()
        copies.append(copy)
    order = [lax.rem(z_me + d, chips) for d in range(1, chips)] + [z_me]
    for d, k in enumerate(order, start=1):
        incoming = pltpu.make_async_remote_copy(
            src_ref=pair_recv.at[k], dst_ref=pair_recv.at[k], send_sem=pair_send_sems.at[k],
            recv_sem=pair_recv_sems.at[k], device_id=sibling, device_id_type=pl.DeviceIdType.MESH)
        incoming.wait_recv()
        pair_sum[k] = (x_ref[c_me, k].astype(jnp.float32)
                       + pair_recv[k].astype(jnp.float32)).astype(pair_sum.dtype)
        if d < chips:
            copy = pltpu.make_async_remote_copy(
                src_ref=pair_sum.at[k], dst_ref=z_recv.at[z_me], send_sem=z_send_sems.at[d],
                recv_sem=z_recv_sems.at[z_me], device_id=z_member(k),
                device_id_type=pl.DeviceIdType.MESH)
            copy.start()
            copies.append(copy)
    total = pair_sum[z_me].astype(jnp.float32)
    for d in range(1, chips):
        src_dev = lax.rem(z_me + chips - d, chips)
        incoming = pltpu.make_async_remote_copy(
            src_ref=z_recv.at[src_dev], dst_ref=z_recv.at[src_dev], send_sem=z_send_sems.at[d],
            recv_sem=z_recv_sems.at[src_dev], device_id=z_member(src_dev),
            device_id_type=pl.DeviceIdType.MESH)
        incoming.wait_recv()
        total = total + z_recv[src_dev].astype(jnp.float32)
    for copy in copies:
        copy.wait_send()
    o_ref[...] = total.astype(o_ref.dtype)


def row_scatter(x, chips, collective_id):
    block = x.shape[2:]
    return pl.pallas_call(
        functools.partial(row_scatter_kernel, chips),
        out_shape=jax.ShapeDtypeStruct(block, x.dtype),
        in_specs=[pl.BlockSpec(memory_space=pltpu.VMEM)],
        out_specs=pl.BlockSpec(memory_space=pltpu.VMEM),
        scratch_shapes=[pltpu.VMEM((chips,) + block, x.dtype)] * 3
        + [pltpu.SemaphoreType.DMA((chips,))] * 4,
        compiler_params=pltpu.CompilerParams(collective_id=collective_id, has_side_effects=True),
    )(x)


def feat_push(value_ref, halves_ref, send_sems, recv_sems, slot):
    n = lax.axis_size("feat")
    me = lax.axis_index("feat")
    halves_ref[me] = value_ref[...]
    copies = []
    for d in range(1, n):
        peer = lax.rem(me + d, n)
        copy = pltpu.make_async_remote_copy(
            src_ref=halves_ref.at[me], dst_ref=halves_ref.at[me], send_sem=send_sems.at[slot, d],
            recv_sem=recv_sems.at[slot, me], device_id=mesh_coords("feat", peer),
            device_id_type=pl.DeviceIdType.MESH)
        copy.start()
        copies.append(copy)
    for d in range(1, n):
        src_dev = lax.rem(me + n - d, n)
        pltpu.make_async_remote_copy(
            src_ref=halves_ref.at[src_dev], dst_ref=halves_ref.at[src_dev],
            send_sem=send_sems.at[slot, d], recv_sem=recv_sems.at[slot, src_dev],
            device_id=mesh_coords("feat", src_dev), device_id_type=pl.DeviceIdType.MESH).wait_recv()
    for copy in copies:
        copy.wait_send()


def layer_kernel(scale, x_ref, w_ref, wr_ref, cot_ref, hidden_ref, panel_ref, sum_ref,
                 recv_ref, send_sems, recv_sems, summed_ref, agg_ref, grad_out_ref, grad_ref,
                 f_send, f_recv, term_ref, spread_ref, g_send, g_recv, *reduce_scratch):
    n_col = lax.axis_size("col")
    n_feat = lax.axis_size("feat")
    me = lax.axis_index("feat")
    peers = [mesh_coords("feat", lax.rem(me + d, n_feat)) for d in range(1, n_feat)]
    radix = len(reduce_scratch) == 4
    others = reduce_radix_targets() if radix else reduce_targets(term_ref.shape[0])
    enter(exchange_targets("col", 1, n_col) + peers + exchange_targets("col", 1, n_col) + others)
    copies = exchange_start("col", 1, n_col, "scatter", x_ref, recv_ref, send_sems, recv_sems)
    exchange_finish("col", 1, n_col, "scatter", x_ref, summed_ref, recv_ref, send_sems, recv_sems,
                    copies)
    feat_push(summed_ref, agg_ref, f_send, f_recv, 0)
    half = agg_ref.shape[-1]
    hidden = jnp.dot(agg_ref[0], w_ref[pl.ds(0, half), :], preferred_element_type=jnp.float32)
    for h in range(1, n_feat):
        hidden = hidden + jnp.dot(agg_ref[h], w_ref[pl.ds(h * half, half), :],
                                  preferred_element_type=jnp.float32)
    hidden_ref[...] = hidden
    slope = jnp.where(hidden > 0, 1.0, jnp.exp(jnp.minimum(hidden, 0.0)))
    grad_out_ref[...] = (cot_ref[...].astype(jnp.float32) * slope).astype(grad_out_ref.dtype)
    feat_push(grad_out_ref, grad_ref, f_send, f_recv, 1)
    spread = None
    for h in range(n_feat):
        columns = pl.ds(h * half, half)
        term_ref[:, columns] = lax.dot_general(
            summed_ref[...], grad_ref[h], (((0,), (0,)), ((), ())),
            preferred_element_type=jnp.float32)
        part = lax.dot_general(grad_ref[h], wr_ref[:, columns], (((1,), (1,)), ((), ())),
                               preferred_element_type=jnp.float32)
        spread = part if spread is None else spread + part
    spread_ref[...] = spread.astype(spread_ref.dtype)
    copies = exchange_start("col", 1, n_col, "gather", spread_ref, panel_ref, g_send, g_recv)
    if radix:
        reduce_radix(term_ref, sum_ref, *reduce_scratch, scale=scale)
    else:
        reduce_rounds(term_ref, sum_ref, *reduce_scratch)
        sum_ref[...] = sum_ref[...] * scale
    exchange_finish("col", 1, n_col, "gather", spread_ref, panel_ref, panel_ref, g_send, g_recv,
                    copies)


def layer_step(partials, weight_cols, weight_rows, cotangent, collective_id, scale):
    n_col = lax.axis_size("col")
    n_feat = lax.axis_size("feat")
    block = partials.shape[1:]
    half = block[-1]
    term = jax.ShapeDtypeStruct((half, n_feat * half), jnp.float32)
    reduce_space = radix_scratch(term) if radix_fits(term) else reduce_scratch(term)
    vmem = pl.BlockSpec(memory_space=pltpu.VMEM)
    return pl.pallas_call(
        functools.partial(layer_kernel, scale),
        out_shape=(
            jax.ShapeDtypeStruct(block, jnp.float32),
            jax.ShapeDtypeStruct((n_col,) + block, jnp.bfloat16),
            term,
        ),
        in_specs=[vmem] * 4,
        out_specs=(vmem,) * 3,
        scratch_shapes=exchange_scratch(partials, "scatter", n_col) + [
            pltpu.VMEM(block, partials.dtype),
            pltpu.VMEM((n_feat,) + block, partials.dtype),
            pltpu.VMEM(block, jnp.bfloat16),
            pltpu.VMEM((n_feat,) + block, jnp.bfloat16),
            pltpu.SemaphoreType.DMA((2, n_feat)),
            pltpu.SemaphoreType.DMA((2, n_feat)),
            pltpu.VMEM(term.shape, term.dtype),
            pltpu.VMEM(block, jnp.bfloat16),
            pltpu.SemaphoreType.DMA((n_col,)),
            pltpu.SemaphoreType.DMA((n_col,)),
        ] + reduce_space,
        compiler_params=pltpu.CompilerParams(collective_id=collective_id, has_side_effects=True),
    )(partials, weight_cols, weight_rows, cotangent)


def reduction_plan(rows):
    pairs = []
    for bit in (1, 2, 4, 8, 16, 32, 64):
        for axis in ("row", "col"):
            if bit < lax.axis_size(axis):
                pairs.append((axis, bit))
    halving = []
    while pairs and rows // 2 >= 8 and rows % 16 == 0:
        halving.append(pairs.pop(0))
        rows //= 2
    return halving, pairs


def bitval(axis, bit):
    return (lax.axis_index(axis) // bit) % 2


def partner(axis, bit):
    return mesh_coords(axis, lax.axis_index(axis) + bit * (1 - 2 * bitval(axis, bit)))


def reduce_targets(rows):
    halving, whole = reduction_plan(rows)
    return [partner(axis, bit) for axis, bit in halving + whole]


def reduce_rounds(x_ref, o_ref, recv, send_sems, recv_sems):
    halving, whole = reduction_plan(x_ref.shape[0])
    o_ref[...] = x_ref[...]
    k = 0

    def swap(k, axis, bit, send_rows, length):
        copy = pltpu.make_async_remote_copy(
            src_ref=o_ref.at[pl.ds(send_rows, length)], dst_ref=recv.at[k, pl.ds(0, length)],
            send_sem=send_sems.at[k], recv_sem=recv_sems.at[k],
            device_id=partner(axis, bit), device_id_type=pl.DeviceIdType.MESH)
        copy.start()
        copy.wait()

    lo = jnp.int32(0)
    length = x_ref.shape[0]
    starts = []
    for axis, bit in halving:
        length //= 2
        mine = bitval(axis, bit)
        starts.append(lo)
        keep = pl.multiple_of(lo + mine * length, 8)
        give = pl.multiple_of(lo + (1 - mine) * length, 8)
        swap(k, axis, bit, give, length)
        o_ref[pl.ds(keep, length)] = o_ref[pl.ds(keep, length)] + recv[k, pl.ds(0, length)]
        lo = keep
        k += 1
    for axis, bit in whole:
        swap(k, axis, bit, lo, length)
        o_ref[pl.ds(lo, length)] = o_ref[pl.ds(lo, length)] + recv[k, pl.ds(0, length)]
        k += 1
    for (axis, bit), base in zip(reversed(halving), reversed(starts)):
        mine = bitval(axis, bit)
        other = pl.multiple_of(base + (1 - mine) * length, 8)
        swap(k, axis, bit, lo, length)
        o_ref[pl.ds(other, length)] = recv[k, pl.ds(0, length)]
        lo = base
        length *= 2
        k += 1


def reduce_scratch(w):
    halving, whole = reduction_plan(w.shape[0])
    steps = 2 * len(halving) + len(whole)
    return [
        pltpu.VMEM((steps, w.shape[0] // 2) + w.shape[1:], w.dtype),
        pltpu.SemaphoreType.DMA((steps,)),
        pltpu.SemaphoreType.DMA((steps,)),
    ]


def radix_groups():
    n_row, n_col = lax.axis_size("row"), lax.axis_size("col")
    if n_row % 2 or n_col % 4:
        return None
    return ((("row", 1, 2), ("col", 1, 4)), ("row", 2, n_row // 2), ("col", 4, n_col // 4))


def first_group():
    (core, ring), _, _ = radix_groups()
    me_a, _ = group_of(*core)
    me_b, _ = group_of(*ring)
    size = core[2] * ring[2]
    me = me_a + core[2] * me_b
    row = lax.axis_index("row") - me_a * core[1]
    col = lax.axis_index("col") - me_b * ring[1]

    def member(m):
        return (row + (m % core[2]) * core[1], col + (m // core[2]) * ring[1], lax.axis_index("feat"))

    return me, size, member


def reduce_radix_targets():
    me, size, member = first_group()
    targets = [member(lax.rem(me + d, size)) for d in range(1, size)]
    _, z_group, x_group = radix_groups()
    return targets + exchange_targets(*z_group) + exchange_targets(*x_group)


def ordered_allreduce(group, value, recv, send_sems, recv_sems):
    axis, stride, size = group
    me, member = group_of(axis, stride, size)
    recv[me] = value
    copies = []
    for d in range(1, size):
        peer = lax.rem(me + d, size)
        copy = pltpu.make_async_remote_copy(
            src_ref=recv.at[me], dst_ref=recv.at[me], send_sem=send_sems.at[d],
            recv_sem=recv_sems.at[me], device_id=member(peer), device_id_type=pl.DeviceIdType.MESH)
        copy.start()
        copies.append(copy)
    for d in range(1, size):
        src_dev = lax.rem(me + size - d, size)
        pltpu.make_async_remote_copy(
            src_ref=recv.at[src_dev], dst_ref=recv.at[src_dev], send_sem=send_sems.at[d],
            recv_sem=recv_sems.at[src_dev], device_id=member(src_dev),
            device_id_type=pl.DeviceIdType.MESH).wait_recv()
    for copy in copies:
        copy.wait_send()
    total = recv[0]
    for k in range(1, size):
        total = total + recv[k]
    return total


def reduce_radix(w_ref, o_ref, seg_recv, z_recv, x_recv, sems, scale=1.0):
    _, z_group, x_group = radix_groups()
    me, size, member = first_group()
    seg = w_ref.shape[0] // size
    mine = pl.ds(pl.multiple_of(me * seg, 8), seg)
    copies = []
    for d in range(1, size):
        peer = lax.rem(me + d, size)
        copy = pltpu.make_async_remote_copy(
            src_ref=w_ref.at[pl.ds(pl.multiple_of(peer * seg, 8), seg)], dst_ref=seg_recv.at[me],
            send_sem=sems.at[0, d], recv_sem=sems.at[1, me], device_id=member(peer),
            device_id_type=pl.DeviceIdType.MESH)
        copy.start()
        copies.append(copy)
    total = w_ref[mine]
    for d in range(1, size):
        src_dev = lax.rem(me + size - d, size)
        pltpu.make_async_remote_copy(
            src_ref=seg_recv.at[src_dev], dst_ref=seg_recv.at[src_dev], send_sem=sems.at[0, d],
            recv_sem=sems.at[1, src_dev], device_id=member(src_dev),
            device_id_type=pl.DeviceIdType.MESH).wait_recv()
        total = total + seg_recv[src_dev]
    for copy in copies:
        copy.wait_send()
    total = ordered_allreduce(z_group, total, z_recv, sems.at[2], sems.at[3])
    total = ordered_allreduce(x_group, total, x_recv, sems.at[4], sems.at[5])
    o_ref[mine] = total * scale
    copies = []
    for d in range(1, size):
        peer = lax.rem(me + d, size)
        copy = pltpu.make_async_remote_copy(
            src_ref=o_ref.at[mine], dst_ref=o_ref.at[mine], send_sem=sems.at[6, d],
            recv_sem=sems.at[7, me], device_id=member(peer), device_id_type=pl.DeviceIdType.MESH)
        copy.start()
        copies.append(copy)
    for d in range(1, size):
        src_dev = lax.rem(me + size - d, size)
        rows = pl.ds(pl.multiple_of(src_dev * seg, 8), seg)
        pltpu.make_async_remote_copy(
            src_ref=o_ref.at[rows], dst_ref=o_ref.at[rows], send_sem=sems.at[6, d],
            recv_sem=sems.at[7, src_dev], device_id=member(src_dev),
            device_id_type=pl.DeviceIdType.MESH).wait_recv()
    for copy in copies:
        copy.wait_send()


def radix_scratch(w):
    (core, ring), z_group, x_group = radix_groups()
    size = core[2] * ring[2]
    seg = (w.shape[0] // size,) + w.shape[1:]
    width = max(size, z_group[2], x_group[2])
    return [
        pltpu.VMEM((size,) + seg, w.dtype),
        pltpu.VMEM((z_group[2],) + seg, w.dtype),
        pltpu.VMEM((x_group[2],) + seg, w.dtype),
        pltpu.SemaphoreType.DMA((8, width)),
    ]


def radix_fits(w):
    groups = radix_groups()
    if groups is None:
        return False
    size = groups[0][0][2] * groups[0][1][2]
    return w.shape[0] % (8 * size) == 0


def gather_radix_kernel(axis, x_ref, w_ref, o_ref, ow_ref, g_send, g_recv, *scratch):
    size = lax.axis_size(axis)
    enter(exchange_targets(axis, 1, size) + reduce_radix_targets())
    copies = exchange_start(axis, 1, size, "gather", x_ref, o_ref, g_send, g_recv)
    reduce_radix(w_ref, ow_ref, *scratch)
    exchange_finish(axis, 1, size, "gather", x_ref, o_ref, o_ref, g_send, g_recv, copies)


def gather_reduce_kernel(axis, x_ref, w_ref, o_ref, ow_ref, g_send, g_recv, recv, send_sems, recv_sems):
    size = lax.axis_size(axis)
    enter(exchange_targets(axis, 1, size) + reduce_targets(w_ref.shape[0]))
    copies = exchange_start(axis, 1, size, "gather", x_ref, o_ref, g_send, g_recv)
    reduce_rounds(w_ref, ow_ref, recv, send_sems, recv_sems)
    exchange_finish(axis, 1, size, "gather", x_ref, o_ref, o_ref, g_send, g_recv, copies)


def gather_and_reduce(x, w, axis, collective_id):
    size = lax.axis_size(axis)
    if radix_fits(w):
        kernel, scratch = gather_radix_kernel, radix_scratch(w)
    else:
        kernel, scratch = gather_reduce_kernel, reduce_scratch(w)
    return pl.pallas_call(
        functools.partial(kernel, axis),
        out_shape=(exchange_shape(x, "gather", size), jax.ShapeDtypeStruct(w.shape, w.dtype)),
        in_specs=[pl.BlockSpec(memory_space=pltpu.VMEM)] * 2,
        out_specs=(pl.BlockSpec(memory_space=pltpu.VMEM),) * 2,
        scratch_shapes=exchange_scratch(x, "gather", size) + scratch,
        compiler_params=pltpu.CompilerParams(collective_id=collective_id, has_side_effects=True),
    )(x, w)


def shards(features, tile_rows, tile_cols, tile_count, tile_values, weights, cotangent):
    width = tile_values.shape[-1]
    local_tiles = tile_values[0, 0]
    block_rows = tile_rows[0, 0]
    block_cols = tile_cols[0, 0]
    count = tile_count[0, 0].reshape(1)
    n_rowdev = lax.axis_size("row")
    n_coldev = lax.axis_size("col")
    local_blocks = features.shape[0] // width
    feat_half = features.shape[1]
    feat_index = lax.axis_index("feat")
    row_blocks = local_blocks * n_coldev
    col_blocks = local_blocks * n_rowdev
    node_total = features.shape[0] * n_rowdev * n_coldev
    pair = 2 if n_rowdev % 2 == 0 else 1
    chips = n_rowdev // pair
    if pair == 2:
        panel = row_gather(features, chips, 0).reshape(-1, feat_half)
    else:
        panel = exchange(features, "row", "gather", 0).reshape(-1, feat_half)
    owner = block_cols // local_blocks
    block_cols = ((owner % pair) * chips + owner // pair) * local_blocks + block_cols % local_blocks
    partial_value = tile_products(local_tiles, block_rows, block_cols, count, panel,
                                  row_blocks, transpose=False)
    weight_cols = lax.dynamic_slice_in_dim(weights, feat_index * feat_half, feat_half, 1)
    weight_rows = lax.dynamic_slice_in_dim(weights, feat_index * feat_half, feat_half, 0)
    hidden, spread_panel, weight_sum = layer_step(partial_value.reshape(n_coldev, -1, feat_half),
                                                  weight_cols, weight_rows, cotangent, 1,
                                                  node_total ** (-0.5))
    negative = jnp.minimum(hidden, 0.0)
    activated = jnp.where(hidden > 0, hidden, jnp.expm1(negative)).astype(jnp.bfloat16)
    spread_panel = spread_panel.reshape(-1, feat_half)
    weight_grad = weight_sum
    back_partial = tile_products(local_tiles, block_rows, block_cols, count, spread_panel,
                                 col_blocks, transpose=True)
    if pair == 2:
        back_summed = row_scatter(back_partial.reshape(pair, chips, -1, feat_half), chips, 3)
    else:
        back_summed = exchange(back_partial.reshape(n_rowdev, -1, feat_half), "row", "scatter", 3)
    return (activated, back_summed, weight_grad)


def solution(mesh):
    return jax.shard_map(
        shards,
        mesh=mesh,
        in_specs=(
            P(("col", "row"), "feat"),
            P("row", "col", None),
            P("row", "col", None),
            P("row", "col"),
            P("row", "col", None, None, None),
            P(),
            P(("row", "col"), "feat"),
        ),
        out_specs=(P(("row", "col"), "feat"), P(("col", "row"), "feat"), P("feat", None)),
        check_vma=False,
    )
```

```python
import functools

import jax
import jax.numpy as jnp
from jax import lax
from jax.experimental import pallas as pl
from jax.experimental.pallas import tpu as pltpu
from jax.sharding import PartitionSpec as P

GROUP = 64


def tile_kernel(transpose, remap, rows_ref, cols_ref, count_ref, tiles_ref, panel_ref, out_ref, acc_ref):
    step = pl.program_id(0)
    width = tiles_ref.shape[-1]
    count = count_ref[0]
    src_blocks = panel_ref.shape[0] // width
    dst_blocks = acc_ref.shape[0] // width

    @pl.when(step == 0)
    def _():
        acc_ref[...] = jnp.zeros_like(acc_ref)

    @pl.when(step * GROUP < count)
    def _():
        terms = []
        for j in range(GROUP):
            slot = step * GROUP + j
            src = rows_ref[slot] if transpose else remap(cols_ref[slot])
            src = jnp.minimum(jnp.maximum(src, 0), src_blocks - 1)
            block = panel_ref[pl.ds(pl.multiple_of(src * width, width), width), :]
            tile = tiles_ref[j]
            if transpose:
                term = lax.dot_general(tile, block, (((0,), (0,)), ((), ())),
                                       preferred_element_type=jnp.float32)
            else:
                term = jnp.dot(tile, block, preferred_element_type=jnp.float32)
            terms.append(jnp.where(slot < count, term, 0.0))
        for j in range(GROUP):
            slot = step * GROUP + j
            dst = remap(cols_ref[slot]) if transpose else rows_ref[slot]
            dst = jnp.minimum(jnp.maximum(dst, 0), dst_blocks - 1)
            rows = pl.ds(pl.multiple_of(dst * width, width), width)
            acc_ref[rows, :] += terms[j]

    @pl.when(step == pl.num_programs(0) - 1)
    def _():
        out_ref[...] = acc_ref[...].astype(out_ref.dtype)


def tile_products(tiles, rows, cols, count, panel, out_blocks, transpose, remap):
    slots, width, _ = tiles.shape
    feat = panel.shape[1]
    steps = slots // GROUP

    def tiles_map(i, rows_ref, cols_ref, count_ref):
        last = jnp.maximum(count_ref[0] - 1, 0) // GROUP
        return (jnp.minimum(i, last), 0, 0)

    return pl.pallas_call(
        functools.partial(tile_kernel, transpose, remap),
        out_shape=jax.ShapeDtypeStruct((out_blocks * width, feat), jnp.bfloat16),
        grid_spec=pltpu.PrefetchScalarGridSpec(
            num_scalar_prefetch=3,
            grid=(steps,),
            in_specs=[
                pl.BlockSpec((GROUP, width, width), tiles_map),
                pl.BlockSpec(panel.shape, lambda i, *_: (0, 0)),
            ],
            out_specs=pl.BlockSpec((out_blocks * width, feat), lambda i, *_: (0, 0)),
            scratch_shapes=[pltpu.VMEM((out_blocks * width, feat), jnp.float32)],
        ),
        compiler_params=pltpu.CompilerParams(dimension_semantics=("arbitrary",)),
        cost_estimate=pl.CostEstimate(
            flops=2 * slots * width * width * feat,
            bytes_accessed=tiles.size * 2 + panel.size * 2 + out_blocks * width * feat * 2,
            transcendentals=0,
        ),
    )(rows, cols, count, tiles, panel)


def mesh_coords(axis, peer):
    return tuple(peer if name == axis else lax.axis_index(name) for name in ("row", "col", "feat"))


def group_of(axis, stride, size):
    index = lax.axis_index(axis)
    me = (index // stride) % size
    base = index - me * stride
    return me, lambda k: mesh_coords(axis, base + k * stride)


def exchange_targets(axis, stride, size):
    me, member = group_of(axis, stride, size)
    return [member(lax.rem(me + d, size)) for d in range(1, size)]


def enter(targets):
    barrier = pltpu.get_barrier_semaphore()
    for target in targets:
        pl.semaphore_signal(barrier, inc=1, device_id=target, device_id_type=pl.DeviceIdType.MESH)
    pl.semaphore_wait(barrier, len(targets))


def exchange_start(axis, stride, size, mode, x_ref, recv_ref, send_sems, recv_sems):
    me, member = group_of(axis, stride, size)
    copies = []
    for d in range(1, size):
        peer = lax.rem(me + d, size)
        src = x_ref if mode == "gather" else x_ref.at[peer]
        copy = pltpu.make_async_remote_copy(
            src_ref=src, dst_ref=recv_ref.at[me], send_sem=send_sems.at[d],
            recv_sem=recv_sems.at[me], device_id=member(peer),
            device_id_type=pl.DeviceIdType.MESH)
        copy.start()
        copies.append(copy)
    return copies


def exchange_finish(axis, stride, size, mode, x_ref, o_ref, recv_ref, send_sems, recv_sems, copies):
    me, member = group_of(axis, stride, size)
    if mode == "gather":
        o_ref[me] = x_ref[...]
    else:
        total = x_ref[me].astype(jnp.float32)
    for d in range(1, size):
        src_dev = lax.rem(me + size - d, size)
        incoming = pltpu.make_async_remote_copy(
            src_ref=recv_ref.at[src_dev], dst_ref=recv_ref.at[src_dev], send_sem=send_sems.at[d],
            recv_sem=recv_sems.at[src_dev], device_id=member(src_dev),
            device_id_type=pl.DeviceIdType.MESH)
        incoming.wait_recv()
        if mode != "gather":
            total = total + recv_ref[src_dev].astype(jnp.float32)
    for copy in copies:
        copy.wait_send()
    if mode != "gather":
        o_ref[...] = total.astype(o_ref.dtype)


def exchange_kernel(axis, stride, size, mode, x_ref, o_ref, *scratch):
    if mode == "gather":
        recv_ref, (send_sems, recv_sems) = o_ref, scratch
    else:
        recv_ref, send_sems, recv_sems = scratch
    enter(exchange_targets(axis, stride, size))
    copies = exchange_start(axis, stride, size, mode, x_ref, recv_ref, send_sems, recv_sems)
    exchange_finish(axis, stride, size, mode, x_ref, o_ref, recv_ref, send_sems, recv_sems, copies)


def exchange_scratch(x, mode, size):
    scratch = [] if mode == "gather" else [pltpu.VMEM(x.shape, x.dtype)]
    return scratch + [pltpu.SemaphoreType.DMA((size,)), pltpu.SemaphoreType.DMA((size,))]


def exchange_shape(x, mode, size):
    shape = (size,) + x.shape if mode == "gather" else x.shape[1:]
    return jax.ShapeDtypeStruct(shape, x.dtype)


def exchange(x, axis, mode, collective_id, stride=1, size=None):
    size = lax.axis_size(axis) if size is None else size
    return pl.pallas_call(
        functools.partial(exchange_kernel, axis, stride, size, mode),
        out_shape=exchange_shape(x, mode, size),
        in_specs=[pl.BlockSpec(memory_space=pltpu.VMEM)],
        out_specs=pl.BlockSpec(memory_space=pltpu.VMEM),
        scratch_shapes=exchange_scratch(x, mode, size),
        compiler_params=pltpu.CompilerParams(collective_id=collective_id, has_side_effects=True),
    )(x)


def pair_targets(chips):
    me, member = group_of("row", 2, chips)
    _, sibling = group_of("row", 1, 2)
    return [member(lax.rem(me + d, chips)) for d in range(1, chips)], sibling


def row_gather_kernel(chips, x_ref, o_ref, send_sems, recv_sems, fwd_send, fwd_recv):
    z_me, z_member = group_of("row", 2, chips)
    c_me, core_member = group_of("row", 1, 2)
    sibling = core_member(1 - c_me)
    peers, _ = pair_targets(chips)
    enter(peers + [sibling])
    copies = []
    for d in range(1, chips):
        peer = lax.rem(z_me + d, chips)
        copy = pltpu.make_async_remote_copy(
            src_ref=x_ref, dst_ref=o_ref.at[c_me, z_me], send_sem=send_sems.at[d],
            recv_sem=recv_sems.at[z_me], device_id=z_member(peer),
            device_id_type=pl.DeviceIdType.MESH)
        copy.start()
        copies.append(copy)
    own = pltpu.make_async_remote_copy(
        src_ref=x_ref, dst_ref=o_ref.at[c_me, z_me], send_sem=fwd_send.at[z_me],
        recv_sem=fwd_recv.at[z_me], device_id=sibling, device_id_type=pl.DeviceIdType.MESH)
    own.start()
    copies.append(own)
    o_ref[c_me, z_me] = x_ref[...]
    for d in range(1, chips):
        src_dev = lax.rem(z_me + chips - d, chips)
        incoming = pltpu.make_async_remote_copy(
            src_ref=o_ref.at[c_me, src_dev], dst_ref=o_ref.at[c_me, src_dev],
            send_sem=send_sems.at[d], recv_sem=recv_sems.at[src_dev],
            device_id=z_member(src_dev), device_id_type=pl.DeviceIdType.MESH)
        incoming.wait_recv()
        forward = pltpu.make_async_remote_copy(
            src_ref=o_ref.at[c_me, src_dev], dst_ref=o_ref.at[c_me, src_dev],
            send_sem=fwd_send.at[src_dev], recv_sem=fwd_recv.at[src_dev], device_id=sibling,
            device_id_type=pl.DeviceIdType.MESH)
        forward.start()
        copies.append(forward)
    for k in range(chips):
        incoming = pltpu.make_async_remote_copy(
            src_ref=o_ref.at[1 - c_me, k], dst_ref=o_ref.at[1 - c_me, k],
            send_sem=fwd_send.at[k], recv_sem=fwd_recv.at[k], device_id=sibling,
            device_id_type=pl.DeviceIdType.MESH)
        incoming.wait_recv()
    for copy in copies:
        copy.wait_send()


def row_gather(x, chips, collective_id):
    return pl.pallas_call(
        functools.partial(row_gather_kernel, chips),
        out_shape=jax.ShapeDtypeStruct((2, chips) + x.shape, x.dtype),
        in_specs=[pl.BlockSpec(memory_space=pltpu.VMEM)],
        out_specs=pl.BlockSpec(memory_space=pltpu.VMEM),
        scratch_shapes=[pltpu.SemaphoreType.DMA((chips,))] * 4,
        compiler_params=pltpu.CompilerParams(collective_id=collective_id, has_side_effects=True),
    )(x)


def row_scatter_kernel(chips, x_ref, o_ref, pair_recv, pair_sum, z_recv,
                       pair_send_sems, pair_recv_sems, z_send_sems, z_recv_sems):
    z_me, z_member = group_of("row", 2, chips)
    c_me, core_member = group_of("row", 1, 2)
    sibling = core_member(1 - c_me)
    peers, _ = pair_targets(chips)
    enter(peers + [sibling])
    copies = []
    for k in range(chips):
        copy = pltpu.make_async_remote_copy(
            src_ref=x_ref.at[1 - c_me, k], dst_ref=pair_recv.at[k], send_sem=pair_send_sems.at[k],
            recv_sem=pair_recv_sems.at[k], device_id=sibling, device_id_type=pl.DeviceIdType.MESH)
        copy.start()
        copies.append(copy)
    order = [lax.rem(z_me + d, chips) for d in range(1, chips)] + [z_me]
    for d, k in enumerate(order, start=1):
        incoming = pltpu.make_async_remote_copy(
            src_ref=pair_recv.at[k], dst_ref=pair_recv.at[k], send_sem=pair_send_sems.at[k],
            recv_sem=pair_recv_sems.at[k], device_id=sibling, device_id_type=pl.DeviceIdType.MESH)
        incoming.wait_recv()
        pair_sum[k] = (x_ref[c_me, k].astype(jnp.float32)
                       + pair_recv[k].astype(jnp.float32)).astype(pair_sum.dtype)
        if d < chips:
            copy = pltpu.make_async_remote_copy(
                src_ref=pair_sum.at[k], dst_ref=z_recv.at[z_me], send_sem=z_send_sems.at[d],
                recv_sem=z_recv_sems.at[z_me], device_id=z_member(k),
                device_id_type=pl.DeviceIdType.MESH)
            copy.start()
            copies.append(copy)
    total = pair_sum[z_me].astype(jnp.float32)
    for d in range(1, chips):
        src_dev = lax.rem(z_me + chips - d, chips)
        incoming = pltpu.make_async_remote_copy(
            src_ref=z_recv.at[src_dev], dst_ref=z_recv.at[src_dev], send_sem=z_send_sems.at[d],
            recv_sem=z_recv_sems.at[src_dev], device_id=z_member(src_dev),
            device_id_type=pl.DeviceIdType.MESH)
        incoming.wait_recv()
        total = total + z_recv[src_dev].astype(jnp.float32)
    for copy in copies:
        copy.wait_send()
    o_ref[...] = total.astype(o_ref.dtype)


def row_scatter(x, chips, collective_id):
    block = x.shape[2:]
    return pl.pallas_call(
        functools.partial(row_scatter_kernel, chips),
        out_shape=jax.ShapeDtypeStruct(block, x.dtype),
        in_specs=[pl.BlockSpec(memory_space=pltpu.VMEM)],
        out_specs=pl.BlockSpec(memory_space=pltpu.VMEM),
        scratch_shapes=[pltpu.VMEM((chips,) + block, x.dtype)] * 3
        + [pltpu.SemaphoreType.DMA((chips,))] * 4,
        compiler_params=pltpu.CompilerParams(collective_id=collective_id, has_side_effects=True),
    )(x)


def feat_push(value_ref, halves_ref, send_sems, recv_sems, slot):
    n = lax.axis_size("feat")
    me = lax.axis_index("feat")
    halves_ref[me] = value_ref[...]
    copies = []
    for d in range(1, n):
        peer = lax.rem(me + d, n)
        copy = pltpu.make_async_remote_copy(
            src_ref=halves_ref.at[me], dst_ref=halves_ref.at[me], send_sem=send_sems.at[slot, d],
            recv_sem=recv_sems.at[slot, me], device_id=mesh_coords("feat", peer),
            device_id_type=pl.DeviceIdType.MESH)
        copy.start()
        copies.append(copy)
    for d in range(1, n):
        src_dev = lax.rem(me + n - d, n)
        pltpu.make_async_remote_copy(
            src_ref=halves_ref.at[src_dev], dst_ref=halves_ref.at[src_dev],
            send_sem=send_sems.at[slot, d], recv_sem=recv_sems.at[slot, src_dev],
            device_id=mesh_coords("feat", src_dev), device_id_type=pl.DeviceIdType.MESH).wait_recv()
    for copy in copies:
        copy.wait_send()


def layer_kernel(scale, x_ref, w_ref, wr_ref, cot_ref, hidden_ref, panel_ref, sum_ref,
                 recv_ref, send_sems, recv_sems, summed_ref, agg_ref, grad_out_ref, grad_ref,
                 f_send, f_recv, term_ref, spread_ref, g_send, g_recv, *reduce_scratch):
    n_col = lax.axis_size("col")
    n_feat = lax.axis_size("feat")
    me = lax.axis_index("feat")
    peers = [mesh_coords("feat", lax.rem(me + d, n_feat)) for d in range(1, n_feat)]
    radix = len(reduce_scratch) == 4
    others = reduce_radix_targets() if radix else reduce_targets(term_ref.shape[0])
    enter(exchange_targets("col", 1, n_col) + peers + exchange_targets("col", 1, n_col) + others)
    copies = exchange_start("col", 1, n_col, "scatter", x_ref, recv_ref, send_sems, recv_sems)
    exchange_finish("col", 1, n_col, "scatter", x_ref, summed_ref, recv_ref, send_sems, recv_sems,
                    copies)
    feat_push(summed_ref, agg_ref, f_send, f_recv, 0)
    half = agg_ref.shape[-1]
    hidden = jnp.dot(agg_ref[0], w_ref[pl.ds(0, half), :], preferred_element_type=jnp.float32)
    for h in range(1, n_feat):
        hidden = hidden + jnp.dot(agg_ref[h], w_ref[pl.ds(h * half, half), :],
                                  preferred_element_type=jnp.float32)
    hidden_ref[...] = hidden
    slope = jnp.where(hidden > 0, 1.0, jnp.exp(jnp.minimum(hidden, 0.0)))
    grad_out_ref[...] = (cot_ref[...].astype(jnp.float32) * slope).astype(grad_out_ref.dtype)
    feat_push(grad_out_ref, grad_ref, f_send, f_recv, 1)
    spread = None
    for h in range(n_feat):
        columns = pl.ds(h * half, half)
        term_ref[:, columns] = lax.dot_general(
            summed_ref[...], grad_ref[h], (((0,), (0,)), ((), ())),
            preferred_element_type=jnp.float32)
        part = lax.dot_general(grad_ref[h], wr_ref[:, columns], (((1,), (1,)), ((), ())),
                               preferred_element_type=jnp.float32)
        spread = part if spread is None else spread + part
    spread_ref[...] = spread.astype(spread_ref.dtype)
    copies = exchange_start("col", 1, n_col, "gather", spread_ref, panel_ref, g_send, g_recv)
    if radix:
        reduce_radix(term_ref, sum_ref, *reduce_scratch, scale=scale)
    else:
        reduce_rounds(term_ref, sum_ref, *reduce_scratch)
        sum_ref[...] = sum_ref[...] * scale
    exchange_finish("col", 1, n_col, "gather", spread_ref, panel_ref, panel_ref, g_send, g_recv,
                    copies)


def layer_step(partials, weight_cols, weight_rows, cotangent, collective_id, scale):
    n_col = lax.axis_size("col")
    n_feat = lax.axis_size("feat")
    block = partials.shape[1:]
    half = block[-1]
    term = jax.ShapeDtypeStruct((half, n_feat * half), jnp.float32)
    reduce_space = radix_scratch(term) if radix_fits(term) else reduce_scratch(term)
    vmem = pl.BlockSpec(memory_space=pltpu.VMEM)
    return pl.pallas_call(
        functools.partial(layer_kernel, scale),
        out_shape=(
            jax.ShapeDtypeStruct(block, jnp.float32),
            jax.ShapeDtypeStruct((n_col,) + block, jnp.bfloat16),
            term,
        ),
        in_specs=[vmem] * 4,
        out_specs=(vmem,) * 3,
        scratch_shapes=exchange_scratch(partials, "scatter", n_col) + [
            pltpu.VMEM(block, partials.dtype),
            pltpu.VMEM((n_feat,) + block, partials.dtype),
            pltpu.VMEM(block, jnp.bfloat16),
            pltpu.VMEM((n_feat,) + block, jnp.bfloat16),
            pltpu.SemaphoreType.DMA((2, n_feat)),
            pltpu.SemaphoreType.DMA((2, n_feat)),
            pltpu.VMEM(term.shape, term.dtype),
            pltpu.VMEM(block, jnp.bfloat16),
            pltpu.SemaphoreType.DMA((n_col,)),
            pltpu.SemaphoreType.DMA((n_col,)),
        ] + reduce_space,
        compiler_params=pltpu.CompilerParams(collective_id=collective_id, has_side_effects=True),
    )(partials, weight_cols, weight_rows, cotangent)


def reduction_plan(rows):
    pairs = []
    for bit in (1, 2, 4, 8, 16, 32, 64):
        for axis in ("row", "col"):
            if bit < lax.axis_size(axis):
                pairs.append((axis, bit))
    halving = []
    while pairs and rows // 2 >= 8 and rows % 16 == 0:
        halving.append(pairs.pop(0))
        rows //= 2
    return halving, pairs


def bitval(axis, bit):
    return (lax.axis_index(axis) // bit) % 2


def partner(axis, bit):
    return mesh_coords(axis, lax.axis_index(axis) + bit * (1 - 2 * bitval(axis, bit)))


def reduce_targets(rows):
    halving, whole = reduction_plan(rows)
    return [partner(axis, bit) for axis, bit in halving + whole]


def reduce_rounds(x_ref, o_ref, recv, send_sems, recv_sems):
    halving, whole = reduction_plan(x_ref.shape[0])
    o_ref[...] = x_ref[...]
    k = 0

    def swap(k, axis, bit, send_rows, length):
        copy = pltpu.make_async_remote_copy(
            src_ref=o_ref.at[pl.ds(send_rows, length)], dst_ref=recv.at[k, pl.ds(0, length)],
            send_sem=send_sems.at[k], recv_sem=recv_sems.at[k],
            device_id=partner(axis, bit), device_id_type=pl.DeviceIdType.MESH)
        copy.start()
        copy.wait()

    lo = jnp.int32(0)
    length = x_ref.shape[0]
    starts = []
    for axis, bit in halving:
        length //= 2
        mine = bitval(axis, bit)
        starts.append(lo)
        keep = pl.multiple_of(lo + mine * length, 8)
        give = pl.multiple_of(lo + (1 - mine) * length, 8)
        swap(k, axis, bit, give, length)
        o_ref[pl.ds(keep, length)] = o_ref[pl.ds(keep, length)] + recv[k, pl.ds(0, length)]
        lo = keep
        k += 1
    for axis, bit in whole:
        swap(k, axis, bit, lo, length)
        o_ref[pl.ds(lo, length)] = o_ref[pl.ds(lo, length)] + recv[k, pl.ds(0, length)]
        k += 1
    for (axis, bit), base in zip(reversed(halving), reversed(starts)):
        mine = bitval(axis, bit)
        other = pl.multiple_of(base + (1 - mine) * length, 8)
        swap(k, axis, bit, lo, length)
        o_ref[pl.ds(other, length)] = recv[k, pl.ds(0, length)]
        lo = base
        length *= 2
        k += 1


def reduce_scratch(w):
    halving, whole = reduction_plan(w.shape[0])
    steps = 2 * len(halving) + len(whole)
    return [
        pltpu.VMEM((steps, w.shape[0] // 2) + w.shape[1:], w.dtype),
        pltpu.SemaphoreType.DMA((steps,)),
        pltpu.SemaphoreType.DMA((steps,)),
    ]


def radix_groups():
    n_row, n_col = lax.axis_size("row"), lax.axis_size("col")
    if n_row % 2 or n_col % 4:
        return None
    return ((("row", 1, 2), ("col", 1, 4)), ("row", 2, n_row // 2), ("col", 4, n_col // 4))


def first_group():
    (core, ring), _, _ = radix_groups()
    me_a, _ = group_of(*core)
    me_b, _ = group_of(*ring)
    size = core[2] * ring[2]
    me = me_a + core[2] * me_b
    row = lax.axis_index("row") - me_a * core[1]
    col = lax.axis_index("col") - me_b * ring[1]

    def member(m):
        return (row + (m % core[2]) * core[1], col + (m // core[2]) * ring[1], lax.axis_index("feat"))

    return me, size, member


def reduce_radix_targets():
    me, size, member = first_group()
    targets = [member(lax.rem(me + d, size)) for d in range(1, size)]
    _, z_group, x_group = radix_groups()
    return targets + exchange_targets(*z_group) + exchange_targets(*x_group)


def ordered_allreduce(group, value, recv, send_sems, recv_sems):
    axis, stride, size = group
    me, member = group_of(axis, stride, size)
    recv[me] = value
    copies = []
    for d in range(1, size):
        peer = lax.rem(me + d, size)
        copy = pltpu.make_async_remote_copy(
            src_ref=recv.at[me], dst_ref=recv.at[me], send_sem=send_sems.at[d],
            recv_sem=recv_sems.at[me], device_id=member(peer), device_id_type=pl.DeviceIdType.MESH)
        copy.start()
        copies.append(copy)
    for d in range(1, size):
        src_dev = lax.rem(me + size - d, size)
        pltpu.make_async_remote_copy(
            src_ref=recv.at[src_dev], dst_ref=recv.at[src_dev], send_sem=send_sems.at[d],
            recv_sem=recv_sems.at[src_dev], device_id=member(src_dev),
            device_id_type=pl.DeviceIdType.MESH).wait_recv()
    for copy in copies:
        copy.wait_send()
    total = recv[0]
    for k in range(1, size):
        total = total + recv[k]
    return total


def reduce_radix(w_ref, o_ref, seg_recv, z_recv, x_recv, sems, scale=1.0):
    _, z_group, x_group = radix_groups()
    me, size, member = first_group()
    seg = w_ref.shape[0] // size
    mine = pl.ds(pl.multiple_of(me * seg, 8), seg)
    copies = []
    for d in range(1, size):
        peer = lax.rem(me + d, size)
        copy = pltpu.make_async_remote_copy(
            src_ref=w_ref.at[pl.ds(pl.multiple_of(peer * seg, 8), seg)], dst_ref=seg_recv.at[me],
            send_sem=sems.at[0, d], recv_sem=sems.at[1, me], device_id=member(peer),
            device_id_type=pl.DeviceIdType.MESH)
        copy.start()
        copies.append(copy)
    total = w_ref[mine]
    for d in range(1, size):
        src_dev = lax.rem(me + size - d, size)
        pltpu.make_async_remote_copy(
            src_ref=seg_recv.at[src_dev], dst_ref=seg_recv.at[src_dev], send_sem=sems.at[0, d],
            recv_sem=sems.at[1, src_dev], device_id=member(src_dev),
            device_id_type=pl.DeviceIdType.MESH).wait_recv()
        total = total + seg_recv[src_dev]
    for copy in copies:
        copy.wait_send()
    total = ordered_allreduce(z_group, total, z_recv, sems.at[2], sems.at[3])
    total = ordered_allreduce(x_group, total, x_recv, sems.at[4], sems.at[5])
    o_ref[mine] = total * scale
    copies = []
    for d in range(1, size):
        peer = lax.rem(me + d, size)
        copy = pltpu.make_async_remote_copy(
            src_ref=o_ref.at[mine], dst_ref=o_ref.at[mine], send_sem=sems.at[6, d],
            recv_sem=sems.at[7, me], device_id=member(peer), device_id_type=pl.DeviceIdType.MESH)
        copy.start()
        copies.append(copy)
    for d in range(1, size):
        src_dev = lax.rem(me + size - d, size)
        rows = pl.ds(pl.multiple_of(src_dev * seg, 8), seg)
        pltpu.make_async_remote_copy(
            src_ref=o_ref.at[rows], dst_ref=o_ref.at[rows], send_sem=sems.at[6, d],
            recv_sem=sems.at[7, src_dev], device_id=member(src_dev),
            device_id_type=pl.DeviceIdType.MESH).wait_recv()
    for copy in copies:
        copy.wait_send()


def radix_scratch(w):
    (core, ring), z_group, x_group = radix_groups()
    size = core[2] * ring[2]
    seg = (w.shape[0] // size,) + w.shape[1:]
    width = max(size, z_group[2], x_group[2])
    return [
        pltpu.VMEM((size,) + seg, w.dtype),
        pltpu.VMEM((z_group[2],) + seg, w.dtype),
        pltpu.VMEM((x_group[2],) + seg, w.dtype),
        pltpu.SemaphoreType.DMA((8, width)),
    ]


def radix_fits(w):
    groups = radix_groups()
    if groups is None:
        return False
    size = groups[0][0][2] * groups[0][1][2]
    return w.shape[0] % (8 * size) == 0


def gather_radix_kernel(axis, x_ref, w_ref, o_ref, ow_ref, g_send, g_recv, *scratch):
    size = lax.axis_size(axis)
    enter(exchange_targets(axis, 1, size) + reduce_radix_targets())
    copies = exchange_start(axis, 1, size, "gather", x_ref, o_ref, g_send, g_recv)
    reduce_radix(w_ref, ow_ref, *scratch)
    exchange_finish(axis, 1, size, "gather", x_ref, o_ref, o_ref, g_send, g_recv, copies)


def gather_reduce_kernel(axis, x_ref, w_ref, o_ref, ow_ref, g_send, g_recv, recv, send_sems, recv_sems):
    size = lax.axis_size(axis)
    enter(exchange_targets(axis, 1, size) + reduce_targets(w_ref.shape[0]))
    copies = exchange_start(axis, 1, size, "gather", x_ref, o_ref, g_send, g_recv)
    reduce_rounds(w_ref, ow_ref, recv, send_sems, recv_sems)
    exchange_finish(axis, 1, size, "gather", x_ref, o_ref, o_ref, g_send, g_recv, copies)


def gather_and_reduce(x, w, axis, collective_id):
    size = lax.axis_size(axis)
    if radix_fits(w):
        kernel, scratch = gather_radix_kernel, radix_scratch(w)
    else:
        kernel, scratch = gather_reduce_kernel, reduce_scratch(w)
    return pl.pallas_call(
        functools.partial(kernel, axis),
        out_shape=(exchange_shape(x, "gather", size), jax.ShapeDtypeStruct(w.shape, w.dtype)),
        in_specs=[pl.BlockSpec(memory_space=pltpu.VMEM)] * 2,
        out_specs=(pl.BlockSpec(memory_space=pltpu.VMEM),) * 2,
        scratch_shapes=exchange_scratch(x, "gather", size) + scratch,
        compiler_params=pltpu.CompilerParams(collective_id=collective_id, has_side_effects=True),
    )(x, w)


def shards(features, tile_rows, tile_cols, tile_count, tile_values, weights, cotangent):
    width = tile_values.shape[-1]
    local_tiles = tile_values[0, 0]
    block_rows = tile_rows[0, 0]
    block_cols = tile_cols[0, 0]
    count = tile_count[0, 0].reshape(1)
    n_rowdev = lax.axis_size("row")
    n_coldev = lax.axis_size("col")
    local_blocks = features.shape[0] // width
    feat_half = features.shape[1]
    feat_index = lax.axis_index("feat")
    row_blocks = local_blocks * n_coldev
    col_blocks = local_blocks * n_rowdev
    node_total = features.shape[0] * n_rowdev * n_coldev
    pair = 2 if n_rowdev % 2 == 0 else 1
    chips = n_rowdev // pair
    if pair == 2:
        panel = row_gather(features, chips, 0).reshape(-1, feat_half)
    else:
        panel = exchange(features, "row", "gather", 0).reshape(-1, feat_half)

    def remap(col):
        owner = col // local_blocks
        return ((owner % pair) * chips + owner // pair) * local_blocks + col % local_blocks

    partial_value = tile_products(local_tiles, block_rows, block_cols, count, panel,
                                  row_blocks, transpose=False, remap=remap)
    weight_cols = lax.dynamic_slice_in_dim(weights, feat_index * feat_half, feat_half, 1)
    weight_rows = lax.dynamic_slice_in_dim(weights, feat_index * feat_half, feat_half, 0)
    hidden, spread_panel, weight_sum = layer_step(partial_value.reshape(n_coldev, -1, feat_half),
                                                  weight_cols, weight_rows, cotangent, 1,
                                                  node_total ** (-0.5))
    negative = jnp.minimum(hidden, 0.0)
    activated = jnp.where(hidden > 0, hidden, jnp.expm1(negative)).astype(jnp.bfloat16)
    spread_panel = spread_panel.reshape(-1, feat_half)
    weight_grad = weight_sum
    back_partial = tile_products(local_tiles, block_rows, block_cols, count, spread_panel,
                                 col_blocks, transpose=True, remap=remap)
    if pair == 2:
        back_summed = row_scatter(back_partial.reshape(pair, chips, -1, feat_half), chips, 3)
    else:
        back_summed = exchange(back_partial.reshape(n_rowdev, -1, feat_half), "row", "scatter", 3)
    return (activated, back_summed, weight_grad)


def solution(mesh):
    return jax.shard_map(
        shards,
        mesh=mesh,
        in_specs=(
            P(("col", "row"), "feat"),
            P("row", "col", None),
            P("row", "col", None),
            P("row", "col"),
            P("row", "col", None, None, None),
            P(),
            P(("row", "col"), "feat"),
        ),
        out_specs=(P(("row", "col"), "feat"), P(("col", "row"), "feat"), P("feat", None)),
        check_vma=False,
    )
```
